32 devices in a mesh: ctx: 8 (over z, x), wt: 4 (over y, core).
Axes of the slice: x: 2, y: 2, z: 4, core: 2. Of those that a mesh axis runs over, the one named last changes fastest.
Arguments:
- tokens: bfloat16 [8, 2048, 768], P('wt', 'ctx'), may hold values from -6 to 6
- documents: int32 [8, 2048], P('wt', 'ctx'), may hold values from 0 to 11, never falling along the last dimension, each value on 1 to 1280 neighbouring positions
- first_gain: bfloat16 [768], P('wt'), may hold values from 0.5 to 1.5
- query_weight: bfloat16 [768, 768], P('wt'), may hold values from -0.4375 to 0.4375
- shared_weight: bfloat16 [768, 128], P('wt'), may hold values from -0.21875 to 0.21875
- mixing_weight: bfloat16 [768, 768], P('wt'), may hold values from -0.875 to 0.875
- second_gain: bfloat16 [768], P('wt'), may hold values from 0.5 to 1.5
- up_weight: bfloat16 [768, 3072], P('wt'), may hold values from -0.21875 to 0.21875
- down_weight: bfloat16 [3072, 768], P('wt'), may hold values from -0.109375 to 0.109375
- cotangent: bfloat16 [8, 2048, 768], P('wt', 'ctx'), may hold values from -6 to 6
Outputs:
- layer_out: bfloat16 [8, 2048, 768], P('wt', 'ctx')
- input_grad: float32 [8, 2048, 768], P('wt', 'ctx')
- first_grad: float32 [768], P('wt')
- query_grad: float32 [768, 768], P('wt')
- shared_grad: float32 [768, 128], P('wt')
- mixing_grad: float32 [768, 768], P('wt')
- second_grad: float32 [768], P('wt')
- up_grad: float32 [768, 3072], P('wt')
- down_grad: float32 [3072, 768], P('wt')
The draws below stay inside these ranges and needn't reach their ends.
Inputs may be any that keep to these rules, and one draw needn't show every extreme that they name: `documents`: document numbers never fall along a sequence; each document holds 1 to 1280 positions, and one holds exactly 1280.
All inputs are finite; a program needn't handle non-finite values.
Results may differ from the reference program's by a relative error of at most 0.013.
The reference program's roundings to bfloat16 on the way count: a program that leaves them out, or rounds other values in their place, can miss the bound.
Values may be sent and summed in bfloat16 or wider, within the bound.
No kernel may reach another device: no remote copies, remote signals or barrier semaphores. Data moves between devices by JAX's collectives and lax.ppermute only.
A program may use at most 128 MiB of HBM per device.

```python
import math
import jax
import jax.numpy as jnp
import numpy as np
from jax import lax

D = 768
HEADS = 12
HEAD_DIM = 64
FF = 3072
DOCS = 12
QUERY_WIDTH = 768
LEN = 2048
SEQS = 8
DOC_MOST = 1280


def with_spikes(values, key, source, target, shards_of, factor):
    def block_of(position):
        return (jnp.arange(values.shape[position]) // (values.shape[position] // shards_of)).reshape((-1,) + (1,) * (values.ndim - 1 - position))

    first = jax.random.permutation(key, shards_of)[block_of(target)]
    far = (block_of(target) + shards_of // 2) % shards_of
    return jnp.where((block_of(source) == first) | (block_of(source) == far), factor * values, values)


def levels(rng, shape, split, least, high):
    def one(position, parts):
        steps = jax.random.uniform(jax.random.fold_in(jax.random.fold_in(rng, 6), position), (parts,), jnp.float32, least / len(split), high / len(split))
        return jnp.repeat(jnp.exp(steps), shape[position] // parts).reshape((-1,) + (1,) * (len(shape) - position - 1))

    level = one(*split[0])
    for cut in split[1:]:
        level = level * one(*cut)
    return level


def length_profile(count, total, limit, slope):
    weights = [(1 << 20) // math.isqrt(standing ** slope) + 1 for standing in range(2, count + 1)]
    rest, given = total - limit - (count - 1), [1] * (count - 1)
    while rest > 0:
        free = [i for i in range(count - 1) if given[i] < limit]
        pool, left = sum([weights[i] for i in free]), rest
        for i in free:
            addition = min(limit - given[i], max(1, left * weights[i] // pool), rest)
            given[i] = given[i] + addition
            rest = rest - addition
    return np.array([limit] + given)


def uneven(rng, count, total, bound, slope):
    if count == 2:
        one = jax.random.randint(rng, (), max(1, total - bound), min(bound, total - 1) + 1)
        return jnp.stack([one, total - one])
    tallies = jnp.asarray(length_profile(count, total, bound, slope), jnp.int32)
    twos = (count - 1) // 2
    donor, taker = tallies[1:1 + 2 * twos:2], tallies[2:2 + 2 * twos:2]
    slack = jnp.minimum(donor - 1, bound - taker)
    shifted = jax.random.randint(jax.random.fold_in(rng, 1), (twos,), 0, 1 << 20) % (slack + 1)
    tallies = tallies.at[1:1 + 2 * twos:2].set(donor - shifted).at[2:2 + 2 * twos:2].set(taker + shifted)
    return tallies[jax.random.permutation(jax.random.fold_in(rng, 2), count)]


def centred(stream_key, extent, scale, reach, shards=(), dtype=jnp.bfloat16):
    values = scale * jax.random.normal(stream_key, extent, jnp.float32)
    if shards:
        values = values * levels(stream_key, extent, shards, -0.22, 0.18)
    return jnp.clip(values, -reach, reach).astype(dtype)


def gaussian_with(rng, extent, width, most, cuts, heavy, held_as=jnp.bfloat16):
    values = width * jax.random.normal(rng, extent, jnp.float32)
    if cuts:
        values = values * levels(rng, extent, cuts, -0.22, 0.18)
    return jnp.clip(with_spikes(values, jax.random.fold_in(rng, 3), *heavy), -most, most).astype(held_as)


def setup_inputs(seed: int = 0) -> dict:
    splits = jax.random.split(jax.random.key(seed), 11)
    return {
        "tokens": centred(splits[0], (SEQS, LEN, D), 1.0, 6.0, ((0, 4), (1, 8))),
        "documents": jax.vmap(lambda own: jnp.searchsorted(jnp.cumsum(uneven(own, DOCS, LEN, DOC_MOST, 2)), jnp.arange(LEN), side="right"))(jax.random.split(splits[1], SEQS)).reshape((SEQS, LEN)).astype(jnp.int32),
        "first_gain": jnp.clip(1.0 + 0.1 * jax.random.normal(splits[2], (D,), jnp.float32), 0.5, 1.5).astype(jnp.bfloat16),
        "query_weight": centred(splits[3], (D, QUERY_WIDTH), (D // 4) ** -0.5, 0.4375, ((0, 4),)),
        "shared_weight": centred(splits[4], (D, 2 * HEAD_DIM), D ** -0.5, 0.21875, ((0, 4),)),
        "mixing_weight": centred(splits[5], (QUERY_WIDTH, D), (QUERY_WIDTH // 16) ** -0.5, 0.875, ((0, 4),)),
        "second_gain": jnp.clip(1.0 + 0.1 * jax.random.normal(splits[6], (D,), jnp.float32), 0.5, 1.5).astype(jnp.bfloat16),
        "up_weight": centred(splits[7], (D, FF), D ** -0.5, 0.21875, ((0, 4),)),
        "down_weight": centred(splits[8], (FF, D), FF ** -0.5, 0.109375, ((0, 4),)),
        "cotangent": gaussian_with(splits[9], (SEQS, LEN, D), 1.0, 6.0, ((0, 4), (1, 8)), (1, 2, 8, 2.0)),
    }


@jax.custom_vjp
def low(v):
    return lax.optimization_barrier(v.astype(jnp.bfloat16)).astype(jnp.float32)

@jax.custom_vjp
def low_back(v):
    return v

def low_keep(v):
    return (low(v), None)

def low_pass(kept, grad):
    return (grad,)

def back_keep(v):
    return (v, None)

def back_low(kept, grad):
    return (low(grad),)
low.defvjp(low_keep, low_pass)
low_back.defvjp(back_keep, back_low)

def layer_norm(values):
    center = values - lax.optimization_barrier(jnp.mean(values, axis=-1, keepdims=True))
    spread = lax.optimization_barrier(jnp.mean(center * center, axis=-1, keepdims=True))
    return center * lax.rsqrt(spread + 1e-05)

def product(operand, matrix):
    return jnp.einsum('...i,ij->...j', operand, matrix, precision=lax.Precision.HIGHEST)

def gelu_tanh(values):
    return jax.nn.gelu(values, approximate=True)

def attend_sequence(queries, keyvals, documents):
    block_len = min(512, LEN)
    block_count = LEN // block_len
    positions = jnp.arange(LEN).astype(jnp.int32)
    key_part = keyvals[:, :HEAD_DIM]
    value_part = keyvals[:, HEAD_DIM:]
    inverse_root = 1.0 / HEAD_DIM ** 0.5

    def one_block(begin_row):
        query_rows = lax.dynamic_slice_in_dim(queries, begin_row, block_len, 0)
        doc_rows = lax.dynamic_slice_in_dim(documents, begin_row, block_len, 0)
        row_places = begin_row + jnp.arange(block_len).astype(jnp.int32)
        scores = jnp.einsum('qhd,kd->qhk', query_rows, key_part, precision=lax.Precision.HIGHEST) * inverse_root
        scores = low_back(scores)
        allowed = (doc_rows[:, None, None] == documents[None, None, :]) & (row_places[:, None, None] >= positions[None, None, :])
        scores = jnp.where(allowed, scores, -1e+30)
        chances = low(jax.nn.softmax(scores, axis=-1))
        return jnp.einsum('qhk,kd->qhd', chances, value_part, precision=lax.Precision.HIGHEST)
    begins = (jnp.arange(block_count) * block_len).astype(jnp.int32)
    blocks = lax.map(jax.checkpoint(one_block), begins)
    return blocks.reshape(LEN, HEADS, HEAD_DIM)

def forward(inputs, first_gain, query_weight, shared_weight, mixing_weight, second_gain, up_weight, down_weight, documents):
    normed_one = layer_norm(inputs)
    scaled_one = low(normed_one * first_gain)
    queries = low(low_back(product(scaled_one, query_weight)))
    keyvals = low(low_back(product(scaled_one, shared_weight)))
    queries = queries.reshape(SEQS, LEN, HEADS, HEAD_DIM)
    attended = lax.map(lambda entries: attend_sequence(entries[0], entries[1], entries[2]), (queries, keyvals, documents))
    attended = low(low_back(attended.reshape(SEQS, LEN, QUERY_WIDTH)))
    hidden = inputs + low_back(product(attended, mixing_weight))
    normed_two = layer_norm(hidden)
    scaled_two = low(normed_two * second_gain)
    upper = low_back(product(scaled_two, up_weight))
    activation = low(gelu_tanh(upper))
    return hidden + product(activation, down_weight)

def reference(tokens, documents, first_gain, query_weight, shared_weight, mixing_weight, second_gain, up_weight, down_weight, cotangent):
    floats = (tokens.astype(jnp.float32), first_gain.astype(jnp.float32), query_weight.astype(jnp.float32), shared_weight.astype(jnp.float32), mixing_weight.astype(jnp.float32), second_gain.astype(jnp.float32), up_weight.astype(jnp.float32), down_weight.astype(jnp.float32))

    def wrapped(inputs, gain_one, weight_query, weight_shared, weight_mixing, gain_two, weight_up, weight_down):
        return forward(inputs, gain_one, weight_query, weight_shared, weight_mixing, gain_two, weight_up, weight_down, documents)
    result, pullback = jax.vjp(wrapped, *floats)
    gradients = pullback(cotangent.astype(jnp.float32))
    return (result.astype(jnp.bfloat16), gradients[0], gradients[1], gradients[2], gradients[3], gradients[4], gradients[5], gradients[6], gradients[7])
```

```python
import functools
import math

import jax
import jax.numpy as jnp
from jax import lax
from jax.experimental import pallas as pl
from jax.experimental.pallas import tpu as pltpu
from jax.sharding import PartitionSpec as P

HEADS = 12
HEAD_DIM = 64
PAIRS = HEADS // 2
LANES = 128
EPSILON = 1e-05
BIAS = -1e30
SCALE = math.log2(math.e) / HEAD_DIM**0.5
F32 = jnp.float32
BF16 = jnp.bfloat16
GELU_ROOT = math.sqrt(2.0 / math.pi)
GELU_CUBE = 0.044715


def params(*semantics):
    return pltpu.CompilerParams(
        dimension_semantics=semantics or None, vmem_limit_bytes=56 * 1024 * 1024
    )


def cost(flops, bytes_accessed, transcendentals=0):
    return pl.CostEstimate(
        flops=flops, bytes_accessed=bytes_accessed, transcendentals=transcendentals
    )


def dot_nn(a, b):
    return lax.dot_general(a, b, (((1,), (0,)), ((), ())), preferred_element_type=F32)


def dot_nt(a, b):
    return lax.dot_general(a, b, (((1,), (1,)), ((), ())), preferred_element_type=F32)


def dot_tn(a, b):
    return lax.dot_general(a, b, (((0,), (0,)), ((), ())), preferred_element_type=F32)


def normalize(values):
    center = values - jnp.mean(values, axis=-1, keepdims=True)
    spread = jnp.mean(center * center, axis=-1, keepdims=True)
    inverse = lax.rsqrt(spread + EPSILON)
    return center * inverse, inverse


def norm_back(grad, normed, inverse):
    mean_grad = jnp.mean(grad, axis=-1, keepdims=True)
    mean_both = jnp.mean(grad * normed, axis=-1, keepdims=True)
    return (grad - mean_grad - normed * mean_both) * inverse


def place_rows(spot, pieces, scratch):
    height = scratch.shape[0] // len(pieces)
    for r, piece in enumerate(pieces):
        begin = pl.multiple_of((spot ^ r) * height, height)
        scratch[pl.ds(begin, height), :] = piece[0:height, :]


STEP = 128


def over_rows(rows, run):
    def one(index, carried):
        run(pl.ds(pl.multiple_of(index * STEP, STEP), STEP))
        return carried

    lax.fori_loop(0, rows // STEP, one, 0)


def first_kernel(spot_ref, tokens, gain, *rest, pieces):
    weights = rest[:pieces]
    scaled_out, shared_out, weight = rest[pieces:]
    place_rows(spot_ref[0], weights, weight)

    def run(rows):
        normed, unused = normalize(tokens[rows, :].astype(F32))
        scaled = (normed * gain[...]).astype(BF16)
        scaled_out[rows, :] = scaled
        shared_out[rows, :] = dot_nn(scaled, weight[...]).astype(BF16)

    over_rows(tokens.shape[0], run)


def first_stage(spot, tokens, gain, weights):
    rows, width = tokens.shape
    columns = weights[0].shape[1]
    return pl.pallas_call(
        functools.partial(first_kernel, pieces=len(weights)),
        grid_spec=pltpu.PrefetchScalarGridSpec(
            num_scalar_prefetch=1,
            grid=(),
            in_specs=[pl.BlockSpec(memory_space=pltpu.VMEM)] * (2 + len(weights)),
            out_specs=[pl.BlockSpec(memory_space=pltpu.VMEM)] * 2,
            scratch_shapes=[pltpu.VMEM((width, columns), BF16)],
        ),
        out_shape=[
            jax.ShapeDtypeStruct((rows, width), BF16),
            jax.ShapeDtypeStruct((rows, columns), BF16),
        ],
        compiler_params=params(),
        cost_estimate=cost(2 * rows * width * columns, 4 * rows * width),
        name="first_norm",
    )(spot, tokens, gain, *weights)


def project_kernel(spot_ref, operand, *rest, pieces):
    weights = rest[:pieces]
    out, weight = rest[pieces:]
    place_rows(spot_ref[0], weights, weight)
    out[...] = dot_nn(operand[...], weight[...]).astype(out.dtype)


def project(spot, operand, weights):
    rows, width = operand.shape
    columns = weights[0].shape[1]
    return pl.pallas_call(
        functools.partial(project_kernel, pieces=len(weights)),
        grid_spec=pltpu.PrefetchScalarGridSpec(
            num_scalar_prefetch=1,
            grid=(),
            in_specs=[pl.BlockSpec(memory_space=pltpu.VMEM)] * (1 + len(weights)),
            out_specs=pl.BlockSpec(memory_space=pltpu.VMEM),
            scratch_shapes=[pltpu.VMEM((width, columns), BF16)],
        ),
        out_shape=jax.ShapeDtypeStruct((rows, columns), BF16),
        compiler_params=params(),
        cost_estimate=cost(2 * rows * width * columns, 4 * rows * width),
        name="project",
    )(spot, operand, *weights)


def low_lanes(shape):
    return lax.broadcasted_iota(jnp.int32, shape, len(shape) - 1) < HEAD_DIM


def swap_halves(values):
    return pltpu.roll(values, HEAD_DIM, 1)


def stacked_pairs(ref):
    return jnp.concatenate(
        [ref[0, :, p * LANES : (p + 1) * LANES] for p in range(PAIRS)], axis=0
    )


def tile_bias(starts, key_begin, row_begin, tile_rows, tile_keys):
    key_place = key_begin + lax.broadcasted_iota(jnp.int32, (tile_rows, tile_keys), 1)
    row_place = row_begin + lax.broadcasted_iota(jnp.int32, (tile_rows, tile_keys), 0)
    first = jnp.concatenate([starts] * (tile_keys // LANES), axis=1)
    allowed = (key_place >= first) & (key_place <= row_place)
    bias = jnp.where(allowed, 0.0, BIAS)
    bias = jnp.concatenate([bias, bias], axis=1)
    return jnp.concatenate([bias] * PAIRS, axis=0)


def attend_kernel(
    first_ref, last_ref, queries, starts, *rest, blocks, tile_rows, tile_keys
):
    keyvals = rest[:blocks]
    exact_out, rounded_out, logs_out = rest[blocks : blocks + 3]
    key_even, key_odd, value_even, value_odd, score_scratch, most, total = rest[blocks + 3 :]
    rows = keyvals[0].shape[1]
    seq, tile = pl.program_id(0), pl.program_id(1)

    @pl.when(tile == 0)
    def _():
        low = low_lanes((rows, LANES))
        for j in range(blocks):
            whole = keyvals[j][0].astype(F32)
            turned = swap_halves(whole)
            place = pl.ds(j * rows, rows)
            key_even[place, :] = jnp.where(low, whole, 0.0).astype(BF16)
            key_odd[place, :] = jnp.where(low, 0.0, turned).astype(BF16)
            value_even[place, 0:LANES] = jnp.where(low, turned, 0.0).astype(BF16)
            value_even[place, LANES:] = jnp.where(low, 1.0, 0.0).astype(BF16)
            value_odd[place, 0:LANES] = jnp.where(low, 0.0, whole).astype(BF16)
            value_odd[place, LANES:] = jnp.where(low, 0.0, 1.0).astype(BF16)

    row_begin = (blocks - 1) * rows + tile * tile_rows
    first, last = first_ref[seq, tile], last_ref[seq, tile]
    begin = first // tile_keys
    end = (row_begin + tile_rows - 1) // tile_keys + 1
    stacked = stacked_pairs(queries)
    most[...] = jnp.full_like(most, -3e38)

    def score_step(index, carried):
        key_begin = pl.multiple_of(index * tile_keys, tile_keys)
        place = pl.ds(key_begin, tile_keys)
        both = jnp.concatenate([key_even[place, :], key_odd[place, :]], axis=0)
        scores = dot_nt(stacked, both)
        whole = (key_begin >= last) & (key_begin + tile_keys - 1 <= row_begin)

        def keep(values):
            score_scratch[index - begin] = values
            half = []
            for h in range(2):
                part = values[:, h * tile_keys : h * tile_keys + LANES]
                for q in range(1, tile_keys // LANES):
                    at = h * tile_keys + q * LANES
                    part = jnp.maximum(part, values[:, at : at + LANES])
                half.append(part)
            most[...] = jnp.maximum(most[...], jnp.concatenate(half, axis=1))

        @pl.when(whole)
        def _():
            keep(scores)

        @pl.when(jnp.logical_not(whole))
        def _():
            keep(
                scores
                + tile_bias(starts[0], key_begin, row_begin, tile_rows, tile_keys)
            )

        return carried

    lax.fori_loop(begin, end, score_step, 0)
    stack = PAIRS * tile_rows
    for h in range(2):
        part = jnp.max(most[:, h * LANES : (h + 1) * LANES], axis=1, keepdims=True)
        most[:, h * LANES : (h + 1) * LANES] = jnp.broadcast_to(part, (stack, LANES))
    total[...] = jnp.zeros_like(total)

    def output_step(index, carried):
        place = pl.ds(pl.multiple_of(index * tile_keys, tile_keys), tile_keys)
        both = jnp.concatenate([value_even[place, :], value_odd[place, :]], axis=0)
        shift = jnp.concatenate(
            [most[:, 0:LANES]] * (tile_keys // LANES) + [most[:, LANES:]] * (tile_keys // LANES),
            axis=1,
        )
        powers = jnp.exp2((score_scratch[index - begin] - shift) * SCALE).astype(BF16)
        total[...] += dot_nn(powers, both)
        return carried

    lax.fori_loop(begin, end, output_step, 0)
    low = low_lanes((tile_rows, LANES))
    for p in range(PAIRS):
        at = pl.ds(p * tile_rows, tile_rows)
        lanes = slice(p * LANES, (p + 1) * LANES)
        sums = total[at, LANES:]
        out = total[at, 0:LANES] / sums
        exact_out[0, :, lanes] = out
        rounded_out[0, :, lanes] = out.astype(BF16)
        shift = jnp.where(low, most[at, 0:LANES], most[at, LANES:])
        logs_out[0, :, lanes] = shift * SCALE + jnp.log2(sums)


def attend_back_kernel(
    first_ref, last_ref, queries, starts, exact, logs, grads, *rest, blocks, tile_rows, tile_keys
):
    keyvals = rest[:blocks]
    grad_queries = rest[blocks]
    terms = rest[blocks + 1 : 2 * blocks + 1]
    (
        key_even, key_odd, value_even, value_odd,
        key_total, value_total, query_total,
        log_even, log_odd, delta_even, delta_odd,
    ) = rest[2 * blocks + 1 :]
    rows = keyvals[0].shape[1]
    seq, tile = pl.program_id(0), pl.program_id(1)

    @pl.when(tile == 0)
    def _():
        low = low_lanes((rows, LANES))
        for j in range(blocks):
            whole = keyvals[j][0].astype(F32)
            turned = swap_halves(whole)
            place = pl.ds(j * rows, rows)
            key_even[place, :] = jnp.where(low, whole, 0.0).astype(BF16)
            key_odd[place, :] = jnp.where(low, 0.0, turned).astype(BF16)
            value_even[place, :] = jnp.where(low, turned, 0.0).astype(BF16)
            value_odd[place, :] = jnp.where(low, 0.0, whole).astype(BF16)
        key_total[...] = jnp.zeros_like(key_total)
        value_total[...] = jnp.zeros_like(value_total)

    row_begin = (blocks - 1) * rows + tile * tile_rows
    first, last = first_ref[seq, tile], last_ref[seq, tile]
    begin = first // tile_keys
    end = (row_begin + tile_rows - 1) // tile_keys + 1
    stacked = stacked_pairs(queries)
    grad_stacked = stacked_pairs(grads)
    stacked_turned = stacked.T
    grad_turned = grad_stacked.T
    stack = PAIRS * tile_rows
    low = low_lanes((tile_rows, LANES))
    for p in range(PAIRS):
        at = pl.ds(p * tile_rows, tile_rows)
        lanes = slice(p * LANES, (p + 1) * LANES)
        log = logs[0, :, lanes]
        log_turned = swap_halves(log)
        log_even[at, :] = jnp.where(low, log, log_turned)
        log_odd[at, :] = jnp.where(low, log_turned, log)
        terms_here = exact[0, :, lanes] * grads[0, :, lanes].astype(F32)
        even = jnp.sum(jnp.where(low, terms_here, 0.0), axis=1, keepdims=True)
        odd = jnp.sum(jnp.where(low, 0.0, terms_here), axis=1, keepdims=True)
        delta_even[at, :] = jnp.broadcast_to(even, (tile_rows, LANES))
        delta_odd[at, :] = jnp.broadcast_to(odd, (tile_rows, LANES))
    query_total[...] = jnp.zeros_like(query_total)

    def step(index, carried):
        key_begin = pl.multiple_of(index * tile_keys, tile_keys)
        place = pl.ds(key_begin, tile_keys)
        keys = jnp.concatenate([key_even[place, :], key_odd[place, :]], axis=0)
        values = jnp.concatenate([value_even[place, :], value_odd[place, :]], axis=0)
        scores = dot_nt(stacked, keys)
        copies = tile_keys // LANES
        whole = (key_begin >= last) & (key_begin + tile_keys - 1 <= row_begin)
        log = jnp.concatenate([log_even[...]] * copies + [log_odd[...]] * copies, axis=1)
        delta = jnp.concatenate([delta_even[...]] * copies + [delta_odd[...]] * copies, axis=1)

        def update(scores):
            chances = jnp.exp2(scores * SCALE - log)
            grad_probs = dot_nt(grad_stacked, values)
            grad_scores = (chances * (grad_probs - delta)).astype(BF16)
            query_total[...] += dot_nn(grad_scores, keys)
            key_total[index] += dot_nn(stacked_turned, grad_scores)
            value_total[index] += dot_nn(grad_turned, chances.astype(BF16))

        @pl.when(whole)
        def _():
            update(scores)

        @pl.when(jnp.logical_not(whole))
        def _():
            update(
                scores
                + tile_bias(starts[0], key_begin, row_begin, tile_rows, tile_keys)
            )

        return carried

    lax.fori_loop(begin, end, step, 0)
    root = 1.0 / HEAD_DIM**0.5
    for p in range(PAIRS):
        at = pl.ds(p * tile_rows, tile_rows)
        lanes = slice(p * LANES, (p + 1) * LANES)
        grad_queries[0, :, lanes] = (query_total[at, :] * root).astype(BF16)

    @pl.when(tile == pl.num_programs(1) - 1)
    def _():
        per_block = rows // tile_keys
        for j in range(blocks):
            for i in range(per_block):
                index = j * per_block + i
                key = key_total[index]
                value = value_total[index]
                key = key[0:HEAD_DIM, 0:tile_keys] + key[HEAD_DIM:, tile_keys:]
                value = value[0:HEAD_DIM, 0:tile_keys] + value[HEAD_DIM:, tile_keys:]
                both = jnp.concatenate([key * root, value], axis=0)
                terms[j][0, i * tile_keys : (i + 1) * tile_keys, :] = both.T.astype(BF16)


def attention_sizes(rows, blocks):
    tile_rows = 128 if rows % 128 == 0 else rows
    tile_keys = 256 if rows % 256 == 0 else 128
    return tile_rows, tile_keys, blocks * rows // tile_keys


def attend(firsts, lasts, queries, starts, keyvals):
    seqs, rows, width = queries.shape
    blocks = len(keyvals)
    tile_rows, tile_keys, key_tiles = attention_sizes(rows, blocks)
    stack = PAIRS * tile_rows
    keys = blocks * rows
    row_spec = lambda lanes: pl.BlockSpec((1, tile_rows, lanes), lambda s, t, *_: (s, t, 0))
    key_spec = pl.BlockSpec((1, rows, LANES), lambda s, t, *_: (s, 0, 0))
    return pl.pallas_call(
        functools.partial(
            attend_kernel, blocks=blocks, tile_rows=tile_rows, tile_keys=tile_keys
        ),
        grid_spec=pltpu.PrefetchScalarGridSpec(
            num_scalar_prefetch=2,
            grid=(seqs, rows // tile_rows),
            in_specs=[row_spec(width), row_spec(LANES)] + [key_spec] * blocks,
            out_specs=[row_spec(width)] * 3,
            scratch_shapes=[
                pltpu.VMEM((keys, LANES), BF16),
                pltpu.VMEM((keys, LANES), BF16),
                pltpu.VMEM((keys, 2 * LANES), BF16),
                pltpu.VMEM((keys, 2 * LANES), BF16),
                pltpu.VMEM((key_tiles, stack, 2 * tile_keys), F32),
                pltpu.VMEM((stack, 2 * LANES), F32),
                pltpu.VMEM((stack, 2 * LANES), F32),
            ],
        ),
        out_shape=[
            jax.ShapeDtypeStruct((seqs, rows, width), F32),
            jax.ShapeDtypeStruct((seqs, rows, width), BF16),
            jax.ShapeDtypeStruct((seqs, rows, width), F32),
        ],
        compiler_params=params("arbitrary", "arbitrary"),
        cost_estimate=cost(16 * seqs * rows * keys * width, 12 * seqs * rows * width),
        name="attend",
    )(firsts, lasts, queries, starts, *keyvals)


def attend_back(firsts, lasts, queries, starts, exact, logs, grads, keyvals):
    seqs, rows, width = queries.shape
    blocks = len(keyvals)
    tile_rows, tile_keys, key_tiles = attention_sizes(rows, blocks)
    stack = PAIRS * tile_rows
    keys = blocks * rows
    row_spec = lambda lanes: pl.BlockSpec((1, tile_rows, lanes), lambda s, t, *_: (s, t, 0))
    key_spec = pl.BlockSpec((1, rows, LANES), lambda s, t, *_: (s, 0, 0))
    return pl.pallas_call(
        functools.partial(
            attend_back_kernel, blocks=blocks, tile_rows=tile_rows, tile_keys=tile_keys
        ),
        grid_spec=pltpu.PrefetchScalarGridSpec(
            num_scalar_prefetch=2,
            grid=(seqs, rows // tile_rows),
            in_specs=[row_spec(width), row_spec(LANES)]
            + [row_spec(width)] * 3
            + [key_spec] * blocks,
            out_specs=[row_spec(width)] + [key_spec] * blocks,
            scratch_shapes=[pltpu.VMEM((keys, LANES), BF16)] * 4
            + [pltpu.VMEM((key_tiles, LANES, 2 * tile_keys), F32)] * 2
            + [pltpu.VMEM((stack, LANES), F32)] * 5,
        ),
        out_shape=[jax.ShapeDtypeStruct((seqs, rows, width), BF16)]
        + [jax.ShapeDtypeStruct((seqs, rows, LANES), BF16)] * blocks,
        compiler_params=params("arbitrary", "arbitrary"),
        cost_estimate=cost(40 * seqs * rows * keys * width, 12 * seqs * rows * width),
        name="attend_back",
    )(firsts, lasts, queries, starts, exact, logs, grads, *keyvals)


def mix_kernel(spot_ref, attended, tokens, gain, *rest, pieces):
    weights = rest[:pieces]
    hidden_out, scaled_out, weight = rest[pieces:]
    place_rows(spot_ref[0], weights, weight)

    def run(rows):
        mixed = dot_nn(attended[rows, :], weight[...])
        hidden = tokens[rows, :].astype(F32) + mixed
        hidden_out[rows, :] = hidden
        normed, unused = normalize(hidden)
        scaled_out[rows, :] = (normed * gain[...]).astype(BF16)

    over_rows(tokens.shape[0], run)


def mix_stage(spot, attended, tokens, gain, weights):
    rows, width = tokens.shape
    return pl.pallas_call(
        functools.partial(mix_kernel, pieces=len(weights)),
        grid_spec=pltpu.PrefetchScalarGridSpec(
            num_scalar_prefetch=1,
            grid=(),
            in_specs=[pl.BlockSpec(memory_space=pltpu.VMEM)] * (3 + len(weights)),
            out_specs=[pl.BlockSpec(memory_space=pltpu.VMEM)] * 2,
            scratch_shapes=[pltpu.VMEM(attended.shape[1:] + (width,), BF16)],
        ),
        out_shape=[
            jax.ShapeDtypeStruct((rows, width), F32),
            jax.ShapeDtypeStruct((rows, width), BF16),
        ],
        compiler_params=params(),
        cost_estimate=cost(2 * rows * width * width, 8 * rows * width),
        name="mix",
    )(spot, attended, tokens, gain, *weights)


TILE = 256


def feed_kernel(spot_ref, scaled, cotangent, *rest, pieces, chunk, chunks):
    ups, downs = rest[:pieces], rest[pieces : 2 * pieces]
    rest = rest[2 * pieces :]
    if chunk:
        reduced_in, grads_in = rest[:2]
        rest = rest[2:]
    reduced_out, grads_out = rest[:2]
    keep_out, send_out = rest[2:4]
    up_tile, down_tile, up_sems, down_sems, up_term = rest[4:]
    spot = spot_ref[0]
    step = pl.program_id(0)
    width = scaled.shape[1]
    height = width // pieces
    groups = width // TILE

    def up_copy(s, r):
        column = pl.multiple_of(((spot ^ s) * chunks + chunk) * TILE, TILE)
        row = pl.multiple_of((spot ^ r) * height, height)
        return pltpu.make_async_copy(
            ups[r].at[:, pl.ds(column, TILE)],
            up_tile.at[s, pl.ds(row, height), :],
            up_sems.at[s, r],
        )

    def down_copy(s):
        return pltpu.make_async_copy(
            downs[s].at[pl.ds(chunk * TILE, TILE), :], down_tile.at[s], down_sems.at[s]
        )

    @pl.when(step == 0)
    def _():
        for s in range(pieces):
            for r in range(pieces):
                up_copy(s, r).start()
            down_copy(s).start()
        if chunk:
            reduced_out[...] = reduced_in[...]
            grads_out[...] = grads_in[...]
        else:
            reduced_out[...] = jnp.zeros_like(reduced_out)
            grads_out[...] = jnp.zeros_like(grads_out)

    for s in range(pieces):

        @pl.when(step == s)
        def _():
            for r in range(pieces):
                up_copy(s, r).wait()
            down_copy(s).wait()

    up = up_tile[step]
    down = down_tile[step]
    upper = dot_nn(scaled[...], up)
    grad_act = dot_nt(cotangent[...], down)
    square = upper * upper
    inner = jnp.tanh(GELU_ROOT * (upper + GELU_CUBE * upper * square))
    half = 0.5 * (1.0 + inner)
    slope = half + 0.5 * upper * (1.0 - inner * inner) * (
        GELU_ROOT * (1.0 + 3.0 * GELU_CUBE * square)
    )
    active = (upper * half).astype(BF16)
    grad_upper = (grad_act * slope).astype(BF16)
    reduced_out[...] += dot_nn(active, down)
    grads_out[...] += dot_nt(grad_upper, up)
    down_term = dot_tn(active, cotangent[...]).astype(BF16)
    up_term[...] = dot_tn(scaled[...], grad_upper)

    def place(s):
        return (keep_out if (s & 1) == 0 else send_out), s >> 1

    for s in range(pieces):

        @pl.when(step == s)
        def _():
            out, at = place(s)
            for g in range(groups):
                out[at, g * TILE : (g + 1) * TILE, :] = down_term[
                    :, g * TILE : (g + 1) * TILE
                ]

    row = pl.multiple_of(groups * TILE + (spot ^ step) * height, height)
    for s in range(pieces):
        out, at = place(s)
        begin = pl.multiple_of((spot ^ s) * height, height)
        out[at, pl.ds(row, height), :] = up_term[pl.ds(begin, height), :].astype(BF16)


def feed_stage(spot, scaled, cotangent, ups, downs, totals, chunk, chunks):
    rows, width = scaled.shape
    pieces = len(ups)
    height = width // pieces
    tall = width + pieces * height
    whole = pl.BlockSpec((rows, width), lambda i, *_: (0, 0))
    message = pl.BlockSpec((pieces // 2, tall, TILE), lambda i, *_: (0, 0, 0))
    message_shape = jax.ShapeDtypeStruct((pieces // 2, tall, TILE), BF16)
    count = 3 + 2 * pieces
    return pl.pallas_call(
        functools.partial(feed_kernel, pieces=pieces, chunk=chunk, chunks=chunks),
        grid_spec=pltpu.PrefetchScalarGridSpec(
            num_scalar_prefetch=1,
            grid=(pieces,),
            in_specs=[whole] * 2
            + [pl.BlockSpec(memory_space=pl.ANY)] * (2 * pieces)
            + [whole] * len(totals),
            out_specs=[whole] * 2 + [message] * 2,
            scratch_shapes=[
                pltpu.VMEM((pieces, width, TILE), BF16),
                pltpu.VMEM((pieces, TILE, width), BF16),
                pltpu.SemaphoreType.DMA((pieces, pieces)),
                pltpu.SemaphoreType.DMA((pieces,)),
                pltpu.VMEM((width, TILE), F32),
            ],
        ),
        out_shape=[jax.ShapeDtypeStruct((rows, width), F32)] * 2 + [message_shape] * 2,
        input_output_aliases={count: 0, count + 1: 1} if totals else {},
        compiler_params=params("arbitrary"),
        cost_estimate=cost(
            12 * rows * width * TILE * pieces, 12 * rows * width + 8 * tall * TILE * pieces
        ),
        name="feed",
    )(spot, scaled, cotangent, *ups, *downs, *totals)


def split_out(spot, pieces, source, keep_out, send_out, lanes):
    height = source.shape[0] // pieces
    for s in range(pieces):
        out = keep_out if (s & 1) == 0 else send_out
        begin = pl.multiple_of((spot ^ s) * height, height)
        out[s >> 1, :, lanes] = source[pl.ds(begin, height), :].astype(BF16)


def put_vector(pieces, vector, keep_out, send_out, begin):
    height = keep_out.shape[1]
    count = vector.shape[1] // LANES
    row = lax.broadcasted_iota(jnp.int32, (height, LANES), 0)
    block = jnp.zeros((height, LANES), F32)
    for i in range(count):
        block = jnp.where(row == i, vector[:, i * LANES : (i + 1) * LANES], block)
    for s in range(pieces):
        out = keep_out if (s & 1) == 0 else send_out
        out[s >> 1, :, begin : begin + LANES] = block.astype(BF16)


def after_kernel(spot_ref, hidden, reduced, grads, gain, cotangent, attended, *rest, pieces):
    weights = rest[:pieces]
    layer_out, grad_hidden_out, grad_attended_out, keep_out, send_out = rest[pieces : pieces + 5]
    weight, grad_mixed, sums, term = rest[pieces + 5 :]
    spot = spot_ref[0]
    width = hidden.shape[1]
    place_rows(spot, weights, weight)
    sums[...] = jnp.zeros_like(sums)

    def run(rows):
        values = hidden[rows, :]
        layer_out[rows, :] = (values + reduced[rows, :]).astype(BF16)
        normed, inverse = normalize(values)
        grad = grads[rows, :]
        sums[...] += jnp.sum((grad * normed).reshape(STEP // 8, 8, width), axis=0)
        grad_hidden = cotangent[rows, :].astype(F32) + norm_back(
            grad * gain[...], normed, inverse
        )
        grad_hidden_out[rows, :] = grad_hidden
        rounded = grad_hidden.astype(BF16)
        grad_mixed[rows, :] = rounded
        grad_attended_out[rows, :] = dot_nt(rounded, weight[...]).astype(BF16)

    over_rows(hidden.shape[0], run)
    term[...] = dot_tn(attended[...], grad_mixed[...])
    split_out(spot, pieces, term, keep_out, send_out, slice(0, width))
    put_vector(
        pieces, jnp.sum(sums[...], axis=0, keepdims=True), keep_out, send_out, width
    )


def after_stage(spot, hidden, reduced, grads, gain, cotangent, attended, weights):
    rows, width = hidden.shape
    pieces = len(weights)
    message = jax.ShapeDtypeStruct((pieces // 2, width // pieces, width + LANES), BF16)
    return pl.pallas_call(
        functools.partial(after_kernel, pieces=pieces),
        grid_spec=pltpu.PrefetchScalarGridSpec(
            num_scalar_prefetch=1,
            grid=(),
            in_specs=[pl.BlockSpec(memory_space=pltpu.VMEM)] * (6 + pieces),
            out_specs=[pl.BlockSpec(memory_space=pltpu.VMEM)] * 5,
            scratch_shapes=[
                pltpu.VMEM((width, width), BF16),
                pltpu.VMEM((rows, width), BF16),
                pltpu.VMEM((8, width), F32),
                pltpu.VMEM((width, width), F32),
            ],
        ),
        out_shape=[
            jax.ShapeDtypeStruct((rows, width), BF16),
            jax.ShapeDtypeStruct((rows, width), F32),
            jax.ShapeDtypeStruct((rows, width), BF16),
            message,
            message,
        ],
        compiler_params=params(),
        cost_estimate=cost(4 * rows * width * width, 24 * rows * width),
        name="after",
    )(spot, hidden, reduced, grads, gain, cotangent, attended, *weights)


def query_kernel(spot_ref, scaled, grad_queries, *rest, pieces):
    weights = rest[:pieces]
    grad_out, keep_out, send_out, weight, term = rest[pieces:]
    spot = spot_ref[0]
    width = scaled.shape[1]
    term[...] = dot_tn(scaled[...], grad_queries[...])
    split_out(spot, pieces, term, keep_out, send_out, slice(0, width))
    place_rows(spot, weights, weight)
    grad_out[...] = dot_nt(grad_queries[...], weight[...])


def query_stage(spot, scaled, grad_queries, weights):
    rows, width = scaled.shape
    pieces = len(weights)
    message = jax.ShapeDtypeStruct((pieces // 2, width // pieces, width), BF16)
    return pl.pallas_call(
        functools.partial(query_kernel, pieces=pieces),
        grid_spec=pltpu.PrefetchScalarGridSpec(
            num_scalar_prefetch=1,
            grid=(),
            in_specs=[pl.BlockSpec(memory_space=pltpu.VMEM)] * (2 + pieces),
            out_specs=[pl.BlockSpec(memory_space=pltpu.VMEM)] * 3,
            scratch_shapes=[
                pltpu.VMEM((width, width), BF16),
                pltpu.VMEM((width, width), F32),
            ],
        ),
        out_shape=[jax.ShapeDtypeStruct((rows, width), F32), message, message],
        compiler_params=params(),
        cost_estimate=cost(4 * rows * width * width, 12 * rows * width),
        name="query_grad",
    )(spot, scaled, grad_queries, *weights)


def last_kernel(spot_ref, tokens, gain, scaled, grad_shared, grad_scaled, grad_hidden, *rest, pieces):
    weights = rest[:pieces]
    input_grad, keep_out, send_out, weight, sums, term = rest[pieces:]
    spot = spot_ref[0]
    width = tokens.shape[1]
    place_rows(spot, weights, weight)
    sums[...] = jnp.zeros_like(sums)
    term[...] = dot_tn(scaled[...], grad_shared[...])
    split_out(spot, pieces, term, keep_out, send_out, slice(0, LANES))

    def run(rows):
        normed, inverse = normalize(tokens[rows, :].astype(F32))
        grad = grad_scaled[rows, :] + dot_nt(grad_shared[rows, :], weight[...])
        sums[...] += jnp.sum((grad * normed).reshape(STEP // 8, 8, width), axis=0)
        input_grad[rows, :] = grad_hidden[rows, :] + norm_back(
            grad * gain[...], normed, inverse
        )

    over_rows(tokens.shape[0], run)
    put_vector(
        pieces, jnp.sum(sums[...], axis=0, keepdims=True), keep_out, send_out, LANES
    )


def last_stage(spot, tokens, gain, scaled, grad_shared, grad_scaled, grad_hidden, weights):
    rows, width = tokens.shape
    pieces = len(weights)
    message = jax.ShapeDtypeStruct((pieces // 2, width // pieces, 2 * LANES), BF16)
    return pl.pallas_call(
        functools.partial(last_kernel, pieces=pieces),
        grid_spec=pltpu.PrefetchScalarGridSpec(
            num_scalar_prefetch=1,
            grid=(),
            in_specs=[pl.BlockSpec(memory_space=pltpu.VMEM)] * (6 + pieces),
            out_specs=[pl.BlockSpec(memory_space=pltpu.VMEM)] * 3,
            scratch_shapes=[
                pltpu.VMEM((width, LANES), BF16),
                pltpu.VMEM((8, width), F32),
                pltpu.VMEM((width, LANES), F32),
            ],
        ),
        out_shape=[jax.ShapeDtypeStruct((rows, width), F32), message, message],
        compiler_params=params(),
        cost_estimate=cost(4 * rows * width * LANES, 20 * rows * width),
        name="last",
    )(spot, tokens, gain, scaled, grad_shared, grad_scaled, grad_hidden, *weights)


def swap(values, axis, size, mask):
    return lax.ppermute(values, axis, [(i, i ^ mask) for i in range(size)])


def gather_pieces(piece, size):
    found = [piece]
    order = [0]
    mask = size // 2
    while mask:
        found = found + [swap(one, "wt", size, mask) for one in found]
        order = order + [r ^ mask for r in order]
        mask //= 2
    placed = [None] * size
    for r, one in zip(order, found):
        placed[r] = one
    return placed


def own_order(values, spot, size):
    mask = 1
    while mask < size:
        split = values.reshape((size // (2 * mask), 2, mask) + values.shape[1:])
        split = jnp.where((spot & mask) != 0, split[:, ::-1], split)
        values = split.reshape(values.shape)
        mask *= 2
    return values


def reduce_all(keep, send, place, sizes):
    wt_size, ctx_size = sizes
    half = swap(send, "wt", wt_size, 1)
    mask = wt_size // 2
    total = keep.astype(F32) + half.astype(F32)
    while mask > 1:
        count = total.shape[0] // 2
        sent = swap(total[count:].astype(BF16), "wt", wt_size, mask)
        total = total[:count] + sent.astype(F32)
        mask //= 2
    total = total[0]
    rows, lanes = total.shape
    total = total.reshape(2, rows // 2, lanes)
    low = place & 1
    sent = swap(
        lax.dynamic_index_in_dim(total, 1 - low, 0, False).astype(BF16), "ctx", ctx_size, 1
    )
    total = lax.dynamic_index_in_dim(total, low, 0, False) + sent.astype(F32)
    groups = ctx_size // 2
    high = place >> 1
    total = total.reshape(groups, rows // ctx_size, lanes)
    rounded = total.astype(BF16)
    result = lax.dynamic_index_in_dim(total, high, 0, False)
    for k in range(1, groups):
        sent = swap(
            lax.dynamic_index_in_dim(rounded, high ^ k, 0, False), "ctx", ctx_size, 2 * k
        )
        result = result + sent.astype(F32)
    result = result.astype(BF16)
    whole = jnp.zeros((groups,) + result.shape, BF16)
    whole = lax.dynamic_update_index_in_dim(whole, result, high, 0)
    for k in range(1, groups):
        whole = lax.dynamic_update_index_in_dim(
            whole, swap(result, "ctx", ctx_size, 2 * k), high ^ k, 0
        )
    other = swap(whole, "ctx", ctx_size, 1)
    both = jnp.where(low == 0, jnp.stack([whole, other]), jnp.stack([other, whole]))
    return both.reshape(rows, lanes).astype(F32)


def shift(values, size, k):
    pairs = [(i, i + k) for i in range(size - k)] if k > 0 else [(i, i + k) for i in range(-k, size)]
    return lax.ppermute(values, "ctx", pairs)


def body(
    tokens,
    documents,
    first_gain,
    query_weight,
    shared_weight,
    mixing_weight,
    second_gain,
    up_weight,
    down_weight,
    cotangent,
    *,
    wt_size,
    ctx_size,
):
    sizes = (wt_size, ctx_size)
    seqs, rows, width = tokens.shape
    count = seqs * rows
    spot_index = lax.axis_index("wt")
    place = lax.axis_index("ctx")
    spot = spot_index.astype(jnp.int32).reshape(1)
    length = ctx_size * rows
    doc_most = length * 5 // 8
    before = min(ctx_size - 1, -(-(doc_most - 1) // rows))
    blocks = before + 1
    height = width // wt_size

    gain_rows = -(-height // LANES)
    pad = lambda gain: jnp.pad(gain, (0, gain_rows * LANES - height)).reshape(gain_rows, LANES)
    small = jnp.concatenate([shared_weight, pad(first_gain), pad(second_gain)], axis=0)
    small = jnp.pad(small, ((0, -small.shape[0] % 16), (0, 0)))
    small_pieces = gather_pieces(small, wt_size)
    query_pieces = gather_pieces(query_weight, wt_size)
    mixing_pieces = gather_pieces(mixing_weight, wt_size)
    up_pieces = gather_pieces(up_weight, wt_size)
    down_pieces = gather_pieces(down_weight, wt_size)

    gains = jnp.stack([one[height : height + 2 * gain_rows] for one in small_pieces])
    gains = gains.reshape(wt_size, 2, gain_rows * LANES)[:, :, :height].astype(F32)
    gains = own_order(gains, spot_index, wt_size)
    gain_one = gains[:, 0].reshape(1, width)
    gain_two = gains[:, 1].reshape(1, width)

    window = [
        jnp.where(place >= k, shift(documents, ctx_size, k), -1) if k else documents
        for k in range(before, -1, -1)
    ]
    window = jnp.concatenate(window, axis=1)
    starts = jnp.sum(
        (window[:, None, :] < documents[:, :, None]).astype(jnp.int32), axis=-1
    )
    tile_rows = attention_sizes(rows, blocks)[0]
    firsts = starts[:, ::tile_rows]
    lasts = starts[:, tile_rows - 1 :: tile_rows]
    starts = jnp.broadcast_to(starts[:, :, None], (seqs, rows, LANES))

    inputs = tokens.reshape(count, width)
    scaled_one, shared = first_stage(spot, inputs, gain_one, small_pieces)
    shared = shared.reshape(seqs, rows, 2 * HEAD_DIM)
    keyvals = [shift(shared, ctx_size, k) for k in range(before, 0, -1)] + [shared]
    queries = project(spot, scaled_one, query_pieces).reshape(seqs, rows, width)

    exact, attended, logs = attend(firsts, lasts, queries, starts, keyvals)
    attended = attended.reshape(count, width)
    hidden, scaled_two = mix_stage(spot, attended, inputs, gain_two, mixing_pieces)

    grads_in = cotangent.reshape(count, width)
    chunks = up_weight.shape[1] // wt_size // TILE
    totals = ()
    messages = []
    for chunk in range(chunks):
        reduced, grads, keep, send = feed_stage(
            spot, scaled_two, grads_in, up_pieces, down_pieces, totals, chunk, chunks
        )
        totals = (reduced, grads)
        messages.append((keep, send))
    layer_out, grad_hidden, grad_attended, keep, send = after_stage(
        spot, hidden, reduced, grads, gain_two, grads_in, attended, mixing_pieces
    )
    feed_sums = [reduce_all(*message, place, sizes) for message in messages]
    mixing_sum = reduce_all(keep, send, place, sizes)

    grad_queries, *terms = attend_back(
        firsts,
        lasts,
        queries,
        starts,
        exact,
        logs,
        grad_attended.reshape(seqs, rows, width),
        keyvals,
    )
    grad_shared = terms[-1].astype(F32)
    for k in range(1, before + 1):
        grad_shared = grad_shared + shift(terms[before - k], ctx_size, -k).astype(F32)
    grad_shared = grad_shared.astype(BF16).reshape(count, 2 * HEAD_DIM)
    grad_scaled, keep, send = query_stage(
        spot, scaled_one, grad_queries.reshape(count, width), query_pieces
    )
    query_sum = reduce_all(keep, send, place, sizes)
    input_grad, keep, send = last_stage(
        spot, inputs, gain_one, scaled_one, grad_shared, grad_scaled, grad_hidden, small_pieces
    )
    shared_sum = reduce_all(keep, send, place, sizes)

    def own_gain(columns):
        vector = columns[: width // LANES].reshape(width)
        return lax.dynamic_slice_in_dim(vector, spot_index * height, height, 0)

    down_grad = jnp.stack(
        [one[:width].reshape(width // TILE, TILE, TILE).transpose(1, 0, 2) for one in feed_sums]
    ).reshape(chunks * TILE, width)
    up_grad = jnp.stack(
        [one[width:].reshape(wt_size, height, TILE).transpose(1, 0, 2) for one in feed_sums], axis=2
    ).reshape(height, wt_size * chunks * TILE)
    return (
        layer_out.reshape(seqs, rows, width),
        input_grad.reshape(seqs, rows, width),
        own_gain(shared_sum[:, LANES:]),
        query_sum,
        shared_sum[:, :LANES],
        mixing_sum[:, :width],
        own_gain(mixing_sum[:, width:]),
        up_grad,
        down_grad,
    )


def solution(mesh):
    in_specs = (
        P("wt", "ctx", None),
        P("wt", "ctx"),
        P("wt"),
        P("wt", None),
        P("wt", None),
        P("wt", None),
        P("wt"),
        P("wt", None),
        P("wt", None),
        P("wt", "ctx", None),
    )
    out_specs = (
        P("wt", "ctx", None),
        P("wt", "ctx", None),
        P("wt"),
        P("wt", None),
        P("wt", None),
        P("wt", None),
        P("wt"),
        P("wt", None),
        P("wt", None),
    )
    run = functools.partial(body, wt_size=mesh.shape["wt"], ctx_size=mesh.shape["ctx"])
    return jax.shard_map(run, mesh=mesh, in_specs=in_specs, out_specs=out_specs, check_vma=False)
```

```python
import functools
import math

import jax
import jax.numpy as jnp
from jax import lax
from jax.experimental import pallas as pl
from jax.experimental.pallas import tpu as pltpu
from jax.sharding import PartitionSpec as P

HEADS = 12
HEAD_DIM = 64
PAIRS = HEADS // 2
LANES = 128
EPSILON = 1e-05
BIAS = -1e30
SCALE = math.log2(math.e) / HEAD_DIM**0.5
F32 = jnp.float32
BF16 = jnp.bfloat16
GELU_ROOT = math.sqrt(2.0 / math.pi)
GELU_CUBE = 0.044715


def params(*semantics):
    return pltpu.CompilerParams(
        dimension_semantics=semantics or None, vmem_limit_bytes=56 * 1024 * 1024
    )


def weight():
    return pl.CostEstimate(flops=1, bytes_accessed=1, transcendentals=0)


def dot_nn(a, b):
    return lax.dot_general(a, b, (((1,), (0,)), ((), ())), preferred_element_type=F32)


def dot_nt(a, b):
    return lax.dot_general(a, b, (((1,), (1,)), ((), ())), preferred_element_type=F32)


def dot_tn(a, b):
    return lax.dot_general(a, b, (((0,), (0,)), ((), ())), preferred_element_type=F32)


def normalize(values):
    center = values - jnp.mean(values, axis=-1, keepdims=True)
    spread = jnp.mean(center * center, axis=-1, keepdims=True)
    inverse = lax.rsqrt(spread + EPSILON)
    return center * inverse, inverse


def norm_back(grad, normed, inverse):
    mean_grad = jnp.mean(grad, axis=-1, keepdims=True)
    mean_both = jnp.mean(grad * normed, axis=-1, keepdims=True)
    return (grad - mean_grad - normed * mean_both) * inverse


def place_rows(spot, pieces, scratch):
    height = scratch.shape[0] // len(pieces)
    for r, piece in enumerate(pieces):
        begin = pl.multiple_of((spot ^ r) * height, height)
        scratch[pl.ds(begin, height), :] = piece[0:height, :]


STEP = 128


def over_rows(rows, run):
    def one(index, carried):
        run(pl.ds(pl.multiple_of(index * STEP, STEP), STEP))
        return carried

    lax.fori_loop(0, rows // STEP, one, 0)


def first_kernel(spot_ref, tokens, gain, *rest, pieces):
    weights = rest[:pieces]
    scaled_out, shared_out, weight = rest[pieces:]
    place_rows(spot_ref[0], weights, weight)

    def run(rows):
        normed, unused = normalize(tokens[rows, :].astype(F32))
        scaled = (normed * gain[...]).astype(BF16)
        scaled_out[rows, :] = scaled
        shared_out[rows, :] = dot_nn(scaled, weight[...]).astype(BF16)

    over_rows(tokens.shape[0], run)


def first_stage(spot, tokens, gain, weights):
    rows, width = tokens.shape
    columns = weights[0].shape[1]
    return pl.pallas_call(
        functools.partial(first_kernel, pieces=len(weights)),
        grid_spec=pltpu.PrefetchScalarGridSpec(
            num_scalar_prefetch=1,
            grid=(),
            in_specs=[pl.BlockSpec(memory_space=pltpu.VMEM)] * (2 + len(weights)),
            out_specs=[pl.BlockSpec(memory_space=pltpu.VMEM)] * 2,
            scratch_shapes=[pltpu.VMEM((width, columns), BF16)],
        ),
        out_shape=[
            jax.ShapeDtypeStruct((rows, width), BF16),
            jax.ShapeDtypeStruct((rows, columns), BF16),
        ],
        compiler_params=params(),
        cost_estimate=weight(),
        name="first_norm",
    )(spot, tokens, gain, *weights)


def project_kernel(spot_ref, operand, *rest, pieces):
    weights = rest[:pieces]
    out, weight = rest[pieces:]
    place_rows(spot_ref[0], weights, weight)
    out[...] = dot_nn(operand[...], weight[...]).astype(out.dtype)


def project(spot, operand, weights):
    rows, width = operand.shape
    columns = weights[0].shape[1]
    return pl.pallas_call(
        functools.partial(project_kernel, pieces=len(weights)),
        grid_spec=pltpu.PrefetchScalarGridSpec(
            num_scalar_prefetch=1,
            grid=(),
            in_specs=[pl.BlockSpec(memory_space=pltpu.VMEM)] * (1 + len(weights)),
            out_specs=pl.BlockSpec(memory_space=pltpu.VMEM),
            scratch_shapes=[pltpu.VMEM((width, columns), BF16)],
        ),
        out_shape=jax.ShapeDtypeStruct((rows, columns), BF16),
        compiler_params=params(),
        cost_estimate=weight(),
        name="project",
    )(spot, operand, *weights)


def low_lanes(shape):
    return lax.broadcasted_iota(jnp.int32, shape, len(shape) - 1) < HEAD_DIM


def swap_halves(values):
    return pltpu.roll(values, HEAD_DIM, 1)


def stacked_pairs(ref):
    return jnp.concatenate(
        [ref[0, :, p * LANES : (p + 1) * LANES] for p in range(PAIRS)], axis=0
    )


def tile_bias(starts, key_begin, row_begin, tile_rows, tile_keys):
    key_place = key_begin + lax.broadcasted_iota(jnp.int32, (tile_rows, tile_keys), 1)
    row_place = row_begin + lax.broadcasted_iota(jnp.int32, (tile_rows, tile_keys), 0)
    first = jnp.concatenate([starts] * (tile_keys // LANES), axis=1)
    allowed = (key_place >= first) & (key_place <= row_place)
    bias = jnp.where(allowed, 0.0, BIAS)
    bias = jnp.concatenate([bias, bias], axis=1)
    return jnp.concatenate([bias] * PAIRS, axis=0)


def block_at(place_ref, j, blocks):
    return jnp.maximum(place_ref[0] - (blocks - 1) + j, 0)


def attend_kernel(
    first_ref, place_ref, queries, starts, keyvals, exact_out, rounded_out, logs_out,
    key_even, key_odd, value_even, value_odd, score_scratch, most, total,
    *, blocks, tile_rows, tile_keys
):
    rows = keyvals.shape[2]
    seq, tile = pl.program_id(0), pl.program_id(1)

    @pl.when(tile == 0)
    def _():
        low = low_lanes((rows, LANES))
        for j in range(blocks):
            whole = keyvals[block_at(place_ref, j, blocks), 0].astype(F32)
            turned = swap_halves(whole)
            place = pl.ds(j * rows, rows)
            key_even[place, :] = jnp.where(low, whole, 0.0).astype(BF16)
            key_odd[place, :] = jnp.where(low, 0.0, turned).astype(BF16)
            value_even[place, 0:LANES] = jnp.where(low, turned, 0.0).astype(BF16)
            value_even[place, LANES:] = jnp.where(low, 1.0, 0.0).astype(BF16)
            value_odd[place, 0:LANES] = jnp.where(low, 0.0, whole).astype(BF16)
            value_odd[place, LANES:] = jnp.where(low, 0.0, 1.0).astype(BF16)

    row_begin = (blocks - 1) * rows + tile * tile_rows
    begin = first_ref[seq, tile] // tile_keys
    end = (row_begin + tile_rows - 1) // tile_keys + 1
    stacked = stacked_pairs(queries)
    most[...] = jnp.full_like(most, -3e38)
    copies = tile_keys // LANES

    def score(index):
        key_begin = pl.multiple_of(index * tile_keys, tile_keys)
        place = pl.ds(key_begin, tile_keys)
        both = jnp.concatenate([key_even[place, :], key_odd[place, :]], axis=0)
        values = dot_nt(stacked, both) + tile_bias(
            starts[0], key_begin, row_begin, tile_rows, tile_keys
        )
        score_scratch[index - begin] = values
        half = []
        for h in range(2):
            part = values[:, h * tile_keys : h * tile_keys + LANES]
            for q in range(1, copies):
                at = h * tile_keys + q * LANES
                part = jnp.maximum(part, values[:, at : at + LANES])
            half.append(part)
        return jnp.concatenate(half, axis=1)

    def output(index):
        place = pl.ds(pl.multiple_of(index * tile_keys, tile_keys), tile_keys)
        both = jnp.concatenate([value_even[place, :], value_odd[place, :]], axis=0)
        shift = jnp.concatenate([most[:, 0:LANES]] * copies + [most[:, LANES:]] * copies, axis=1)
        powers = jnp.exp2((score_scratch[index - begin] - shift) * SCALE).astype(BF16)
        return dot_nn(powers, both)

    def in_pairs(one, join, total):
        def two(index, carried):
            at = begin + 2 * index
            total[...] = join(total[...], join(one(at), one(at + 1)))
            return carried

        count = end - begin
        lax.fori_loop(0, count // 2, two, 0)

        @pl.when(count % 2 == 1)
        def _():
            total[...] = join(total[...], one(end - 1))

    in_pairs(score, jnp.maximum, most)
    stack = PAIRS * tile_rows
    for h in range(2):
        part = jnp.max(most[:, h * LANES : (h + 1) * LANES], axis=1, keepdims=True)
        most[:, h * LANES : (h + 1) * LANES] = jnp.broadcast_to(part, (stack, LANES))
    total[...] = jnp.zeros_like(total)
    in_pairs(output, jnp.add, total)
    low = low_lanes((tile_rows, LANES))
    for p in range(PAIRS):
        at = pl.ds(p * tile_rows, tile_rows)
        lanes = slice(p * LANES, (p + 1) * LANES)
        sums = total[at, LANES:]
        out = total[at, 0:LANES] / sums
        exact_out[0, :, lanes] = out
        rounded_out[0, :, lanes] = out.astype(BF16)
        shift = jnp.where(low, most[at, 0:LANES], most[at, LANES:])
        logs_out[0, :, lanes] = shift * SCALE + jnp.log2(sums)


def attend_back_kernel(
    first_ref, place_ref, queries, starts, exact, logs, grads, keyvals, grad_queries, terms,
    *rest, seq, blocks, tile_rows, tile_keys
):
    (
        key_even, key_odd, value_even, value_odd,
        key_total, value_total, query_total,
        log_even, log_odd, delta_even, delta_odd,
    ) = rest
    rows = keyvals.shape[2]
    tile = pl.program_id(0)

    @pl.when(tile == 0)
    def _():
        low = low_lanes((rows, LANES))
        for j in range(blocks):
            whole = keyvals[block_at(place_ref, j, blocks), 0].astype(F32)
            turned = swap_halves(whole)
            place = pl.ds(j * rows, rows)
            key_even[place, :] = jnp.where(low, whole, 0.0).astype(BF16)
            key_odd[place, :] = jnp.where(low, 0.0, turned).astype(BF16)
            value_even[place, :] = jnp.where(low, turned, 0.0).astype(BF16)
            value_odd[place, :] = jnp.where(low, 0.0, whole).astype(BF16)
        key_total[...] = jnp.zeros_like(key_total)
        value_total[...] = jnp.zeros_like(value_total)

    row_begin = (blocks - 1) * rows + tile * tile_rows
    begin = first_ref[seq, tile] // tile_keys
    end = (row_begin + tile_rows - 1) // tile_keys + 1
    stacked = stacked_pairs(queries)
    grad_stacked = stacked_pairs(grads)
    stacked_turned = stacked.T
    grad_turned = grad_stacked.T
    stack = PAIRS * tile_rows
    low = low_lanes((tile_rows, LANES))
    for p in range(PAIRS):
        at = pl.ds(p * tile_rows, tile_rows)
        lanes = slice(p * LANES, (p + 1) * LANES)
        log = logs[0, :, lanes]
        log_turned = swap_halves(log)
        log_even[at, :] = jnp.where(low, log, log_turned)
        log_odd[at, :] = jnp.where(low, log_turned, log)
        terms_here = exact[0, :, lanes] * grads[0, :, lanes].astype(F32)
        even = jnp.sum(jnp.where(low, terms_here, 0.0), axis=1, keepdims=True)
        odd = jnp.sum(jnp.where(low, 0.0, terms_here), axis=1, keepdims=True)
        delta_even[at, :] = jnp.broadcast_to(even, (tile_rows, LANES))
        delta_odd[at, :] = jnp.broadcast_to(odd, (tile_rows, LANES))
    query_total[...] = jnp.zeros_like(query_total)

    def step(index, carried):
        key_begin = pl.multiple_of(index * tile_keys, tile_keys)
        place = pl.ds(key_begin, tile_keys)
        keys = jnp.concatenate([key_even[place, :], key_odd[place, :]], axis=0)
        values = jnp.concatenate([value_even[place, :], value_odd[place, :]], axis=0)
        copies = tile_keys // LANES
        log = jnp.concatenate([log_even[...]] * copies + [log_odd[...]] * copies, axis=1)
        delta = jnp.concatenate([delta_even[...]] * copies + [delta_odd[...]] * copies, axis=1)
        scores = dot_nt(stacked, keys) + tile_bias(
            starts[0], key_begin, row_begin, tile_rows, tile_keys
        )
        chances = jnp.exp2(scores * SCALE - log)
        grad_probs = dot_nt(grad_stacked, values)
        grad_scores = (chances * (grad_probs - delta)).astype(BF16)
        query_total[...] += dot_nn(grad_scores, keys)
        key_total[index] += dot_nn(stacked_turned, grad_scores)
        value_total[index] += dot_nn(grad_turned, chances.astype(BF16))
        return carried

    lax.fori_loop(begin, end, step, 0)
    root = 1.0 / HEAD_DIM**0.5
    for p in range(PAIRS):
        at = pl.ds(p * tile_rows, tile_rows)
        lanes = slice(p * LANES, (p + 1) * LANES)
        grad_queries[0, :, lanes] = (query_total[at, :] * root).astype(BF16)

    @pl.when(tile == pl.num_programs(0) - 1)
    def _():
        per_block = rows // tile_keys
        terms[...] = jnp.zeros_like(terms)

        def block_terms(j, carried):
            for i in range(per_block):
                index = j * per_block + i
                key = key_total[index]
                value = value_total[index]
                key = key[0:HEAD_DIM, 0:tile_keys] + key[HEAD_DIM:, tile_keys:]
                value = value[0:HEAD_DIM, 0:tile_keys] + value[HEAD_DIM:, tile_keys:]
                both = jnp.concatenate([key * root, value], axis=0)
                owner = block_at(place_ref, j, blocks)
                terms[owner, i * tile_keys : (i + 1) * tile_keys, :] = both.T.astype(BF16)
            return carried

        missing = jnp.maximum(blocks - 1 - place_ref[0], 0)
        lax.fori_loop(missing, blocks, block_terms, 0)


def attention_sizes(rows, blocks):
    tile_rows = 128 if rows % 128 == 0 else rows
    tile_keys = 256 if rows % 256 == 0 else 128
    return tile_rows, tile_keys, blocks * rows // tile_keys


def attend(firsts, place, queries, starts, keyvals, blocks):
    seqs, rows, width = queries.shape
    tile_rows, tile_keys, key_tiles = attention_sizes(rows, blocks)
    stack = PAIRS * tile_rows
    keys = blocks * rows
    row_spec = lambda lanes: pl.BlockSpec((1, tile_rows, lanes), lambda s, t, *_: (s, t, 0))
    return pl.pallas_call(
        functools.partial(
            attend_kernel, blocks=blocks, tile_rows=tile_rows, tile_keys=tile_keys
        ),
        grid_spec=pltpu.PrefetchScalarGridSpec(
            num_scalar_prefetch=2,
            grid=(seqs, rows // tile_rows),
            in_specs=[
                row_spec(width),
                row_spec(LANES),
                pl.BlockSpec((keyvals.shape[0], 1, rows, LANES), lambda s, t, *_: (0, s, 0, 0)),
            ],
            out_specs=[row_spec(width)] * 3,
            scratch_shapes=[
                pltpu.VMEM((keys, LANES), BF16),
                pltpu.VMEM((keys, LANES), BF16),
                pltpu.VMEM((keys, 2 * LANES), BF16),
                pltpu.VMEM((keys, 2 * LANES), BF16),
                pltpu.VMEM((key_tiles, stack, 2 * tile_keys), F32),
                pltpu.VMEM((stack, 2 * LANES), F32),
                pltpu.VMEM((stack, 2 * LANES), F32),
            ],
        ),
        out_shape=[
            jax.ShapeDtypeStruct((seqs, rows, width), F32),
            jax.ShapeDtypeStruct((seqs, rows, width), BF16),
            jax.ShapeDtypeStruct((seqs, rows, width), F32),
        ],
        compiler_params=params("arbitrary", "arbitrary"),
        cost_estimate=weight(),
        name="attend",
    )(firsts, place, queries, starts, keyvals)


def attend_back(
    seq, firsts, place, queries, starts, exact, logs, grads, keyvals, blocks
):
    seqs, rows, width = queries.shape
    ctx_size = keyvals.shape[0]
    tile_rows, tile_keys, key_tiles = attention_sizes(rows, blocks)
    stack = PAIRS * tile_rows
    keys = blocks * rows
    row_spec = lambda lanes: pl.BlockSpec((1, tile_rows, lanes), lambda t, *_: (seq, t, 0))
    return pl.pallas_call(
        functools.partial(
            attend_back_kernel, seq=seq, blocks=blocks, tile_rows=tile_rows, tile_keys=tile_keys
        ),
        grid_spec=pltpu.PrefetchScalarGridSpec(
            num_scalar_prefetch=2,
            grid=(rows // tile_rows,),
            in_specs=[row_spec(width), row_spec(LANES)]
            + [row_spec(width)] * 3
            + [pl.BlockSpec((ctx_size, 1, rows, LANES), lambda t, *_: (0, seq, 0, 0))],
            out_specs=[
                pl.BlockSpec((1, tile_rows, width), lambda t, *_: (0, t, 0)),
                pl.BlockSpec((ctx_size, rows, LANES), lambda t, *_: (0, 0, 0)),
            ],
            scratch_shapes=[pltpu.VMEM((keys, LANES), BF16)] * 4
            + [pltpu.VMEM((key_tiles, LANES, 2 * tile_keys), F32)] * 2
            + [pltpu.VMEM((stack, LANES), F32)] * 5,
        ),
        out_shape=[
            jax.ShapeDtypeStruct((1, rows, width), BF16),
            jax.ShapeDtypeStruct((ctx_size, rows, LANES), BF16),
        ],
        compiler_params=params("arbitrary"),
        cost_estimate=weight(),
        name="attend_back",
    )(firsts, place, queries, starts, exact, logs, grads, keyvals)


TILE = 256


def round_up(count, unit):
    return -(-count // unit) * unit


def mixing_rows(width, pieces, ctx_size):
    unit = 8 * ctx_size
    tall = 2 * width + width // pieces * (width // TILE)
    return round_up(tall + width // LANES, unit) - 2 * width


def message_of(keep, send, s):
    return (keep if (s & 1) == 0 else send), s >> 1


def split_out(spot, pieces, source, keep_out, send_out, first_row=0):
    height, lanes = source.shape[0] // pieces, keep_out.shape[2]
    across = min(lanes, source.shape[1])
    for s in range(pieces):
        out, at = message_of(keep_out, send_out, s)
        begin = pl.multiple_of((spot ^ s) * height, height)
        for g in range(source.shape[1] // across):
            row = first_row + g * height
            out[at, row : row + height, 0:across] = source[
                pl.ds(begin, height), g * lanes : g * lanes + across
            ].astype(BF16)


def put_vector(pieces, vector, keep_out, send_out, first_row, begin):
    height, lanes = keep_out.shape[1] - first_row, keep_out.shape[2]
    count = vector.shape[1] // LANES
    row = lax.broadcasted_iota(jnp.int32, (height, LANES), 0)
    block = jnp.zeros((height, LANES), F32)
    for i in range(count):
        block = jnp.where(row == i, vector[:, i * LANES : (i + 1) * LANES], block)
    for s in range(pieces):
        out, at = message_of(keep_out, send_out, s)
        out[at, first_row:, begin : begin + LANES] = block.astype(BF16)
        if begin == 0:
            out[at, first_row:, LANES:] = jnp.zeros((height, lanes - LANES), BF16)


def feed_kernel(spot_ref, *refs, pieces, chunk, chunks, names):
    use = dict(zip(names, refs))
    spot = spot_ref[0]
    step = pl.program_id(0)
    last_step = pl.num_programs(0) - 1
    first, last = chunk == 0, chunk == chunks - 1
    group = lambda key: [use[f"{key}{r}"] for r in range(pieces)]
    ups, downs, mixings = group("up"), group("down"), group("mixing") if first or last else None
    cotangent, keep_out, send_out = use["cotangent"], use["keep"], use["send"]
    reduced, grads, scaled, hidden = use["reduced"], use["grads"], use["scaled"], use["hidden"]
    up_tile, down_tile, up_sems, down_sems = (
        use["up_tile"], use["down_tile"], use["up_sems"], use["down_sems"]
    )
    rows, width = cotangent.shape
    height = width // pieces
    groups = width // TILE
    both = 2 * TILE

    def copies(at):
        for h in range(2):
            s = 2 * at + h
            column = pl.multiple_of(((spot ^ s) * chunks + chunk) * TILE, TILE)
            for r in range(pieces):
                row = pl.multiple_of((spot ^ r) * height, height)
                yield pltpu.make_async_copy(
                    ups[r].at[:, pl.ds(column, TILE)],
                    up_tile.at[at, pl.ds(row, height), pl.ds(h * TILE, TILE)],
                    up_sems.at[s, r],
                )
            yield pltpu.make_async_copy(
                downs[s].at[pl.ds(chunk * TILE, TILE), :],
                down_tile.at[at, pl.ds(h * TILE, TILE), :],
                down_sems.at[s],
            )

    @pl.when(step == 0)
    def _():
        for at in range(pieces // 2):
            for one in copies(at):
                one.start()
        if first or last:
            place_rows(spot, mixings, use["mixing_all"])
        if first:

            def begin(here):
                mixed = dot_nn(use["attended"][here, :], use["mixing_all"][...])
                values = use["tokens"][here, :].astype(F32) + mixed
                hidden[here, :] = values
                normed, unused = normalize(values)
                scaled[here, :] = (normed * use["gain"][...]).astype(BF16)

            over_rows(rows, begin)

    for at in range(pieces // 2):

        @pl.when(step == at)
        def _():
            for one in copies(at):
                one.wait()

    up = up_tile[step]
    down = down_tile[step]
    upper = dot_nn(scaled[...], up)
    grad_act = dot_nt(cotangent[...], down)
    square = upper * upper
    inner = jnp.tanh(GELU_ROOT * (upper + GELU_CUBE * upper * square))
    half = 0.5 * (1.0 + inner)
    slope = half + 0.5 * upper * (1.0 - inner * inner) * (
        GELU_ROOT * (1.0 + 3.0 * GELU_CUBE * square)
    )
    active = (upper * half).astype(BF16)
    grad_upper = (grad_act * slope).astype(BF16)
    reduced_here = dot_nn(active, down)
    grads_here = dot_nt(grad_upper, up)

    @pl.when(step == 0)
    def _():
        if first:
            reduced[...] = reduced_here
            grads[...] = grads_here
        else:
            reduced[...] = use["reduced_in"][...] + reduced_here
            grads[...] = use["grads_in"][...] + grads_here

    @pl.when(step > 0)
    def _():
        reduced[...] += reduced_here
        grads[...] += grads_here

    down_term = dot_tn(active, cotangent[...]).astype(BF16)
    for g in range(groups):
        column = slice(g * TILE, (g + 1) * TILE)
        keep_out[step, column, :] = down_term[0:TILE, column]
        send_out[step, column, :] = down_term[TILE:, column]
    up_term = use["up_term"]
    up_term[...] = dot_tn(scaled[...], grad_upper)
    for s in range(pieces):
        out, at = message_of(keep_out, send_out, s)
        begin = pl.multiple_of((spot ^ s) * height, height)
        for h in range(2):
            row = pl.multiple_of(groups * TILE + (spot ^ (2 * step + h)) * height, height)
            out[at, pl.ds(row, height), :] = up_term[
                pl.ds(begin, height), h * TILE : (h + 1) * TILE
            ].astype(BF16)

    if last:

        @pl.when(step == last_step)
        def _():
            sums, grad_mixed, term = use["sums"], use["grad_mixed"], use["term"]
            sums[...] = jnp.zeros_like(sums)

            def end(here):
                values = hidden[here, :]
                use["layer_out"][here, :] = (values + reduced[here, :]).astype(BF16)
                normed, inverse = normalize(values)
                grad = grads[here, :]
                sums[...] += jnp.sum((grad * normed).reshape(STEP // 8, 8, width), axis=0)
                grad_hidden = cotangent[here, :].astype(F32) + norm_back(
                    grad * use["gain"][...], normed, inverse
                )
                use["grad_hidden"][here, :] = grad_hidden
                rounded = grad_hidden.astype(BF16)
                grad_mixed[here, :] = rounded
                use["grad_attended"][here, :] = dot_nt(rounded, use["mixing_all"][...]).astype(
                    BF16
                )

            over_rows(rows, end)
            term[...] = dot_tn(use["attended"][...], grad_mixed[...])
            tall = 2 * width
            split_out(spot, pieces, term, keep_out, send_out, tall)
            put_vector(
                pieces,
                jnp.sum(sums[...], axis=0, keepdims=True),
                keep_out,
                send_out,
                tall + height * groups,
                0,
            )


def feed_stage(spot, arrays, ups, downs, mixings, chunk, chunks, ctx_size):
    first, last = chunk == 0, chunk == chunks - 1
    rows, width = arrays["cotangent"].shape
    pieces = len(ups)
    tall = 2 * width + (mixing_rows(width, pieces, ctx_size) if last else 0)
    wide = jax.ShapeDtypeStruct((rows, width), F32)
    narrow = jax.ShapeDtypeStruct((rows, width), BF16)
    message = jax.ShapeDtypeStruct((pieces // 2, tall, TILE), BF16)
    inputs, scratch = {}, {}
    inputs["cotangent"] = arrays["cotangent"]
    for r in range(pieces):
        inputs[f"up{r}"], inputs[f"down{r}"] = ups[r], downs[r]
    outputs = {"keep": message, "send": message}
    if first:
        for name in ("attended", "tokens", "gain"):
            inputs[name] = arrays[name]
        outputs.update(hidden=wide, scaled=narrow, reduced=wide, grads=wide)
    else:
        inputs["scaled"], inputs["hidden"] = arrays["scaled"], arrays["hidden"]
        inputs["reduced_in"], inputs["grads_in"] = arrays["reduced"], arrays["grads"]
        if not last:
            outputs.update(reduced=wide, grads=wide)
    if last:
        for name in ("attended", "gain"):
            inputs[name] = arrays[name]
        outputs.update(layer_out=narrow, grad_hidden=wide, grad_attended=narrow)
        scratch.update(
            reduced=pltpu.VMEM((rows, width), F32),
            grads=pltpu.VMEM((rows, width), F32),
            sums=pltpu.VMEM((8, width), F32),
            grad_mixed=pltpu.VMEM((rows, width), BF16),
            term=pltpu.VMEM((width, width), F32),
        )
    if first or last:
        for r in range(pieces):
            inputs[f"mixing{r}"] = mixings[r]
        scratch["mixing_all"] = pltpu.VMEM((width, width), BF16)
    scratch.update(
        up_tile=pltpu.VMEM((pieces // 2, width, 2 * TILE), BF16),
        down_tile=pltpu.VMEM((pieces // 2, 2 * TILE, width), BF16),
        up_sems=pltpu.SemaphoreType.DMA((pieces, pieces)),
        down_sems=pltpu.SemaphoreType.DMA((pieces,)),
        up_term=pltpu.VMEM((width, 2 * TILE), F32),
    )

    def spec(name, array):
        if name[:2] == "up" or name[:4] == "down" or (name == "hidden" and not (first or last)):
            return pl.BlockSpec(memory_space=pl.ANY)
        rank = len(array.shape)
        return pl.BlockSpec(
            array.shape, lambda i, *_: (0,) * rank, pipeline_mode=pl.Buffered(1)
        )

    results = pl.pallas_call(
        functools.partial(
            feed_kernel,
            pieces=pieces,
            chunk=chunk,
            chunks=chunks,
            names=(*inputs, *outputs, *scratch),
        ),
        grid_spec=pltpu.PrefetchScalarGridSpec(
            num_scalar_prefetch=1,
            grid=(pieces // 2,),
            in_specs=[spec(*one) for one in inputs.items()],
            out_specs=[spec(*one) for one in outputs.items()],
            scratch_shapes=list(scratch.values()),
        ),
        out_shape=list(outputs.values()),
        compiler_params=params("arbitrary"),
        cost_estimate=weight(),
        name=f"feed{chunk}",
    )(spot, *inputs.values())
    return {**arrays, **dict(zip(outputs, results))}


def query_kernel(spot_ref, scaled, *rest, pieces, seqs):
    grad_queries, weights = rest[:seqs], rest[seqs : seqs + pieces]
    grad_out, keep_out, send_out, weight, term = rest[seqs + pieces :]
    spot = spot_ref[0]
    rows = scaled.shape[0] // seqs
    place_rows(spot, weights, weight)
    for i, one in enumerate(grad_queries):
        here = slice(i * rows, (i + 1) * rows)
        part = dot_tn(scaled[here, :], one[...])
        term[...] = part if i == 0 else term[...] + part
        grad_out[here, :] = dot_nt(one[...], weight[...])
    split_out(spot, pieces, term, keep_out, send_out)


def query_stage(spot, scaled, grad_queries, weights, ctx_size):
    rows, width = scaled.shape
    pieces = len(weights)
    tall = round_up(width // pieces * (width // TILE), 8 * ctx_size)
    message = jax.ShapeDtypeStruct((pieces // 2, tall, TILE), BF16)
    return pl.pallas_call(
        functools.partial(query_kernel, pieces=pieces, seqs=len(grad_queries)),
        grid_spec=pltpu.PrefetchScalarGridSpec(
            num_scalar_prefetch=1,
            grid=(),
            in_specs=[pl.BlockSpec(memory_space=pltpu.VMEM)] * (1 + len(grad_queries) + pieces),
            out_specs=[pl.BlockSpec(memory_space=pltpu.VMEM)] * 3,
            scratch_shapes=[
                pltpu.VMEM((width, width), BF16),
                pltpu.VMEM((width, width), F32),
            ],
        ),
        out_shape=[jax.ShapeDtypeStruct((rows, width), F32), message, message],
        compiler_params=params(),
        cost_estimate=weight(),
        name="query_grad",
    )(spot, scaled, *grad_queries, *weights)


def last_kernel(spot_ref, tokens, gain, scaled, arrived, grad_scaled, grad_hidden, *rest, pieces):
    weights = rest[:pieces]
    input_grad, keep_out, send_out, weight, sums, term, grad_shared = rest[pieces:]
    spot = spot_ref[0]
    width = tokens.shape[1]
    place_rows(spot, weights, weight)
    sums[...] = jnp.zeros_like(sums)
    places, seqs, here, unused = arrived.shape
    for i in range(seqs):
        total = arrived[0, i].astype(F32)
        for j in range(1, places):
            total = total + arrived[j, i].astype(F32)
        grad_shared[i * here : (i + 1) * here, :] = total.astype(BF16)
    term[...] = dot_tn(scaled[...], grad_shared[...])
    split_out(spot, pieces, term, keep_out, send_out)

    def run(rows):
        normed, inverse = normalize(tokens[rows, :].astype(F32))
        grad = grad_scaled[rows, :] + dot_nt(grad_shared[rows, :], weight[...])
        sums[...] += jnp.sum((grad * normed).reshape(STEP // 8, 8, width), axis=0)
        input_grad[rows, :] = grad_hidden[rows, :] + norm_back(
            grad * gain[...], normed, inverse
        )

    over_rows(tokens.shape[0], run)
    put_vector(
        pieces, jnp.sum(sums[...], axis=0, keepdims=True), keep_out, send_out, 0, LANES
    )


def last_stage(spot, tokens, gain, scaled, arrived, grad_scaled, grad_hidden, weights):
    rows, width = tokens.shape
    pieces = len(weights)
    message = jax.ShapeDtypeStruct((pieces // 2, width // pieces, 2 * LANES), BF16)
    return pl.pallas_call(
        functools.partial(last_kernel, pieces=pieces),
        grid_spec=pltpu.PrefetchScalarGridSpec(
            num_scalar_prefetch=1,
            grid=(),
            in_specs=[pl.BlockSpec(memory_space=pltpu.VMEM)] * (6 + pieces),
            out_specs=[pl.BlockSpec(memory_space=pltpu.VMEM)] * 3,
            scratch_shapes=[
                pltpu.VMEM((width, LANES), BF16),
                pltpu.VMEM((8, width), F32),
                pltpu.VMEM((width, LANES), F32),
                pltpu.VMEM((rows, LANES), BF16),
            ],
        ),
        out_shape=[jax.ShapeDtypeStruct((rows, width), F32), message, message],
        compiler_params=params(),
        cost_estimate=weight(),
        name="last",
    )(spot, tokens, gain, scaled, arrived, grad_scaled, grad_hidden, *weights)


def final_kernel(place_ref, *refs, count, chunks, pieces, width):
    messages, refs = refs[:count], refs[count:]
    shared_sum, down_out, up_out, mixing_out, query_out, shared_out, first_out, second_out, whole = refs
    height = width // pieces
    groups = width // TILE
    low, high = place_ref[0] & 1, place_ref[0] >> 1

    def load(halves):
        deep, rows, unused = halves[0].shape
        for half, x in zip(halves, (low, 1 - low)):
            for k in range(deep):
                begin = pl.multiple_of((2 * (high ^ k) + x) * rows, 8)
                whole[pl.ds(begin, rows), :] = half[k].astype(F32)

    def columns(out, first_row, rows, out_row, step, across):
        for g in range(across):
            row = first_row + g * rows
            out[out_row : out_row + rows, g * step : g * step + TILE] = whole[row : row + rows, :]

    for chunk in range(chunks):
        load(messages[2 * chunk : 2 * chunk + 2])
        columns(down_out, 0, TILE, chunk * TILE, TILE, groups)
        for j in range(pieces):
            row = width + j * height
            column = (j * chunks + chunk) * TILE
            up_out[:, column : column + TILE] = whole[row : row + height, :]
    columns(mixing_out, 2 * width, height, 0, TILE, groups)
    row = 2 * width + groups * height
    second_out[...] = whole[row : row + second_out.shape[0], 0:LANES]
    load(messages[-2:])
    columns(query_out, 0, height, 0, TILE, groups)
    shared_out[...] = shared_sum[:, 0:LANES]
    first_out[...] = shared_sum[0 : first_out.shape[0], LANES:]


def final_stage(place, messages, shared_sum, chunks, pieces, width):
    height = width // pieces
    tallest = max(2 * one.shape[0] * one.shape[1] for one in messages)
    shape = lambda *dims: jax.ShapeDtypeStruct(dims, F32)
    vector = round_up(width // LANES, 8)
    return pl.pallas_call(
        functools.partial(
            final_kernel, count=len(messages), chunks=chunks, pieces=pieces, width=width
        ),
        grid_spec=pltpu.PrefetchScalarGridSpec(
            num_scalar_prefetch=1,
            grid=(),
            in_specs=[pl.BlockSpec(memory_space=pltpu.VMEM)] * (len(messages) + 1),
            out_specs=[pl.BlockSpec(memory_space=pltpu.VMEM)] * 7,
            scratch_shapes=[pltpu.VMEM((tallest, TILE), F32)],
        ),
        out_shape=[
            shape(chunks * TILE, width),
            shape(height, pieces * chunks * TILE),
            shape(height, width),
            shape(height, width),
            shape(height, LANES),
            shape(vector, LANES),
            shape(vector, LANES),
        ],
        compiler_params=params(),
        cost_estimate=weight(),
        name="final",
    )(place, *messages, shared_sum.reshape(height, 2 * LANES))


def swap(values, axis, size, mask):
    return lax.ppermute(values, axis, [(i, i ^ mask) for i in range(size)])


class Gather:
    def __init__(self, piece, size):
        self.size, self.own = size, piece
        self.far = swap(piece, "wt", size, 2)
        self.near = swap(piece, "wt", size, 1)

    def finish(self):
        return [self.own, self.near, self.far, swap(self.far, "wt", self.size, 1)]


def own_order(values, spot, size):
    mask = 1
    while mask < size:
        split = values.reshape((size // (2 * mask), 2, mask) + values.shape[1:])
        split = jnp.where((spot & mask) != 0, split[:, ::-1], split)
        values = split.reshape(values.shape)
        mask *= 2
    return values


class Reduction:
    def __init__(self, keep, send, place, sizes):
        self.wt_size, self.ctx_size = sizes
        self.groups = self.ctx_size // 2
        self.low, self.high = place & 1, place >> 1
        self.owners, self.rows, self.lanes = keep.shape
        split = (self.owners, self.groups, 2, self.rows // self.ctx_size, self.lanes)
        self.held = keep.reshape(split)
        self.sent = [send.reshape(split)]
        self.routes = [("wt", self.wt_size, 1)]
        self.coming = None

    def launch(self):
        if self.sent:
            self.coming = [swap(one, *route) for one, route in zip(self.sent, self.routes)]
            self.sent = []

    def add(self, pick):
        return pick(self.held).astype(F32) + pick(self.coming[0]).astype(F32)

    def y(self):
        self.held, self.sent = self.add(lambda v: v[0]), [self.add(lambda v: v[1]).astype(BF16)]
        self.routes = [("wt", self.wt_size, 2)]

    def x(self):
        low, axis = self.low, self.held.ndim - 3
        mine = lambda v: lax.dynamic_index_in_dim(v, low, axis, False)
        other = lambda v: lax.dynamic_index_in_dim(v, 1 - low, axis, False)
        self.held, self.sent = self.add(mine), [self.add(other).astype(BF16)]
        self.routes = [("ctx", self.ctx_size, 1)]

    def far(self):
        return [("ctx", self.ctx_size, 2 * k) for k in range(1, self.groups)]

    def z(self):
        pick = lambda k: lambda v: lax.dynamic_index_in_dim(v, self.high ^ k, 0, False)
        self.sent = [self.add(pick(k)).astype(BF16) for k in range(1, self.groups)]
        self.held = self.add(pick(0))
        self.routes = self.far()

    def total(self):
        parts = [self.held.astype(F32)] + [one.astype(F32) for one in self.coming]
        while len(parts) > 1:
            parts = [parts[i] + parts[i + 1] for i in range(0, len(parts), 2)]
        return parts[0]

    def z_back(self):
        self.held = self.total().astype(BF16)
        self.sent = [self.held] * (self.groups - 1)

    def x_back(self):
        self.held = jnp.stack([self.held] + self.coming)
        self.sent = [self.held]
        self.routes = [("ctx", self.ctx_size, 1)]

    def x_all(self):
        self.held = self.add(lambda v: v).astype(BF16)
        self.sent = [self.held]
        self.routes = [("ctx", self.ctx_size, 1)]

    def z_all(self):
        self.held = self.add(lambda v: v).astype(BF16)
        self.sent = [self.held] * (self.groups - 1)
        self.routes = self.far()


def tie(main, *reductions):
    state = [(one.held, one.sent) for one in reductions]
    main, state = lax.optimization_barrier((main, state))
    for one, (held, sent) in zip(reductions, state):
        one.held, one.sent = held, sent
        one.launch()
    return main


def shift(values, size, k):
    pairs = [(i, i + k) for i in range(size) if 0 <= i + k < size]
    return lax.ppermute(values, "ctx", pairs)


def body(
    tokens,
    documents,
    first_gain,
    query_weight,
    shared_weight,
    mixing_weight,
    second_gain,
    up_weight,
    down_weight,
    cotangent,
    *,
    wt_size,
    ctx_size,
):
    sizes = (wt_size, ctx_size)
    seqs, rows, width = tokens.shape
    count = seqs * rows
    spot_index = lax.axis_index("wt")
    place = lax.axis_index("ctx")
    spot = spot_index.astype(jnp.int32).reshape(1)
    length = ctx_size * rows
    doc_most = length * 5 // 8
    before = min(ctx_size - 1, -(-(doc_most - 1) // rows))
    blocks = before + 1
    height = width // wt_size
    chunks = up_weight.shape[1] // wt_size // TILE

    gain_rows = -(-height // LANES)
    pad = lambda gain: jnp.pad(gain, (0, gain_rows * LANES - height)).reshape(gain_rows, LANES)
    small = jnp.concatenate([shared_weight, pad(first_gain), pad(second_gain)], axis=0)
    small = jnp.pad(small, ((0, -small.shape[0] % 16), (0, 0)))
    small_pieces = Gather(small, wt_size).finish()
    query_gather = Gather(query_weight, wt_size)
    mixing_weight, small_pieces[2] = lax.optimization_barrier((mixing_weight, small_pieces[2]))
    mixing_gather = Gather(mixing_weight, wt_size)

    gains = jnp.stack([one[height : height + 2 * gain_rows] for one in small_pieces])
    gains = gains.reshape(wt_size, 2, gain_rows * LANES)[:, :, :height].astype(F32)
    gains = own_order(gains, spot_index, wt_size)
    gain_one = gains[:, 0].reshape(1, width)
    gain_two = gains[:, 1].reshape(1, width)

    inputs = tokens.reshape(count, width)
    scaled_one, shared = first_stage(spot, inputs, gain_one, small_pieces)
    keyvals = jnp.broadcast_to(
        shared.reshape(seqs, rows, 2 * HEAD_DIM), (ctx_size, seqs, rows, 2 * HEAD_DIM)
    )
    keyvals, documents = lax.optimization_barrier((keyvals, documents))
    keyvals = lax.all_to_all(keyvals, "ctx", 0, 0)
    scaled_late, up_weight, down_weight, query_gather.far, mixing_gather.far = (
        lax.optimization_barrier(
            (scaled_one, up_weight, down_weight, query_gather.far, mixing_gather.far)
        )
    )
    up_gather = Gather(up_weight, wt_size)
    down_gather = Gather(down_weight, wt_size)

    everywhere = jnp.broadcast_to(documents, (ctx_size, seqs, rows))
    everywhere = lax.all_to_all(everywhere, "ctx", 0, 0)
    starts = jnp.sum(
        (everywhere[:, :, None, :] < documents[None, :, :, None]).astype(jnp.int32), axis=(0, 3)
    )
    starts = starts - (place - before).astype(jnp.int32) * rows
    tile_rows = attention_sizes(rows, blocks)[0]
    firsts = starts[:, ::tile_rows]
    starts = jnp.broadcast_to(starts[:, :, None], (seqs, rows, LANES))

    query_pieces = query_gather.finish()
    queries = project(spot, scaled_one, query_pieces).reshape(seqs, rows, width)
    queries, mixing_gather.far = lax.optimization_barrier((queries, mixing_gather.far))
    mixing_pieces = mixing_gather.finish()
    place_one = place.astype(jnp.int32).reshape(1)

    exact, attended, logs = attend(firsts, place_one, queries, starts, keyvals, blocks)
    attended, up_gather.far, down_gather.far = lax.optimization_barrier(
        (attended, up_gather.far, down_gather.far)
    )
    up_pieces = up_gather.finish()
    down_pieces = down_gather.finish()

    arrays = {
        "attended": attended.reshape(count, width),
        "tokens": inputs,
        "gain": gain_two,
        "cotangent": cotangent.reshape(count, width),
    }
    feed = lambda chunk, arrays: feed_stage(
        spot, arrays, up_pieces, down_pieces, mixing_pieces, chunk, chunks, ctx_size
    )
    feeds = []
    for chunk in range(chunks):
        arrays = feed(chunk, arrays)
        feeds.append(Reduction(arrays["keep"], arrays["send"], place, sizes))
        if chunk == 0:
            arrays["scaled"] = tie(arrays["scaled"], *feeds)
        elif chunk < chunks - 1:
            arrays["scaled"] = tie(arrays["scaled"], *feeds)
            feeds[-2].y()
            arrays["scaled"] = tie(arrays["scaled"], *feeds)
    grad_attended = tie(arrays["grad_attended"], *feeds)
    feeds[0].x()
    feeds[1].y()
    grad_attended = tie(grad_attended, *feeds)
    grad_attended = grad_attended.reshape(seqs, rows, width)

    backs = []
    for seq in range(seqs):
        back = attend_back(
            seq, firsts, place_one, queries, starts, exact, logs, grad_attended, keyvals, blocks
        )
        back, grad_attended = tie((back, grad_attended), *feeds)
        backs.append(back)
        if seq == 0:
            feeds[0].z()
            feeds[1].x()
            feeds[2].y()
            grad_attended = tie(grad_attended, *feeds)
    grad_queries = [one[0][0] for one in backs]
    arriving = jnp.stack([one[1] for one in backs], axis=1)
    arriving, *grad_queries = tie((arriving, *grad_queries))
    arriving = lax.all_to_all(arriving, "ctx", 0, 0)
    feeds[0].z_back()
    feeds[1].z()
    grad_queries = tie(grad_queries, *feeds)
    grad_scaled, keep, send = query_stage(spot, scaled_late, grad_queries, query_pieces, ctx_size)
    query = Reduction(keep, send, place, sizes)
    grad_scaled = tie(grad_scaled, *feeds, query)
    feeds[2].x()
    query.y()
    grad_scaled = tie(grad_scaled, *feeds, query)
    input_grad, keep, send = last_stage(
        spot, inputs, gain_one, scaled_late, arriving, grad_scaled, arrays["grad_hidden"], small_pieces
    )
    shared = Reduction(keep, send, place, sizes)
    input_grad = tie(input_grad, *feeds, query, shared)
    feeds[2].z()
    shared.y()
    input_grad = tie(input_grad, *feeds, query, shared)
    feeds[1].z_back()
    query.x()
    shared.x_all()
    input_grad = tie(input_grad, *feeds, query, shared)
    feeds[2].z_back()
    query.z()
    input_grad = tie(input_grad, *feeds, query, shared)
    shared.z_all()
    feeds[0].x_back()
    feeds[1].x_back()
    input_grad = tie(input_grad, *feeds, query, shared)
    query.z_back()
    feeds[2].x_back()
    input_grad = tie(input_grad, *feeds, query, shared)
    query.x_back()
    query.launch()
    messages = []
    for one in (*feeds, query):
        messages += [one.held, one.coming[0]]
    down_grad, up_grad, mixing_grad, query_grad, shared_grad, first_grad, second_grad = final_stage(
        place_one, messages, shared.total(), chunks, wt_size, width
    )

    def own_gain(lines):
        vector = lines[: width // LANES].reshape(width)
        return lax.dynamic_slice_in_dim(vector, spot_index * height, height, 0)

    return (
        arrays["layer_out"].reshape(seqs, rows, width),
        input_grad.reshape(seqs, rows, width),
        own_gain(first_grad),
        query_grad,
        shared_grad,
        mixing_grad,
        own_gain(second_grad),
        up_grad,
        down_grad,
    )


def solution(mesh):
    in_specs = (
        P("wt", "ctx", None),
        P("wt", "ctx"),
        P("wt"),
        P("wt", None),
        P("wt", None),
        P("wt", None),
        P("wt"),
        P("wt", None),
        P("wt", None),
        P("wt", "ctx", None),
    )
    out_specs = (
        P("wt", "ctx", None),
        P("wt", "ctx", None),
        P("wt"),
        P("wt", None),
        P("wt", None),
        P("wt", None),
        P("wt"),
        P("wt", None),
        P("wt", None),
    )
    run = functools.partial(body, wt_size=mesh.shape["wt"], ctx_size=mesh.shape["ctx"])
    return jax.shard_map(run, mesh=mesh, in_specs=in_specs, out_specs=out_specs, check_vma=False)
```

```python
import functools
import math

import jax
import jax.numpy as jnp
from jax import lax
from jax.experimental import pallas as pl
from jax.experimental.pallas import tpu as pltpu
from jax.sharding import PartitionSpec as P

HEADS = 12
HEAD_DIM = 64
PAIRS = HEADS // 2
LANES = 128
EPSILON = 1e-05
BIAS = -1e30
SCALE = math.log2(math.e) / HEAD_DIM**0.5
F32 = jnp.float32
BF16 = jnp.bfloat16
GELU_ROOT = math.sqrt(2.0 / math.pi)
GELU_CUBE = 0.044715


def params(*semantics):
    return pltpu.CompilerParams(
        dimension_semantics=semantics or None, vmem_limit_bytes=56 * 1024 * 1024
    )


def weight():
    return pl.CostEstimate(flops=1, bytes_accessed=1, transcendentals=0)


def dot_nn(a, b):
    return lax.dot_general(a, b, (((1,), (0,)), ((), ())), preferred_element_type=F32)


def dot_nt(a, b):
    return lax.dot_general(a, b, (((1,), (1,)), ((), ())), preferred_element_type=F32)


def dot_tn(a, b):
    return lax.dot_general(a, b, (((0,), (0,)), ((), ())), preferred_element_type=F32)


def normalize(values):
    center = values - jnp.mean(values, axis=-1, keepdims=True)
    spread = jnp.mean(center * center, axis=-1, keepdims=True)
    inverse = lax.rsqrt(spread + EPSILON)
    return center * inverse, inverse


def norm_back(grad, normed, inverse):
    mean_grad = jnp.mean(grad, axis=-1, keepdims=True)
    mean_both = jnp.mean(grad * normed, axis=-1, keepdims=True)
    return (grad - mean_grad - normed * mean_both) * inverse


def place_rows(spot, pieces, scratch):
    height = scratch.shape[0] // len(pieces)
    for r, piece in enumerate(pieces):
        begin = pl.multiple_of((spot ^ r) * height, height)
        scratch[pl.ds(begin, height), :] = piece[0:height, :]


STEP = 128


def over_rows(rows, run):
    def one(index, carried):
        run(pl.ds(pl.multiple_of(index * STEP, STEP), STEP))
        return carried

    lax.fori_loop(0, rows // STEP, one, 0)


TILE = 256


def pack_kernel(up, down, *outs, chunks, pieces):
    width = down.shape[1]
    height = up.shape[0]
    for chunk, out in enumerate(outs):
        for g in range(width // TILE):
            out[g * TILE : (g + 1) * TILE, :] = down[
                chunk * TILE : (chunk + 1) * TILE, g * TILE : (g + 1) * TILE
            ]
        for j in range(pieces):
            row, column = width + j * height, (j * chunks + chunk) * TILE
            out[row : row + height, :] = up[:, column : column + TILE]


def pack_stage(up, down, chunks, pieces):
    width = down.shape[1]
    return pl.pallas_call(
        functools.partial(pack_kernel, chunks=chunks, pieces=pieces),
        in_specs=[pl.BlockSpec(memory_space=pltpu.VMEM)] * 2,
        out_specs=[pl.BlockSpec(memory_space=pltpu.VMEM)] * chunks,
        out_shape=[jax.ShapeDtypeStruct((2 * width, TILE), BF16)] * chunks,
        compiler_params=params(),
        cost_estimate=weight(),
        name="pack",
    )(up, down)


DOC_ROWS = 16


def first_kernel(spot_ref, tokens, gain, documents, *rest, pieces):
    weights = rest[:pieces]
    scaled_out, shared_out, weight = rest[pieces:]
    place_rows(spot_ref[0], weights, weight)
    seqs, doc_lines, unused = documents.shape
    places, tall, unused = shared_out.shape
    tall = tall // seqs
    rows = tall - DOC_ROWS
    per_seq = rows // STEP

    def run(index, carried):
        here = pl.ds(pl.multiple_of(index * STEP, STEP), STEP)
        seq = index // per_seq
        there = pl.multiple_of(seq * tall + (index - seq * per_seq) * STEP, DOC_ROWS)
        normed, unused = normalize(tokens[here, :].astype(F32))
        scaled = (normed * gain[...]).astype(BF16)
        scaled_out[here, :] = scaled
        shared = dot_nn(scaled, weight[...]).astype(BF16)

        def put(c, carried):
            shared_out[c, pl.ds(there, STEP), :] = shared
            return carried

        return lax.fori_loop(0, places, put, carried)

    lax.fori_loop(0, seqs * per_seq, run, 0)

    def put(c, carried):
        for seq in range(seqs):
            begin = seq * tall + rows
            shared_out[c, begin : begin + DOC_ROWS, :] = jnp.zeros((DOC_ROWS, LANES), BF16)
            shared_out[c, begin : begin + doc_lines, :] = documents[seq]
        return carried

    lax.fori_loop(0, places, put, 0)


def first_stage(spot, tokens, gain, documents, weights, places):
    count, width = tokens.shape
    columns = weights[0].shape[1]
    seqs, doc_lines, unused = documents.shape
    return pl.pallas_call(
        functools.partial(first_kernel, pieces=len(weights)),
        grid_spec=pltpu.PrefetchScalarGridSpec(
            num_scalar_prefetch=1,
            grid=(),
            in_specs=[pl.BlockSpec(memory_space=pltpu.VMEM)] * (3 + len(weights)),
            out_specs=[pl.BlockSpec(memory_space=pltpu.VMEM)] * 2,
            scratch_shapes=[pltpu.VMEM((width, columns), BF16)],
        ),
        out_shape=[
            jax.ShapeDtypeStruct((count, width), BF16),
            jax.ShapeDtypeStruct((places, count + seqs * DOC_ROWS, columns), BF16),
        ],
        compiler_params=params(),
        cost_estimate=weight(),
        name="first_norm",
    )(spot, tokens, gain, documents, *weights)


def low_lanes(shape):
    return lax.broadcasted_iota(jnp.int32, shape, len(shape) - 1) < HEAD_DIM


def swap_halves(values):
    return pltpu.roll(values, HEAD_DIM, 1)


def stacked_pairs(ref):
    return jnp.concatenate(
        [ref[0, :, p * LANES : (p + 1) * LANES] for p in range(PAIRS)], axis=0
    )


def tile_bias(starts, key_begin, row_begin, tile_rows, tile_keys):
    key_place = key_begin + lax.broadcasted_iota(jnp.int32, (tile_rows, tile_keys), 1)
    row_place = row_begin + lax.broadcasted_iota(jnp.int32, (tile_rows, tile_keys), 0)
    first = jnp.concatenate([starts] * (tile_keys // LANES), axis=1)
    allowed = (key_place >= first) & (key_place <= row_place)
    bias = jnp.where(allowed, 0.0, BIAS)
    bias = jnp.concatenate([bias, bias], axis=1)
    return jnp.concatenate([bias] * PAIRS, axis=0)


def block_at(place_ref, j, blocks):
    return jnp.maximum(place_ref[0] - (blocks - 1) + j, 0)


def attend_kernel(
    spot_ref, place_ref, scaled, marks, keyvals, *rest, blocks, tile_rows, tile_keys, pieces
):
    weights, rest = rest[:pieces], rest[pieces:]
    queries, starts_out, exact_out, rounded_out, logs_out = rest[:5]
    (
        key_even, key_odd, value_even, value_odd, score_scratch, most, total, weight_all, projected,
    ) = rest[5:]
    rows = keyvals.shape[2] - DOC_ROWS
    seq, tile = pl.program_id(0), pl.program_id(1)

    @pl.when((seq == 0) & (tile == 0))
    def _():
        place_rows(spot_ref[0], weights, weight_all)

    @pl.when(tile == 0)
    def _():
        projected[...] = dot_nn(scaled[...], weight_all[...]).astype(BF16)
        low = low_lanes((rows, LANES))
        for j in range(blocks):
            whole = keyvals[block_at(place_ref, j, blocks), 0, 0:rows, :].astype(F32)
            turned = swap_halves(whole)
            place = pl.ds(j * rows, rows)
            key_even[place, :] = jnp.where(low, whole, 0.0).astype(BF16)
            key_odd[place, :] = jnp.where(low, 0.0, turned).astype(BF16)
            value_even[place, 0:LANES] = jnp.where(low, turned, 0.0).astype(BF16)
            value_even[place, LANES:] = jnp.where(low, 1.0, 0.0).astype(BF16)
            value_odd[place, 0:LANES] = jnp.where(low, 0.0, whole).astype(BF16)
            value_odd[place, LANES:] = jnp.where(low, 0.0, 1.0).astype(BF16)

    queries[0] = projected[pl.ds(pl.multiple_of(tile * tile_rows, tile_rows), tile_rows), :]

    def smaller(j, count):
        lines = keyvals[block_at(place_ref, j, blocks), 0, rows:, :].astype(F32)
        missing = place_ref[0] - (blocks - 1) + j < 0
        for h in range(rows // LANES):
            line = jnp.where(missing, -1.0, lines[h : h + 1, :])
            count = count + jnp.where(line < marks[0], 1.0, 0.0)
        return count

    count = lax.fori_loop(0, blocks, smaller, jnp.zeros((tile_rows, LANES), F32))
    count = jnp.sum(count, axis=1, keepdims=True).astype(jnp.int32)
    starts = starts_out
    starts[0] = jnp.broadcast_to(count, (tile_rows, LANES))
    row_begin = (blocks - 1) * rows + tile * tile_rows
    begin = jnp.min(starts[0]) // tile_keys
    end = (row_begin + tile_rows - 1) // tile_keys + 1
    stacked = stacked_pairs(queries)
    most[...] = jnp.full_like(most, -3e38)
    copies = tile_keys // LANES

    def score(index):
        key_begin = pl.multiple_of(index * tile_keys, tile_keys)
        place = pl.ds(key_begin, tile_keys)
        both = jnp.concatenate([key_even[place, :], key_odd[place, :]], axis=0)
        values = dot_nt(stacked, both) + tile_bias(
            starts[0], key_begin, row_begin, tile_rows, tile_keys
        )
        score_scratch[index - begin] = values
        half = []
        for h in range(2):
            part = values[:, h * tile_keys : h * tile_keys + LANES]
            for q in range(1, copies):
                at = h * tile_keys + q * LANES
                part = jnp.maximum(part, values[:, at : at + LANES])
            half.append(part)
        return jnp.concatenate(half, axis=1)

    def output(index):
        place = pl.ds(pl.multiple_of(index * tile_keys, tile_keys), tile_keys)
        both = jnp.concatenate([value_even[place, :], value_odd[place, :]], axis=0)
        shift = jnp.concatenate([most[:, 0:LANES]] * copies + [most[:, LANES:]] * copies, axis=1)
        powers = jnp.exp2((score_scratch[index - begin] - shift) * SCALE).astype(BF16)
        return dot_nn(powers, both)

    def in_pairs(one, join, total):
        def two(index, carried):
            at = begin + 2 * index
            total[...] = join(total[...], join(one(at), one(at + 1)))
            return carried

        count = end - begin
        lax.fori_loop(0, count // 2, two, 0)

        @pl.when(count % 2 == 1)
        def _():
            total[...] = join(total[...], one(end - 1))

    in_pairs(score, jnp.maximum, most)
    stack = PAIRS * tile_rows
    for h in range(2):
        part = jnp.max(most[:, h * LANES : (h + 1) * LANES], axis=1, keepdims=True)
        most[:, h * LANES : (h + 1) * LANES] = jnp.broadcast_to(part, (stack, LANES))
    total[...] = jnp.zeros_like(total)
    in_pairs(output, jnp.add, total)
    low = low_lanes((tile_rows, LANES))
    for p in range(PAIRS):
        at = pl.ds(p * tile_rows, tile_rows)
        lanes = slice(p * LANES, (p + 1) * LANES)
        sums = total[at, LANES:]
        out = total[at, 0:LANES] / sums
        exact_out[0, :, lanes] = out
        rounded_out[0, :, lanes] = out.astype(BF16)
        shift = jnp.where(low, most[at, 0:LANES], most[at, LANES:])
        logs_out[0, :, lanes] = shift * SCALE + jnp.log2(sums)


def attend_back_kernel(
    place_ref, queries, starts, exact, logs, grads, keyvals, *rest,
    seq, blocks, tile_rows, tile_keys
):
    grad_queries, terms, *rest = rest[1:] if seq else rest
    (
        key_even, key_odd, value_even, value_odd,
        key_total, value_total, query_total,
        log_even, log_odd, delta_even, delta_odd,
    ) = rest
    rows = keyvals.shape[2] - DOC_ROWS
    tile = pl.program_id(0)

    @pl.when(tile == 0)
    def _():
        low = low_lanes((rows, LANES))
        for j in range(blocks):
            whole = keyvals[block_at(place_ref, j, blocks), 0, 0:rows, :].astype(F32)
            turned = swap_halves(whole)
            place = pl.ds(j * rows, rows)
            key_even[place, :] = jnp.where(low, whole, 0.0).astype(BF16)
            key_odd[place, :] = jnp.where(low, 0.0, turned).astype(BF16)
            value_even[place, :] = jnp.where(low, turned, 0.0).astype(BF16)
            value_odd[place, :] = jnp.where(low, 0.0, whole).astype(BF16)
        key_total[...] = jnp.zeros_like(key_total)
        value_total[...] = jnp.zeros_like(value_total)

    row_begin = (blocks - 1) * rows + tile * tile_rows
    begin = jnp.min(starts[0]) // tile_keys
    end = (row_begin + tile_rows - 1) // tile_keys + 1
    stacked = stacked_pairs(queries)
    grad_stacked = stacked_pairs(grads)
    stacked_turned = stacked.T
    grad_turned = grad_stacked.T
    stack = PAIRS * tile_rows
    low = low_lanes((tile_rows, LANES))
    for p in range(PAIRS):
        at = pl.ds(p * tile_rows, tile_rows)
        lanes = slice(p * LANES, (p + 1) * LANES)
        log = logs[0, :, lanes]
        log_turned = swap_halves(log)
        log_even[at, :] = jnp.where(low, log, log_turned)
        log_odd[at, :] = jnp.where(low, log_turned, log)
        terms_here = exact[0, :, lanes] * grads[0, :, lanes].astype(F32)
        even = jnp.sum(jnp.where(low, terms_here, 0.0), axis=1, keepdims=True)
        odd = jnp.sum(jnp.where(low, 0.0, terms_here), axis=1, keepdims=True)
        delta_even[at, :] = jnp.broadcast_to(even, (tile_rows, LANES))
        delta_odd[at, :] = jnp.broadcast_to(odd, (tile_rows, LANES))
    query_total[...] = jnp.zeros_like(query_total)

    def step(index, carried):
        key_begin = pl.multiple_of(index * tile_keys, tile_keys)
        place = pl.ds(key_begin, tile_keys)
        keys = jnp.concatenate([key_even[place, :], key_odd[place, :]], axis=0)
        values = jnp.concatenate([value_even[place, :], value_odd[place, :]], axis=0)
        copies = tile_keys // LANES
        log = jnp.concatenate([log_even[...]] * copies + [log_odd[...]] * copies, axis=1)
        delta = jnp.concatenate([delta_even[...]] * copies + [delta_odd[...]] * copies, axis=1)
        scores = dot_nt(stacked, keys) + tile_bias(
            starts[0], key_begin, row_begin, tile_rows, tile_keys
        )
        chances = jnp.exp2(scores * SCALE - log)
        grad_probs = dot_nt(grad_stacked, values)
        grad_scores = (chances * (grad_probs - delta)).astype(BF16)
        query_total[...] += dot_nn(grad_scores, keys)
        key_total[index] += dot_nn(stacked_turned, grad_scores)
        value_total[index] += dot_nn(grad_turned, chances.astype(BF16))
        return carried

    lax.fori_loop(begin, end, step, 0)
    root = 1.0 / HEAD_DIM**0.5
    for p in range(PAIRS):
        at = pl.ds(p * tile_rows, tile_rows)
        lanes = slice(p * LANES, (p + 1) * LANES)
        grad_queries[0, :, lanes] = (query_total[at, :] * root).astype(BF16)

    @pl.when(tile == pl.num_programs(0) - 1)
    def _():
        per_block = rows // tile_keys
        terms[...] = jnp.zeros_like(terms)

        def block_terms(j, carried):
            for i in range(per_block):
                index = j * per_block + i
                key = key_total[index]
                value = value_total[index]
                key = key[0:HEAD_DIM, 0:tile_keys] + key[HEAD_DIM:, tile_keys:]
                value = value[0:HEAD_DIM, 0:tile_keys] + value[HEAD_DIM:, tile_keys:]
                both = jnp.concatenate([key * root, value], axis=0)
                owner = block_at(place_ref, j, blocks)
                terms[owner, 0, i * tile_keys : (i + 1) * tile_keys, :] = both.T.astype(BF16)
            return carried

        missing = jnp.maximum(blocks - 1 - place_ref[0], 0)
        lax.fori_loop(missing, blocks, block_terms, 0)


def attention_sizes(rows, blocks):
    tile_rows = 128 if rows % 128 == 0 else rows
    tile_keys = 256 if rows % 256 == 0 else 128
    return tile_rows, tile_keys, blocks * rows // tile_keys


def attend(spot, place, scaled, marks, keyvals, weights, blocks):
    unused, seqs, tall, unused = keyvals.shape
    rows = tall - DOC_ROWS
    width = scaled.shape[1]
    tile_rows, tile_keys, key_tiles = attention_sizes(rows, blocks)
    stack = PAIRS * tile_rows
    keys = blocks * rows
    row_spec = lambda lanes: pl.BlockSpec((1, tile_rows, lanes), lambda s, t, *_: (s, t, 0))
    wide = lambda dtype: jax.ShapeDtypeStruct((seqs, rows, width), dtype)
    return pl.pallas_call(
        functools.partial(
            attend_kernel,
            blocks=blocks,
            tile_rows=tile_rows,
            tile_keys=tile_keys,
            pieces=len(weights),
        ),
        grid_spec=pltpu.PrefetchScalarGridSpec(
            num_scalar_prefetch=2,
            grid=(seqs, rows // tile_rows),
            in_specs=[
                pl.BlockSpec((rows, width), lambda s, t, *_: (s, 0)),
                row_spec(LANES),
                pl.BlockSpec((keyvals.shape[0], 1, tall, LANES), lambda s, t, *_: (0, s, 0, 0)),
            ]
            + [
                pl.BlockSpec(
                    (one.shape[0], width), lambda s, t, *_: (0, 0), pipeline_mode=pl.Buffered(1)
                )
                for one in weights
            ],
            out_specs=[row_spec(width), row_spec(LANES)] + [row_spec(width)] * 3,
            scratch_shapes=[
                pltpu.VMEM((keys, LANES), BF16),
                pltpu.VMEM((keys, LANES), BF16),
                pltpu.VMEM((keys, 2 * LANES), BF16),
                pltpu.VMEM((keys, 2 * LANES), BF16),
                pltpu.VMEM((key_tiles, stack, 2 * tile_keys), F32),
                pltpu.VMEM((stack, 2 * LANES), F32),
                pltpu.VMEM((stack, 2 * LANES), F32),
                pltpu.VMEM((width, width), BF16),
                pltpu.VMEM((rows, width), BF16),
            ],
        ),
        out_shape=[
            wide(BF16),
            jax.ShapeDtypeStruct((seqs, rows, LANES), jnp.int32),
            wide(F32),
            wide(BF16),
            wide(F32),
        ],
        compiler_params=params("arbitrary", "arbitrary"),
        cost_estimate=weight(),
        name="attend",
    )(spot, place, scaled, marks, keyvals, *weights)


def attend_back(
    seq, place, queries, starts, exact, logs, grads, keyvals, terms, blocks
):
    seqs, rows, width = queries.shape
    ctx_size = keyvals.shape[0]
    tile_rows, tile_keys, key_tiles = attention_sizes(rows, blocks)
    stack = PAIRS * tile_rows
    keys = blocks * rows
    row_spec = lambda lanes: pl.BlockSpec((1, tile_rows, lanes), lambda t, *_: (seq, t, 0))
    return pl.pallas_call(
        functools.partial(
            attend_back_kernel, seq=seq, blocks=blocks, tile_rows=tile_rows, tile_keys=tile_keys
        ),
        grid_spec=pltpu.PrefetchScalarGridSpec(
            num_scalar_prefetch=1,
            grid=(rows // tile_rows,),
            in_specs=[row_spec(width), row_spec(LANES)]
            + [row_spec(width)] * 3
            + [pl.BlockSpec((ctx_size, 1, keyvals.shape[2], LANES), lambda t, *_: (0, seq, 0, 0))]
            + [pl.BlockSpec(memory_space=pl.ANY)] * len(terms),
            out_specs=[
                pl.BlockSpec((1, tile_rows, width), lambda t, *_: (0, t, 0)),
                pl.BlockSpec((ctx_size, 1, rows, LANES), lambda t, *_: (0, seq, 0, 0)),
            ],
            scratch_shapes=[pltpu.VMEM((keys, LANES), BF16)] * 4
            + [pltpu.VMEM((key_tiles, LANES, 2 * tile_keys), F32)] * 2
            + [pltpu.VMEM((stack, LANES), F32)] * 5,
        ),
        out_shape=[
            jax.ShapeDtypeStruct((1, rows, width), BF16),
            jax.ShapeDtypeStruct((ctx_size, seqs, rows, LANES), BF16),
        ],
        input_output_aliases={7: 1} if terms else {},
        compiler_params=params("arbitrary"),
        cost_estimate=weight(),
        name="attend_back",
    )(place, queries, starts, exact, logs, grads, keyvals, *terms)


def round_up(count, unit):
    return -(-count // unit) * unit


def mixing_rows(width, pieces, ctx_size):
    unit = 8 * ctx_size
    tall = 2 * width + width // pieces * (width // TILE)
    return round_up(tall + width // LANES, unit) - 2 * width


def message_of(messages, s):
    return messages[s & 1], s >> 1


def split_out(spot, pieces, source, messages, first_row=0):
    height, lanes = source.shape[0] // pieces, messages[0].shape[2]
    across = min(lanes, source.shape[1])
    for s in range(pieces):
        out, at = message_of(messages, s)
        begin = pl.multiple_of((spot ^ s) * height, height)
        for g in range(source.shape[1] // across):
            row = first_row + g * height
            out[at, row : row + height, 0:across] = source[
                pl.ds(begin, height), g * lanes : g * lanes + across
            ].astype(BF16)


def put_vector(pieces, vector, messages, first_row, begin):
    height, lanes = messages[0].shape[1] - first_row, messages[0].shape[2]
    count = vector.shape[1] // LANES
    row = lax.broadcasted_iota(jnp.int32, (height, LANES), 0)
    block = jnp.zeros((height, LANES), F32)
    for i in range(count):
        block = jnp.where(row == i, vector[:, i * LANES : (i + 1) * LANES], block)
    for s in range(pieces):
        out, at = message_of(messages, s)
        out[at, first_row:, begin : begin + LANES] = block.astype(BF16)
        if begin == 0:
            out[at, first_row:, LANES:] = jnp.zeros((height, lanes - LANES), BF16)


def feed_kernel(spot_ref, *refs, pieces, part, first, last, names):
    use = dict(zip(names, refs))
    spot = spot_ref[0]
    step = pl.program_id(0)
    steps = len(part) * (pieces // 2)
    cotangent = use["cotangent"]
    reduced, grads, scaled, hidden = use["reduced"], use["grads"], use["scaled"], use["hidden"]
    up_tile, down_tile, up_sems, down_sems = (
        use["up_tile"], use["down_tile"], use["up_sems"], use["down_sems"]
    )
    rows, width = cotangent.shape
    height = width // pieces
    groups = width // TILE

    def messages_of(chunk):
        return use[f"keep{chunk}"], use[f"send{chunk}"]

    def owners(n):
        chunk, at = divmod(n, pieces // 2)
        return part[chunk], (2 * at, 2 * at + 1)

    def copies(n):
        chunk, pair = owners(n)
        for h, s in enumerate(pair):
            source = pl.multiple_of(width + (spot ^ s) * height, height)
            for r in range(pieces):
                row = pl.multiple_of((spot ^ r) * height, height)
                yield pltpu.make_async_copy(
                    use[f"message{chunk}_{r}"].at[pl.ds(source, height), :],
                    up_tile.at[n, pl.ds(row, height), pl.ds(h * TILE, TILE)],
                    up_sems.at[n, h, r],
                )
            for g in range(groups):
                yield pltpu.make_async_copy(
                    use[f"message{chunk}_{s}"].at[pl.ds(g * TILE, TILE), :],
                    down_tile.at[n, pl.ds(h * TILE, TILE), pl.ds(g * TILE, TILE)],
                    down_sems.at[n, h, g],
                )

    @pl.when(step == 0)
    def _():
        for n in range(steps):
            for one in copies(n):
                one.start()
        if first:

            def begin(here):
                mixed = dot_nn(use["attended"][here, :], use["mixing_all"][...])
                values = use["tokens"][here, :].astype(F32) + mixed
                hidden[here, :] = values
                normed, unused = normalize(values)
                scaled[here, :] = (normed * use["gain"][...]).astype(BF16)

            place_rows(spot, [use[f"mixing{r}"] for r in range(pieces)], use["mixing_all"])
            over_rows(rows, begin)

    for n in range(steps):

        @pl.when(step == n)
        def _():
            for one in copies(n):
                one.wait()

    up = up_tile[step]
    down = down_tile[step]
    upper = dot_nn(scaled[...], up)
    grad_act = dot_nt(cotangent[...], down)
    square = upper * upper
    inner = jnp.tanh(GELU_ROOT * (upper + GELU_CUBE * upper * square))
    half = 0.5 * (1.0 + inner)
    slope = half + 0.5 * upper * (1.0 - inner * inner) * (
        GELU_ROOT * (1.0 + 3.0 * GELU_CUBE * square)
    )
    active = (upper * half).astype(BF16)
    grad_upper = (grad_act * slope).astype(BF16)
    reduced_here = dot_nn(active, down)
    grads_here = dot_nt(grad_upper, up)

    @pl.when(step == 0)
    def _():
        if first:
            reduced[...] = reduced_here
            grads[...] = grads_here
        else:
            reduced[...] = use["reduced_in"][...] + reduced_here
            grads[...] = use["grads_in"][...] + grads_here

    @pl.when(step > 0)
    def _():
        reduced[...] += reduced_here
        grads[...] += grads_here

    down_term = dot_tn(active, cotangent[...]).astype(BF16)
    up_term = use["up_term"]
    up_term[...] = dot_tn(scaled[...], grad_upper)
    for n in range(steps):

        @pl.when(step == n)
        def _():
            chunk, pair = owners(n)
            messages = messages_of(chunk)
            for h, s in enumerate(pair):
                out, at = message_of(messages, s)
                for g in range(groups):
                    column = slice(g * TILE, (g + 1) * TILE)
                    out[at, column, :] = down_term[h * TILE : (h + 1) * TILE, column]
            for s in range(pieces):
                out, at = message_of(messages, s)
                begin = pl.multiple_of((spot ^ s) * height, height)
                for h, t in enumerate(pair):
                    row = pl.multiple_of(width + (spot ^ t) * height, height)
                    out[at, pl.ds(row, height), :] = up_term[
                        pl.ds(begin, height), h * TILE : (h + 1) * TILE
                    ].astype(BF16)

    if last:

        @pl.when(step == steps - 1)
        def _():
            sums, grad_mixed, term = use["sums"], use["grad_mixed"], use["term"]
            sums[...] = jnp.zeros_like(sums)
            place_rows(spot, [use[f"mixing{r}"] for r in range(pieces)], use["mixing_all"])

            def end(here):
                values = hidden[here, :]
                use["layer_out"][here, :] = (values + reduced[here, :]).astype(BF16)
                normed, inverse = normalize(values)
                grad = grads[here, :]
                sums[...] += jnp.sum((grad * normed).reshape(STEP // 8, 8, width), axis=0)
                grad_hidden = cotangent[here, :].astype(F32) + norm_back(
                    grad * use["gain"][...], normed, inverse
                )
                use["grad_hidden"][here, :] = grad_hidden
                rounded = grad_hidden.astype(BF16)
                grad_mixed[here, :] = rounded
                use["grad_attended"][here, :] = dot_nt(rounded, use["mixing_all"][...]).astype(
                    BF16
                )

            over_rows(rows, end)
            term[...] = dot_tn(use["attended"][...], grad_mixed[...])
            tall = 2 * width
            messages = messages_of(part[-1])
            split_out(spot, pieces, term, messages, tall)
            put_vector(
                pieces,
                jnp.sum(sums[...], axis=0, keepdims=True),
                messages,
                tall + height * groups,
                0,
            )


def feed_stage(spot, arrays, gathered, mixing_pieces, part, chunks, ctx_size):
    first, last = part[0] == 0, part[-1] == chunks - 1
    rows, width = arrays["cotangent"].shape
    pieces = len(gathered[part[0]])
    wide = jax.ShapeDtypeStruct((rows, width), F32)
    narrow = jax.ShapeDtypeStruct((rows, width), BF16)
    inputs, outputs, scratch = {}, {}, {}
    for chunk in part:
        more = mixing_rows(width, pieces, ctx_size) if chunk == chunks - 1 else 0
        message = jax.ShapeDtypeStruct((pieces // 2, 2 * width + more, TILE), BF16)
        outputs[f"keep{chunk}"] = outputs[f"send{chunk}"] = message
    inputs["cotangent"] = arrays["cotangent"]
    for chunk in part:
        for r in range(pieces):
            inputs[f"message{chunk}_{r}"] = gathered[chunk][r]
    for r in range(pieces):
        inputs[f"mixing{r}"] = mixing_pieces[r]
    scratch["mixing_all"] = pltpu.VMEM((width, width), BF16)
    if first:
        for name in ("attended", "tokens", "gain"):
            inputs[name] = arrays[name]
        outputs.update(hidden=wide, scaled=narrow, reduced=wide, grads=wide)
    if last:
        for name in ("attended", "gain", "scaled", "hidden"):
            inputs[name] = arrays[name]
        inputs["reduced_in"], inputs["grads_in"] = arrays["reduced"], arrays["grads"]
        outputs.update(layer_out=narrow, grad_hidden=wide, grad_attended=narrow)
        scratch.update(
            reduced=pltpu.VMEM((rows, width), F32),
            grads=pltpu.VMEM((rows, width), F32),
            sums=pltpu.VMEM((8, width), F32),
            grad_mixed=pltpu.VMEM((rows, width), BF16),
            term=pltpu.VMEM((width, width), F32),
        )
    steps = len(part) * (pieces // 2)
    scratch.update(
        up_tile=pltpu.VMEM((steps, width, 2 * TILE), BF16),
        down_tile=pltpu.VMEM((steps, 2 * TILE, width), BF16),
        up_sems=pltpu.SemaphoreType.DMA((steps, 2, pieces)),
        down_sems=pltpu.SemaphoreType.DMA((steps, 2, width // TILE)),
        up_term=pltpu.VMEM((width, 2 * TILE), F32),
    )

    def spec(name, array):
        if name[:7] == "message":
            return pl.BlockSpec(memory_space=pl.ANY)
        once = pl.Buffered(1)
        rank = len(array.shape)
        return pl.BlockSpec(array.shape, lambda i, *_: (0,) * rank, pipeline_mode=once)

    results = pl.pallas_call(
        functools.partial(
            feed_kernel,
            pieces=pieces,
            part=part,
            first=first,
            last=last,
            names=(*inputs, *outputs, *scratch),
        ),
        grid_spec=pltpu.PrefetchScalarGridSpec(
            num_scalar_prefetch=1,
            grid=(steps,),
            in_specs=[spec(*one) for one in inputs.items()],
            out_specs=[spec(*one) for one in outputs.items()],
            scratch_shapes=list(scratch.values()),
        ),
        out_shape=list(outputs.values()),
        compiler_params=params("arbitrary"),
        cost_estimate=weight(),
        name=f"feed{part[0]}",
    )(spot, *inputs.values())
    return {**arrays, **dict(zip(outputs, results))}


def query_kernel(spot_ref, scaled, *rest, pieces, seqs):
    grad_queries, weights = rest[:seqs], rest[seqs : seqs + pieces]
    grad_out, keep_out, send_out, weight, term = rest[seqs + pieces :]
    spot = spot_ref[0]
    rows = scaled.shape[0] // seqs
    place_rows(spot, weights, weight)
    for i, one in enumerate(grad_queries):
        here = slice(i * rows, (i + 1) * rows)
        part = dot_tn(scaled[here, :], one[...])
        term[...] = part if i == 0 else term[...] + part
        grad_out[here, :] = dot_nt(one[...], weight[...])
    split_out(spot, pieces, term, (keep_out, send_out))


def query_stage(spot, scaled, grad_queries, weights, ctx_size):
    rows, width = scaled.shape
    pieces = len(weights)
    tall = round_up(width // pieces * (width // TILE), 8 * ctx_size)
    message = jax.ShapeDtypeStruct((pieces // 2, tall, TILE), BF16)
    outs = [jax.ShapeDtypeStruct((rows, width), F32), message, message]
    whole = lambda one: pl.BlockSpec(one.shape, lambda i, *_: (0,) * len(one.shape))
    return pl.pallas_call(
        functools.partial(query_kernel, pieces=pieces, seqs=len(grad_queries)),
        grid_spec=pltpu.PrefetchScalarGridSpec(
            num_scalar_prefetch=1,
            grid=(1,),
            in_specs=[whole(scaled)]
            + [whole(one) for one in grad_queries]
            + [pl.BlockSpec((width // pieces, width), lambda i, *_: (0, 0))] * pieces,
            out_specs=[whole(one) for one in outs],
            scratch_shapes=[
                pltpu.VMEM((width, width), BF16),
                pltpu.VMEM((width, width), F32),
            ],
        ),
        out_shape=outs,
        compiler_params=params(),
        cost_estimate=weight(),
        name="query_grad",
    )(spot, scaled, *grad_queries, *weights)


def last_kernel(spot_ref, tokens, gain, scaled, arrived, grad_scaled, grad_hidden, *rest, pieces):
    weights = rest[:pieces]
    input_grad, keep_out, send_out, weight, sums, term, grad_shared = rest[pieces:]
    spot = spot_ref[0]
    width = tokens.shape[1]
    place_rows(spot, weights, weight)
    sums[...] = jnp.zeros_like(sums)
    places, seqs, here, unused = arrived.shape
    for i in range(seqs):
        total = arrived[0, i].astype(F32)
        for j in range(1, places):
            total = total + arrived[j, i].astype(F32)
        grad_shared[i * here : (i + 1) * here, :] = total.astype(BF16)
    term[...] = dot_tn(scaled[...], grad_shared[...])
    split_out(spot, pieces, term, (keep_out, send_out))

    def run(rows):
        normed, inverse = normalize(tokens[rows, :].astype(F32))
        grad = grad_scaled[rows, :] + dot_nt(grad_shared[rows, :], weight[...])
        sums[...] += jnp.sum((grad * normed).reshape(STEP // 8, 8, width), axis=0)
        input_grad[rows, :] = grad_hidden[rows, :] + norm_back(
            grad * gain[...], normed, inverse
        )

    over_rows(tokens.shape[0], run)
    put_vector(
        pieces, jnp.sum(sums[...], axis=0, keepdims=True), (keep_out, send_out), 0, LANES
    )


def last_stage(spot, tokens, gain, scaled, arrived, grad_scaled, grad_hidden, weights):
    rows, width = tokens.shape
    pieces, places = len(weights), arrived.shape[0]
    message = jax.ShapeDtypeStruct(
        (pieces // 2, round_up(width // pieces, 8 * places), 2 * LANES), BF16
    )
    return pl.pallas_call(
        functools.partial(last_kernel, pieces=pieces),
        grid_spec=pltpu.PrefetchScalarGridSpec(
            num_scalar_prefetch=1,
            grid=(),
            in_specs=[pl.BlockSpec(memory_space=pltpu.VMEM)] * (6 + pieces),
            out_specs=[pl.BlockSpec(memory_space=pltpu.VMEM)] * 3,
            scratch_shapes=[
                pltpu.VMEM((width, LANES), BF16),
                pltpu.VMEM((8, width), F32),
                pltpu.VMEM((width, LANES), F32),
                pltpu.VMEM((rows, LANES), BF16),
            ],
        ),
        out_shape=[jax.ShapeDtypeStruct((rows, width), F32), message, message],
        compiler_params=params(),
        cost_estimate=weight(),
        name="last",
    )(spot, tokens, gain, scaled, arrived, grad_scaled, grad_hidden, *weights)


def final_kernel(
    place_ref, early_own, early_other, last_own, last_other, late,
    down_out, up_out, mixing_out, query_out, shared_out, first_out, second_out, whole,
    *, chunks, pieces, width, query_rows,
):
    height = width // pieces
    groups = width // TILE
    places, deep = late.shape[0], last_own.shape[0]
    low, high = place_ref[0] & 1, place_ref[0] >> 1

    def columns(out, first_row, rows, out_row, across):
        for g in range(across):
            row = first_row + g * rows
            out[out_row : out_row + rows, g * TILE : (g + 1) * TILE] = whole[row : row + rows, :]

    def put_chunk(chunk):
        columns(down_out, 0, TILE, chunk * TILE, groups)
        for j in range(pieces):
            row = width + j * height
            column = (j * chunks + chunk) * TILE
            up_out[:, column : column + TILE] = whole[row : row + height, :]

    def load(source, begin, rows):
        for c in range(places):
            at = ((c & 1) * deep + (c >> 1)) * rows
            whole[at : at + rows, :] = source[c, begin : begin + rows, :].astype(F32)

    def load_halves(own, other, at):
        rows = own.shape[2]
        for half, x in ((own, low), (other, 1 - low)):
            for k in range(deep):
                begin = pl.multiple_of((x * deep + (high ^ k)) * rows, 8)
                whole[pl.ds(begin, rows), :] = half[k, at].astype(F32)

    for chunk in range(chunks - 1):
        load_halves(early_own, early_other, chunk)
        put_chunk(chunk)
    load_halves(last_own, last_other, 0)
    put_chunk(chunks - 1)
    columns(mixing_out, 2 * width, height, 0, groups)
    row = 2 * width + groups * height
    second_out[...] = whole[row : row + second_out.shape[0], 0:LANES]
    load(late, 0, query_rows)
    columns(query_out, 0, height, 0, groups)
    load(late, query_rows, late.shape[1] - query_rows)
    shared_out[...] = whole[0:height, 0:LANES]
    first_out[...] = whole[0 : first_out.shape[0], LANES:]


def final_stage(place, halves, late, query_rows, chunks, pieces, width):
    height = width // pieces
    shape = lambda *dims: jax.ShapeDtypeStruct(dims, F32)
    vector = round_up(width // LANES, 8)
    tallest = max(2 * one.shape[0] * one.shape[2] for one in halves)
    tallest = max(tallest, late.shape[0] * late.shape[1])
    return pl.pallas_call(
        functools.partial(
            final_kernel, chunks=chunks, pieces=pieces, width=width, query_rows=query_rows
        ),
        grid_spec=pltpu.PrefetchScalarGridSpec(
            num_scalar_prefetch=1,
            grid=(),
            in_specs=[pl.BlockSpec(memory_space=pltpu.VMEM)] * 5,
            out_specs=[pl.BlockSpec(memory_space=pltpu.VMEM)] * 7,
            scratch_shapes=[pltpu.VMEM((tallest, TILE), F32)],
        ),
        out_shape=[
            shape(chunks * TILE, width),
            shape(height, pieces * chunks * TILE),
            shape(height, width),
            shape(height, width),
            shape(height, LANES),
            shape(vector, LANES),
            shape(vector, LANES),
        ],
        compiler_params=params(),
        cost_estimate=weight(),
        name="final",
    )(place, *halves, late)


def swap(values, axis, size, mask):
    return lax.ppermute(values, axis, [(i, i ^ mask) for i in range(size)])


class Gather:
    def __init__(self, piece, size):
        self.size, self.own = size, piece
        self.far = swap(piece, "wt", size, 2)
        self.near = swap(piece, "wt", size, 1)

    def finish(self):
        return [self.own, self.near, self.far, swap(self.far, "wt", self.size, 1)]


def own_order(values, spot, size):
    mask = 1
    while mask < size:
        split = values.reshape((size // (2 * mask), 2, mask) + values.shape[1:])
        split = jnp.where((spot & mask) != 0, split[:, ::-1], split)
        values = split.reshape(values.shape)
        mask *= 2
    return values


class Reduction:
    def __init__(self, keep, send, place, sizes):
        self.wt_size, self.ctx_size = sizes
        self.groups = self.ctx_size // 2
        self.low, self.high = place & 1, place >> 1
        self.owners, self.rows, self.lanes = keep.shape
        split = (self.owners, 2, self.groups, self.rows // self.ctx_size, self.lanes)
        self.held = keep.reshape(split)
        self.sent = [send.reshape(split)]
        self.routes = [("wt", self.wt_size, 1)]
        self.coming = []

    def launch(self):
        if self.sent:
            self.coming = [swap(one, *route) for one, route in zip(self.sent, self.routes)]
            self.sent = []

    def add(self, pick):
        return pick(self.held).astype(F32) + pick(self.coming[0]).astype(F32)

    def y(self, cuts=()):
        edges = (0, *cuts, self.rows // self.ctx_size)
        self.later = [
            self.add(lambda v: v[1][..., begin:end, :]).astype(BF16)
            for begin, end in zip(edges, edges[1:])
        ]
        self.held = self.add(lambda v: v[0])
        self.sent = [self.later.pop(0)]
        self.routes = [("wt", self.wt_size, 2)]

    def y_more(self):
        self.before, self.sent = self.coming, [self.later.pop(0)]

    def y_joined(self):
        self.coming = [jnp.concatenate(self.before + self.coming, axis=-2)]

    def x(self):
        low, axis = self.low, self.held.ndim - 4
        half = lambda x: self.add(lambda v: lax.dynamic_index_in_dim(v, x, axis, False))
        self.held, self.sent = half(low), [half(1 - low).astype(BF16)]
        self.routes = [("ctx", self.ctx_size, 1)]

    def far(self):
        return [("ctx", self.ctx_size, 2 * k) for k in range(1, self.groups)]

    def z(self, *others):
        def part(k):
            pick = lambda v: lax.dynamic_index_in_dim(v, self.high ^ k, 0, False)
            return jnp.stack([one.add(pick) for one in (self, *others)])

        self.sent = [part(k).astype(BF16) for k in range(1, self.groups)]
        self.held = part(0)
        self.routes = self.far()

    def total(self):
        parts = [self.held.astype(F32)] + [one.astype(F32) for one in self.coming]
        while len(parts) > 1:
            parts = [parts[i] + parts[i + 1] for i in range(0, len(parts), 2)]
        return parts[0].astype(BF16)

    def z_back(self):
        self.held = self.total()
        self.sent = [self.held] * (self.groups - 1)

    def x_back(self):
        self.held = jnp.stack([self.held] + self.coming)
        self.sent = [self.held]
        self.routes = [("ctx", self.ctx_size, 1)]

    def everywhere(self):
        return self.add(lambda v: v).astype(BF16).swapaxes(0, 1).reshape(
            self.ctx_size, self.rows // self.ctx_size, self.lanes
        )


def tie(main, *reductions, came=()):
    state = [(one.held, one.sent) for one in reductions]
    main, state, coming = lax.optimization_barrier((main, state, [one.coming for one in came]))
    for one, (held, sent) in zip(reductions, state):
        one.held, one.sent = held, sent
    for one, values in zip(came, coming):
        one.coming = values
    for one in reductions:
        one.launch()
    return main


def body(
    tokens,
    documents,
    first_gain,
    query_weight,
    shared_weight,
    mixing_weight,
    second_gain,
    up_weight,
    down_weight,
    cotangent,
    *,
    wt_size,
    ctx_size,
):
    sizes = (wt_size, ctx_size)
    seqs, rows, width = tokens.shape
    count = seqs * rows
    spot_index = lax.axis_index("wt")
    place = lax.axis_index("ctx")
    spot = spot_index.astype(jnp.int32).reshape(1)
    length = ctx_size * rows
    doc_most = length * 5 // 8
    before = min(ctx_size - 1, -(-(doc_most - 1) // rows))
    blocks = before + 1
    height = width // wt_size
    chunks = up_weight.shape[1] // wt_size // TILE

    gain_rows = -(-height // LANES)
    pad = lambda gain: jnp.pad(gain, (0, gain_rows * LANES - height)).reshape(gain_rows, LANES)
    small = jnp.concatenate([shared_weight, pad(first_gain), pad(second_gain)], axis=0)
    small = jnp.pad(small, ((0, -small.shape[0] % 16), (0, 0)))
    small_pieces = Gather(small, wt_size).finish()
    query_gather = Gather(query_weight, wt_size)

    gains = jnp.stack([one[height : height + 2 * gain_rows] for one in small_pieces])
    gains = gains.reshape(wt_size, 2, gain_rows * LANES)[:, :, :height].astype(F32)
    gains = own_order(gains, spot_index, wt_size)
    gain_one = gains[:, 0].reshape(1, width)
    gain_two = gains[:, 1].reshape(1, width)

    inputs = tokens.reshape(count, width)
    doc_lines = documents.astype(BF16).reshape(seqs, rows // LANES, LANES)
    scaled_one, shared = first_stage(spot, inputs, gain_one, doc_lines, small_pieces, ctx_size)
    shared, query_gather.far, mixing_weight, *packed = lax.optimization_barrier(
        (shared, query_gather.far, mixing_weight, up_weight, down_weight)
    )
    keyvals = lax.all_to_all(shared, "ctx", 0, 0).reshape(ctx_size, seqs, rows + DOC_ROWS, LANES)
    packed = list(pack_stage(*packed, chunks, wt_size))
    gathers = [Gather(packed[0], wt_size)]
    mixing_gather = Gather(mixing_weight, wt_size)
    marks = jnp.broadcast_to(documents.astype(F32)[:, :, None], (seqs, rows, LANES))
    query_pieces = query_gather.finish()
    place_one = place.astype(jnp.int32).reshape(1)

    keyvals, gathers[0].far, mixing_gather.far, query_pieces[3], marks, packed[1:] = (
        lax.optimization_barrier(
            (keyvals, gathers[0].far, mixing_gather.far, query_pieces[3], marks, packed[1:])
        )
    )
    gathered = [gathers[0].finish()]
    mixing_pieces = mixing_gather.finish()
    gathers.append(Gather(packed[1], wt_size))
    queries, starts, exact, attended, logs = attend(
        spot, place_one, scaled_one, marks, keyvals, query_pieces, blocks
    )
    attended, gathers[1].far, packed[2:] = lax.optimization_barrier(
        (attended, gathers[1].far, packed[2:])
    )
    gathered.append(gathers[1].finish())
    gathers += [Gather(one, wt_size) for one in packed[2:]]

    arrays = {
        "attended": attended.reshape(count, width),
        "tokens": inputs,
        "gain": gain_two,
        "cotangent": cotangent.reshape(count, width),
    }
    feed = lambda arrays, part: feed_stage(
        spot, arrays, gathered, mixing_pieces, part, chunks, ctx_size
    )
    arrays = feed(arrays, (0, 1))
    zero, one = (
        Reduction(arrays[f"keep{chunk}"], arrays[f"send{chunk}"], place, sizes) for chunk in (0, 1)
    )
    arrays, gathers[-1].far = tie((arrays, gathers[-1].far), zero, one)
    gathered.append(gathers[-1].finish())
    arrays = tie(arrays, zero, one, came=[zero])
    zero.y()
    arrays = tie(arrays, zero, one, came=[one])
    one.x()
    arrays = tie(arrays, zero, one)
    arrays = feed(arrays, (2,))
    two = Reduction(arrays["keep2"], arrays["send2"], place, sizes)
    grad_attended = tie(arrays["grad_attended"], zero, one, two, came=[zero, one])
    zero.x()
    one.y()
    grad_attended = tie(grad_attended, zero, one, two, came=[two])
    two.y([round_up(two.rows // ctx_size * 2 // 5, 8)])
    grad_attended = tie(grad_attended, zero, one, two).reshape(seqs, rows, width)
    grad_queries, terms = [], []
    for seq in range(seqs):
        part, *terms = attend_back(
            seq, place_one, queries, starts, exact, logs, grad_attended, keyvals, terms, blocks
        )
        came = [zero, one, two] if seq == 0 else [zero, two]
        part, grad_attended, terms = tie((part, grad_attended, terms), *came, came=came)
        grad_queries.append(part[0])
        if seq == 0:
            zero.z(one)
            two.y_more()
            grad_attended = tie(grad_attended, zero, two)
    two.y_joined()
    two.x()
    grad_queries, terms = tie((grad_queries, terms), zero, two)
    arriving = lax.all_to_all(terms[0], "ctx", 0, 0)
    zero.z_back()
    grad_scaled, keep, send = query_stage(spot, scaled_one, grad_queries, query_pieces, ctx_size)
    query = Reduction(keep, send, place, sizes)
    grad_scaled = tie(grad_scaled, zero, two, query)
    query.y()
    grad_scaled, arriving = tie((grad_scaled, arriving), zero, query)
    input_grad, keep, send = last_stage(
        spot, inputs, gain_one, scaled_one, arriving, grad_scaled, arrays["grad_hidden"], small_pieces
    )
    shared = Reduction(keep, send, place, sizes)
    input_grad = tie(input_grad, zero, two, shared, query, came=[two, zero])
    two.z()
    zero.x_back()
    input_grad = tie(input_grad, zero, two)
    input_grad = tie(input_grad, shared, query, came=[shared])
    shared.y()
    input_grad = tie(input_grad, shared)
    input_grad = tie(input_grad, shared, query, came=[shared, query])
    late = jnp.concatenate([query.everywhere(), shared.everywhere()], axis=1)
    late = lax.all_to_all(late, "ctx", 0, 0)
    two.z_back()
    input_grad = tie(input_grad, two)
    two.x_back()
    input_grad = tie(input_grad, two)
    late = jnp.sum(late.astype(F32), axis=0).astype(BF16)
    late = lax.all_to_all(jnp.broadcast_to(late, (ctx_size,) + late.shape), "ctx", 0, 0)
    down_grad, up_grad, mixing_grad, query_grad, shared_grad, first_grad, second_grad = final_stage(
        place_one,
        [zero.held, zero.coming[0], two.held, two.coming[0]],
        late,
        query.rows // ctx_size,
        chunks,
        wt_size,
        width,
    )

    def own_gain(lines):
        vector = lines[: width // LANES].reshape(width)
        return lax.dynamic_slice_in_dim(vector, spot_index * height, height, 0)

    return (
        arrays["layer_out"].reshape(seqs, rows, width),
        input_grad.reshape(seqs, rows, width),
        own_gain(first_grad),
        query_grad,
        shared_grad,
        mixing_grad,
        own_gain(second_grad),
        up_grad,
        down_grad,
    )


def solution(mesh):
    in_specs = (
        P("wt", "ctx", None),
        P("wt", "ctx"),
        P("wt"),
        P("wt", None),
        P("wt", None),
        P("wt", None),
        P("wt"),
        P("wt", None),
        P("wt", None),
        P("wt", "ctx", None),
    )
    out_specs = (
        P("wt", "ctx", None),
        P("wt", "ctx", None),
        P("wt"),
        P("wt", None),
        P("wt", None),
        P("wt", None),
        P("wt"),
        P("wt", None),
        P("wt", None),
    )
    run = functools.partial(body, wt_size=mesh.shape["wt"], ctx_size=mesh.shape["ctx"])
    return jax.shard_map(run, mesh=mesh, in_specs=in_specs, out_specs=out_specs, check_vma=False)
```

```python
import functools
import math

import jax
import jax.numpy as jnp
from jax import lax
from jax.experimental import pallas as pl
from jax.experimental.pallas import tpu as pltpu
from jax.sharding import PartitionSpec as P

HEADS = 12
HEAD_DIM = 64
PAIRS = HEADS // 2
LANES = 128
EPSILON = 1e-05
BIAS = -1e30
SCALE = math.log2(math.e) / HEAD_DIM**0.5
F32 = jnp.float32
BF16 = jnp.bfloat16
GELU_ROOT = math.sqrt(2.0 / math.pi)
GELU_CUBE = 0.044715


def params(*semantics):
    return pltpu.CompilerParams(
        dimension_semantics=semantics or None, vmem_limit_bytes=56 * 1024 * 1024
    )


def weight():
    return pl.CostEstimate(flops=1, bytes_accessed=1, transcendentals=0)


def dot_nn(a, b):
    return lax.dot_general(a, b, (((1,), (0,)), ((), ())), preferred_element_type=F32)


def dot_nt(a, b):
    return lax.dot_general(a, b, (((1,), (1,)), ((), ())), preferred_element_type=F32)


def dot_tn(a, b):
    return lax.dot_general(a, b, (((0,), (0,)), ((), ())), preferred_element_type=F32)


def normalize(values):
    center = values - jnp.mean(values, axis=-1, keepdims=True)
    spread = jnp.mean(center * center, axis=-1, keepdims=True)
    inverse = lax.rsqrt(spread + EPSILON)
    return center * inverse, inverse


def norm_back(grad, normed, inverse):
    mean_grad = jnp.mean(grad, axis=-1, keepdims=True)
    mean_both = jnp.mean(grad * normed, axis=-1, keepdims=True)
    return (grad - mean_grad - normed * mean_both) * inverse


def place_rows(spot, pieces, scratch):
    height = scratch.shape[0] // len(pieces)
    for r, piece in enumerate(pieces):
        begin = pl.multiple_of((spot ^ r) * height, height)
        scratch[pl.ds(begin, height), :] = piece[0:height, :]


STEP = 128


def over_rows(rows, run):
    def one(index, carried):
        run(pl.ds(pl.multiple_of(index * STEP, STEP), STEP))
        return carried

    lax.fori_loop(0, rows // STEP, one, 0)


TILE = 256


def pack_kernel(up, down, *outs, chunks, pieces):
    width = down.shape[1]
    height = up.shape[0]
    for chunk, out in enumerate(outs):
        for g in range(width // TILE):
            out[g * TILE : (g + 1) * TILE, :] = down[
                chunk * TILE : (chunk + 1) * TILE, g * TILE : (g + 1) * TILE
            ]
        for j in range(pieces):
            row, column = width + j * height, (j * chunks + chunk) * TILE
            out[row : row + height, :] = up[:, column : column + TILE]


def pack_stage(up, down, chunks, pieces):
    width = down.shape[1]
    return pl.pallas_call(
        functools.partial(pack_kernel, chunks=chunks, pieces=pieces),
        in_specs=[pl.BlockSpec(memory_space=pltpu.VMEM)] * 2,
        out_specs=[pl.BlockSpec(memory_space=pltpu.VMEM)] * chunks,
        out_shape=[jax.ShapeDtypeStruct((2 * width, TILE), BF16)] * chunks,
        compiler_params=params(),
        cost_estimate=weight(),
        name="pack",
    )(up, down)


DOC_ROWS = 16


def first_kernel(spot_ref, tokens, gain, documents, *rest, pieces):
    weights = rest[:pieces]
    scaled_out, shared_out, weight = rest[pieces:]
    place_rows(spot_ref[0], weights, weight)
    seqs, doc_lines, unused = documents.shape
    places, tall, unused = shared_out.shape
    tall = tall // seqs
    rows = tall - DOC_ROWS
    per_seq = rows // STEP

    def run(index, carried):
        here = pl.ds(pl.multiple_of(index * STEP, STEP), STEP)
        seq = index // per_seq
        there = pl.multiple_of(seq * tall + (index - seq * per_seq) * STEP, DOC_ROWS)
        normed, unused = normalize(tokens[here, :].astype(F32))
        scaled = (normed * gain[...]).astype(BF16)
        scaled_out[here, :] = scaled
        shared = dot_nn(scaled, weight[...]).astype(BF16)

        def put(c, carried):
            shared_out[c, pl.ds(there, STEP), :] = shared
            return carried

        return lax.fori_loop(0, places, put, carried)

    lax.fori_loop(0, seqs * per_seq, run, 0)

    def put(c, carried):
        for seq in range(seqs):
            begin = seq * tall + rows
            shared_out[c, begin : begin + DOC_ROWS, :] = jnp.zeros((DOC_ROWS, LANES), BF16)
            shared_out[c, begin : begin + doc_lines, :] = documents[seq]
        return carried

    lax.fori_loop(0, places, put, 0)


def first_stage(spot, tokens, gain, documents, weights, places):
    count, width = tokens.shape
    columns = weights[0].shape[1]
    seqs, doc_lines, unused = documents.shape
    return pl.pallas_call(
        functools.partial(first_kernel, pieces=len(weights)),
        grid_spec=pltpu.PrefetchScalarGridSpec(
            num_scalar_prefetch=1,
            grid=(),
            in_specs=[pl.BlockSpec(memory_space=pltpu.VMEM)] * (3 + len(weights)),
            out_specs=[pl.BlockSpec(memory_space=pltpu.VMEM)] * 2,
            scratch_shapes=[pltpu.VMEM((width, columns), BF16)],
        ),
        out_shape=[
            jax.ShapeDtypeStruct((count, width), BF16),
            jax.ShapeDtypeStruct((places, count + seqs * DOC_ROWS, columns), BF16),
        ],
        compiler_params=params(),
        cost_estimate=weight(),
        name="first_norm",
    )(spot, tokens, gain, documents, *weights)


def project_kernel(spot_ref, operand, *rest, pieces):
    weights = rest[:pieces]
    out, weight_all = rest[pieces:]
    place_rows(spot_ref[0], weights, weight_all)
    out[...] = dot_nn(operand[...], weight_all[...]).astype(out.dtype)


def project(spot, operand, weights):
    rows, width = operand.shape
    columns = weights[0].shape[1]
    return pl.pallas_call(
        functools.partial(project_kernel, pieces=len(weights)),
        grid_spec=pltpu.PrefetchScalarGridSpec(
            num_scalar_prefetch=1,
            grid=(),
            in_specs=[pl.BlockSpec(memory_space=pltpu.VMEM)] * (1 + len(weights)),
            out_specs=pl.BlockSpec(memory_space=pltpu.VMEM),
            scratch_shapes=[pltpu.VMEM((width, columns), BF16)],
        ),
        out_shape=jax.ShapeDtypeStruct((rows, columns), BF16),
        compiler_params=params(),
        cost_estimate=weight(),
        name="project",
    )(spot, operand, *weights)


def low_lanes(shape):
    return lax.broadcasted_iota(jnp.int32, shape, len(shape) - 1) < HEAD_DIM


def swap_halves(values):
    return pltpu.roll(values, HEAD_DIM, 1)


def stacked_pairs(ref):
    return jnp.concatenate(
        [ref[0, :, p * LANES : (p + 1) * LANES] for p in range(PAIRS)], axis=0
    )


def tile_bias(starts, key_begin, row_begin, tile_rows, tile_keys):
    key_place = key_begin + lax.broadcasted_iota(jnp.int32, (tile_rows, tile_keys), 1)
    row_place = row_begin + lax.broadcasted_iota(jnp.int32, (tile_rows, tile_keys), 0)
    first = jnp.concatenate([starts] * (tile_keys // LANES), axis=1)
    allowed = (key_place >= first) & (key_place <= row_place)
    bias = jnp.where(allowed, 0.0, BIAS)
    bias = jnp.concatenate([bias, bias], axis=1)
    return jnp.concatenate([bias] * PAIRS, axis=0)


def block_at(place_ref, j, blocks):
    return jnp.maximum(place_ref[0] - (blocks - 1) + j, 0)


def attend_kernel(
    place_ref, queries, marks, keyvals, starts_out, exact_out, rounded_out, logs_out, *rest,
    blocks, tile_rows, tile_keys
):
    key_even, key_odd, value_even, value_odd, score_scratch, most, total = rest
    rows = keyvals.shape[2] - DOC_ROWS
    tile = pl.program_id(1)

    @pl.when(tile == 0)
    def _():
        low = low_lanes((rows, LANES))
        for j in range(blocks):
            whole = keyvals[block_at(place_ref, j, blocks), 0, 0:rows, :].astype(F32)
            turned = swap_halves(whole)
            place = pl.ds(j * rows, rows)
            key_even[place, :] = jnp.where(low, whole, 0.0).astype(BF16)
            key_odd[place, :] = jnp.where(low, 0.0, turned).astype(BF16)
            value_even[place, 0:LANES] = jnp.where(low, turned, 0.0).astype(BF16)
            value_even[place, LANES:] = jnp.where(low, 1.0, 0.0).astype(BF16)
            value_odd[place, 0:LANES] = jnp.where(low, 0.0, whole).astype(BF16)
            value_odd[place, LANES:] = jnp.where(low, 0.0, 1.0).astype(BF16)

    def smaller(j, count):
        lines = keyvals[block_at(place_ref, j, blocks), 0, rows:, :].astype(F32)
        missing = place_ref[0] - (blocks - 1) + j < 0
        for h in range(rows // LANES):
            line = jnp.where(missing, -1.0, lines[h : h + 1, :])
            count = count + jnp.where(line < marks[0], 1.0, 0.0)
        return count

    count = lax.fori_loop(0, blocks, smaller, jnp.zeros((tile_rows, LANES), F32))
    count = jnp.sum(count, axis=1, keepdims=True).astype(jnp.int32)
    starts = starts_out
    starts[0] = jnp.broadcast_to(count, (tile_rows, LANES))
    row_begin = (blocks - 1) * rows + tile * tile_rows
    begin = jnp.min(starts[0]) // tile_keys
    end = (row_begin + tile_rows - 1) // tile_keys + 1
    stacked = stacked_pairs(queries)
    most[...] = jnp.full_like(most, -3e38)
    copies = tile_keys // LANES

    def score(index):
        key_begin = pl.multiple_of(index * tile_keys, tile_keys)
        place = pl.ds(key_begin, tile_keys)
        both = jnp.concatenate([key_even[place, :], key_odd[place, :]], axis=0)
        values = dot_nt(stacked, both) + tile_bias(
            starts[0], key_begin, row_begin, tile_rows, tile_keys
        )
        score_scratch[index - begin] = values
        half = []
        for h in range(2):
            part = values[:, h * tile_keys : h * tile_keys + LANES]
            for q in range(1, copies):
                at = h * tile_keys + q * LANES
                part = jnp.maximum(part, values[:, at : at + LANES])
            half.append(part)
        return jnp.concatenate(half, axis=1)

    def output(index):
        place = pl.ds(pl.multiple_of(index * tile_keys, tile_keys), tile_keys)
        both = jnp.concatenate([value_even[place, :], value_odd[place, :]], axis=0)
        shift = jnp.concatenate([most[:, 0:LANES]] * copies + [most[:, LANES:]] * copies, axis=1)
        powers = jnp.exp2((score_scratch[index - begin] - shift) * SCALE).astype(BF16)
        return dot_nn(powers, both)

    def in_pairs(one, join, total):
        def two(index, carried):
            at = begin + 2 * index
            total[...] = join(total[...], join(one(at), one(at + 1)))
            return carried

        count = end - begin
        lax.fori_loop(0, count // 2, two, 0)

        @pl.when(count % 2 == 1)
        def _():
            total[...] = join(total[...], one(end - 1))

    in_pairs(score, jnp.maximum, most)
    stack = PAIRS * tile_rows
    for h in range(2):
        part = jnp.max(most[:, h * LANES : (h + 1) * LANES], axis=1, keepdims=True)
        most[:, h * LANES : (h + 1) * LANES] = jnp.broadcast_to(part, (stack, LANES))
    total[...] = jnp.zeros_like(total)
    in_pairs(output, jnp.add, total)
    low = low_lanes((tile_rows, LANES))
    for p in range(PAIRS):
        at = pl.ds(p * tile_rows, tile_rows)
        lanes = slice(p * LANES, (p + 1) * LANES)
        sums = total[at, LANES:]
        out = total[at, 0:LANES] / sums
        exact_out[0, :, lanes] = out
        rounded_out[0, :, lanes] = out.astype(BF16)
        shift = jnp.where(low, most[at, 0:LANES], most[at, LANES:])
        logs_out[0, :, lanes] = shift * SCALE + jnp.log2(sums)


def attend_back_kernel(
    place_ref, queries, starts, exact, logs, grads, keyvals, *rest,
    seq, blocks, tile_rows, tile_keys
):
    grad_queries, keep, send, *rest = rest
    (
        key_even, key_odd, value_even, value_odd,
        key_total, value_total, query_total,
        log_even, log_odd, delta_even, delta_odd,
    ) = rest
    rows = keyvals.shape[2] - DOC_ROWS
    tile = pl.program_id(0)

    @pl.when(tile == 0)
    def _():
        low = low_lanes((rows, LANES))
        for j in range(blocks):
            whole = keyvals[block_at(place_ref, j, blocks), 0, 0:rows, :].astype(F32)
            turned = swap_halves(whole)
            place = pl.ds(j * rows, rows)
            key_even[place, :] = jnp.where(low, whole, 0.0).astype(BF16)
            key_odd[place, :] = jnp.where(low, 0.0, turned).astype(BF16)
            value_even[place, :] = jnp.where(low, turned, 0.0).astype(BF16)
            value_odd[place, :] = jnp.where(low, 0.0, whole).astype(BF16)
        key_total[...] = jnp.zeros_like(key_total)
        value_total[...] = jnp.zeros_like(value_total)

    row_begin = (blocks - 1) * rows + tile * tile_rows
    begin = jnp.min(starts[0]) // tile_keys
    end = (row_begin + tile_rows - 1) // tile_keys + 1
    stacked = stacked_pairs(queries)
    grad_stacked = stacked_pairs(grads)
    stacked_turned = stacked.T
    grad_turned = grad_stacked.T
    stack = PAIRS * tile_rows
    low = low_lanes((tile_rows, LANES))
    for p in range(PAIRS):
        at = pl.ds(p * tile_rows, tile_rows)
        lanes = slice(p * LANES, (p + 1) * LANES)
        log = logs[0, :, lanes]
        log_turned = swap_halves(log)
        log_even[at, :] = jnp.where(low, log, log_turned)
        log_odd[at, :] = jnp.where(low, log_turned, log)
        terms_here = exact[0, :, lanes] * grads[0, :, lanes].astype(F32)
        even = jnp.sum(jnp.where(low, terms_here, 0.0), axis=1, keepdims=True)
        odd = jnp.sum(jnp.where(low, 0.0, terms_here), axis=1, keepdims=True)
        delta_even[at, :] = jnp.broadcast_to(even, (tile_rows, LANES))
        delta_odd[at, :] = jnp.broadcast_to(odd, (tile_rows, LANES))
    query_total[...] = jnp.zeros_like(query_total)

    def step(index, carried):
        key_begin = pl.multiple_of(index * tile_keys, tile_keys)
        place = pl.ds(key_begin, tile_keys)
        keys = jnp.concatenate([key_even[place, :], key_odd[place, :]], axis=0)
        values = jnp.concatenate([value_even[place, :], value_odd[place, :]], axis=0)
        copies = tile_keys // LANES
        log = jnp.concatenate([log_even[...]] * copies + [log_odd[...]] * copies, axis=1)
        delta = jnp.concatenate([delta_even[...]] * copies + [delta_odd[...]] * copies, axis=1)
        scores = dot_nt(stacked, keys) + tile_bias(
            starts[0], key_begin, row_begin, tile_rows, tile_keys
        )
        chances = jnp.exp2(scores * SCALE - log)
        grad_probs = dot_nt(grad_stacked, values)
        grad_scores = (chances * (grad_probs - delta)).astype(BF16)
        query_total[...] += dot_nn(grad_scores, keys)
        key_total[index] += dot_nn(stacked_turned, grad_scores)
        value_total[index] += dot_nn(grad_turned, chances.astype(BF16))
        return carried

    lax.fori_loop(begin, end, step, 0)
    root = 1.0 / HEAD_DIM**0.5
    for p in range(PAIRS):
        at = pl.ds(p * tile_rows, tile_rows)
        lanes = slice(p * LANES, (p + 1) * LANES)
        grad_queries[0, :, lanes] = (query_total[at, :] * root).astype(BF16)

    @pl.when(tile == pl.num_programs(0) - 1)
    def _():
        per_block = rows // tile_keys
        keep[...] = jnp.zeros_like(keep)
        send[...] = jnp.zeros_like(send)

        def block_terms(j, carried):
            for i in range(per_block):
                index = j * per_block + i
                key = key_total[index]
                value = value_total[index]
                key = key[0:HEAD_DIM, 0:tile_keys] + key[HEAD_DIM:, tile_keys:]
                value = value[0:HEAD_DIM, 0:tile_keys] + value[HEAD_DIM:, tile_keys:]
                both = jnp.concatenate([key * root, value], axis=0)
                both = both.T.astype(BF16)
                owner = block_at(place_ref, j, blocks)
                here = slice(i * tile_keys, (i + 1) * tile_keys)
                same = (owner & 1) == (place_ref[0] & 1)

                @pl.when(same)
                def _():
                    keep[owner >> 1, here, :] = both

                @pl.when(jnp.logical_not(same))
                def _():
                    send[owner >> 1, here, :] = both

            return carried

        missing = jnp.maximum(blocks - 1 - place_ref[0], 0)
        lax.fori_loop(missing, blocks, block_terms, 0)


def attention_sizes(rows, blocks):
    tile_rows = 128 if rows % 128 == 0 else rows
    tile_keys = 256 if rows % 256 == 0 else 128
    return tile_rows, tile_keys, blocks * rows // tile_keys


def attend(place, queries, marks, keyvals, blocks):
    unused, seqs, tall, unused = keyvals.shape
    rows = tall - DOC_ROWS
    width = queries.shape[2]
    tile_rows, tile_keys, key_tiles = attention_sizes(rows, blocks)
    stack = PAIRS * tile_rows
    keys = blocks * rows
    row_spec = lambda lanes: pl.BlockSpec((1, tile_rows, lanes), lambda s, t, *_: (s, t, 0))
    wide = lambda dtype: jax.ShapeDtypeStruct((seqs, rows, width), dtype)
    return pl.pallas_call(
        functools.partial(
            attend_kernel, blocks=blocks, tile_rows=tile_rows, tile_keys=tile_keys
        ),
        grid_spec=pltpu.PrefetchScalarGridSpec(
            num_scalar_prefetch=1,
            grid=(seqs, rows // tile_rows),
            in_specs=[
                row_spec(width),
                row_spec(LANES),
                pl.BlockSpec((keyvals.shape[0], 1, tall, LANES), lambda s, t, *_: (0, s, 0, 0)),
            ],
            out_specs=[row_spec(LANES)] + [row_spec(width)] * 3,
            scratch_shapes=[
                pltpu.VMEM((keys, LANES), BF16),
                pltpu.VMEM((keys, LANES), BF16),
                pltpu.VMEM((keys, 2 * LANES), BF16),
                pltpu.VMEM((keys, 2 * LANES), BF16),
                pltpu.VMEM((key_tiles, stack, 2 * tile_keys), F32),
                pltpu.VMEM((stack, 2 * LANES), F32),
                pltpu.VMEM((stack, 2 * LANES), F32),
            ],
        ),
        out_shape=[
            jax.ShapeDtypeStruct((seqs, rows, LANES), jnp.int32),
            wide(F32),
            wide(BF16),
            wide(F32),
        ],
        compiler_params=params("arbitrary", "arbitrary"),
        cost_estimate=weight(),
        name="attend",
    )(place, queries, marks, keyvals)


def attend_back(
    seq, place, queries, starts, exact, logs, grads, keyvals, blocks
):
    seqs, rows, width = queries.shape
    ctx_size = keyvals.shape[0]
    tile_rows, tile_keys, key_tiles = attention_sizes(rows, blocks)
    stack = PAIRS * tile_rows
    keys = blocks * rows
    row_spec = lambda lanes: pl.BlockSpec((1, tile_rows, lanes), lambda t, *_: (seq, t, 0))
    return pl.pallas_call(
        functools.partial(
            attend_back_kernel, seq=seq, blocks=blocks, tile_rows=tile_rows, tile_keys=tile_keys
        ),
        grid_spec=pltpu.PrefetchScalarGridSpec(
            num_scalar_prefetch=1,
            grid=(rows // tile_rows,),
            in_specs=[row_spec(width), row_spec(LANES)]
            + [row_spec(width)] * 3
            + [pl.BlockSpec((ctx_size, 1, keyvals.shape[2], LANES), lambda t, *_: (0, seq, 0, 0))],
            out_specs=[
                pl.BlockSpec((1, tile_rows, width), lambda t, *_: (0, t, 0)),
            ]
            + [pl.BlockSpec((ctx_size // 2, rows, LANES), lambda t, *_: (0, 0, 0))] * 2,
            scratch_shapes=[pltpu.VMEM((keys, LANES), BF16)] * 4
            + [pltpu.VMEM((key_tiles, LANES, 2 * tile_keys), F32)] * 2
            + [pltpu.VMEM((stack, LANES), F32)] * 5,
        ),
        out_shape=[
            jax.ShapeDtypeStruct((1, rows, width), BF16),
        ]
        + [jax.ShapeDtypeStruct((ctx_size // 2, rows, LANES), BF16)] * 2,
        compiler_params=params("arbitrary"),
        cost_estimate=weight(),
        name="attend_back",
    )(place, queries, starts, exact, logs, grads, keyvals)


def round_up(count, unit):
    return -(-count // unit) * unit


def mixing_rows(width, pieces, ctx_size):
    unit = 8 * ctx_size
    tall = 2 * width + width // pieces * (width // TILE)
    return round_up(tall + width // LANES, unit) - 2 * width


def message_of(messages, s):
    return messages[s & 1], s >> 1


def split_out(spot, pieces, source, messages, first_row=0):
    height, lanes = source.shape[0] // pieces, messages[0].shape[2]
    across = min(lanes, source.shape[1])
    for s in range(pieces):
        out, at = message_of(messages, s)
        begin = pl.multiple_of((spot ^ s) * height, height)
        for g in range(source.shape[1] // across):
            row = first_row + g * height
            out[at, row : row + height, 0:across] = source[
                pl.ds(begin, height), g * lanes : g * lanes + across
            ].astype(BF16)


def put_vector(pieces, vector, messages, first_row, begin):
    height, lanes = messages[0].shape[1] - first_row, messages[0].shape[2]
    count = vector.shape[1] // LANES
    row = lax.broadcasted_iota(jnp.int32, (height, LANES), 0)
    block = jnp.zeros((height, LANES), F32)
    for i in range(count):
        block = jnp.where(row == i, vector[:, i * LANES : (i + 1) * LANES], block)
    for s in range(pieces):
        out, at = message_of(messages, s)
        out[at, first_row:, begin : begin + LANES] = block.astype(BF16)
        if begin == 0:
            out[at, first_row:, LANES:] = jnp.zeros((height, lanes - LANES), BF16)


def feed_kernel(spot_ref, *refs, pieces, part, first, last, names):
    use = dict(zip(names, refs))
    spot = spot_ref[0]
    step = pl.program_id(0)
    steps = len(part) * (pieces // 2)
    cotangent = use["cotangent"]
    reduced, grads, scaled, hidden = use["reduced"], use["grads"], use["scaled"], use["hidden"]
    up_tile, down_tile, up_sems, down_sems = (
        use["up_tile"], use["down_tile"], use["up_sems"], use["down_sems"]
    )
    rows, width = cotangent.shape
    height = width // pieces
    groups = width // TILE

    def messages_of(chunk):
        return use[f"keep{chunk}"], use[f"send{chunk}"]

    def owners(n):
        chunk, at = divmod(n, pieces // 2)
        return part[chunk], (2 * at, 2 * at + 1)

    def copies(n):
        chunk, pair = owners(n)
        for h, s in enumerate(pair):
            source = pl.multiple_of(width + (spot ^ s) * height, height)
            for r in range(pieces):
                row = pl.multiple_of((spot ^ r) * height, height)
                yield pltpu.make_async_copy(
                    use[f"message{chunk}_{r}"].at[pl.ds(source, height), :],
                    up_tile.at[n, pl.ds(row, height), pl.ds(h * TILE, TILE)],
                    up_sems.at[n, h, r],
                )
            for g in range(groups):
                yield pltpu.make_async_copy(
                    use[f"message{chunk}_{s}"].at[pl.ds(g * TILE, TILE), :],
                    down_tile.at[n, pl.ds(h * TILE, TILE), pl.ds(g * TILE, TILE)],
                    down_sems.at[n, h, g],
                )

    @pl.when(step == 0)
    def _():
        for n in range(steps):
            for one in copies(n):
                one.start()
        if first:

            def begin(here):
                mixed = dot_nn(use["attended"][here, :], use["mixing_all"][...])
                values = use["tokens"][here, :].astype(F32) + mixed
                hidden[here, :] = values
                normed, unused = normalize(values)
                scaled[here, :] = (normed * use["gain"][...]).astype(BF16)

            place_rows(spot, [use[f"mixing{r}"] for r in range(pieces)], use["mixing_all"])
            over_rows(rows, begin)

    for n in range(steps):

        @pl.when(step == n)
        def _():
            for one in copies(n):
                one.wait()

    up = up_tile[step]
    down = down_tile[step]
    upper = dot_nn(scaled[...], up)
    grad_act = dot_nt(cotangent[...], down)
    square = upper * upper
    inner = jnp.tanh(GELU_ROOT * (upper + GELU_CUBE * upper * square))
    half = 0.5 * (1.0 + inner)
    slope = half + 0.5 * upper * (1.0 - inner * inner) * (
        GELU_ROOT * (1.0 + 3.0 * GELU_CUBE * square)
    )
    active = (upper * half).astype(BF16)
    grad_upper = (grad_act * slope).astype(BF16)
    reduced_here = dot_nn(active, down)
    grads_here = dot_nt(grad_upper, up)

    @pl.when(step == 0)
    def _():
        if first:
            reduced[...] = reduced_here
            grads[...] = grads_here
        else:
            reduced[...] = use["reduced_in"][...] + reduced_here
            grads[...] = use["grads_in"][...] + grads_here

    @pl.when(step > 0)
    def _():
        reduced[...] += reduced_here
        grads[...] += grads_here

    down_term = dot_tn(active, cotangent[...]).astype(BF16)
    up_term = use["up_term"]
    up_term[...] = dot_tn(scaled[...], grad_upper)
    for n in range(steps):

        @pl.when(step == n)
        def _():
            chunk, pair = owners(n)
            messages = messages_of(chunk)
            for h, s in enumerate(pair):
                out, at = message_of(messages, s)
                for g in range(groups):
                    column = slice(g * TILE, (g + 1) * TILE)
                    part_here = down_term[h * TILE : (h + 1) * TILE, column]
                    if chunk == 1:
                        out[0, at, column, :] = part_here
                    else:
                        out[at, column, :] = part_here
            for s in range(pieces):
                out, at = message_of(messages, s)
                begin = pl.multiple_of((spot ^ s) * height, height)
                for h, t in enumerate(pair):
                    part_here = up_term[
                        pl.ds(begin, height), h * TILE : (h + 1) * TILE
                    ].astype(BF16)
                    row = pl.multiple_of((spot ^ t) * height, height)
                    if chunk == 1:
                        out[1, at, pl.ds(row, height), :] = part_here
                    else:
                        out[at, pl.ds(width + row, height), :] = part_here

    if last:

        @pl.when(step == steps - 1)
        def _():
            sums, grad_mixed, term = use["sums"], use["grad_mixed"], use["term"]
            sums[...] = jnp.zeros_like(sums)
            place_rows(spot, [use[f"mixing{r}"] for r in range(pieces)], use["mixing_all"])

            def end(here):
                values = hidden[here, :]
                use["layer_out"][here, :] = (values + reduced[here, :]).astype(BF16)
                normed, inverse = normalize(values)
                grad = grads[here, :]
                sums[...] += jnp.sum((grad * normed).reshape(STEP // 8, 8, width), axis=0)
                grad_hidden = cotangent[here, :].astype(F32) + norm_back(
                    grad * use["gain"][...], normed, inverse
                )
                use["grad_hidden"][here, :] = grad_hidden
                rounded = grad_hidden.astype(BF16)
                grad_mixed[here, :] = rounded
                use["grad_attended"][here, :] = dot_nt(rounded, use["mixing_all"][...]).astype(
                    BF16
                )

            over_rows(rows, end)
            term[...] = dot_tn(use["attended"][...], grad_mixed[...])
            tall = 2 * width
            messages = messages_of(part[-1])
            split_out(spot, pieces, term, messages, tall)
            put_vector(
                pieces,
                jnp.sum(sums[...], axis=0, keepdims=True),
                messages,
                tall + height * groups,
                0,
            )


def feed_stage(spot, arrays, gathered, mixing_pieces, part, chunks, ctx_size):
    first, last = part[0] == 0, part[-1] == chunks - 1
    rows, width = arrays["cotangent"].shape
    pieces = len(gathered[part[0]])
    wide = jax.ShapeDtypeStruct((rows, width), F32)
    narrow = jax.ShapeDtypeStruct((rows, width), BF16)
    inputs, outputs, scratch = {}, {}, {}
    for chunk in part:
        more = mixing_rows(width, pieces, ctx_size) if chunk == chunks - 1 else 0
        message = jax.ShapeDtypeStruct((pieces // 2, 2 * width + more, TILE), BF16)
        if chunk == 1:
            message = jax.ShapeDtypeStruct((2, pieces // 2, width, TILE), BF16)
        outputs[f"keep{chunk}"] = outputs[f"send{chunk}"] = message
    inputs["cotangent"] = arrays["cotangent"]
    for chunk in part:
        for r in range(pieces):
            inputs[f"message{chunk}_{r}"] = gathered[chunk][r]
    for r in range(pieces):
        inputs[f"mixing{r}"] = mixing_pieces[r]
    scratch["mixing_all"] = pltpu.VMEM((width, width), BF16)
    if first:
        for name in ("attended", "tokens", "gain"):
            inputs[name] = arrays[name]
        outputs.update(hidden=wide, scaled=narrow, reduced=wide, grads=wide)
    if last:
        for name in ("attended", "gain", "scaled", "hidden"):
            inputs[name] = arrays[name]
        inputs["reduced_in"], inputs["grads_in"] = arrays["reduced"], arrays["grads"]
        outputs.update(layer_out=narrow, grad_hidden=wide, grad_attended=narrow)
        scratch.update(
            reduced=pltpu.VMEM((rows, width), F32),
            grads=pltpu.VMEM((rows, width), F32),
            sums=pltpu.VMEM((8, width), F32),
            grad_mixed=pltpu.VMEM((rows, width), BF16),
            term=pltpu.VMEM((width, width), F32),
        )
    steps = len(part) * (pieces // 2)
    scratch.update(
        up_tile=pltpu.VMEM((steps, width, 2 * TILE), BF16),
        down_tile=pltpu.VMEM((steps, 2 * TILE, width), BF16),
        up_sems=pltpu.SemaphoreType.DMA((steps, 2, pieces)),
        down_sems=pltpu.SemaphoreType.DMA((steps, 2, width // TILE)),
        up_term=pltpu.VMEM((width, 2 * TILE), F32),
    )

    def spec(name, array):
        if name[:7] == "message":
            return pl.BlockSpec(memory_space=pl.ANY)
        once = pl.Buffered(1)
        rank = len(array.shape)
        return pl.BlockSpec(array.shape, lambda i, *_: (0,) * rank, pipeline_mode=once)

    results = pl.pallas_call(
        functools.partial(
            feed_kernel,
            pieces=pieces,
            part=part,
            first=first,
            last=last,
            names=(*inputs, *outputs, *scratch),
        ),
        grid_spec=pltpu.PrefetchScalarGridSpec(
            num_scalar_prefetch=1,
            grid=(steps,),
            in_specs=[spec(*one) for one in inputs.items()],
            out_specs=[spec(*one) for one in outputs.items()],
            scratch_shapes=list(scratch.values()),
        ),
        out_shape=list(outputs.values()),
        compiler_params=params("arbitrary"),
        cost_estimate=weight(),
        name=f"feed{part[0]}",
    )(spot, *inputs.values())
    return {**arrays, **dict(zip(outputs, results))}


def query_kernel(spot_ref, scaled, *rest, pieces, seqs):
    grad_queries, weights = rest[:seqs], rest[seqs : seqs + pieces]
    grad_out, keep_out, send_out, weight, term = rest[seqs + pieces :]
    spot = spot_ref[0]
    rows = scaled.shape[0] // seqs
    place_rows(spot, weights, weight)
    for i, one in enumerate(grad_queries):
        here = slice(i * rows, (i + 1) * rows)
        part = dot_tn(scaled[here, :], one[...])
        term[...] = part if i == 0 else term[...] + part
        grad_out[here, :] = dot_nt(one[...], weight[...])
    split_out(spot, pieces, term, (keep_out, send_out))


def query_stage(spot, scaled, grad_queries, weights, ctx_size):
    rows, width = scaled.shape
    pieces = len(weights)
    tall = round_up(width // pieces * (width // TILE), 8 * ctx_size)
    message = jax.ShapeDtypeStruct((pieces // 2, tall, TILE), BF16)
    outs = [jax.ShapeDtypeStruct((rows, width), F32), message, message]
    whole = lambda one: pl.BlockSpec(one.shape, lambda i, *_: (0,) * len(one.shape))
    return pl.pallas_call(
        functools.partial(query_kernel, pieces=pieces, seqs=len(grad_queries)),
        grid_spec=pltpu.PrefetchScalarGridSpec(
            num_scalar_prefetch=1,
            grid=(1,),
            in_specs=[whole(scaled)]
            + [whole(one) for one in grad_queries]
            + [pl.BlockSpec((width // pieces, width), lambda i, *_: (0, 0))] * pieces,
            out_specs=[whole(one) for one in outs],
            scratch_shapes=[
                pltpu.VMEM((width, width), BF16),
                pltpu.VMEM((width, width), F32),
            ],
        ),
        out_shape=outs,
        compiler_params=params(),
        cost_estimate=weight(),
        name="query_grad",
    )(spot, scaled, *grad_queries, *weights)


def last_kernel(spot_ref, tokens, gain, scaled, arrived, grad_scaled, grad_hidden, *rest, pieces):
    weights = rest[:pieces]
    input_grad, keep_out, send_out, weight, sums, term, grad_shared = rest[pieces:]
    spot = spot_ref[0]
    width = tokens.shape[1]
    place_rows(spot, weights, weight)
    sums[...] = jnp.zeros_like(sums)
    places, seqs, here, unused = arrived.shape
    for i in range(seqs):
        total = arrived[0, i].astype(F32)
        for j in range(1, places):
            total = total + arrived[j, i].astype(F32)
        grad_shared[i * here : (i + 1) * here, :] = total.astype(BF16)
    term[...] = dot_tn(scaled[...], grad_shared[...])
    split_out(spot, pieces, term, (keep_out, send_out))

    def run(rows):
        normed, inverse = normalize(tokens[rows, :].astype(F32))
        grad = grad_scaled[rows, :] + dot_nt(grad_shared[rows, :], weight[...])
        sums[...] += jnp.sum((grad * normed).reshape(STEP // 8, 8, width), axis=0)
        input_grad[rows, :] = grad_hidden[rows, :] + norm_back(
            grad * gain[...], normed, inverse
        )

    over_rows(tokens.shape[0], run)
    put_vector(
        pieces, jnp.sum(sums[...], axis=0, keepdims=True), (keep_out, send_out), 0, LANES
    )


def last_stage(spot, tokens, gain, scaled, arrived, grad_scaled, grad_hidden, weights, places):
    rows, width = tokens.shape
    pieces = len(weights)
    message = jax.ShapeDtypeStruct(
        (pieces // 2, round_up(width // pieces, 8 * places), 2 * LANES), BF16
    )
    return pl.pallas_call(
        functools.partial(last_kernel, pieces=pieces),
        grid_spec=pltpu.PrefetchScalarGridSpec(
            num_scalar_prefetch=1,
            grid=(),
            in_specs=[pl.BlockSpec(memory_space=pltpu.VMEM)] * (6 + pieces),
            out_specs=[pl.BlockSpec(memory_space=pltpu.VMEM)] * 3,
            scratch_shapes=[
                pltpu.VMEM((width, LANES), BF16),
                pltpu.VMEM((8, width), F32),
                pltpu.VMEM((width, LANES), F32),
                pltpu.VMEM((rows, LANES), BF16),
            ],
        ),
        out_shape=[jax.ShapeDtypeStruct((rows, width), F32), message, message],
        compiler_params=params(),
        cost_estimate=weight(),
        name="last",
    )(spot, tokens, gain, scaled, arrived, grad_scaled, grad_hidden, *weights)


def final_kernel(
    place_ref, early_own, early_other, last_own, last_other, late,
    down_out, up_out, mixing_out, query_out, shared_out, first_out, second_out, whole,
    *, chunks, pieces, width, query_rows,
):
    height = width // pieces
    groups = width // TILE
    places, deep = late.shape[0], last_own.shape[0]
    low, high = place_ref[0] & 1, place_ref[0] >> 1

    def columns(out, first_row, rows, out_row, across):
        for g in range(across):
            row = first_row + g * rows
            out[out_row : out_row + rows, g * TILE : (g + 1) * TILE] = whole[row : row + rows, :]

    def put_chunk(chunk):
        columns(down_out, 0, TILE, chunk * TILE, groups)
        for j in range(pieces):
            row = width + j * height
            column = (j * chunks + chunk) * TILE
            up_out[:, column : column + TILE] = whole[row : row + height, :]

    def load(source, begin, rows):
        for c in range(places):
            whole[c * rows : (c + 1) * rows, :] = source[c, begin : begin + rows, :].astype(F32)

    def load_halves(own, other, at):
        rows = own.shape[2]
        for half, x in ((own, low), (other, 1 - low)):
            for k in range(deep):
                begin = pl.multiple_of((x * deep + (high ^ k)) * rows, 8)
                whole[pl.ds(begin, rows), :] = half[k, at].astype(F32)

    for chunk in range(chunks - 1):
        load_halves(early_own, early_other, chunk)
        put_chunk(chunk)
    load_halves(last_own, last_other, 0)
    put_chunk(chunks - 1)
    columns(mixing_out, 2 * width, height, 0, groups)
    row = 2 * width + groups * height
    second_out[...] = whole[row : row + second_out.shape[0], 0:LANES]
    load(late, 0, query_rows)
    columns(query_out, 0, height, 0, groups)
    load(late, query_rows, late.shape[1] - query_rows)
    shared_out[...] = whole[0:height, 0:LANES]
    first_out[...] = whole[0 : first_out.shape[0], LANES:]


def final_stage(place, halves, late, query_rows, chunks, pieces, width):
    height = width // pieces
    shape = lambda *dims: jax.ShapeDtypeStruct(dims, F32)
    vector = round_up(width // LANES, 8)
    tallest = max(2 * one.shape[0] * one.shape[2] for one in halves)
    tallest = max(tallest, late.shape[0] * late.shape[1])
    return pl.pallas_call(
        functools.partial(
            final_kernel, chunks=chunks, pieces=pieces, width=width, query_rows=query_rows
        ),
        grid_spec=pltpu.PrefetchScalarGridSpec(
            num_scalar_prefetch=1,
            grid=(),
            in_specs=[pl.BlockSpec(memory_space=pltpu.VMEM)] * 5,
            out_specs=[pl.BlockSpec(memory_space=pltpu.VMEM)] * 7,
            scratch_shapes=[pltpu.VMEM((tallest, TILE), F32)],
        ),
        out_shape=[
            shape(chunks * TILE, width),
            shape(height, pieces * chunks * TILE),
            shape(height, width),
            shape(height, width),
            shape(height, LANES),
            shape(vector, LANES),
            shape(vector, LANES),
        ],
        compiler_params=params(),
        cost_estimate=weight(),
        name="final",
    )(place, *halves, late)


def swap(values, axis, size, mask):
    return lax.ppermute(values, axis, [(i, i ^ mask) for i in range(size)])


class Gather:
    def __init__(self, piece, size):
        self.size, self.own = size, piece
        self.far = swap(piece, "wt", size, 2)
        self.near = swap(piece, "wt", size, 1)

    def finish(self):
        return [self.own, self.near, self.far, swap(self.far, "wt", self.size, 1)]


def own_order(values, spot, size):
    mask = 1
    while mask < size:
        split = values.reshape((size // (2 * mask), 2, mask) + values.shape[1:])
        split = jnp.where((spot & mask) != 0, split[:, ::-1], split)
        values = split.reshape(values.shape)
        mask *= 2
    return values


class Transfer:
    def __init__(self, held, sent, routes):
        self.held, self.sent, self.routes, self.coming = held, sent, routes, []

    def launch(self):
        if self.sent:
            self.coming = [swap(one, *route) for one, route in zip(self.sent, self.routes)]
            self.sent = []

    def add(self, pick):
        return pick(self.held).astype(F32) + pick(self.coming[0]).astype(F32)


class Reduction(Transfer):
    def __init__(self, keep, send, place, sizes):
        self.wt_size, self.ctx_size = sizes
        self.groups = self.ctx_size // 2
        self.low, self.high = place & 1, place >> 1
        *outer, rows, self.lanes = keep.shape
        self.rows = rows if len(outer) == 1 else 2 * rows
        inner = (self.groups, self.rows // self.ctx_size, self.lanes)
        split = (*outer, *inner) if len(outer) == 2 else (*outer, 2, *inner)
        super().__init__(
            keep.reshape(split), [send.reshape(split)], [("wt", self.wt_size, 1)]
        )

    def y(self, cuts=()):
        edges = (0, *cuts, self.rows // self.ctx_size)
        self.later = [
            self.add(lambda v: v[1][..., begin:end, :]).astype(BF16)
            for begin, end in zip(edges, edges[1:])
        ]
        self.held = self.add(lambda v: v[0])
        self.sent = [self.later.pop(0)]
        self.routes = [("wt", self.wt_size, 2)]

    def y_more(self):
        self.before, self.sent = self.coming, [self.later.pop(0)]

    def y_joined(self):
        self.coming = [jnp.concatenate(self.before + self.coming, axis=-2)]

    def x(self):
        half = lambda x: self.add(lambda v: lax.dynamic_index_in_dim(v, x, 0, False))
        self.held, self.sent = half(self.low), [half(1 - self.low).astype(BF16)]
        self.routes = [("ctx", self.ctx_size, 1)]

    def far(self):
        return [("ctx", self.ctx_size, 2 * k) for k in range(1, self.groups)]

    def z(self, *others):
        def part(k):
            pick = lambda v: lax.dynamic_index_in_dim(v, self.high ^ k, 0, False)
            return jnp.stack([one.add(pick) for one in (self, *others)])

        self.sent = [part(k).astype(BF16) for k in range(1, self.groups)]
        self.held = part(0)
        self.routes = self.far()

    def total(self):
        parts = [self.held.astype(F32)] + [one.astype(F32) for one in self.coming]
        while len(parts) > 1:
            parts = [parts[i] + parts[i + 1] for i in range(0, len(parts), 2)]
        return parts[0].astype(BF16)

    def z_back(self):
        self.held = self.total()
        self.sent = [self.held] * (self.groups - 1)

    def x_back(self):
        self.held = jnp.stack([self.held] + self.coming)
        self.sent = [self.held]
        self.routes = [("ctx", self.ctx_size, 1)]

    def everywhere(self):
        return self.add(lambda v: v).astype(BF16).reshape(
            self.ctx_size, self.rows // self.ctx_size, self.lanes
        )


def tie(main, *reductions, came=()):
    state = [(one.held, one.sent) for one in reductions]
    main, state, coming = lax.optimization_barrier((main, state, [one.coming for one in came]))
    for one, (held, sent) in zip(reductions, state):
        one.held, one.sent = held, sent
    for one, values in zip(came, coming):
        one.coming = values
    for one in reductions:
        one.launch()
    return main


def body(
    tokens,
    documents,
    first_gain,
    query_weight,
    shared_weight,
    mixing_weight,
    second_gain,
    up_weight,
    down_weight,
    cotangent,
    *,
    wt_size,
    ctx_size,
):
    sizes = (wt_size, ctx_size)
    seqs, rows, width = tokens.shape
    count = seqs * rows
    spot_index = lax.axis_index("wt")
    place = lax.axis_index("ctx")
    spot = spot_index.astype(jnp.int32).reshape(1)
    length = ctx_size * rows
    doc_most = length * 5 // 8
    before = min(ctx_size - 1, -(-(doc_most - 1) // rows))
    blocks = before + 1
    height = width // wt_size
    chunks = up_weight.shape[1] // wt_size // TILE

    gain_rows = -(-height // LANES)
    pad = lambda gain: jnp.pad(gain, (0, gain_rows * LANES - height)).reshape(gain_rows, LANES)
    small = jnp.concatenate([shared_weight, pad(first_gain), pad(second_gain)], axis=0)
    small = jnp.pad(small, ((0, -small.shape[0] % 16), (0, 0)))
    small_pieces = Gather(small, wt_size).finish()
    query_gather = Gather(query_weight, wt_size)

    gains = jnp.stack([one[height : height + 2 * gain_rows] for one in small_pieces])
    gains = gains.reshape(wt_size, 2, gain_rows * LANES)[:, :, :height].astype(F32)
    gains = own_order(gains, spot_index, wt_size)
    gain_one = gains[:, 0].reshape(1, width)
    gain_two = gains[:, 1].reshape(1, width)

    inputs = tokens.reshape(count, width)
    doc_lines = documents.astype(BF16).reshape(seqs, rows // LANES, LANES)
    scaled_one, shared = first_stage(spot, inputs, gain_one, doc_lines, small_pieces, ctx_size)
    shared, query_gather.far, mixing_weight, *packed = lax.optimization_barrier(
        (shared, query_gather.far, mixing_weight, up_weight, down_weight)
    )
    keyvals = lax.all_to_all(shared, "ctx", 0, 0).reshape(ctx_size, seqs, rows + DOC_ROWS, LANES)
    packed = list(pack_stage(*packed, chunks, wt_size))
    gathers = [Gather(packed[0], wt_size)]
    mixing_gather = Gather(mixing_weight, wt_size)
    marks = jnp.broadcast_to(documents.astype(F32)[:, :, None], (seqs, rows, LANES))
    query_pieces = query_gather.finish()
    place_one = place.astype(jnp.int32).reshape(1)

    queries = project(spot, scaled_one, query_pieces).reshape(seqs, rows, width)
    keyvals, gathers[0].far, mixing_gather.far, queries, marks, packed[1:] = (
        lax.optimization_barrier(
            (keyvals, gathers[0].far, mixing_gather.far, queries, marks, packed[1:])
        )
    )
    gathered = [gathers[0].finish()]
    mixing_pieces = mixing_gather.finish()
    gathers.append(Gather(packed[1], wt_size))
    starts, exact, attended, logs = attend(place_one, queries, marks, keyvals, blocks)
    attended, gathers[1].far, packed[2:] = lax.optimization_barrier(
        (attended, gathers[1].far, packed[2:])
    )
    gathered.append(gathers[1].finish())
    gathers += [Gather(one, wt_size) for one in packed[2:]]

    arrays = {
        "attended": attended.reshape(count, width),
        "tokens": inputs,
        "gain": gain_two,
        "cotangent": cotangent.reshape(count, width),
    }
    feed = lambda arrays, part: feed_stage(
        spot, arrays, gathered, mixing_pieces, part, chunks, ctx_size
    )
    arrays = feed(arrays, (0, 1))
    zero, one = (
        Reduction(arrays[f"keep{chunk}"], arrays[f"send{chunk}"], place, sizes) for chunk in (0, 1)
    )
    arrays, gathers[-1].far = tie((arrays, gathers[-1].far), zero, one)
    gathered.append(gathers[-1].finish())
    arrays = tie(arrays, zero, one, came=[zero])
    zero.y()
    arrays = tie(arrays, zero, one, came=[one])
    one.x()
    arrays = tie(arrays, zero, one)
    arrays = feed(arrays, (2,))
    two = Reduction(arrays["keep2"], arrays["send2"], place, sizes)
    grad_attended = tie(arrays["grad_attended"], zero, one, two, came=[zero, one])
    zero.x()
    one.y()
    grad_attended = tie(grad_attended, zero, one, two, came=[two])
    two.y([round_up(two.rows // ctx_size * 2 // 5, 8)])
    grad_attended = tie(grad_attended, zero, one, two).reshape(seqs, rows, width)
    grad_queries, terms = [], []
    for seq in range(seqs):
        part, keep, send = attend_back(
            seq, place_one, queries, starts, exact, logs, grad_attended, keyvals, blocks
        )
        came = [zero, one, two] if seq == 0 else [zero, two]
        term = Transfer(keep, [send], [("ctx", ctx_size, 1)])
        part, grad_attended = tie((part, grad_attended), *came, term, *terms, came=came + terms)
        grad_queries.append(part[0])
        terms.append(term)
        if seq == 0:
            zero.z(one)
            two.y_more()
            grad_attended = tie(grad_attended, zero, two)
    two.y_joined()
    two.x()
    zero.z_back()
    grad_queries = tie(grad_queries, zero, two)
    grad_scaled, keep, send = query_stage(spot, scaled_one, grad_queries, query_pieces, ctx_size)
    query = Reduction(keep, send, place, sizes)
    grad_scaled = tie(grad_scaled, zero, query, *terms, came=terms[1:])
    arriving = jnp.stack([one.add(lambda v: v).astype(BF16) for one in terms], axis=1)
    arriving, grad_scaled = tie((arriving, grad_scaled), query)
    arriving = lax.all_to_all(
        arriving,
        "ctx",
        0,
        0,
        axis_index_groups=[list(range(x, ctx_size, 2)) for x in range(2)],
    )
    query.y()
    grad_scaled = tie(grad_scaled, query)
    grad_scaled = tie(grad_scaled, two, came=[two])
    two.z()
    grad_scaled, arriving = tie((grad_scaled, arriving), two)
    input_grad, keep, send = last_stage(
        spot, inputs, gain_one, scaled_one, arriving, grad_scaled, arrays["grad_hidden"], small_pieces, ctx_size
    )
    shared = Reduction(keep, send, place, sizes)
    input_grad = tie(input_grad, zero, two, shared, query, came=[two, query])
    two.z_back()
    input_grad = tie(input_grad, two)
    zero.x_back()
    input_grad = tie(input_grad, zero)
    input_grad = tie(input_grad, shared, query, came=[shared])
    shared.y()
    input_grad = tie(input_grad, shared)
    input_grad = tie(input_grad, shared, query, came=[shared])
    late = jnp.concatenate([query.everywhere(), shared.everywhere()], axis=1)
    late = lax.all_to_all(late, "ctx", 0, 0)
    two.x_back()
    input_grad = tie(input_grad, two)
    late = jnp.sum(late.astype(F32), axis=0).astype(BF16)
    late = lax.all_to_all(jnp.broadcast_to(late, (ctx_size,) + late.shape), "ctx", 0, 0)
    down_grad, up_grad, mixing_grad, query_grad, shared_grad, first_grad, second_grad = final_stage(
        place_one,
        [zero.held, zero.coming[0], two.held, two.coming[0]],
        late,
        query.rows // ctx_size,
        chunks,
        wt_size,
        width,
    )

    def own_gain(lines):
        vector = lines[: width // LANES].reshape(width)
        return lax.dynamic_slice_in_dim(vector, spot_index * height, height, 0)

    return (
        arrays["layer_out"].reshape(seqs, rows, width),
        input_grad.reshape(seqs, rows, width),
        own_gain(first_grad),
        query_grad,
        shared_grad,
        mixing_grad,
        own_gain(second_grad),
        up_grad,
        down_grad,
    )


def solution(mesh):
    in_specs = (
        P("wt", "ctx", None),
        P("wt", "ctx"),
        P("wt"),
        P("wt", None),
        P("wt", None),
        P("wt", None),
        P("wt"),
        P("wt", None),
        P("wt", None),
        P("wt", "ctx", None),
    )
    out_specs = (
        P("wt", "ctx", None),
        P("wt", "ctx", None),
        P("wt"),
        P("wt", None),
        P("wt", None),
        P("wt", None),
        P("wt"),
        P("wt", None),
        P("wt", None),
    )
    run = functools.partial(body, wt_size=mesh.shape["wt"], ctx_size=mesh.shape["ctx"])
    return jax.shard_map(run, mesh=mesh, in_specs=in_specs, out_specs=out_specs, check_vma=False)
```

```python
import functools
import math

import jax
import jax.numpy as jnp
from jax import lax
from jax.experimental import pallas as pl
from jax.experimental.pallas import tpu as pltpu
from jax.sharding import PartitionSpec as P

HEADS = 12
HEAD_DIM = 64
PAIRS = HEADS // 2
LANES = 128
EPSILON = 1e-05
BIAS = -1e30
SCALE = math.log2(math.e) / HEAD_DIM**0.5
F32 = jnp.float32
BF16 = jnp.bfloat16
GELU_ROOT = math.sqrt(2.0 / math.pi)
GELU_CUBE = 0.044715


def params(*semantics):
    return pltpu.CompilerParams(
        dimension_semantics=semantics or None, vmem_limit_bytes=56 * 1024 * 1024
    )


def weight():
    return pl.CostEstimate(flops=1, bytes_accessed=1, transcendentals=0)


def dot_nn(a, b):
    return lax.dot_general(a, b, (((1,), (0,)), ((), ())), preferred_element_type=F32)


def dot_nt(a, b):
    return lax.dot_general(a, b, (((1,), (1,)), ((), ())), preferred_element_type=F32)


def dot_tn(a, b):
    return lax.dot_general(a, b, (((0,), (0,)), ((), ())), preferred_element_type=F32)


def normalize(values):
    center = values - jnp.mean(values, axis=-1, keepdims=True)
    spread = jnp.mean(center * center, axis=-1, keepdims=True)
    inverse = lax.rsqrt(spread + EPSILON)
    return center * inverse, inverse


def norm_back(grad, normed, inverse):
    mean_grad = jnp.mean(grad, axis=-1, keepdims=True)
    mean_both = jnp.mean(grad * normed, axis=-1, keepdims=True)
    return (grad - mean_grad - normed * mean_both) * inverse


def place_rows(spot, pieces, scratch):
    height = scratch.shape[0] // len(pieces)
    for r, piece in enumerate(pieces):
        begin = pl.multiple_of((spot ^ r) * height, height)
        scratch[pl.ds(begin, height), :] = piece[0:height, :]


STEP = 128


def over_rows(rows, run):
    def one(index, carried):
        run(pl.ds(pl.multiple_of(index * STEP, STEP), STEP))
        return carried

    lax.fori_loop(0, rows // STEP, one, 0)


TILE = 256


def pack_kernel(up, down, *outs, chunks, pieces):
    width = down.shape[1]
    height = up.shape[0]
    for chunk, out in enumerate(outs):
        for g in range(width // TILE):
            out[g * TILE : (g + 1) * TILE, :] = down[
                chunk * TILE : (chunk + 1) * TILE, g * TILE : (g + 1) * TILE
            ]
        for j in range(pieces):
            row, column = width + j * height, (j * chunks + chunk) * TILE
            out[row : row + height, :] = up[:, column : column + TILE]


def pack_stage(up, down, chunks, pieces):
    width = down.shape[1]
    return pl.pallas_call(
        functools.partial(pack_kernel, chunks=chunks, pieces=pieces),
        in_specs=[pl.BlockSpec(memory_space=pltpu.VMEM)] * 2,
        out_specs=[pl.BlockSpec(memory_space=pltpu.VMEM)] * chunks,
        out_shape=[jax.ShapeDtypeStruct((2 * width, TILE), BF16)] * chunks,
        compiler_params=params(),
        cost_estimate=weight(),
        name="pack",
    )(up, down)


DOC_ROWS = 16


def first_kernel(spot_ref, tokens, gain, documents, *rest, pieces):
    weights = rest[:pieces]
    scaled_out, shared_out, weight = rest[pieces:]
    place_rows(spot_ref[0], weights, weight)
    seqs, doc_lines, unused = documents.shape
    places, tall, unused = shared_out.shape
    tall = tall // seqs
    rows = tall - DOC_ROWS
    per_seq = rows // STEP

    def run(index, carried):
        here = pl.ds(pl.multiple_of(index * STEP, STEP), STEP)
        seq = index // per_seq
        there = pl.multiple_of(seq * tall + (index - seq * per_seq) * STEP, DOC_ROWS)
        normed, unused = normalize(tokens[here, :].astype(F32))
        scaled = (normed * gain[...]).astype(BF16)
        scaled_out[here, :] = scaled
        shared = dot_nn(scaled, weight[...]).astype(BF16)

        def put(c, carried):
            shared_out[c, pl.ds(there, STEP), :] = shared
            return carried

        return lax.fori_loop(0, places, put, carried)

    lax.fori_loop(0, seqs * per_seq, run, 0)

    def put(c, carried):
        for seq in range(seqs):
            begin = seq * tall + rows
            shared_out[c, begin : begin + DOC_ROWS, :] = jnp.zeros((DOC_ROWS, LANES), BF16)
            shared_out[c, begin : begin + doc_lines, :] = documents[seq]
        return carried

    lax.fori_loop(0, places, put, 0)


def first_stage(spot, tokens, gain, documents, weights, places):
    count, width = tokens.shape
    columns = weights[0].shape[1]
    seqs, doc_lines, unused = documents.shape
    return pl.pallas_call(
        functools.partial(first_kernel, pieces=len(weights)),
        grid_spec=pltpu.PrefetchScalarGridSpec(
            num_scalar_prefetch=1,
            grid=(),
            in_specs=[pl.BlockSpec(memory_space=pltpu.VMEM)] * (3 + len(weights)),
            out_specs=[pl.BlockSpec(memory_space=pltpu.VMEM)] * 2,
            scratch_shapes=[pltpu.VMEM((width, columns), BF16)],
        ),
        out_shape=[
            jax.ShapeDtypeStruct((count, width), BF16),
            jax.ShapeDtypeStruct((places, count + seqs * DOC_ROWS, columns), BF16),
        ],
        compiler_params=params(),
        cost_estimate=weight(),
        name="first_norm",
    )(spot, tokens, gain, documents, *weights)


def project_kernel(spot_ref, operand, *rest, pieces):
    weights = rest[:pieces]
    out, weight_all = rest[pieces:]
    place_rows(spot_ref[0], weights, weight_all)
    out[...] = dot_nn(operand[...], weight_all[...]).astype(out.dtype)


def project(spot, operand, weights):
    rows, width = operand.shape
    columns = weights[0].shape[1]
    return pl.pallas_call(
        functools.partial(project_kernel, pieces=len(weights)),
        grid_spec=pltpu.PrefetchScalarGridSpec(
            num_scalar_prefetch=1,
            grid=(),
            in_specs=[pl.BlockSpec(memory_space=pltpu.VMEM)] * (1 + len(weights)),
            out_specs=pl.BlockSpec(memory_space=pltpu.VMEM),
            scratch_shapes=[pltpu.VMEM((width, columns), BF16)],
        ),
        out_shape=jax.ShapeDtypeStruct((rows, columns), BF16),
        compiler_params=params(),
        cost_estimate=weight(),
        name="project",
    )(spot, operand, *weights)


def low_lanes(shape):
    return lax.broadcasted_iota(jnp.int32, shape, len(shape) - 1) < HEAD_DIM


def swap_halves(values):
    return pltpu.roll(values, HEAD_DIM, 1)


def stacked_pairs(ref):
    return jnp.concatenate(
        [ref[0, :, p * LANES : (p + 1) * LANES] for p in range(PAIRS)], axis=0
    )


def tile_bias(starts, key_begin, row_begin, tile_rows, tile_keys):
    key_place = key_begin + lax.broadcasted_iota(jnp.int32, (tile_rows, tile_keys), 1)
    row_place = row_begin + lax.broadcasted_iota(jnp.int32, (tile_rows, tile_keys), 0)
    first = jnp.concatenate([starts] * (tile_keys // LANES), axis=1)
    allowed = (key_place >= first) & (key_place <= row_place)
    bias = jnp.where(allowed, 0.0, BIAS)
    bias = jnp.concatenate([bias, bias], axis=1)
    return jnp.concatenate([bias] * PAIRS, axis=0)


def block_at(place_ref, j, blocks):
    return jnp.maximum(place_ref[0] - (blocks - 1) + j, 0)


def attend_kernel(
    place_ref, queries, keyvals, starts_out, exact_out, rounded_out, logs_out, *rest,
    blocks, tile_rows, tile_keys
):
    key_even, key_odd, value_even, value_odd, score_scratch, most, total = rest
    rows = keyvals.shape[2] - DOC_ROWS
    tile = pl.program_id(1)

    @pl.when(tile == 0)
    def _():
        low = low_lanes((rows, LANES))
        for j in range(blocks):
            whole = keyvals[block_at(place_ref, j, blocks), 0, 0:rows, :].astype(F32)
            turned = swap_halves(whole)
            place = pl.ds(j * rows, rows)
            key_even[place, :] = jnp.where(low, whole, 0.0).astype(BF16)
            key_odd[place, :] = jnp.where(low, 0.0, turned).astype(BF16)
            value_even[place, 0:LANES] = jnp.where(low, turned, 0.0).astype(BF16)
            value_even[place, LANES:] = jnp.where(low, 1.0, 0.0).astype(BF16)
            value_odd[place, 0:LANES] = jnp.where(low, 0.0, whole).astype(BF16)
            value_odd[place, LANES:] = jnp.where(low, 0.0, 1.0).astype(BF16)

    own = keyvals[place_ref[0], 0, rows:, :].astype(F32)
    lines = rows // LANES
    marks = [jnp.broadcast_to(own[h : h + 1, :], (LANES, LANES)).T for h in range(lines)]
    marks = jnp.concatenate(marks, axis=0)
    if tile_rows != rows:
        marks = sum(
            jnp.where(tile == t, marks[t * tile_rows : (t + 1) * tile_rows, :], 0.0)
            for t in range(rows // tile_rows)
        )

    def smaller(j, count):
        lines = keyvals[block_at(place_ref, j, blocks), 0, rows:, :].astype(F32)
        missing = place_ref[0] - (blocks - 1) + j < 0
        for h in range(rows // LANES):
            line = jnp.where(missing, -1.0, lines[h : h + 1, :])
            count = count + jnp.where(line < marks, 1.0, 0.0)
        return count

    count = lax.fori_loop(0, blocks, smaller, jnp.zeros((tile_rows, LANES), F32))
    count = jnp.sum(count, axis=1, keepdims=True).astype(jnp.int32)
    starts = starts_out
    starts[0] = jnp.broadcast_to(count, (tile_rows, LANES))
    row_begin = (blocks - 1) * rows + tile * tile_rows
    begin = jnp.min(starts[0]) // tile_keys
    end = (row_begin + tile_rows - 1) // tile_keys + 1
    stacked = stacked_pairs(queries)
    most[...] = jnp.full_like(most, -3e38)
    copies = tile_keys // LANES

    def score(index):
        key_begin = pl.multiple_of(index * tile_keys, tile_keys)
        place = pl.ds(key_begin, tile_keys)
        both = jnp.concatenate([key_even[place, :], key_odd[place, :]], axis=0)
        values = dot_nt(stacked, both) + tile_bias(
            starts[0], key_begin, row_begin, tile_rows, tile_keys
        )
        score_scratch[index - begin] = values
        half = []
        for h in range(2):
            part = values[:, h * tile_keys : h * tile_keys + LANES]
            for q in range(1, copies):
                at = h * tile_keys + q * LANES
                part = jnp.maximum(part, values[:, at : at + LANES])
            half.append(part)
        return jnp.concatenate(half, axis=1)

    def output(index):
        place = pl.ds(pl.multiple_of(index * tile_keys, tile_keys), tile_keys)
        both = jnp.concatenate([value_even[place, :], value_odd[place, :]], axis=0)
        shift = jnp.concatenate([most[:, 0:LANES]] * copies + [most[:, LANES:]] * copies, axis=1)
        powers = jnp.exp2((score_scratch[index - begin] - shift) * SCALE).astype(BF16)
        return dot_nn(powers, both)

    def in_pairs(one, join, total):
        def two(index, carried):
            at = begin + 2 * index
            total[...] = join(total[...], join(one(at), one(at + 1)))
            return carried

        count = end - begin
        lax.fori_loop(0, count // 2, two, 0)

        @pl.when(count % 2 == 1)
        def _():
            total[...] = join(total[...], one(end - 1))

    in_pairs(score, jnp.maximum, most)
    stack = PAIRS * tile_rows
    for h in range(2):
        part = jnp.max(most[:, h * LANES : (h + 1) * LANES], axis=1, keepdims=True)
        most[:, h * LANES : (h + 1) * LANES] = jnp.broadcast_to(part, (stack, LANES))
    total[...] = jnp.zeros_like(total)
    in_pairs(output, jnp.add, total)
    low = low_lanes((tile_rows, LANES))
    for p in range(PAIRS):
        at = pl.ds(p * tile_rows, tile_rows)
        lanes = slice(p * LANES, (p + 1) * LANES)
        sums = total[at, LANES:]
        out = total[at, 0:LANES] / sums
        exact_out[0, :, lanes] = out
        rounded_out[0, :, lanes] = out.astype(BF16)
        shift = jnp.where(low, most[at, 0:LANES], most[at, LANES:])
        logs_out[0, :, lanes] = shift * SCALE + jnp.log2(sums)


def attend_back_kernel(
    place_ref, queries, starts, exact, logs, grads, keyvals, *rest,
    seq, blocks, tile_rows, tile_keys
):
    grad_queries, keep, send, *rest = rest
    (
        key_even, key_odd, value_even, value_odd,
        key_total, value_total, query_total,
        log_even, log_odd, delta_even, delta_odd,
    ) = rest
    rows = keyvals.shape[2] - DOC_ROWS
    tile = pl.program_id(0)

    @pl.when(tile == 0)
    def _():
        low = low_lanes((rows, LANES))
        for j in range(blocks):
            whole = keyvals[block_at(place_ref, j, blocks), 0, 0:rows, :].astype(F32)
            turned = swap_halves(whole)
            place = pl.ds(j * rows, rows)
            key_even[place, :] = jnp.where(low, whole, 0.0).astype(BF16)
            key_odd[place, :] = jnp.where(low, 0.0, turned).astype(BF16)
            value_even[place, :] = jnp.where(low, turned, 0.0).astype(BF16)
            value_odd[place, :] = jnp.where(low, 0.0, whole).astype(BF16)
        key_total[...] = jnp.zeros_like(key_total)
        value_total[...] = jnp.zeros_like(value_total)

    row_begin = (blocks - 1) * rows + tile * tile_rows
    begin = jnp.min(starts[0]) // tile_keys
    end = (row_begin + tile_rows - 1) // tile_keys + 1
    stacked = stacked_pairs(queries)
    grad_stacked = stacked_pairs(grads)
    stacked_turned = stacked.T
    grad_turned = grad_stacked.T
    stack = PAIRS * tile_rows
    low = low_lanes((tile_rows, LANES))
    for p in range(PAIRS):
        at = pl.ds(p * tile_rows, tile_rows)
        lanes = slice(p * LANES, (p + 1) * LANES)
        log = logs[0, :, lanes]
        log_turned = swap_halves(log)
        log_even[at, :] = jnp.where(low, log, log_turned)
        log_odd[at, :] = jnp.where(low, log_turned, log)
        terms_here = exact[0, :, lanes] * grads[0, :, lanes].astype(F32)
        even = jnp.sum(jnp.where(low, terms_here, 0.0), axis=1, keepdims=True)
        odd = jnp.sum(jnp.where(low, 0.0, terms_here), axis=1, keepdims=True)
        delta_even[at, :] = jnp.broadcast_to(even, (tile_rows, LANES))
        delta_odd[at, :] = jnp.broadcast_to(odd, (tile_rows, LANES))
    query_total[...] = jnp.zeros_like(query_total)

    def step(index, carried):
        key_begin = pl.multiple_of(index * tile_keys, tile_keys)
        place = pl.ds(key_begin, tile_keys)
        keys = jnp.concatenate([key_even[place, :], key_odd[place, :]], axis=0)
        values = jnp.concatenate([value_even[place, :], value_odd[place, :]], axis=0)
        copies = tile_keys // LANES
        log = jnp.concatenate([log_even[...]] * copies + [log_odd[...]] * copies, axis=1)
        delta = jnp.concatenate([delta_even[...]] * copies + [delta_odd[...]] * copies, axis=1)
        scores = dot_nt(stacked, keys) + tile_bias(
            starts[0], key_begin, row_begin, tile_rows, tile_keys
        )
        chances = jnp.exp2(scores * SCALE - log)
        grad_probs = dot_nt(grad_stacked, values)
        grad_scores = (chances * (grad_probs - delta)).astype(BF16)
        query_total[...] += dot_nn(grad_scores, keys)
        key_total[index] += dot_nn(stacked_turned, grad_scores)
        value_total[index] += dot_nn(grad_turned, chances.astype(BF16))
        return carried

    lax.fori_loop(begin, end, step, 0)
    root = 1.0 / HEAD_DIM**0.5
    for p in range(PAIRS):
        at = pl.ds(p * tile_rows, tile_rows)
        lanes = slice(p * LANES, (p + 1) * LANES)
        grad_queries[0, :, lanes] = (query_total[at, :] * root).astype(BF16)

    @pl.when(tile == pl.num_programs(0) - 1)
    def _():
        per_block = rows // tile_keys
        keep[...] = jnp.zeros_like(keep)
        send[...] = jnp.zeros_like(send)

        def block_terms(j, carried):
            for i in range(per_block):
                index = j * per_block + i
                key = key_total[index]
                value = value_total[index]
                key = key[0:HEAD_DIM, 0:tile_keys] + key[HEAD_DIM:, tile_keys:]
                value = value[0:HEAD_DIM, 0:tile_keys] + value[HEAD_DIM:, tile_keys:]
                both = jnp.concatenate([key * root, value], axis=0)
                both = both.T.astype(BF16)
                owner = block_at(place_ref, j, blocks)
                here = slice(i * tile_keys, (i + 1) * tile_keys)
                same = (owner & 1) == (place_ref[0] & 1)

                @pl.when(same)
                def _():
                    keep[owner >> 1, here, :] = both

                @pl.when(jnp.logical_not(same))
                def _():
                    send[owner >> 1, here, :] = both

            return carried

        missing = jnp.maximum(blocks - 1 - place_ref[0], 0)
        lax.fori_loop(missing, blocks, block_terms, 0)


def attention_sizes(rows, blocks, kept):
    tile_keys = 256 if rows % 256 == 0 else 128
    tile_rows = 128
    if kept and rows % 256 == 0 and blocks * rows * 256 * HEADS * 4 < 24 * 1024 * 1024:
        tile_rows = 256
    return tile_rows, tile_keys, blocks * rows // tile_keys


def attend(place, queries, keyvals, blocks):
    unused, seqs, tall, unused = keyvals.shape
    rows = tall - DOC_ROWS
    width = queries.shape[2]
    tile_rows, tile_keys, key_tiles = attention_sizes(rows, blocks, True)
    stack = PAIRS * tile_rows
    keys = blocks * rows
    row_spec = lambda lanes: pl.BlockSpec((1, tile_rows, lanes), lambda s, t, *_: (s, t, 0))
    wide = lambda dtype: jax.ShapeDtypeStruct((seqs, rows, width), dtype)
    return pl.pallas_call(
        functools.partial(
            attend_kernel, blocks=blocks, tile_rows=tile_rows, tile_keys=tile_keys
        ),
        grid_spec=pltpu.PrefetchScalarGridSpec(
            num_scalar_prefetch=1,
            grid=(seqs, rows // tile_rows),
            in_specs=[
                row_spec(width),
                pl.BlockSpec((keyvals.shape[0], 1, tall, LANES), lambda s, t, *_: (0, s, 0, 0)),
            ],
            out_specs=[row_spec(LANES)] + [row_spec(width)] * 3,
            scratch_shapes=[
                pltpu.VMEM((keys, LANES), BF16),
                pltpu.VMEM((keys, LANES), BF16),
                pltpu.VMEM((keys, 2 * LANES), BF16),
                pltpu.VMEM((keys, 2 * LANES), BF16),
                pltpu.VMEM((key_tiles, stack, 2 * tile_keys), F32),
                pltpu.VMEM((stack, 2 * LANES), F32),
                pltpu.VMEM((stack, 2 * LANES), F32),
            ],
        ),
        out_shape=[
            jax.ShapeDtypeStruct((seqs, rows, LANES), jnp.int32),
            wide(F32),
            wide(BF16),
            wide(F32),
        ],
        compiler_params=params("arbitrary", "arbitrary"),
        cost_estimate=weight(),
        name="attend",
    )(place, queries, keyvals)


def attend_back(
    seq, place, queries, starts, exact, logs, grads, keyvals, blocks
):
    seqs, rows, width = queries.shape
    ctx_size = keyvals.shape[0]
    tile_rows, tile_keys, key_tiles = attention_sizes(rows, blocks, False)
    stack = PAIRS * tile_rows
    keys = blocks * rows
    row_spec = lambda lanes: pl.BlockSpec((1, tile_rows, lanes), lambda t, *_: (seq, t, 0))
    return pl.pallas_call(
        functools.partial(
            attend_back_kernel, seq=seq, blocks=blocks, tile_rows=tile_rows, tile_keys=tile_keys
        ),
        grid_spec=pltpu.PrefetchScalarGridSpec(
            num_scalar_prefetch=1,
            grid=(rows // tile_rows,),
            in_specs=[row_spec(width), row_spec(LANES)]
            + [row_spec(width)] * 3
            + [pl.BlockSpec((ctx_size, 1, keyvals.shape[2], LANES), lambda t, *_: (0, seq, 0, 0))],
            out_specs=[
                pl.BlockSpec((1, tile_rows, width), lambda t, *_: (0, t, 0)),
            ]
            + [pl.BlockSpec((ctx_size // 2, rows, LANES), lambda t, *_: (0, 0, 0))] * 2,
            scratch_shapes=[pltpu.VMEM((keys, LANES), BF16)] * 4
            + [pltpu.VMEM((key_tiles, LANES, 2 * tile_keys), F32)] * 2
            + [pltpu.VMEM((stack, LANES), F32)] * 5,
        ),
        out_shape=[
            jax.ShapeDtypeStruct((1, rows, width), BF16),
        ]
        + [jax.ShapeDtypeStruct((ctx_size // 2, rows, LANES), BF16)] * 2,
        compiler_params=params("arbitrary"),
        cost_estimate=weight(),
        name="attend_back",
    )(place, queries, starts, exact, logs, grads, keyvals)


def round_up(count, unit):
    return -(-count // unit) * unit


def mixing_rows(width, pieces, ctx_size):
    unit = 8 * ctx_size
    tall = 2 * width + width // pieces * (width // TILE)
    return round_up(tall + width // LANES, unit) - 2 * width


def message_of(messages, s):
    return messages[s & 1], s >> 1


def split_out(spot, pieces, source, messages, first_row=0):
    height, lanes = source.shape[0] // pieces, messages[0].shape[2]
    across = min(lanes, source.shape[1])
    for s in range(pieces):
        out, at = message_of(messages, s)
        begin = pl.multiple_of((spot ^ s) * height, height)
        for g in range(source.shape[1] // across):
            row = first_row + g * height
            out[at, row : row + height, 0:across] = source[
                pl.ds(begin, height), g * lanes : g * lanes + across
            ].astype(BF16)


def put_vector(pieces, vector, messages, first_row, begin):
    height, lanes = messages[0].shape[1] - first_row, messages[0].shape[2]
    count = vector.shape[1] // LANES
    row = lax.broadcasted_iota(jnp.int32, (height, LANES), 0)
    block = jnp.zeros((height, LANES), F32)
    for i in range(count):
        block = jnp.where(row == i, vector[:, i * LANES : (i + 1) * LANES], block)
    for s in range(pieces):
        out, at = message_of(messages, s)
        out[at, first_row:, begin : begin + LANES] = block.astype(BF16)
        if begin == 0:
            out[at, first_row:, LANES:] = jnp.zeros((height, lanes - LANES), BF16)


def feed_kernel(spot_ref, *refs, pieces, part, first, last, names, early, late):
    use = dict(zip(names, refs))
    spot = spot_ref[0]
    step = pl.program_id(0)
    steps = len(part) * (pieces // 2)
    cotangent = use["cotangent"]
    reduced, grads, scaled, hidden = use["reduced"], use["grads"], use["scaled"], use["hidden"]
    up_tile, down_tile, up_sems, down_sems = (
        use["up_tile"], use["down_tile"], use["up_sems"], use["down_sems"]
    )
    rows, width = cotangent.shape
    height = width // pieces
    groups = width // TILE

    def messages_of(chunk):
        return use[f"keep{chunk}"], use[f"send{chunk}"]

    def owners(n):
        chunk, at = divmod(n, pieces // 2)
        return part[chunk], (2 * at, 2 * at + 1)

    def copies(n):
        chunk, pair = owners(n)
        for h, s in enumerate(pair):
            source = pl.multiple_of(width + (spot ^ s) * height, height)
            for r in range(pieces):
                row = pl.multiple_of((spot ^ r) * height, height)
                yield pltpu.make_async_copy(
                    use[f"message{chunk}_{r}"].at[pl.ds(source, height), :],
                    up_tile.at[n, pl.ds(row, height), pl.ds(h * TILE, TILE)],
                    up_sems.at[n, h, r],
                )
            for g in range(groups):
                yield pltpu.make_async_copy(
                    use[f"message{chunk}_{s}"].at[pl.ds(g * TILE, TILE), :],
                    down_tile.at[n, pl.ds(h * TILE, TILE), pl.ds(g * TILE, TILE)],
                    down_sems.at[n, h, g],
                )

    def beside(kind, names):
        for name in names:
            pair = use[f"{name}_far"], use[name]
            source, target = pair if kind == "in" else pair[::-1]
            yield pltpu.make_async_copy(source, target, use[f"{name}_sem"])

    @pl.when(step == 0)
    def _():
        for n in range(steps):
            for one in copies(n):
                one.start()
        for one in beside("in", late):
            one.start()
        if first:

            def begin(here):
                mixed = dot_nn(use["attended"][here, :], use["mixing_all"][...])
                values = use["tokens"][here, :].astype(F32) + mixed
                hidden[here, :] = values
                normed, unused = normalize(values)
                scaled[here, :] = (normed * use["gain"][...]).astype(BF16)

            place_rows(spot, [use[f"mixing{r}"] for r in range(pieces)], use["mixing_all"])
            over_rows(rows, begin)
            for one in beside("out", ("hidden", "scaled")):
                one.start()

    if first:

        @pl.when(step == pieces // 2)
        def _():
            for one in beside("out", ("keep0", "send0")):
                one.start()

        @pl.when(step == steps - 1)
        def _():
            for one in beside("out", early):
                one.wait()

    for n in range(steps):

        @pl.when(step == n)
        def _():
            for one in copies(n):
                one.wait()

    up = up_tile[step]
    down = down_tile[step]
    upper = dot_nn(scaled[...], up)
    grad_act = dot_nt(cotangent[...], down)
    square = upper * upper
    inner = jnp.tanh(GELU_ROOT * (upper + GELU_CUBE * upper * square))
    half = 0.5 * (1.0 + inner)
    slope = half + 0.5 * upper * (1.0 - inner * inner) * (
        GELU_ROOT * (1.0 + 3.0 * GELU_CUBE * square)
    )
    active = (upper * half).astype(BF16)
    grad_upper = (grad_act * slope).astype(BF16)
    reduced_here = dot_nn(active, down)
    grads_here = dot_nt(grad_upper, up)

    @pl.when(step == 0)
    def _():
        reduced[...] = reduced_here
        grads[...] = grads_here

    @pl.when(step > 0)
    def _():
        reduced[...] += reduced_here
        grads[...] += grads_here

    down_term = dot_tn(active, cotangent[...]).astype(BF16)
    up_term = use["up_term"]
    up_term[...] = dot_tn(scaled[...], grad_upper)
    for n in range(steps):

        @pl.when(step == n)
        def _():
            chunk, pair = owners(n)
            messages = messages_of(chunk)
            for h, s in enumerate(pair):
                out, at = message_of(messages, s)
                for g in range(groups):
                    column = slice(g * TILE, (g + 1) * TILE)
                    part_here = down_term[h * TILE : (h + 1) * TILE, column]
                    if chunk == 1:
                        out[0, at, column, :] = part_here
                    else:
                        out[at, column, :] = part_here
            for s in range(pieces):
                out, at = message_of(messages, s)
                begin = pl.multiple_of((spot ^ s) * height, height)
                for h, t in enumerate(pair):
                    part_here = up_term[
                        pl.ds(begin, height), h * TILE : (h + 1) * TILE
                    ].astype(BF16)
                    row = pl.multiple_of((spot ^ t) * height, height)
                    if chunk == 1:
                        out[1, at, pl.ds(row, height), :] = part_here
                    else:
                        out[at, pl.ds(width + row, height), :] = part_here

    if last:

        @pl.when(step == steps - 1)
        def _():
            sums, grad_mixed, term = use["sums"], use["grad_mixed"], use["term"]
            for one in beside("in", late):
                one.wait()
            sums[...] = jnp.zeros_like(sums)
            place_rows(spot, [use[f"mixing{r}"] for r in range(pieces)], use["mixing_all"])

            def end(here):
                values = hidden[here, :]
                total = use["reduced_in"][here, :] + reduced[here, :]
                use["layer_out"][here, :] = (values + total).astype(BF16)
                normed, inverse = normalize(values)
                grad = use["grads_in"][here, :] + grads[here, :]
                sums[...] += jnp.sum((grad * normed).reshape(STEP // 8, 8, width), axis=0)
                grad_hidden = cotangent[here, :].astype(F32) + norm_back(
                    grad * use["gain"][...], normed, inverse
                )
                use["grad_hidden"][here, :] = grad_hidden
                rounded = grad_hidden.astype(BF16)
                grad_mixed[here, :] = rounded
                use["grad_attended"][here, :] = dot_nt(rounded, use["mixing_all"][...]).astype(
                    BF16
                )

            over_rows(rows, end)
            term[...] = dot_tn(use["attended"][...], grad_mixed[...])
            tall = 2 * width
            messages = messages_of(part[-1])
            split_out(spot, pieces, term, messages, tall)
            put_vector(
                pieces,
                jnp.sum(sums[...], axis=0, keepdims=True),
                messages,
                tall + height * groups,
                0,
            )


def feed_stage(spot, arrays, gathered, mixing_pieces, part, chunks, ctx_size):
    first, last = part[0] == 0, part[-1] == chunks - 1
    rows, width = arrays["cotangent"].shape
    pieces = len(gathered[part[0]])
    wide = jax.ShapeDtypeStruct((rows, width), F32)
    narrow = jax.ShapeDtypeStruct((rows, width), BF16)
    inputs, outputs, scratch = {}, {}, {}
    for chunk in part:
        more = mixing_rows(width, pieces, ctx_size) if chunk == chunks - 1 else 0
        message = jax.ShapeDtypeStruct((pieces // 2, 2 * width + more, TILE), BF16)
        if chunk == 1:
            message = jax.ShapeDtypeStruct((2, pieces // 2, width, TILE), BF16)
        outputs[f"keep{chunk}"] = outputs[f"send{chunk}"] = message
    inputs["cotangent"] = arrays["cotangent"]
    for chunk in part:
        for r in range(pieces):
            inputs[f"message{chunk}_{r}"] = gathered[chunk][r]
    for r in range(pieces):
        inputs[f"mixing{r}"] = mixing_pieces[r]
    scratch["mixing_all"] = pltpu.VMEM((width, width), BF16)
    early, late = (), ()
    if first:
        for name in ("attended", "tokens", "gain"):
            inputs[name] = arrays[name]
        outputs.update(hidden=wide, scaled=narrow, reduced=wide, grads=wide)
        early = ("hidden", "scaled", "keep0", "send0")
    if last:
        for name in ("gain", "scaled"):
            inputs[name] = arrays[name]
        late = ("attended", "hidden", "reduced_in", "grads_in")
        for name in late:
            inputs[f"{name}_far"] = arrays[name.removesuffix("_in")]
        outputs.update(layer_out=narrow, grad_hidden=wide, grad_attended=narrow)
        scratch.update(
            reduced=pltpu.VMEM((rows, width), F32),
            grads=pltpu.VMEM((rows, width), F32),
            sums=pltpu.VMEM((8, width), F32),
            grad_mixed=pltpu.VMEM((rows, width), BF16),
            term=pltpu.VMEM((width, width), F32),
        )
    for name in early:
        scratch[name] = pltpu.VMEM(outputs[name].shape, outputs[name].dtype)
    for name in late:
        scratch[name] = pltpu.VMEM(inputs[f"{name}_far"].shape, inputs[f"{name}_far"].dtype)
    for name in early + late:
        scratch[f"{name}_sem"] = pltpu.SemaphoreType.DMA
    outputs = {f"{name}_far" if name in early else name: one for name, one in outputs.items()}
    steps = len(part) * (pieces // 2)
    scratch.update(
        up_tile=pltpu.VMEM((steps, width, 2 * TILE), BF16),
        down_tile=pltpu.VMEM((steps, 2 * TILE, width), BF16),
        up_sems=pltpu.SemaphoreType.DMA((steps, 2, pieces)),
        down_sems=pltpu.SemaphoreType.DMA((steps, 2, width // TILE)),
        up_term=pltpu.VMEM((width, 2 * TILE), F32),
    )

    def spec(name, array):
        if name[:7] == "message" or name[-4:] == "_far":
            return pl.BlockSpec(memory_space=pl.ANY)
        once = pl.Buffered(1)
        rank = len(array.shape)
        return pl.BlockSpec(array.shape, lambda i, *_: (0,) * rank, pipeline_mode=once)

    results = pl.pallas_call(
        functools.partial(
            feed_kernel,
            pieces=pieces,
            part=part,
            first=first,
            last=last,
            names=(*inputs, *outputs, *scratch),
            early=early,
            late=late,
        ),
        grid_spec=pltpu.PrefetchScalarGridSpec(
            num_scalar_prefetch=1,
            grid=(steps,),
            in_specs=[spec(*one) for one in inputs.items()],
            out_specs=[spec(*one) for one in outputs.items()],
            scratch_shapes=list(scratch.values()),
        ),
        out_shape=list(outputs.values()),
        compiler_params=params("arbitrary"),
        cost_estimate=weight(),
        name=f"feed{part[0]}",
    )(spot, *inputs.values())
    return {**arrays, **dict(zip((name.removesuffix("_far") for name in outputs), results))}


def query_kernel(spot_ref, scaled, *rest, pieces, seqs):
    grad_queries, weights = rest[:seqs], rest[seqs : seqs + pieces]
    grad_out, keep_out, send_out, weight, term = rest[seqs + pieces :]
    spot = spot_ref[0]
    rows = scaled.shape[0] // seqs
    place_rows(spot, weights, weight)
    for i, one in enumerate(grad_queries):
        here = slice(i * rows, (i + 1) * rows)
        part = dot_tn(scaled[here, :], one[...])
        term[...] = part if i == 0 else term[...] + part
        grad_out[here, :] = dot_nt(one[...], weight[...])
    split_out(spot, pieces, term, (keep_out, send_out))


def query_stage(spot, scaled, grad_queries, weights, ctx_size):
    rows, width = scaled.shape
    pieces = len(weights)
    tall = round_up(width // pieces * (width // TILE), 8 * ctx_size)
    message = jax.ShapeDtypeStruct((pieces // 2, tall, TILE), BF16)
    outs = [jax.ShapeDtypeStruct((rows, width), F32), message, message]
    whole = lambda one: pl.BlockSpec(one.shape, lambda i, *_: (0,) * len(one.shape))
    return pl.pallas_call(
        functools.partial(query_kernel, pieces=pieces, seqs=len(grad_queries)),
        grid_spec=pltpu.PrefetchScalarGridSpec(
            num_scalar_prefetch=1,
            grid=(1,),
            in_specs=[whole(scaled)]
            + [whole(one) for one in grad_queries]
            + [pl.BlockSpec((width // pieces, width), lambda i, *_: (0, 0))] * pieces,
            out_specs=[whole(one) for one in outs],
            scratch_shapes=[
                pltpu.VMEM((width, width), BF16),
                pltpu.VMEM((width, width), F32),
            ],
        ),
        out_shape=outs,
        compiler_params=params(),
        cost_estimate=weight(),
        name="query_grad",
    )(spot, scaled, *grad_queries, *weights)


def last_kernel(spot_ref, tokens, gain, scaled, arrived, grad_scaled, grad_hidden, *rest, pieces):
    weights = rest[:pieces]
    input_grad, keep_out, send_out, weight, sums, term, grad_shared = rest[pieces:]
    spot = spot_ref[0]
    width = tokens.shape[1]
    place_rows(spot, weights, weight)
    sums[...] = jnp.zeros_like(sums)
    places, seqs, here, unused = arrived.shape
    for i in range(seqs):
        total = arrived[0, i].astype(F32)
        for j in range(1, places):
            total = total + arrived[j, i].astype(F32)
        grad_shared[i * here : (i + 1) * here, :] = total.astype(BF16)
    term[...] = dot_tn(scaled[...], grad_shared[...])
    split_out(spot, pieces, term, (keep_out, send_out))

    def run(rows):
        normed, inverse = normalize(tokens[rows, :].astype(F32))
        grad = grad_scaled[rows, :] + dot_nt(grad_shared[rows, :], weight[...])
        sums[...] += jnp.sum((grad * normed).reshape(STEP // 8, 8, width), axis=0)
        input_grad[rows, :] = grad_hidden[rows, :] + norm_back(
            grad * gain[...], normed, inverse
        )

    over_rows(tokens.shape[0], run)
    put_vector(
        pieces, jnp.sum(sums[...], axis=0, keepdims=True), (keep_out, send_out), 0, LANES
    )


def last_stage(spot, tokens, gain, scaled, arrived, grad_scaled, grad_hidden, weights, places):
    rows, width = tokens.shape
    pieces = len(weights)
    message = jax.ShapeDtypeStruct(
        (pieces // 2, round_up(width // pieces, 8 * places), 2 * LANES), BF16
    )
    return pl.pallas_call(
        functools.partial(last_kernel, pieces=pieces),
        grid_spec=pltpu.PrefetchScalarGridSpec(
            num_scalar_prefetch=1,
            grid=(),
            in_specs=[pl.BlockSpec(memory_space=pltpu.VMEM)] * (6 + pieces),
            out_specs=[pl.BlockSpec(memory_space=pltpu.VMEM)] * 3,
            scratch_shapes=[
                pltpu.VMEM((width, LANES), BF16),
                pltpu.VMEM((8, width), F32),
                pltpu.VMEM((width, LANES), F32),
                pltpu.VMEM((rows, LANES), BF16),
            ],
        ),
        out_shape=[jax.ShapeDtypeStruct((rows, width), F32), message, message],
        compiler_params=params(),
        cost_estimate=weight(),
        name="last",
    )(spot, tokens, gain, scaled, arrived, grad_scaled, grad_hidden, *weights)


def final_kernel(
    place_ref, early_own, early_other, last_own, last_other, late,
    down_out, up_out, mixing_out, query_out, shared_out, gains_out, whole,
    *, chunks, pieces, width, query_rows,
):
    height = width // pieces
    groups = width // TILE
    places, deep = late.shape[0], last_own.shape[0]
    low, high = place_ref[0] & 1, place_ref[0] >> 1

    def columns(out, first_row, rows, out_row, across):
        for g in range(across):
            row = first_row + g * rows
            out[out_row : out_row + rows, g * TILE : (g + 1) * TILE] = whole[row : row + rows, :]

    def put_chunk(chunk):
        columns(down_out, 0, TILE, chunk * TILE, groups)
        for j in range(pieces):
            row = width + j * height
            column = (j * chunks + chunk) * TILE
            up_out[:, column : column + TILE] = whole[row : row + height, :]

    def load(source, begin, rows):
        for c in range(places):
            whole[c * rows : (c + 1) * rows, :] = source[c, begin : begin + rows, :].astype(F32)

    def load_halves(own, other, at):
        rows = own.shape[2]
        for half, x in ((own, low), (other, 1 - low)):
            for k in range(deep):
                begin = pl.multiple_of((x * deep + (high ^ k)) * rows, 8)
                whole[pl.ds(begin, rows), :] = half[k, at].astype(F32)

    for chunk in range(chunks - 1):
        load_halves(early_own, early_other, chunk)
        put_chunk(chunk)
    load_halves(last_own, last_other, 0)
    put_chunk(chunks - 1)
    columns(mixing_out, 2 * width, height, 0, groups)
    row = 2 * width + groups * height
    for i in range(width // LANES):
        gains_out[1:2, i * LANES : (i + 1) * LANES] = whole[row + i : row + i + 1, 0:LANES]
    load(late, 0, query_rows)
    columns(query_out, 0, height, 0, groups)
    load(late, query_rows, late.shape[1] - query_rows)
    shared_out[...] = whole[0:height, 0:LANES]
    for i in range(width // LANES):
        gains_out[0:1, i * LANES : (i + 1) * LANES] = whole[i : i + 1, LANES:]


def final_stage(place, halves, late, query_rows, chunks, pieces, width):
    height = width // pieces
    shape = lambda *dims: jax.ShapeDtypeStruct(dims, F32)
    tallest = max(2 * one.shape[0] * one.shape[2] for one in halves)
    tallest = max(tallest, late.shape[0] * late.shape[1])
    return pl.pallas_call(
        functools.partial(
            final_kernel, chunks=chunks, pieces=pieces, width=width, query_rows=query_rows
        ),
        grid_spec=pltpu.PrefetchScalarGridSpec(
            num_scalar_prefetch=1,
            grid=(),
            in_specs=[pl.BlockSpec(memory_space=pltpu.VMEM)] * 5,
            out_specs=[pl.BlockSpec(memory_space=pltpu.VMEM)] * 6,
            scratch_shapes=[pltpu.VMEM((tallest, TILE), F32)],
        ),
        out_shape=[
            shape(chunks * TILE, width),
            shape(height, pieces * chunks * TILE),
            shape(height, width),
            shape(height, width),
            shape(height, LANES),
            shape(2, width),
        ],
        compiler_params=params(),
        cost_estimate=weight(),
        name="final",
    )(place, *halves, late)


def swap(values, axis, size, mask):
    return lax.ppermute(values, axis, [(i, i ^ mask) for i in range(size)])


class Gather:
    def __init__(self, piece, size):
        self.size, self.own = size, piece
        self.far = swap(piece, "wt", size, 2)
        self.near = swap(piece, "wt", size, 1)

    def finish(self):
        return [self.own, self.near, self.far, swap(self.far, "wt", self.size, 1)]


def own_order(values, spot, size):
    mask = 1
    while mask < size:
        split = values.reshape((size // (2 * mask), 2, mask) + values.shape[1:])
        split = jnp.where((spot & mask) != 0, split[:, ::-1], split)
        values = split.reshape(values.shape)
        mask *= 2
    return values


class Transfer:
    def __init__(self, held, sent, routes):
        self.held, self.sent, self.routes, self.coming = held, sent, routes, []

    def launch(self):
        if self.sent:
            self.coming = [swap(one, *route) for one, route in zip(self.sent, self.routes)]
            self.sent = []

    def add(self, pick):
        return pick(self.held).astype(F32) + pick(self.coming[0]).astype(F32)


class Reduction(Transfer):
    def __init__(self, keep, send, place, sizes):
        self.wt_size, self.ctx_size = sizes
        self.groups = self.ctx_size // 2
        self.low, self.high = place & 1, place >> 1
        *outer, rows, self.lanes = keep.shape
        self.rows = rows if len(outer) == 1 else 2 * rows
        inner = (self.groups, self.rows // self.ctx_size, self.lanes)
        split = (*outer, *inner) if len(outer) == 2 else (*outer, 2, *inner)
        super().__init__(
            keep.reshape(split), [send.reshape(split)], [("wt", self.wt_size, 1)]
        )

    def y(self, cuts=()):
        edges = (0, *cuts, self.rows // self.ctx_size)
        self.later = [
            self.add(lambda v: v[1][..., begin:end, :]).astype(BF16)
            for begin, end in zip(edges, edges[1:])
        ]
        self.held = self.add(lambda v: v[0])
        self.sent = [self.later.pop(0)]
        self.routes = [("wt", self.wt_size, 2)]

    def y_more(self):
        self.before, self.sent = self.coming, [self.later.pop(0)]

    def y_joined(self):
        self.coming = [jnp.concatenate(self.before + self.coming, axis=-2)]

    def x(self):
        half = lambda x: self.add(lambda v: lax.dynamic_index_in_dim(v, x, 0, False))
        self.held, self.sent = half(self.low), [half(1 - self.low).astype(BF16)]
        self.routes = [("ctx", self.ctx_size, 1)]

    def far(self):
        return [("ctx", self.ctx_size, 2 * k) for k in range(1, self.groups)]

    def z(self, *others):
        def part(k):
            pick = lambda v: lax.dynamic_index_in_dim(v, self.high ^ k, 0, False)
            return jnp.stack([one.add(pick) for one in (self, *others)])

        self.sent = [part(k).astype(BF16) for k in range(1, self.groups)]
        self.held = part(0)
        self.routes = self.far()

    def total(self):
        parts = [self.held.astype(F32)] + [one.astype(F32) for one in self.coming]
        while len(parts) > 1:
            parts = [parts[i] + parts[i + 1] for i in range(0, len(parts), 2)]
        return parts[0].astype(BF16)

    def z_back(self):
        self.held = self.total()
        self.sent = [self.held] * (self.groups - 1)

    def x_back(self):
        self.held = jnp.stack([self.held] + self.coming)
        self.sent = [self.held]
        self.routes = [("ctx", self.ctx_size, 1)]

    def everywhere(self):
        return self.add(lambda v: v).astype(BF16).reshape(
            self.ctx_size, self.rows // self.ctx_size, self.lanes
        )


def tie(main, *reductions, came=()):
    state = [(one.held, one.sent) for one in reductions]
    main, state, coming = lax.optimization_barrier((main, state, [one.coming for one in came]))
    for one, (held, sent) in zip(reductions, state):
        one.held, one.sent = held, sent
    for one, values in zip(came, coming):
        one.coming = values
    for one in reductions:
        one.launch()
    return main


def body(
    tokens,
    documents,
    first_gain,
    query_weight,
    shared_weight,
    mixing_weight,
    second_gain,
    up_weight,
    down_weight,
    cotangent,
    *,
    wt_size,
    ctx_size,
):
    sizes = (wt_size, ctx_size)
    seqs, rows, width = tokens.shape
    count = seqs * rows
    spot_index = lax.axis_index("wt")
    place = lax.axis_index("ctx")
    spot = spot_index.astype(jnp.int32).reshape(1)
    length = ctx_size * rows
    doc_most = length * 5 // 8
    before = min(ctx_size - 1, -(-(doc_most - 1) // rows))
    blocks = before + 1
    height = width // wt_size
    chunks = up_weight.shape[1] // wt_size // TILE

    gain_rows = -(-height // LANES)
    pad = lambda gain: jnp.pad(gain, (0, gain_rows * LANES - height)).reshape(gain_rows, LANES)
    small = jnp.concatenate([shared_weight, pad(first_gain), pad(second_gain)], axis=0)
    small = jnp.pad(small, ((0, -small.shape[0] % 16), (0, 0)))
    small_pieces = Gather(small, wt_size).finish()
    query_gather = Gather(query_weight, wt_size)

    gains = jnp.stack([one[height : height + 2 * gain_rows] for one in small_pieces])
    gains = gains.reshape(wt_size, 2, gain_rows * LANES)[:, :, :height].astype(F32)
    gains = own_order(gains, spot_index, wt_size)
    gain_one = gains[:, 0].reshape(1, width)
    gain_two = gains[:, 1].reshape(1, width)

    inputs = tokens.reshape(count, width)
    doc_lines = documents.astype(BF16).reshape(seqs, rows // LANES, LANES)
    scaled_one, shared = first_stage(spot, inputs, gain_one, doc_lines, small_pieces, ctx_size)
    shared, query_gather.far, mixing_weight, *packed = lax.optimization_barrier(
        (shared, query_gather.far, mixing_weight, up_weight, down_weight)
    )
    keyvals = lax.all_to_all(shared, "ctx", 0, 0).reshape(ctx_size, seqs, rows + DOC_ROWS, LANES)
    packed = list(pack_stage(*packed, chunks, wt_size))
    gathers = [Gather(packed[0], wt_size)]
    mixing_gather = Gather(mixing_weight, wt_size)
    query_pieces = query_gather.finish()
    place_one = place.astype(jnp.int32).reshape(1)

    queries = project(spot, scaled_one, query_pieces).reshape(seqs, rows, width)
    keyvals, gathers[0].far, mixing_gather.far, queries, packed[1:] = lax.optimization_barrier(
        (keyvals, gathers[0].far, mixing_gather.far, queries, packed[1:])
    )
    gathered = [gathers[0].finish()]
    mixing_pieces = mixing_gather.finish()
    gathers.append(Gather(packed[1], wt_size))
    starts, exact, attended, logs = attend(place_one, queries, keyvals, blocks)
    attended, gathers[1].far, packed[2:] = lax.optimization_barrier(
        (attended, gathers[1].far, packed[2:])
    )
    gathered.append(gathers[1].finish())
    gathers += [Gather(one, wt_size) for one in packed[2:]]

    arrays = {
        "attended": attended.reshape(count, width),
        "tokens": inputs,
        "gain": gain_two,
        "cotangent": cotangent.reshape(count, width),
    }
    feed = lambda arrays, part: feed_stage(
        spot, arrays, gathered, mixing_pieces, part, chunks, ctx_size
    )
    arrays = feed(arrays, (0, 1))
    zero, one = (
        Reduction(arrays[f"keep{chunk}"], arrays[f"send{chunk}"], place, sizes) for chunk in (0, 1)
    )
    arrays, gathers[-1].far = tie((arrays, gathers[-1].far), zero, one)
    gathered.append(gathers[-1].finish())
    arrays = tie(arrays, zero, one, came=[zero])
    zero.y()
    arrays = tie(arrays, zero, one, came=[one])
    one.x()
    arrays = tie(arrays, zero, one)
    arrays = feed(arrays, (2,))
    two = Reduction(arrays["keep2"], arrays["send2"], place, sizes)
    grad_attended = tie(arrays["grad_attended"], zero, one, two, came=[zero, one])
    zero.x()
    one.y()
    grad_attended = tie(grad_attended, zero, one, two, came=[two])
    two.y([round_up(two.rows // ctx_size * 2 // 5, 8)])
    grad_attended = tie(grad_attended, zero, one, two).reshape(seqs, rows, width)
    grad_queries, terms = [], []
    for seq in range(seqs):
        part, keep, send = attend_back(
            seq, place_one, queries, starts, exact, logs, grad_attended, keyvals, blocks
        )
        came = [zero, one, two] if seq == 0 else [zero, two]
        term = Transfer(keep, [send], [("ctx", ctx_size, 1)])
        part, grad_attended = tie((part, grad_attended), *came, term, *terms, came=came + terms)
        grad_queries.append(part[0])
        terms.append(term)
        if seq == 0:
            zero.z(one)
            two.y_more()
            grad_attended = tie(grad_attended, zero, two)
    two.y_joined()
    two.x()
    zero.z_back()
    grad_queries = tie(grad_queries, zero, two)
    grad_scaled, keep, send = query_stage(spot, scaled_one, grad_queries, query_pieces, ctx_size)
    query = Reduction(keep, send, place, sizes)
    grad_scaled = tie(grad_scaled, zero, query, *terms, came=terms[1:])
    arriving = jnp.stack([one.add(lambda v: v).astype(BF16) for one in terms], axis=1)
    arriving, grad_scaled = tie((arriving, grad_scaled), query)
    arriving = lax.all_to_all(
        arriving,
        "ctx",
        0,
        0,
        axis_index_groups=[list(range(x, ctx_size, 2)) for x in range(2)],
    )
    query.y()
    grad_scaled = tie(grad_scaled, query)
    grad_scaled = tie(grad_scaled, two, came=[two])
    two.z()
    grad_scaled, arriving = tie((grad_scaled, arriving), two)
    input_grad, keep, send = last_stage(
        spot, inputs, gain_one, scaled_one, arriving, grad_scaled, arrays["grad_hidden"], small_pieces, ctx_size
    )
    shared = Reduction(keep, send, place, sizes)
    input_grad = tie(input_grad, zero, two, shared, query, came=[two, query])
    two.z_back()
    input_grad = tie(input_grad, two)
    zero.x_back()
    input_grad = tie(input_grad, zero)
    input_grad = tie(input_grad, shared, query, came=[shared])
    shared.y()
    input_grad = tie(input_grad, shared)
    input_grad = tie(input_grad, shared, query, came=[shared])
    late = jnp.concatenate([query.everywhere(), shared.everywhere()], axis=1)
    late = lax.all_to_all(late, "ctx", 0, 0)
    two.x_back()
    input_grad = tie(input_grad, two)
    late = jnp.sum(late.astype(F32), axis=0).astype(BF16)
    late = lax.all_to_all(jnp.broadcast_to(late, (ctx_size,) + late.shape), "ctx", 0, 0)
    down_grad, up_grad, mixing_grad, query_grad, shared_grad, gain_grads = final_stage(
        place_one,
        [zero.held, zero.coming[0], two.held, two.coming[0]],
        late,
        query.rows // ctx_size,
        chunks,
        wt_size,
        width,
    )

    gain_grads = lax.dynamic_slice_in_dim(gain_grads, spot_index * height, height, 1)
    return (
        arrays["layer_out"].reshape(seqs, rows, width),
        input_grad.reshape(seqs, rows, width),
        gain_grads[0],
        query_grad,
        shared_grad,
        mixing_grad,
        gain_grads[1],
        up_grad,
        down_grad,
    )


def solution(mesh):
    in_specs = (
        P("wt", "ctx", None),
        P("wt", "ctx"),
        P("wt"),
        P("wt", None),
        P("wt", None),
        P("wt", None),
        P("wt"),
        P("wt", None),
        P("wt", None),
        P("wt", "ctx", None),
    )
    out_specs = (
        P("wt", "ctx", None),
        P("wt", "ctx", None),
        P("wt"),
        P("wt", None),
        P("wt", None),
        P("wt", None),
        P("wt"),
        P("wt", None),
        P("wt", None),
    )
    run = functools.partial(body, wt_size=mesh.shape["wt"], ctx_size=mesh.shape["ctx"])
    return jax.shard_map(run, mesh=mesh, in_specs=in_specs, out_specs=out_specs, check_vma=False)
```

```python
import functools
import math

import jax
import jax.numpy as jnp
from jax import lax
from jax.experimental import pallas as pl
from jax.experimental.pallas import tpu as pltpu
from jax.sharding import PartitionSpec as P

HEADS = 12
HEAD_DIM = 64
PAIRS = HEADS // 2
LANES = 128
EPSILON = 1e-05
BIAS = -1e30
SCALE = math.log2(math.e) / HEAD_DIM**0.5
F32 = jnp.float32
BF16 = jnp.bfloat16
GELU_ROOT = math.sqrt(2.0 / math.pi)
GELU_CUBE = 0.044715


def params(*semantics):
    return pltpu.CompilerParams(
        dimension_semantics=semantics or None, vmem_limit_bytes=56 * 1024 * 1024
    )


def weight():
    return pl.CostEstimate(flops=1, bytes_accessed=1, transcendentals=0)


def dot_nn(a, b):
    return lax.dot_general(a, b, (((1,), (0,)), ((), ())), preferred_element_type=F32)


def dot_nt(a, b):
    return lax.dot_general(a, b, (((1,), (1,)), ((), ())), preferred_element_type=F32)


def dot_tn(a, b):
    return lax.dot_general(a, b, (((0,), (0,)), ((), ())), preferred_element_type=F32)


def normalize(values):
    center = values - jnp.mean(values, axis=-1, keepdims=True)
    spread = jnp.mean(center * center, axis=-1, keepdims=True)
    inverse = lax.rsqrt(spread + EPSILON)
    return center * inverse, inverse


def norm_back(grad, normed, inverse):
    mean_grad = jnp.mean(grad, axis=-1, keepdims=True)
    mean_both = jnp.mean(grad * normed, axis=-1, keepdims=True)
    return (grad - mean_grad - normed * mean_both) * inverse


def place_rows(spot, pieces, scratch):
    height = scratch.shape[0] // len(pieces)
    for r, piece in enumerate(pieces):
        begin = pl.multiple_of((spot ^ r) * height, height)
        scratch[pl.ds(begin, height), :] = piece[0:height, :]


STEP = 128


def over_rows(rows, run):
    def one(index, carried):
        run(pl.ds(pl.multiple_of(index * STEP, STEP), STEP))
        return carried

    lax.fori_loop(0, rows // STEP, one, 0)


TILE = 256


def pack_kernel(up, down, *outs, chunks, pieces):
    width = down.shape[1]
    height = up.shape[0]
    for chunk, out in enumerate(outs):
        for g in range(width // TILE):
            out[g * TILE : (g + 1) * TILE, :] = down[
                chunk * TILE : (chunk + 1) * TILE, g * TILE : (g + 1) * TILE
            ]
        for j in range(pieces):
            row, column = width + j * height, (j * chunks + chunk) * TILE
            out[row : row + height, :] = up[:, column : column + TILE]


def pack_stage(up, down, chunks, pieces):
    width = down.shape[1]
    return pl.pallas_call(
        functools.partial(pack_kernel, chunks=chunks, pieces=pieces),
        in_specs=[pl.BlockSpec(memory_space=pltpu.VMEM)] * 2,
        out_specs=[pl.BlockSpec(memory_space=pltpu.VMEM)] * chunks,
        out_shape=[jax.ShapeDtypeStruct((2 * width, TILE), BF16)] * chunks,
        compiler_params=params(),
        cost_estimate=weight(),
        name="pack",
    )(up, down)


DOC_ROWS = 16


def first_kernel(spot_ref, tokens, gain, documents, *rest, pieces):
    weights = rest[:pieces]
    scaled_out, shared_out, weight = rest[pieces:]
    place_rows(spot_ref[0], weights, weight)
    seqs, doc_lines, unused = documents.shape
    places, tall, unused = shared_out.shape
    tall = tall // seqs
    rows = tall - DOC_ROWS
    per_seq = rows // STEP

    def run(index, carried):
        here = pl.ds(pl.multiple_of(index * STEP, STEP), STEP)
        normed, unused = normalize(tokens[here, :].astype(F32))
        scaled_out[here, :] = (normed * gain[...]).astype(BF16)
        return carried

    lax.fori_loop(0, seqs * per_seq, run, 0)
    shared = dot_nn(scaled_out[...], weight[...]).astype(BF16)

    def put(c, carried):
        for seq in range(seqs):
            begin = seq * tall
            shared_out[c, begin : begin + rows, :] = shared[seq * rows : (seq + 1) * rows, :]
            begin = begin + rows
            shared_out[c, begin : begin + DOC_ROWS, :] = jnp.zeros((DOC_ROWS, LANES), BF16)
            shared_out[c, begin : begin + doc_lines, :] = documents[seq]
        return carried

    lax.fori_loop(0, places, put, 0)


def first_stage(spot, tokens, gain, documents, weights, places):
    count, width = tokens.shape
    columns = weights[0].shape[1]
    seqs, doc_lines, unused = documents.shape
    return pl.pallas_call(
        functools.partial(first_kernel, pieces=len(weights)),
        grid_spec=pltpu.PrefetchScalarGridSpec(
            num_scalar_prefetch=1,
            grid=(),
            in_specs=[pl.BlockSpec(memory_space=pltpu.VMEM)] * (3 + len(weights)),
            out_specs=[pl.BlockSpec(memory_space=pltpu.VMEM)] * 2,
            scratch_shapes=[pltpu.VMEM((width, columns), BF16)],
        ),
        out_shape=[
            jax.ShapeDtypeStruct((count, width), BF16),
            jax.ShapeDtypeStruct((places, count + seqs * DOC_ROWS, columns), BF16),
        ],
        compiler_params=params(),
        cost_estimate=weight(),
        name="first_norm",
    )(spot, tokens, gain, documents, *weights)


def project_kernel(spot_ref, operand, *rest, pieces):
    weights = rest[:pieces]
    out, weight_all = rest[pieces:]
    place_rows(spot_ref[0], weights, weight_all)
    out[...] = dot_nn(operand[...], weight_all[...]).astype(out.dtype)


def project(spot, operand, weights):
    rows, width = operand.shape
    columns = weights[0].shape[1]
    return pl.pallas_call(
        functools.partial(project_kernel, pieces=len(weights)),
        grid_spec=pltpu.PrefetchScalarGridSpec(
            num_scalar_prefetch=1,
            grid=(),
            in_specs=[pl.BlockSpec(memory_space=pltpu.VMEM)] * (1 + len(weights)),
            out_specs=pl.BlockSpec(memory_space=pltpu.VMEM),
            scratch_shapes=[pltpu.VMEM((width, columns), BF16)],
        ),
        out_shape=jax.ShapeDtypeStruct((rows, columns), BF16),
        compiler_params=params(),
        cost_estimate=weight(),
        name="project",
    )(spot, operand, *weights)


def low_lanes(shape):
    return lax.broadcasted_iota(jnp.int32, shape, len(shape) - 1) < HEAD_DIM


def swap_halves(values):
    return pltpu.roll(values, HEAD_DIM, 1)


def stacked_pairs(ref):
    return jnp.concatenate(
        [ref[0, :, p * LANES : (p + 1) * LANES] for p in range(PAIRS)], axis=0
    )


def tile_bias(starts, key_begin, row_begin, tile_rows, tile_keys):
    key_place = key_begin + lax.broadcasted_iota(jnp.int32, (tile_rows, tile_keys), 1)
    row_place = row_begin + lax.broadcasted_iota(jnp.int32, (tile_rows, tile_keys), 0)
    first = jnp.concatenate([starts] * (tile_keys // LANES), axis=1)
    allowed = (key_place >= first) & (key_place <= row_place)
    bias = jnp.where(allowed, 0.0, BIAS)
    bias = jnp.concatenate([bias, bias], axis=1)
    return jnp.concatenate([bias] * PAIRS, axis=0)


def block_at(place_ref, j, blocks):
    return jnp.maximum(place_ref[0] - (blocks - 1) + j, 0)


def attend_kernel(
    place_ref, queries, keyvals, starts_out, exact_out, rounded_out, logs_out, *rest,
    blocks, tile_rows, tile_keys
):
    key_even, key_odd, value_even, value_odd, score_scratch, most, total = rest
    rows = keyvals.shape[2] - DOC_ROWS
    tile = pl.program_id(1)

    @pl.when(tile == 0)
    def _():
        low = low_lanes((rows, LANES))
        for j in range(blocks):
            whole = keyvals[block_at(place_ref, j, blocks), 0, 0:rows, :].astype(F32)
            turned = swap_halves(whole)
            place = pl.ds(j * rows, rows)
            key_even[place, :] = jnp.where(low, whole, 0.0).astype(BF16)
            key_odd[place, :] = jnp.where(low, 0.0, turned).astype(BF16)
            value_even[place, 0:LANES] = jnp.where(low, turned, 0.0).astype(BF16)
            value_even[place, LANES:] = jnp.where(low, 1.0, 0.0).astype(BF16)
            value_odd[place, 0:LANES] = jnp.where(low, 0.0, whole).astype(BF16)
            value_odd[place, LANES:] = jnp.where(low, 0.0, 1.0).astype(BF16)

    own = keyvals[place_ref[0], 0, rows:, :].astype(F32)
    lines = rows // LANES
    marks = [jnp.broadcast_to(own[h : h + 1, :], (LANES, LANES)).T for h in range(lines)]
    marks = jnp.concatenate(marks, axis=0)
    if tile_rows != rows:
        marks = sum(
            jnp.where(tile == t, marks[t * tile_rows : (t + 1) * tile_rows, :], 0.0)
            for t in range(rows // tile_rows)
        )

    def smaller(j, count):
        lines = keyvals[block_at(place_ref, j, blocks), 0, rows:, :].astype(F32)
        missing = place_ref[0] - (blocks - 1) + j < 0
        for h in range(rows // LANES):
            line = jnp.where(missing, -1.0, lines[h : h + 1, :])
            count = count + jnp.where(line < marks, 1.0, 0.0)
        return count

    count = lax.fori_loop(0, blocks, smaller, jnp.zeros((tile_rows, LANES), F32))
    count = jnp.sum(count, axis=1, keepdims=True).astype(jnp.int32)
    starts = starts_out
    starts[0] = jnp.broadcast_to(count, (tile_rows, LANES))
    row_begin = (blocks - 1) * rows + tile * tile_rows
    begin = jnp.min(starts[0]) // tile_keys
    end = (row_begin + tile_rows - 1) // tile_keys + 1
    stacked = stacked_pairs(queries)
    most[...] = jnp.full_like(most, -3e38)
    copies = tile_keys // LANES

    def score(index):
        key_begin = pl.multiple_of(index * tile_keys, tile_keys)
        place = pl.ds(key_begin, tile_keys)
        both = jnp.concatenate([key_even[place, :], key_odd[place, :]], axis=0)
        values = dot_nt(stacked, both) + tile_bias(
            starts[0], key_begin, row_begin, tile_rows, tile_keys
        )
        score_scratch[index - begin] = values
        half = []
        for h in range(2):
            part = values[:, h * tile_keys : h * tile_keys + LANES]
            for q in range(1, copies):
                at = h * tile_keys + q * LANES
                part = jnp.maximum(part, values[:, at : at + LANES])
            half.append(part)
        return jnp.concatenate(half, axis=1)

    def output(index):
        place = pl.ds(pl.multiple_of(index * tile_keys, tile_keys), tile_keys)
        both = jnp.concatenate([value_even[place, :], value_odd[place, :]], axis=0)
        shift = jnp.concatenate([most[:, 0:LANES]] * copies + [most[:, LANES:]] * copies, axis=1)
        powers = jnp.exp2((score_scratch[index - begin] - shift) * SCALE).astype(BF16)
        return dot_nn(powers, both)

    def in_pairs(one, join, total):
        def two(index, carried):
            at = begin + 2 * index
            total[...] = join(total[...], join(one(at), one(at + 1)))
            return carried

        count = end - begin
        lax.fori_loop(0, count // 2, two, 0)

        @pl.when(count % 2 == 1)
        def _():
            total[...] = join(total[...], one(end - 1))

    in_pairs(score, jnp.maximum, most)
    stack = PAIRS * tile_rows
    for h in range(2):
        part = jnp.max(most[:, h * LANES : (h + 1) * LANES], axis=1, keepdims=True)
        most[:, h * LANES : (h + 1) * LANES] = jnp.broadcast_to(part, (stack, LANES))
    total[...] = jnp.zeros_like(total)
    in_pairs(output, jnp.add, total)
    low = low_lanes((tile_rows, LANES))
    for p in range(PAIRS):
        at = pl.ds(p * tile_rows, tile_rows)
        lanes = slice(p * LANES, (p + 1) * LANES)
        sums = total[at, LANES:]
        out = total[at, 0:LANES] / sums
        exact_out[0, :, lanes] = out
        rounded_out[0, :, lanes] = out.astype(BF16)
        shift = jnp.where(low, most[at, 0:LANES], most[at, LANES:])
        logs_out[0, :, lanes] = shift * SCALE + jnp.log2(sums)


def attend_back_kernel(
    place_ref, queries, starts, exact, logs, grads, keyvals, *rest,
    seq, blocks, tile_rows, tile_keys
):
    grad_queries, keep, send, *rest = rest
    (
        key_even, key_odd, value_even, value_odd,
        key_total, value_total, query_total,
        log_even, log_odd, delta_even, delta_odd,
    ) = rest
    rows = keyvals.shape[2] - DOC_ROWS
    tile = pl.program_id(0)

    @pl.when(tile == 0)
    def _():
        low = low_lanes((rows, LANES))
        for j in range(blocks):
            whole = keyvals[block_at(place_ref, j, blocks), 0, 0:rows, :].astype(F32)
            turned = swap_halves(whole)
            place = pl.ds(j * rows, rows)
            key_even[place, :] = jnp.where(low, whole, 0.0).astype(BF16)
            key_odd[place, :] = jnp.where(low, 0.0, turned).astype(BF16)
            value_even[place, :] = jnp.where(low, turned, 0.0).astype(BF16)
            value_odd[place, :] = jnp.where(low, 0.0, whole).astype(BF16)
        key_total[...] = jnp.zeros_like(key_total)
        value_total[...] = jnp.zeros_like(value_total)

    row_begin = (blocks - 1) * rows + tile * tile_rows
    begin = jnp.min(starts[0]) // tile_keys
    end = (row_begin + tile_rows - 1) // tile_keys + 1
    stacked = stacked_pairs(queries)
    grad_stacked = stacked_pairs(grads)
    stacked_turned = stacked.T
    grad_turned = grad_stacked.T
    stack = PAIRS * tile_rows
    low = low_lanes((tile_rows, LANES))
    for p in range(PAIRS):
        at = pl.ds(p * tile_rows, tile_rows)
        lanes = slice(p * LANES, (p + 1) * LANES)
        log = logs[0, :, lanes]
        log_turned = swap_halves(log)
        log_even[at, :] = jnp.where(low, log, log_turned)
        log_odd[at, :] = jnp.where(low, log_turned, log)
        terms_here = exact[0, :, lanes] * grads[0, :, lanes].astype(F32)
        even = jnp.sum(jnp.where(low, terms_here, 0.0), axis=1, keepdims=True)
        odd = jnp.sum(jnp.where(low, 0.0, terms_here), axis=1, keepdims=True)
        delta_even[at, :] = jnp.broadcast_to(even, (tile_rows, LANES))
        delta_odd[at, :] = jnp.broadcast_to(odd, (tile_rows, LANES))
    query_total[...] = jnp.zeros_like(query_total)

    def step(index, carried):
        key_begin = pl.multiple_of(index * tile_keys, tile_keys)
        place = pl.ds(key_begin, tile_keys)
        keys = jnp.concatenate([key_even[place, :], key_odd[place, :]], axis=0)
        values = jnp.concatenate([value_even[place, :], value_odd[place, :]], axis=0)
        copies = tile_keys // LANES
        log = jnp.concatenate([log_even[...]] * copies + [log_odd[...]] * copies, axis=1)
        delta = jnp.concatenate([delta_even[...]] * copies + [delta_odd[...]] * copies, axis=1)
        scores = dot_nt(stacked, keys) + tile_bias(
            starts[0], key_begin, row_begin, tile_rows, tile_keys
        )
        chances = jnp.exp2(scores * SCALE - log)
        grad_probs = dot_nt(grad_stacked, values)
        grad_scores = (chances * (grad_probs - delta)).astype(BF16)
        query_total[...] += dot_nn(grad_scores, keys)
        key_total[index] += dot_nn(stacked_turned, grad_scores)
        value_total[index] += dot_nn(grad_turned, chances.astype(BF16))
        return carried

    lax.fori_loop(begin, end, step, 0)
    root = 1.0 / HEAD_DIM**0.5
    for p in range(PAIRS):
        at = pl.ds(p * tile_rows, tile_rows)
        lanes = slice(p * LANES, (p + 1) * LANES)
        grad_queries[0, :, lanes] = (query_total[at, :] * root).astype(BF16)

    @pl.when(tile == pl.num_programs(0) - 1)
    def _():
        per_block = rows // tile_keys
        keep[...] = jnp.zeros_like(keep)
        send[...] = jnp.zeros_like(send)

        def block_terms(j, carried):
            for i in range(per_block):
                index = j * per_block + i
                key = key_total[index]
                value = value_total[index]
                key = key[0:HEAD_DIM, 0:tile_keys] + key[HEAD_DIM:, tile_keys:]
                value = value[0:HEAD_DIM, 0:tile_keys] + value[HEAD_DIM:, tile_keys:]
                both = jnp.concatenate([key * root, value], axis=0)
                both = both.T.astype(BF16)
                owner = block_at(place_ref, j, blocks)
                here = slice(i * tile_keys, (i + 1) * tile_keys)
                same = (owner & 1) == (place_ref[0] & 1)

                @pl.when(same)
                def _():
                    keep[owner >> 1, here, :] = both

                @pl.when(jnp.logical_not(same))
                def _():
                    send[owner >> 1, here, :] = both

            return carried

        missing = jnp.maximum(blocks - 1 - place_ref[0], 0)
        lax.fori_loop(missing, blocks, block_terms, 0)


def attention_sizes(rows, blocks, kept):
    tile_keys = 256 if rows % 256 == 0 else 128
    tile_rows = 128
    if kept and rows % 256 == 0 and blocks * rows * 256 * HEADS * 4 < 24 * 1024 * 1024:
        tile_rows = 256
    return tile_rows, tile_keys, blocks * rows // tile_keys


def attend(place, queries, keyvals, blocks):
    unused, seqs, tall, unused = keyvals.shape
    rows = tall - DOC_ROWS
    width = queries.shape[2]
    tile_rows, tile_keys, key_tiles = attention_sizes(rows, blocks, True)
    stack = PAIRS * tile_rows
    keys = blocks * rows
    row_spec = lambda lanes: pl.BlockSpec((1, tile_rows, lanes), lambda s, t, *_: (s, t, 0))
    wide = lambda dtype: jax.ShapeDtypeStruct((seqs, rows, width), dtype)
    return pl.pallas_call(
        functools.partial(
            attend_kernel, blocks=blocks, tile_rows=tile_rows, tile_keys=tile_keys
        ),
        grid_spec=pltpu.PrefetchScalarGridSpec(
            num_scalar_prefetch=1,
            grid=(seqs, rows // tile_rows),
            in_specs=[
                row_spec(width),
                pl.BlockSpec((keyvals.shape[0], 1, tall, LANES), lambda s, t, *_: (0, s, 0, 0)),
            ],
            out_specs=[row_spec(LANES)] + [row_spec(width)] * 3,
            scratch_shapes=[
                pltpu.VMEM((keys, LANES), BF16),
                pltpu.VMEM((keys, LANES), BF16),
                pltpu.VMEM((keys, 2 * LANES), BF16),
                pltpu.VMEM((keys, 2 * LANES), BF16),
                pltpu.VMEM((key_tiles, stack, 2 * tile_keys), F32),
                pltpu.VMEM((stack, 2 * LANES), F32),
                pltpu.VMEM((stack, 2 * LANES), F32),
            ],
        ),
        out_shape=[
            jax.ShapeDtypeStruct((seqs, rows, LANES), jnp.int32),
            wide(F32),
            wide(BF16),
            wide(F32),
        ],
        compiler_params=params("arbitrary", "arbitrary"),
        cost_estimate=weight(),
        name="attend",
    )(place, queries, keyvals)


def attend_back(
    seq, place, queries, starts, exact, logs, grads, keyvals, blocks
):
    seqs, rows, width = queries.shape
    ctx_size = keyvals.shape[0]
    tile_rows, tile_keys, key_tiles = attention_sizes(rows, blocks, False)
    stack = PAIRS * tile_rows
    keys = blocks * rows
    row_spec = lambda lanes: pl.BlockSpec((1, tile_rows, lanes), lambda t, *_: (seq, t, 0))
    return pl.pallas_call(
        functools.partial(
            attend_back_kernel, seq=seq, blocks=blocks, tile_rows=tile_rows, tile_keys=tile_keys
        ),
        grid_spec=pltpu.PrefetchScalarGridSpec(
            num_scalar_prefetch=1,
            grid=(rows // tile_rows,),
            in_specs=[row_spec(width), row_spec(LANES)]
            + [row_spec(width)] * 3
            + [pl.BlockSpec((ctx_size, 1, keyvals.shape[2], LANES), lambda t, *_: (0, seq, 0, 0))],
            out_specs=[
                pl.BlockSpec((1, tile_rows, width), lambda t, *_: (0, t, 0)),
            ]
            + [pl.BlockSpec((ctx_size // 2, rows, LANES), lambda t, *_: (0, 0, 0))] * 2,
            scratch_shapes=[pltpu.VMEM((keys, LANES), BF16)] * 4
            + [pltpu.VMEM((key_tiles, LANES, 2 * tile_keys), F32)] * 2
            + [pltpu.VMEM((stack, LANES), F32)] * 5,
        ),
        out_shape=[
            jax.ShapeDtypeStruct((1, rows, width), BF16),
        ]
        + [jax.ShapeDtypeStruct((ctx_size // 2, rows, LANES), BF16)] * 2,
        compiler_params=params("arbitrary"),
        cost_estimate=weight(),
        name="attend_back",
    )(place, queries, starts, exact, logs, grads, keyvals)


def round_up(count, unit):
    return -(-count // unit) * unit


def mixing_rows(width, pieces, ctx_size):
    unit = 8 * ctx_size
    tall = 2 * width + width // pieces * (width // TILE)
    return round_up(tall + width // LANES, unit) - 2 * width


def message_of(messages, s):
    return messages[s & 1], s >> 1


def split_out(spot, pieces, source, messages, first_row=0):
    height, lanes = source.shape[0] // pieces, messages[0].shape[2]
    across = min(lanes, source.shape[1])
    for s in range(pieces):
        out, at = message_of(messages, s)
        begin = pl.multiple_of((spot ^ s) * height, height)
        for g in range(source.shape[1] // across):
            row = first_row + g * height
            out[at, row : row + height, 0:across] = source[
                pl.ds(begin, height), g * lanes : g * lanes + across
            ].astype(BF16)


def put_vector(pieces, vector, messages, first_row, begin):
    height, lanes = messages[0].shape[1] - first_row, messages[0].shape[2]
    count = vector.shape[1] // LANES
    row = lax.broadcasted_iota(jnp.int32, (height, LANES), 0)
    block = jnp.zeros((height, LANES), F32)
    for i in range(count):
        block = jnp.where(row == i, vector[:, i * LANES : (i + 1) * LANES], block)
    for s in range(pieces):
        out, at = message_of(messages, s)
        out[at, first_row:, begin : begin + LANES] = block.astype(BF16)
        if begin == 0:
            out[at, first_row:, LANES:] = jnp.zeros((height, lanes - LANES), BF16)


def feed_kernel(spot_ref, *refs, pieces, part, first, last, names, early, late):
    use = dict(zip(names, refs))
    spot = spot_ref[0]
    step = pl.program_id(0)
    steps = len(part) * (pieces // 2)
    cotangent = use["cotangent"]
    reduced, grads, scaled, hidden = use["reduced"], use["grads"], use["scaled"], use["hidden"]
    up_tile, down_tile, up_sems, down_sems = (
        use["up_tile"], use["down_tile"], use["up_sems"], use["down_sems"]
    )
    rows, width = cotangent.shape
    height = width // pieces
    groups = width // TILE

    def messages_of(chunk):
        return use[f"keep{chunk}"], use[f"send{chunk}"]

    def owners(n):
        chunk, at = divmod(n, pieces // 2)
        return part[chunk], (2 * at, 2 * at + 1)

    def copies(n):
        chunk, pair = owners(n)
        for h, s in enumerate(pair):
            source = pl.multiple_of(width + (spot ^ s) * height, height)
            for r in range(pieces):
                row = pl.multiple_of((spot ^ r) * height, height)
                yield pltpu.make_async_copy(
                    use[f"message{chunk}_{r}"].at[pl.ds(source, height), :],
                    up_tile.at[n, pl.ds(row, height), pl.ds(h * TILE, TILE)],
                    up_sems.at[n, h, r],
                )
            for g in range(groups):
                yield pltpu.make_async_copy(
                    use[f"message{chunk}_{s}"].at[pl.ds(g * TILE, TILE), :],
                    down_tile.at[n, pl.ds(h * TILE, TILE), pl.ds(g * TILE, TILE)],
                    down_sems.at[n, h, g],
                )

    def beside(kind, names):
        for name in names:
            pair = use[f"{name}_far"], use[name]
            source, target = pair if kind == "in" else pair[::-1]
            yield pltpu.make_async_copy(source, target, use[f"{name}_sem"])

    @pl.when(step == 0)
    def _():
        for n in range(steps):
            for one in copies(n):
                one.start()
        for one in beside("in", late):
            one.start()
        if first:

            def begin(here):
                values = use["tokens"][here, :].astype(F32) + hidden[here, :]
                hidden[here, :] = values
                normed, unused = normalize(values)
                scaled[here, :] = (normed * use["gain"][...]).astype(BF16)

            place_rows(spot, [use[f"mixing{r}"] for r in range(pieces)], use["mixing_all"])
            hidden[...] = dot_nn(use["attended"][...], use["mixing_all"][...])
            over_rows(rows, begin)
            for one in beside("out", ("hidden", "scaled")):
                one.start()

    if first:

        @pl.when(step == pieces // 2)
        def _():
            for one in beside("out", ("keep0", "send0")):
                one.start()

        @pl.when(step == steps - 1)
        def _():
            for one in beside("out", early):
                one.wait()

    for n in range(steps):

        @pl.when(step == n)
        def _():
            for one in copies(n):
                one.wait()

    up = up_tile[step]
    down = down_tile[step]
    upper = dot_nn(scaled[...], up)
    grad_act = dot_nt(cotangent[...], down)
    square = upper * upper
    inner = jnp.tanh(GELU_ROOT * (upper + GELU_CUBE * upper * square))
    half = 0.5 * (1.0 + inner)
    slope = half + 0.5 * upper * (1.0 - inner * inner) * (
        GELU_ROOT * (1.0 + 3.0 * GELU_CUBE * square)
    )
    active = (upper * half).astype(BF16)
    grad_upper = (grad_act * slope).astype(BF16)
    reduced_here = dot_nn(active, down)
    grads_here = dot_nt(grad_upper, up)

    @pl.when(step == 0)
    def _():
        reduced[...] = reduced_here
        grads[...] = grads_here

    @pl.when(step > 0)
    def _():
        reduced[...] += reduced_here
        grads[...] += grads_here

    down_term = dot_tn(active, cotangent[...]).astype(BF16)
    up_term = use["up_term"]
    up_term[...] = dot_tn(scaled[...], grad_upper)
    for n in range(steps):

        @pl.when(step == n)
        def _():
            chunk, pair = owners(n)
            messages = messages_of(chunk)
            for h, s in enumerate(pair):
                out, at = message_of(messages, s)
                for g in range(groups):
                    column = slice(g * TILE, (g + 1) * TILE)
                    part_here = down_term[h * TILE : (h + 1) * TILE, column]
                    if chunk == 1:
                        out[0, at, column, :] = part_here
                    else:
                        out[at, column, :] = part_here
            for s in range(pieces):
                out, at = message_of(messages, s)
                begin = pl.multiple_of((spot ^ s) * height, height)
                for h, t in enumerate(pair):
                    part_here = up_term[
                        pl.ds(begin, height), h * TILE : (h + 1) * TILE
                    ].astype(BF16)
                    row = pl.multiple_of((spot ^ t) * height, height)
                    if chunk == 1:
                        out[1, at, pl.ds(row, height), :] = part_here
                    else:
                        out[at, pl.ds(width + row, height), :] = part_here

    if last:

        @pl.when(step == steps - 1)
        def _():
            sums, grad_mixed, term = use["sums"], use["grad_mixed"], use["term"]
            for one in beside("in", late):
                one.wait()
            sums[...] = jnp.zeros_like(sums)
            place_rows(spot, [use[f"mixing{r}"] for r in range(pieces)], use["mixing_all"])

            def end(here):
                values = hidden[here, :]
                total = use["reduced_in"][here, :] + reduced[here, :]
                use["layer_out"][here, :] = (values + total).astype(BF16)
                normed, inverse = normalize(values)
                grad = use["grads_in"][here, :] + grads[here, :]
                sums[...] += jnp.sum((grad * normed).reshape(STEP // 8, 8, width), axis=0)
                grad_hidden = cotangent[here, :].astype(F32) + norm_back(
                    grad * use["gain"][...], normed, inverse
                )
                use["grad_hidden"][here, :] = grad_hidden
                grad_mixed[here, :] = grad_hidden.astype(BF16)

            over_rows(rows, end)
            use["grad_attended"][...] = dot_nt(grad_mixed[...], use["mixing_all"][...]).astype(BF16)
            term[...] = dot_tn(use["attended"][...], grad_mixed[...])
            tall = 2 * width
            messages = messages_of(part[-1])
            split_out(spot, pieces, term, messages, tall)
            put_vector(
                pieces,
                jnp.sum(sums[...], axis=0, keepdims=True),
                messages,
                tall + height * groups,
                0,
            )


def feed_stage(spot, arrays, gathered, mixing_pieces, part, chunks, ctx_size):
    first, last = part[0] == 0, part[-1] == chunks - 1
    rows, width = arrays["cotangent"].shape
    pieces = len(gathered[part[0]])
    wide = jax.ShapeDtypeStruct((rows, width), F32)
    narrow = jax.ShapeDtypeStruct((rows, width), BF16)
    inputs, outputs, scratch = {}, {}, {}
    for chunk in part:
        more = mixing_rows(width, pieces, ctx_size) if chunk == chunks - 1 else 0
        message = jax.ShapeDtypeStruct((pieces // 2, 2 * width + more, TILE), BF16)
        if chunk == 1:
            message = jax.ShapeDtypeStruct((2, pieces // 2, width, TILE), BF16)
        outputs[f"keep{chunk}"] = outputs[f"send{chunk}"] = message
    inputs["cotangent"] = arrays["cotangent"]
    for chunk in part:
        for r in range(pieces):
            inputs[f"message{chunk}_{r}"] = gathered[chunk][r]
    for r in range(pieces):
        inputs[f"mixing{r}"] = mixing_pieces[r]
    scratch["mixing_all"] = pltpu.VMEM((width, width), BF16)
    early, late = (), ()
    if first:
        for name in ("attended", "tokens", "gain"):
            inputs[name] = arrays[name]
        outputs.update(hidden=wide, scaled=narrow, reduced=wide, grads=wide)
        early = ("hidden", "scaled", "keep0", "send0")
    if last:
        for name in ("gain", "scaled"):
            inputs[name] = arrays[name]
        late = ("attended", "hidden", "reduced_in", "grads_in")
        for name in late:
            inputs[f"{name}_far"] = arrays[name.removesuffix("_in")]
        outputs.update(layer_out=narrow, grad_hidden=wide, grad_attended=narrow)
        scratch.update(
            reduced=pltpu.VMEM((rows, width), F32),
            grads=pltpu.VMEM((rows, width), F32),
            sums=pltpu.VMEM((8, width), F32),
            grad_mixed=pltpu.VMEM((rows, width), BF16),
            term=pltpu.VMEM((width, width), F32),
        )
    for name in early:
        scratch[name] = pltpu.VMEM(outputs[name].shape, outputs[name].dtype)
    for name in late:
        scratch[name] = pltpu.VMEM(inputs[f"{name}_far"].shape, inputs[f"{name}_far"].dtype)
    for name in early + late:
        scratch[f"{name}_sem"] = pltpu.SemaphoreType.DMA
    outputs = {f"{name}_far" if name in early else name: one for name, one in outputs.items()}
    steps = len(part) * (pieces // 2)
    scratch.update(
        up_tile=pltpu.VMEM((steps, width, 2 * TILE), BF16),
        down_tile=pltpu.VMEM((steps, 2 * TILE, width), BF16),
        up_sems=pltpu.SemaphoreType.DMA((steps, 2, pieces)),
        down_sems=pltpu.SemaphoreType.DMA((steps, 2, width // TILE)),
        up_term=pltpu.VMEM((width, 2 * TILE), F32),
    )

    def spec(name, array):
        if name[:7] == "message" or name[-4:] == "_far":
            return pl.BlockSpec(memory_space=pl.ANY)
        once = pl.Buffered(1)
        rank = len(array.shape)
        return pl.BlockSpec(array.shape, lambda i, *_: (0,) * rank, pipeline_mode=once)

    results = pl.pallas_call(
        functools.partial(
            feed_kernel,
            pieces=pieces,
            part=part,
            first=first,
            last=last,
            names=(*inputs, *outputs, *scratch),
            early=early,
            late=late,
        ),
        grid_spec=pltpu.PrefetchScalarGridSpec(
            num_scalar_prefetch=1,
            grid=(steps,),
            in_specs=[spec(*one) for one in inputs.items()],
            out_specs=[spec(*one) for one in outputs.items()],
            scratch_shapes=list(scratch.values()),
        ),
        out_shape=list(outputs.values()),
        compiler_params=params("arbitrary"),
        cost_estimate=weight(),
        name=f"feed{part[0]}",
    )(spot, *inputs.values())
    return {**arrays, **dict(zip((name.removesuffix("_far") for name in outputs), results))}


def query_kernel(spot_ref, scaled, *rest, pieces, seqs):
    grad_queries, weights = rest[:seqs], rest[seqs : seqs + pieces]
    grad_out, keep_out, send_out, weight, term = rest[seqs + pieces :]
    spot = spot_ref[0]
    rows = scaled.shape[0] // seqs
    place_rows(spot, weights, weight)
    for i, one in enumerate(grad_queries):
        here = slice(i * rows, (i + 1) * rows)
        part = dot_tn(scaled[here, :], one[...])
        term[...] = part if i == 0 else term[...] + part
        grad_out[here, :] = dot_nt(one[...], weight[...])
    split_out(spot, pieces, term, (keep_out, send_out))


def query_stage(spot, scaled, grad_queries, weights, ctx_size):
    rows, width = scaled.shape
    pieces = len(weights)
    tall = round_up(width // pieces * (width // TILE), 8 * ctx_size)
    message = jax.ShapeDtypeStruct((pieces // 2, tall, TILE), BF16)
    outs = [jax.ShapeDtypeStruct((rows, width), F32), message, message]
    whole = lambda one: pl.BlockSpec(one.shape, lambda i, *_: (0,) * len(one.shape))
    return pl.pallas_call(
        functools.partial(query_kernel, pieces=pieces, seqs=len(grad_queries)),
        grid_spec=pltpu.PrefetchScalarGridSpec(
            num_scalar_prefetch=1,
            grid=(1,),
            in_specs=[whole(scaled)]
            + [whole(one) for one in grad_queries]
            + [pl.BlockSpec((width // pieces, width), lambda i, *_: (0, 0))] * pieces,
            out_specs=[whole(one) for one in outs],
            scratch_shapes=[
                pltpu.VMEM((width, width), BF16),
                pltpu.VMEM((width, width), F32),
            ],
        ),
        out_shape=outs,
        compiler_params=params(),
        cost_estimate=weight(),
        name="query_grad",
    )(spot, scaled, *grad_queries, *weights)


def last_kernel(spot_ref, tokens, gain, scaled, arrived, grad_scaled, grad_hidden, *rest, pieces):
    weights = rest[:pieces]
    input_grad, keep_out, send_out, weight, sums, term, grad_shared = rest[pieces:]
    spot = spot_ref[0]
    width = tokens.shape[1]
    place_rows(spot, weights, weight)
    sums[...] = jnp.zeros_like(sums)
    places, seqs, here, unused = arrived.shape
    for i in range(seqs):
        total = arrived[0, i].astype(F32)
        for j in range(1, places):
            total = total + arrived[j, i].astype(F32)
        grad_shared[i * here : (i + 1) * here, :] = total.astype(BF16)
    term[...] = dot_tn(scaled[...], grad_shared[...])
    split_out(spot, pieces, term, (keep_out, send_out))

    def run(rows):
        normed, inverse = normalize(tokens[rows, :].astype(F32))
        grad = grad_scaled[rows, :] + dot_nt(grad_shared[rows, :], weight[...])
        sums[...] += jnp.sum((grad * normed).reshape(STEP // 8, 8, width), axis=0)
        input_grad[rows, :] = grad_hidden[rows, :] + norm_back(
            grad * gain[...], normed, inverse
        )

    over_rows(tokens.shape[0], run)
    put_vector(
        pieces, jnp.sum(sums[...], axis=0, keepdims=True), (keep_out, send_out), 0, LANES
    )


def last_stage(spot, tokens, gain, scaled, arrived, grad_scaled, grad_hidden, weights, places):
    rows, width = tokens.shape
    pieces = len(weights)
    message = jax.ShapeDtypeStruct(
        (pieces // 2, round_up(width // pieces, 8 * places), 2 * LANES), BF16
    )
    return pl.pallas_call(
        functools.partial(last_kernel, pieces=pieces),
        grid_spec=pltpu.PrefetchScalarGridSpec(
            num_scalar_prefetch=1,
            grid=(),
            in_specs=[pl.BlockSpec(memory_space=pltpu.VMEM)] * (6 + pieces),
            out_specs=[pl.BlockSpec(memory_space=pltpu.VMEM)] * 3,
            scratch_shapes=[
                pltpu.VMEM((width, LANES), BF16),
                pltpu.VMEM((8, width), F32),
                pltpu.VMEM((width, LANES), F32),
                pltpu.VMEM((rows, LANES), BF16),
            ],
        ),
        out_shape=[jax.ShapeDtypeStruct((rows, width), F32), message, message],
        compiler_params=params(),
        cost_estimate=weight(),
        name="last",
    )(spot, tokens, gain, scaled, arrived, grad_scaled, grad_hidden, *weights)


def put_halves(whole, own, other, at, place, first):
    deep, unused, rows, unused = own.shape
    low = place & 1
    for half, x in ((own, low), (other, 1 - low)):
        for k in range(deep):
            begin = pl.multiple_of((x * deep + (first ^ k)) * rows, 8)
            whole[pl.ds(begin, rows), :] = half[k, at].astype(F32)


def early_kernel(place_ref, own, other, down_out, up_out, whole, *, chunks, pieces):
    width = down_out.shape[1]
    height = width // pieces
    place = place_ref[0]
    for chunk in range(own.shape[1]):
        put_halves(whole, own, other, chunk, place, place >> 1)
        for g in range(width // TILE):
            down_out[chunk * TILE : (chunk + 1) * TILE, g * TILE : (g + 1) * TILE] = whole[
                g * TILE : (g + 1) * TILE, :
            ]
        for j in range(pieces):
            row, column = width + j * height, (j * chunks + chunk) * TILE
            up_out[:, column : column + TILE] = whole[row : row + height, :]


def early_stage(place, own, other, chunks, pieces, width):
    shape = lambda *dims: jax.ShapeDtypeStruct(dims, F32)
    vmem = pl.BlockSpec(memory_space=pltpu.VMEM)
    return pl.pallas_call(
        functools.partial(early_kernel, chunks=chunks, pieces=pieces),
        grid_spec=pltpu.PrefetchScalarGridSpec(
            num_scalar_prefetch=1,
            grid=(),
            in_specs=[vmem] * 2,
            out_specs=[vmem] * 2,
            scratch_shapes=[pltpu.VMEM((2 * width, TILE), F32)],
        ),
        out_shape=[shape(chunks * TILE, width), shape(width // pieces, pieces * chunks * TILE)],
        compiler_params=params(),
        cost_estimate=weight(),
        name="early_sums",
    )(place, own, other)


def final_kernel(
    place_ref, own, other, late, down_in, up_in,
    down_out, up_out, mixing_out, query_out, shared_out, gains_out,
    whole, down_part, up_part, sems,
    *, chunks, pieces, query_rows,
):
    height, width = mixing_out.shape
    groups = width // TILE
    place = place_ref[0]

    def columns(out, first_row, rows):
        for g in range(groups):
            row = first_row + g * rows
            out[:, g * TILE : (g + 1) * TILE] = whole[row : row + rows, :]

    def load(begin, rows):
        for c in range(late.shape[0]):
            whole[c * rows : (c + 1) * rows, :] = late[c, begin : begin + rows, :].astype(F32)

    put_halves(whole, own, other, 0, place, place >> 1)
    columns(down_part, 0, TILE)
    copies = [
        pltpu.make_async_copy(
            down_part, down_out.at[pl.ds((chunks - 1) * TILE, TILE), :], sems.at[pieces]
        )
    ]
    for j in range(pieces):
        up_part[j] = whole[width + j * height : width + (j + 1) * height, :]
        column = (j * chunks + chunks - 1) * TILE
        copies.append(
            pltpu.make_async_copy(up_part.at[j], up_out.at[:, pl.ds(column, TILE)], sems.at[j])
        )
    for one in copies:
        one.start()
    columns(mixing_out, 2 * width, height)
    row = 2 * width + groups * height
    for i in range(width // LANES):
        gains_out[1:2, i * LANES : (i + 1) * LANES] = whole[row + i : row + i + 1, 0:LANES]
    load(0, query_rows)
    columns(query_out, 0, height)
    load(query_rows, late.shape[1] - query_rows)
    shared_out[...] = whole[0:height, 0:LANES]
    for i in range(width // LANES):
        gains_out[0:1, i * LANES : (i + 1) * LANES] = whole[i : i + 1, LANES:]
    for one in copies:
        one.wait()


def final_stage(place, own, other, late, down, up, query_rows, chunks, pieces, width):
    height = width // pieces
    shape = lambda *dims: jax.ShapeDtypeStruct(dims, F32)
    tallest = max(2 * own.shape[0] * own.shape[2], late.shape[0] * late.shape[1])
    vmem, anywhere = pl.BlockSpec(memory_space=pltpu.VMEM), pl.BlockSpec(memory_space=pl.ANY)
    return pl.pallas_call(
        functools.partial(
            final_kernel, chunks=chunks, pieces=pieces, query_rows=query_rows
        ),
        grid_spec=pltpu.PrefetchScalarGridSpec(
            num_scalar_prefetch=1,
            grid=(),
            in_specs=[vmem] * 3 + [anywhere] * 2,
            out_specs=[anywhere] * 2 + [vmem] * 4,
            scratch_shapes=[
                pltpu.VMEM((tallest, TILE), F32),
                pltpu.VMEM((TILE, width), F32),
                pltpu.VMEM((pieces, height, TILE), F32),
                pltpu.SemaphoreType.DMA((pieces + 1,)),
            ],
        ),
        out_shape=[
            shape(*down.shape),
            shape(*up.shape),
            shape(height, width),
            shape(height, width),
            shape(height, LANES),
            shape(2, width),
        ],
        input_output_aliases={4: 0, 5: 1},
        compiler_params=params(),
        cost_estimate=weight(),
        name="final",
    )(place, own, other, late, down, up)


def swap(values, axis, size, mask):
    return lax.ppermute(values, axis, [(i, i ^ mask) for i in range(size)])


class Gather:
    def __init__(self, piece, size):
        self.size, self.own = size, piece
        self.far = swap(piece, "wt", size, 2)
        self.near = swap(piece, "wt", size, 1)

    def finish(self):
        return [self.own, self.near, self.far, swap(self.far, "wt", self.size, 1)]


def own_order(values, spot, size):
    mask = 1
    while mask < size:
        split = values.reshape((size // (2 * mask), 2, mask) + values.shape[1:])
        split = jnp.where((spot & mask) != 0, split[:, ::-1], split)
        values = split.reshape(values.shape)
        mask *= 2
    return values


class Transfer:
    def __init__(self, held, sent, routes):
        self.held, self.sent, self.routes, self.coming = held, sent, routes, []

    def launch(self):
        if self.sent:
            self.coming = [swap(one, *route) for one, route in zip(self.sent, self.routes)]
            self.sent = []

    def add(self, pick):
        return pick(self.held).astype(F32) + pick(self.coming[0]).astype(F32)


class Reduction(Transfer):
    def __init__(self, keep, send, place, sizes):
        self.wt_size, self.ctx_size = sizes
        self.groups = self.ctx_size // 2
        self.low, self.high = place & 1, place >> 1
        *outer, rows, self.lanes = keep.shape
        self.rows = rows if len(outer) == 1 else 2 * rows
        inner = (self.groups, self.rows // self.ctx_size, self.lanes)
        split = (*outer, *inner) if len(outer) == 2 else (*outer, 2, *inner)
        super().__init__(
            keep.reshape(split), [send.reshape(split)], [("wt", self.wt_size, 1)]
        )

    def y(self, cuts=()):
        edges = (0, *cuts, self.rows // self.ctx_size)
        self.later = [
            self.add(lambda v: v[1][..., begin:end, :]).astype(BF16)
            for begin, end in zip(edges, edges[1:])
        ]
        self.held = self.add(lambda v: v[0]).astype(BF16)
        self.sent = [self.later.pop(0)]
        self.routes = [("wt", self.wt_size, 2)]

    def y_more(self):
        self.before, self.sent = self.coming, [self.later.pop(0)]

    def y_joined(self):
        self.coming = [jnp.concatenate(self.before + self.coming, axis=-2)]

    def x(self):
        half = lambda x: self.add(lambda v: lax.dynamic_index_in_dim(v, x, 0, False)).astype(BF16)
        self.held, self.sent = half(self.low), [half(1 - self.low)]
        self.routes = [("ctx", self.ctx_size, 1)]

    def far(self):
        return [("ctx", self.ctx_size, 2 * k) for k in range(1, self.groups)]

    def z(self, *others):
        def part(k):
            pick = lambda v: lax.dynamic_index_in_dim(v, self.high ^ k, 0, False)
            return jnp.stack([one.add(pick) for one in (self, *others)]).astype(BF16)

        self.sent = [part(k) for k in range(1, self.groups)]
        self.held = part(0)
        self.routes = self.far()

    def total(self):
        parts = [self.held.astype(F32)] + [one.astype(F32) for one in self.coming]
        while len(parts) > 1:
            parts = [parts[i] + parts[i + 1] for i in range(0, len(parts), 2)]
        return parts[0].astype(BF16)

    def z_back(self):
        self.held = self.total()
        self.sent = [self.held] * (self.groups - 1)

    def x_back(self):
        self.held = jnp.stack([self.held] + self.coming)
        self.sent = [self.held]
        self.routes = [("ctx", self.ctx_size, 1)]

    def everywhere(self):
        return self.add(lambda v: v).astype(BF16).reshape(
            self.ctx_size, self.rows // self.ctx_size, self.lanes
        )


def tie(main, *reductions, came=()):
    state = [(one.held, one.sent) for one in reductions]
    main, state, coming = lax.optimization_barrier((main, state, [one.coming for one in came]))
    for one, (held, sent) in zip(reductions, state):
        one.held, one.sent = held, sent
    for one, values in zip(came, coming):
        one.coming = values
    for one in reductions:
        one.launch()
    return main


def body(
    tokens,
    documents,
    first_gain,
    query_weight,
    shared_weight,
    mixing_weight,
    second_gain,
    up_weight,
    down_weight,
    cotangent,
    *,
    wt_size,
    ctx_size,
):
    sizes = (wt_size, ctx_size)
    seqs, rows, width = tokens.shape
    count = seqs * rows
    spot_index = lax.axis_index("wt")
    place = lax.axis_index("ctx")
    spot = spot_index.astype(jnp.int32).reshape(1)
    length = ctx_size * rows
    doc_most = length * 5 // 8
    before = min(ctx_size - 1, -(-(doc_most - 1) // rows))
    blocks = before + 1
    height = width // wt_size
    chunks = up_weight.shape[1] // wt_size // TILE

    gain_rows = -(-height // LANES)
    pad = lambda gain: jnp.pad(gain, (0, gain_rows * LANES - height)).reshape(gain_rows, LANES)
    small = jnp.concatenate([shared_weight, pad(first_gain), pad(second_gain)], axis=0)
    small = jnp.pad(small, ((0, -small.shape[0] % 16), (0, 0)))
    small_pieces = Gather(small, wt_size).finish()
    query_gather = Gather(query_weight, wt_size)

    gains = jnp.stack([one[height : height + 2 * gain_rows] for one in small_pieces])
    gains = gains.reshape(wt_size, 2, gain_rows * LANES)[:, :, :height].astype(F32)
    gains = own_order(gains, spot_index, wt_size)
    gain_one = gains[:, 0].reshape(1, width)
    gain_two = gains[:, 1].reshape(1, width)

    inputs = tokens.reshape(count, width)
    doc_lines = documents.astype(BF16).reshape(seqs, rows // LANES, LANES)
    scaled_one, shared = first_stage(spot, inputs, gain_one, doc_lines, small_pieces, ctx_size)
    shared, query_gather.far, mixing_weight, *packed = lax.optimization_barrier(
        (shared, query_gather.far, mixing_weight, up_weight, down_weight)
    )
    keyvals = lax.all_to_all(shared, "ctx", 0, 0).reshape(ctx_size, seqs, rows + DOC_ROWS, LANES)
    packed = list(pack_stage(*packed, chunks, wt_size))
    gathers = [Gather(packed[0], wt_size)]
    mixing_gather = Gather(mixing_weight, wt_size)
    query_pieces = query_gather.finish()
    place_one = place.astype(jnp.int32).reshape(1)

    queries = project(spot, scaled_one, query_pieces).reshape(seqs, rows, width)
    keyvals, gathers[0].far, mixing_gather.far, queries, packed[1:] = lax.optimization_barrier(
        (keyvals, gathers[0].far, mixing_gather.far, queries, packed[1:])
    )
    gathered = [gathers[0].finish()]
    mixing_pieces = mixing_gather.finish()
    gathers.append(Gather(packed[1], wt_size))
    starts, exact, attended, logs = attend(place_one, queries, keyvals, blocks)
    attended, gathers[1].far, packed[2:] = lax.optimization_barrier(
        (attended, gathers[1].far, packed[2:])
    )
    gathered.append(gathers[1].finish())
    gathers += [Gather(one, wt_size) for one in packed[2:]]

    arrays = {
        "attended": attended.reshape(count, width),
        "tokens": inputs,
        "gain": gain_two,
        "cotangent": cotangent.reshape(count, width),
    }
    feed = lambda arrays, part: feed_stage(
        spot, arrays, gathered, mixing_pieces, part, chunks, ctx_size
    )
    arrays = feed(arrays, (0, 1))
    zero, one = (
        Reduction(arrays[f"keep{chunk}"], arrays[f"send{chunk}"], place, sizes) for chunk in (0, 1)
    )
    arrays, gathers[-1].far = tie((arrays, gathers[-1].far), zero, one)
    gathered.append(gathers[-1].finish())
    arrays = tie(arrays, zero, one, came=[zero])
    zero.y()
    arrays = tie(arrays, zero, one, came=[one])
    one.x()
    arrays = tie(arrays, zero, one)
    arrays = feed(arrays, (2,))
    two = Reduction(arrays["keep2"], arrays["send2"], place, sizes)
    grad_attended = tie(arrays["grad_attended"], zero, one, two, came=[zero, one])
    zero.x()
    one.y()
    grad_attended = tie(grad_attended, zero, one, two, came=[two])
    two.y([round_up(two.rows // ctx_size * 2 // 5, 8)])
    grad_attended = tie(grad_attended, zero, one, two).reshape(seqs, rows, width)
    grad_queries, terms = [], []
    for seq in range(seqs):
        part, keep, send = attend_back(
            seq, place_one, queries, starts, exact, logs, grad_attended, keyvals, blocks
        )
        came = [zero, one, two] if seq == 0 else [zero, two]
        term = Transfer(keep, [send], [("ctx", ctx_size, 1)])
        part, grad_attended = tie((part, grad_attended), *came, term, *terms, came=came + terms)
        grad_queries.append(part[0])
        terms.append(term)
        if seq == 0:
            zero.z(one)
            two.y_more()
            grad_attended = tie(grad_attended, zero, two)
    two.y_joined()
    two.x()
    zero.z_back()
    grad_queries = tie(grad_queries, zero, two)
    grad_scaled, keep, send = query_stage(spot, scaled_one, grad_queries, query_pieces, ctx_size)
    query = Reduction(keep, send, place, sizes)
    grad_scaled = tie(grad_scaled, zero, query, *terms, came=terms[1:])
    arriving = jnp.stack([one.add(lambda v: v).astype(BF16) for one in terms], axis=1)
    arriving, grad_scaled = tie((arriving, grad_scaled), query)
    arriving = lax.all_to_all(
        arriving,
        "ctx",
        0,
        0,
        axis_index_groups=[list(range(x, ctx_size, 2)) for x in range(2)],
    )
    query.y()
    grad_scaled = tie(grad_scaled, query)
    grad_scaled = tie(grad_scaled, two, came=[two])
    two.z()
    grad_scaled, arriving = tie((grad_scaled, arriving), two)
    input_grad, keep, send = last_stage(
        spot, inputs, gain_one, scaled_one, arriving, grad_scaled, arrays["grad_hidden"], small_pieces, ctx_size
    )
    shared = Reduction(keep, send, place, sizes)
    input_grad = tie(input_grad, zero, two, shared, query, came=[two, query])
    two.z_back()
    input_grad = tie(input_grad, two)
    input_grad = tie(input_grad, shared, query, came=[shared])
    shared.y()
    input_grad = tie(input_grad, shared)
    zero.x_back()
    input_grad = tie(input_grad, zero)
    input_grad = tie(input_grad, shared, query, came=[shared])
    late = jnp.concatenate([query.everywhere(), shared.everywhere()], axis=1)
    late = lax.all_to_all(late, "ctx", 0, 0)
    two.x_back()
    input_grad = tie(input_grad, two)
    late = jnp.sum(late.astype(F32), axis=0).astype(BF16)
    late = lax.all_to_all(jnp.broadcast_to(late, (ctx_size,) + late.shape), "ctx", 0, 0)
    two.launch()
    down_grad, up_grad = early_stage(
        place_one, zero.held, zero.coming[0], chunks, wt_size, width
    )
    down_grad, up_grad, two.coming = lax.optimization_barrier((down_grad, up_grad, two.coming))
    down_grad, up_grad, mixing_grad, query_grad, shared_grad, gain_grads = final_stage(
        place_one,
        two.held,
        two.coming[0],
        late,
        down_grad,
        up_grad,
        query.rows // ctx_size,
        chunks,
        wt_size,
        width,
    )
    gain_grads = lax.dynamic_slice_in_dim(gain_grads, spot_index * height, height, 1)
    return (
        arrays["layer_out"].reshape(seqs, rows, width),
        input_grad.reshape(seqs, rows, width),
        gain_grads[0],
        query_grad,
        shared_grad,
        mixing_grad,
        gain_grads[1],
        up_grad,
        down_grad,
    )


def solution(mesh):
    in_specs = (
        P("wt", "ctx", None),
        P("wt", "ctx"),
        P("wt"),
        P("wt", None),
        P("wt", None),
        P("wt", None),
        P("wt"),
        P("wt", None),
        P("wt", None),
        P("wt", "ctx", None),
    )
    out_specs = (
        P("wt", "ctx", None),
        P("wt", "ctx", None),
        P("wt"),
        P("wt", None),
        P("wt", None),
        P("wt", None),
        P("wt"),
        P("wt", None),
        P("wt", None),
    )
    run = functools.partial(body, wt_size=mesh.shape["wt"], ctx_size=mesh.shape["ctx"])
    return jax.shard_map(run, mesh=mesh, in_specs=in_specs, out_specs=out_specs, check_vma=False)
```

```python
import functools
import math

import jax
import jax.numpy as jnp
from jax import lax
from jax.experimental import pallas as pl
from jax.experimental.pallas import tpu as pltpu
from jax.sharding import PartitionSpec as P

HEADS = 12
HEAD_DIM = 64
PAIRS = HEADS // 2
LANES = 128
EPSILON = 1e-05
BIAS = -1e30
SCALE = math.log2(math.e) / HEAD_DIM**0.5
F32 = jnp.float32
BF16 = jnp.bfloat16
GELU_ROOT = math.sqrt(2.0 / math.pi)
GELU_CUBE = 0.044715


def params(*semantics):
    return pltpu.CompilerParams(
        dimension_semantics=semantics or None, vmem_limit_bytes=56 * 1024 * 1024
    )


def weight():
    return pl.CostEstimate(flops=1, bytes_accessed=1, transcendentals=0)


def dot_nn(a, b):
    return lax.dot_general(a, b, (((1,), (0,)), ((), ())), preferred_element_type=F32)


def dot_nt(a, b):
    return lax.dot_general(a, b, (((1,), (1,)), ((), ())), preferred_element_type=F32)


def dot_tn(a, b):
    return lax.dot_general(a, b, (((0,), (0,)), ((), ())), preferred_element_type=F32)


def normalize(values):
    center = values - jnp.mean(values, axis=-1, keepdims=True)
    spread = jnp.mean(center * center, axis=-1, keepdims=True)
    inverse = lax.rsqrt(spread + EPSILON)
    return center * inverse, inverse


def norm_back(grad, normed, inverse):
    mean_grad = jnp.mean(grad, axis=-1, keepdims=True)
    mean_both = jnp.mean(grad * normed, axis=-1, keepdims=True)
    return (grad - mean_grad - normed * mean_both) * inverse


def place_rows(spot, pieces, scratch):
    height = scratch.shape[0] // len(pieces)
    for r, piece in enumerate(pieces):
        begin = pl.multiple_of((spot ^ r) * height, height)
        scratch[pl.ds(begin, height), :] = piece[0:height, :]


STEP = 256


def over_rows(rows, run):
    def one(index, carried):
        run(pl.ds(pl.multiple_of(index * STEP, STEP), STEP))
        return carried

    lax.fori_loop(0, rows // STEP, one, 0)


TILE = 256


def pack_kernel(up, down, *outs, chunks, pieces):
    width = down.shape[1]
    height = up.shape[0]
    for chunk, out in enumerate(outs):
        for g in range(width // TILE):
            out[g * TILE : (g + 1) * TILE, :] = down[
                chunk * TILE : (chunk + 1) * TILE, g * TILE : (g + 1) * TILE
            ]
        for j in range(pieces):
            row, column = width + j * height, (j * chunks + chunk) * TILE
            out[row : row + height, :] = up[:, column : column + TILE]


def pack_stage(up, down, chunks, pieces):
    width = down.shape[1]
    return pl.pallas_call(
        functools.partial(pack_kernel, chunks=chunks, pieces=pieces),
        in_specs=[pl.BlockSpec(memory_space=pltpu.VMEM)] * 2,
        out_specs=[pl.BlockSpec(memory_space=pltpu.VMEM)] * chunks,
        out_shape=[jax.ShapeDtypeStruct((2 * width, TILE), BF16)] * chunks,
        compiler_params=params(),
        cost_estimate=weight(),
        name="pack",
    )(up, down)


DOC_ROWS = 16


def first_kernel(spot_ref, tokens, gain, documents, *rest, pieces):
    weights = rest[:pieces]
    scaled_out, shared_out, weight = rest[pieces:]
    place_rows(spot_ref[0], weights, weight)
    seqs, doc_lines, unused = documents.shape
    places, tall, unused = shared_out.shape
    tall = tall // seqs
    rows = tall - DOC_ROWS
    per_seq = rows // STEP

    def run(index, carried):
        here = pl.ds(pl.multiple_of(index * STEP, STEP), STEP)
        normed, unused = normalize(tokens[here, :].astype(F32))
        scaled_out[here, :] = (normed * gain[...]).astype(BF16)
        return carried

    lax.fori_loop(0, seqs * per_seq, run, 0)
    shared = dot_nn(scaled_out[...], weight[...]).astype(BF16)

    def put(c, carried):
        for seq in range(seqs):
            begin = seq * tall
            shared_out[c, begin : begin + rows, :] = shared[seq * rows : (seq + 1) * rows, :]
            begin = begin + rows
            shared_out[c, begin : begin + DOC_ROWS, :] = jnp.zeros((DOC_ROWS, LANES), BF16)
            shared_out[c, begin : begin + doc_lines, :] = documents[seq]
        return carried

    lax.fori_loop(0, places, put, 0)


def first_stage(spot, tokens, gain, documents, weights, places):
    count, width = tokens.shape
    columns = weights[0].shape[1]
    seqs, doc_lines, unused = documents.shape
    return pl.pallas_call(
        functools.partial(first_kernel, pieces=len(weights)),
        grid_spec=pltpu.PrefetchScalarGridSpec(
            num_scalar_prefetch=1,
            grid=(),
            in_specs=[pl.BlockSpec(memory_space=pltpu.VMEM)] * (3 + len(weights)),
            out_specs=[pl.BlockSpec(memory_space=pltpu.VMEM)] * 2,
            scratch_shapes=[pltpu.VMEM((width, columns), BF16)],
        ),
        out_shape=[
            jax.ShapeDtypeStruct((count, width), BF16),
            jax.ShapeDtypeStruct((places, count + seqs * DOC_ROWS, columns), BF16),
        ],
        compiler_params=params(),
        cost_estimate=weight(),
        name="first_norm",
    )(spot, tokens, gain, documents, *weights)


def project_kernel(spot_ref, operand, *rest, pieces):
    weights = rest[:pieces]
    out, weight_all = rest[pieces:]
    place_rows(spot_ref[0], weights, weight_all)
    out[...] = dot_nn(operand[...], weight_all[...]).astype(out.dtype)


def project(spot, operand, weights):
    rows, width = operand.shape
    columns = weights[0].shape[1]
    return pl.pallas_call(
        functools.partial(project_kernel, pieces=len(weights)),
        grid_spec=pltpu.PrefetchScalarGridSpec(
            num_scalar_prefetch=1,
            grid=(),
            in_specs=[pl.BlockSpec(memory_space=pltpu.VMEM)] * (1 + len(weights)),
            out_specs=pl.BlockSpec(memory_space=pltpu.VMEM),
            scratch_shapes=[pltpu.VMEM((width, columns), BF16)],
        ),
        out_shape=jax.ShapeDtypeStruct((rows, columns), BF16),
        compiler_params=params(),
        cost_estimate=weight(),
        name="project",
    )(spot, operand, *weights)


def low_lanes(shape):
    return lax.broadcasted_iota(jnp.int32, shape, len(shape) - 1) < HEAD_DIM


def swap_halves(values):
    return pltpu.roll(values, HEAD_DIM, 1)


def stacked_pairs(ref):
    return jnp.concatenate(
        [ref[0, :, p * LANES : (p + 1) * LANES] for p in range(PAIRS)], axis=0
    )


def tile_bias(starts, key_begin, row_begin, tile_rows, tile_keys):
    key_place = key_begin + lax.broadcasted_iota(jnp.int32, (tile_rows, tile_keys), 1)
    row_place = row_begin + lax.broadcasted_iota(jnp.int32, (tile_rows, tile_keys), 0)
    first = jnp.concatenate([starts] * (tile_keys // LANES), axis=1)
    allowed = (key_place >= first) & (key_place <= row_place)
    bias = jnp.where(allowed, 0.0, BIAS)
    bias = jnp.concatenate([bias, bias], axis=1)
    return jnp.concatenate([bias] * PAIRS, axis=0)


def block_at(place_ref, j, blocks):
    return jnp.maximum(place_ref[0] - (blocks - 1) + j, 0)


def attend_kernel(
    place_ref, queries, keyvals, starts_out, exact_out, rounded_out, logs_out, *rest,
    blocks, tile_rows, tile_keys
):
    key_even, key_odd, value_even, value_odd, score_scratch, most, total = rest
    rows = keyvals.shape[2] - DOC_ROWS
    tile = pl.program_id(1)

    @pl.when(tile == 0)
    def _():
        low = low_lanes((rows, LANES))
        for j in range(blocks):
            whole = keyvals[block_at(place_ref, j, blocks), 0, 0:rows, :].astype(F32)
            turned = swap_halves(whole)
            place = pl.ds(j * rows, rows)
            key_even[place, :] = jnp.where(low, whole, 0.0).astype(BF16)
            key_odd[place, :] = jnp.where(low, 0.0, turned).astype(BF16)
            value_even[place, 0:LANES] = jnp.where(low, turned, 0.0).astype(BF16)
            value_even[place, LANES:] = jnp.where(low, 1.0, 0.0).astype(BF16)
            value_odd[place, 0:LANES] = jnp.where(low, 0.0, whole).astype(BF16)
            value_odd[place, LANES:] = jnp.where(low, 0.0, 1.0).astype(BF16)

    own = keyvals[place_ref[0], 0, rows:, :].astype(F32)
    lines = rows // LANES
    marks = [jnp.broadcast_to(own[h : h + 1, :], (LANES, LANES)).T for h in range(lines)]
    marks = jnp.concatenate(marks, axis=0)
    if tile_rows != rows:
        marks = sum(
            jnp.where(tile == t, marks[t * tile_rows : (t + 1) * tile_rows, :], 0.0)
            for t in range(rows // tile_rows)
        )

    def smaller(j, count):
        lines = keyvals[block_at(place_ref, j, blocks), 0, rows:, :].astype(F32)
        missing = place_ref[0] - (blocks - 1) + j < 0
        for h in range(rows // LANES):
            line = jnp.where(missing, -1.0, lines[h : h + 1, :])
            count = count + jnp.where(line < marks, 1.0, 0.0)
        return count

    count = lax.fori_loop(0, blocks, smaller, jnp.zeros((tile_rows, LANES), F32))
    count = jnp.sum(count, axis=1, keepdims=True).astype(jnp.int32)
    starts = starts_out
    starts[0] = jnp.broadcast_to(count, (tile_rows, LANES))
    row_begin = (blocks - 1) * rows + tile * tile_rows
    begin = jnp.min(starts[0]) // tile_keys
    end = (row_begin + tile_rows - 1) // tile_keys + 1
    stacked = stacked_pairs(queries)
    most[...] = jnp.full_like(most, -3e38)
    copies = tile_keys // LANES

    def score(index):
        key_begin = pl.multiple_of(index * tile_keys, tile_keys)
        place = pl.ds(key_begin, tile_keys)
        both = jnp.concatenate([key_even[place, :], key_odd[place, :]], axis=0)
        values = dot_nt(stacked, both) + tile_bias(
            starts[0], key_begin, row_begin, tile_rows, tile_keys
        )
        score_scratch[index - begin] = values
        half = []
        for h in range(2):
            part = values[:, h * tile_keys : h * tile_keys + LANES]
            for q in range(1, copies):
                at = h * tile_keys + q * LANES
                part = jnp.maximum(part, values[:, at : at + LANES])
            half.append(part)
        return jnp.concatenate(half, axis=1)

    def output(index):
        place = pl.ds(pl.multiple_of(index * tile_keys, tile_keys), tile_keys)
        both = jnp.concatenate([value_even[place, :], value_odd[place, :]], axis=0)
        shift = jnp.concatenate([most[:, 0:LANES]] * copies + [most[:, LANES:]] * copies, axis=1)
        powers = jnp.exp2((score_scratch[index - begin] - shift) * SCALE).astype(BF16)
        return dot_nn(powers, both)

    def in_pairs(one, join, total):
        def two(index, carried):
            at = begin + 2 * index
            total[...] = join(total[...], join(one(at), one(at + 1)))
            return carried

        count = end - begin
        lax.fori_loop(0, count // 2, two, 0)

        @pl.when(count % 2 == 1)
        def _():
            total[...] = join(total[...], one(end - 1))

    in_pairs(score, jnp.maximum, most)
    stack = PAIRS * tile_rows
    for h in range(2):
        part = jnp.max(most[:, h * LANES : (h + 1) * LANES], axis=1, keepdims=True)
        most[:, h * LANES : (h + 1) * LANES] = jnp.broadcast_to(part, (stack, LANES))
    total[...] = jnp.zeros_like(total)
    in_pairs(output, jnp.add, total)
    low = low_lanes((tile_rows, LANES))
    for p in range(PAIRS):
        at = pl.ds(p * tile_rows, tile_rows)
        lanes = slice(p * LANES, (p + 1) * LANES)
        sums = total[at, LANES:]
        out = total[at, 0:LANES] / sums
        exact_out[0, :, lanes] = out
        rounded_out[0, :, lanes] = out.astype(BF16)
        shift = jnp.where(low, most[at, 0:LANES], most[at, LANES:])
        logs_out[0, :, lanes] = shift * SCALE + jnp.log2(sums)


def attend_back_kernel(
    place_ref, queries, starts, exact, logs, grads, keyvals, *rest,
    seq, blocks, tile_rows, tile_keys
):
    grad_queries, keep, send, *rest = rest
    (
        key_even, key_odd, value_even, value_odd,
        key_total, value_total, query_total,
        log_even, log_odd, delta_even, delta_odd,
    ) = rest
    rows = keyvals.shape[2] - DOC_ROWS
    tile = pl.program_id(0)

    @pl.when(tile == 0)
    def _():
        low = low_lanes((rows, LANES))
        for j in range(blocks):
            whole = keyvals[block_at(place_ref, j, blocks), 0, 0:rows, :].astype(F32)
            turned = swap_halves(whole)
            place = pl.ds(j * rows, rows)
            key_even[place, :] = jnp.where(low, whole, 0.0).astype(BF16)
            key_odd[place, :] = jnp.where(low, 0.0, turned).astype(BF16)
            value_even[place, :] = jnp.where(low, turned, 0.0).astype(BF16)
            value_odd[place, :] = jnp.where(low, 0.0, whole).astype(BF16)
        key_total[...] = jnp.zeros_like(key_total)
        value_total[...] = jnp.zeros_like(value_total)

    row_begin = (blocks - 1) * rows + tile * tile_rows
    begin = jnp.min(starts[0]) // tile_keys
    end = (row_begin + tile_rows - 1) // tile_keys + 1
    stacked = stacked_pairs(queries)
    grad_stacked = stacked_pairs(grads)
    stacked_turned = stacked.T
    grad_turned = grad_stacked.T
    stack = PAIRS * tile_rows
    low = low_lanes((tile_rows, LANES))
    for p in range(PAIRS):
        at = pl.ds(p * tile_rows, tile_rows)
        lanes = slice(p * LANES, (p + 1) * LANES)
        log = logs[0, :, lanes]
        log_turned = swap_halves(log)
        log_even[at, :] = jnp.where(low, log, log_turned)
        log_odd[at, :] = jnp.where(low, log_turned, log)
        terms_here = exact[0, :, lanes] * grads[0, :, lanes].astype(F32)
        even = jnp.sum(jnp.where(low, terms_here, 0.0), axis=1, keepdims=True)
        odd = jnp.sum(jnp.where(low, 0.0, terms_here), axis=1, keepdims=True)
        delta_even[at, :] = jnp.broadcast_to(even, (tile_rows, LANES))
        delta_odd[at, :] = jnp.broadcast_to(odd, (tile_rows, LANES))
    query_total[...] = jnp.zeros_like(query_total)

    def step(index, carried):
        key_begin = pl.multiple_of(index * tile_keys, tile_keys)
        place = pl.ds(key_begin, tile_keys)
        keys = jnp.concatenate([key_even[place, :], key_odd[place, :]], axis=0)
        values = jnp.concatenate([value_even[place, :], value_odd[place, :]], axis=0)
        copies = tile_keys // LANES
        log = jnp.concatenate([log_even[...]] * copies + [log_odd[...]] * copies, axis=1)
        delta = jnp.concatenate([delta_even[...]] * copies + [delta_odd[...]] * copies, axis=1)
        scores = dot_nt(stacked, keys) + tile_bias(
            starts[0], key_begin, row_begin, tile_rows, tile_keys
        )
        chances = jnp.exp2(scores * SCALE - log)
        grad_probs = dot_nt(grad_stacked, values)
        grad_scores = (chances * (grad_probs - delta)).astype(BF16)
        query_total[...] += dot_nn(grad_scores, keys)
        key_total[index] += dot_nn(stacked_turned, grad_scores)
        value_total[index] += dot_nn(grad_turned, chances.astype(BF16))
        return carried

    lax.fori_loop(begin, end, step, 0)
    root = 1.0 / HEAD_DIM**0.5
    for p in range(PAIRS):
        at = pl.ds(p * tile_rows, tile_rows)
        lanes = slice(p * LANES, (p + 1) * LANES)
        grad_queries[0, :, lanes] = (query_total[at, :] * root).astype(BF16)

    @pl.when(tile == pl.num_programs(0) - 1)
    def _():
        per_block = rows // tile_keys
        keep[...] = jnp.zeros_like(keep)
        send[...] = jnp.zeros_like(send)

        def block_terms(j, carried):
            for i in range(per_block):
                index = j * per_block + i
                key = key_total[index]
                value = value_total[index]
                key = key[0:HEAD_DIM, 0:tile_keys] + key[HEAD_DIM:, tile_keys:]
                value = value[0:HEAD_DIM, 0:tile_keys] + value[HEAD_DIM:, tile_keys:]
                both = jnp.concatenate([key * root, value], axis=0)
                both = both.T.astype(BF16)
                owner = block_at(place_ref, j, blocks)
                here = slice(i * tile_keys, (i + 1) * tile_keys)
                same = (owner & 1) == (place_ref[0] & 1)

                @pl.when(same)
                def _():
                    keep[owner >> 1, here, :] = both

                @pl.when(jnp.logical_not(same))
                def _():
                    send[owner >> 1, here, :] = both

            return carried

        missing = jnp.maximum(blocks - 1 - place_ref[0], 0)
        lax.fori_loop(missing, blocks, block_terms, 0)


def attention_sizes(rows, blocks, kept):
    tile_keys = 256 if rows % 256 == 0 else 128
    tile_rows = 128
    if kept and rows % 256 == 0 and blocks * rows * 256 * HEADS * 4 < 24 * 1024 * 1024:
        tile_rows = 256
    return tile_rows, tile_keys, blocks * rows // tile_keys


def attend(place, queries, keyvals, blocks):
    unused, seqs, tall, unused = keyvals.shape
    rows = tall - DOC_ROWS
    width = queries.shape[2]
    tile_rows, tile_keys, key_tiles = attention_sizes(rows, blocks, True)
    stack = PAIRS * tile_rows
    keys = blocks * rows
    row_spec = lambda lanes: pl.BlockSpec((1, tile_rows, lanes), lambda s, t, *_: (s, t, 0))
    wide = lambda dtype: jax.ShapeDtypeStruct((seqs, rows, width), dtype)
    return pl.pallas_call(
        functools.partial(
            attend_kernel, blocks=blocks, tile_rows=tile_rows, tile_keys=tile_keys
        ),
        grid_spec=pltpu.PrefetchScalarGridSpec(
            num_scalar_prefetch=1,
            grid=(seqs, rows // tile_rows),
            in_specs=[
                row_spec(width),
                pl.BlockSpec((keyvals.shape[0], 1, tall, LANES), lambda s, t, *_: (0, s, 0, 0)),
            ],
            out_specs=[row_spec(LANES)] + [row_spec(width)] * 3,
            scratch_shapes=[
                pltpu.VMEM((keys, LANES), BF16),
                pltpu.VMEM((keys, LANES), BF16),
                pltpu.VMEM((keys, 2 * LANES), BF16),
                pltpu.VMEM((keys, 2 * LANES), BF16),
                pltpu.VMEM((key_tiles, stack, 2 * tile_keys), F32),
                pltpu.VMEM((stack, 2 * LANES), F32),
                pltpu.VMEM((stack, 2 * LANES), F32),
            ],
        ),
        out_shape=[
            jax.ShapeDtypeStruct((seqs, rows, LANES), jnp.int32),
            wide(F32),
            wide(BF16),
            wide(F32),
        ],
        compiler_params=params("arbitrary", "arbitrary"),
        cost_estimate=weight(),
        name="attend",
    )(place, queries, keyvals)


def attend_back(
    seq, place, queries, starts, exact, logs, grads, keyvals, blocks
):
    seqs, rows, width = queries.shape
    ctx_size = keyvals.shape[0]
    tile_rows, tile_keys, key_tiles = attention_sizes(rows, blocks, False)
    stack = PAIRS * tile_rows
    keys = blocks * rows
    row_spec = lambda lanes: pl.BlockSpec((1, tile_rows, lanes), lambda t, *_: (seq, t, 0))
    return pl.pallas_call(
        functools.partial(
            attend_back_kernel, seq=seq, blocks=blocks, tile_rows=tile_rows, tile_keys=tile_keys
        ),
        grid_spec=pltpu.PrefetchScalarGridSpec(
            num_scalar_prefetch=1,
            grid=(rows // tile_rows,),
            in_specs=[row_spec(width), row_spec(LANES)]
            + [row_spec(width)] * 3
            + [pl.BlockSpec((ctx_size, 1, keyvals.shape[2], LANES), lambda t, *_: (0, seq, 0, 0))],
            out_specs=[
                pl.BlockSpec((1, tile_rows, width), lambda t, *_: (0, t, 0)),
            ]
            + [pl.BlockSpec((ctx_size // 2, rows, LANES), lambda t, *_: (0, 0, 0))] * 2,
            scratch_shapes=[pltpu.VMEM((keys, LANES), BF16)] * 4
            + [pltpu.VMEM((key_tiles, LANES, 2 * tile_keys), F32)] * 2
            + [pltpu.VMEM((stack, LANES), F32)] * 5,
        ),
        out_shape=[
            jax.ShapeDtypeStruct((1, rows, width), BF16),
        ]
        + [jax.ShapeDtypeStruct((ctx_size // 2, rows, LANES), BF16)] * 2,
        compiler_params=params("arbitrary"),
        cost_estimate=weight(),
        name="attend_back",
    )(place, queries, starts, exact, logs, grads, keyvals)


def round_up(count, unit):
    return -(-count // unit) * unit


def mixing_rows(width, pieces, ctx_size):
    unit = 8 * ctx_size
    tall = 2 * width + width // pieces * (width // TILE)
    return round_up(tall + width // LANES, unit) - 2 * width


def message_of(messages, s):
    return messages[s & 1], s >> 1


def split_out(spot, pieces, source, messages, first_row=0):
    height, lanes = source.shape[0] // pieces, messages[0].shape[2]
    across = min(lanes, source.shape[1])
    for s in range(pieces):
        out, at = message_of(messages, s)
        begin = pl.multiple_of((spot ^ s) * height, height)
        for g in range(source.shape[1] // across):
            row = first_row + g * height
            out[at, row : row + height, 0:across] = source[
                pl.ds(begin, height), g * lanes : g * lanes + across
            ].astype(BF16)


def put_vector(pieces, vector, messages, first_row, begin):
    height, lanes = messages[0].shape[1] - first_row, messages[0].shape[2]
    count = vector.shape[1] // LANES
    row = lax.broadcasted_iota(jnp.int32, (height, LANES), 0)
    block = jnp.zeros((height, LANES), F32)
    for i in range(count):
        block = jnp.where(row == i, vector[:, i * LANES : (i + 1) * LANES], block)
    for s in range(pieces):
        out, at = message_of(messages, s)
        out[at, first_row:, begin : begin + LANES] = block.astype(BF16)
        if begin == 0:
            out[at, first_row:, LANES:] = jnp.zeros((height, lanes - LANES), BF16)


def feed_kernel(spot_ref, *refs, pieces, part, first, last, names, early, late):
    use = dict(zip(names, refs))
    spot = spot_ref[0]
    step = pl.program_id(0)
    steps = len(part) * (pieces // 2)
    cotangent = use["cotangent"]
    reduced, grads, scaled, hidden = use["reduced"], use["grads"], use["scaled"], use["hidden"]
    up_tile, down_tile, up_sems, down_sems = (
        use["up_tile"], use["down_tile"], use["up_sems"], use["down_sems"]
    )
    rows, width = cotangent.shape
    height = width // pieces
    groups = width // TILE

    def messages_of(chunk):
        return use[f"keep{chunk}"], use[f"send{chunk}"]

    def owners(n):
        chunk, at = divmod(n, pieces // 2)
        return part[chunk], (2 * at, 2 * at + 1)

    def copies(n):
        chunk, pair = owners(n)
        for h, s in enumerate(pair):
            source = pl.multiple_of(width + (spot ^ s) * height, height)
            for r in range(pieces):
                row = pl.multiple_of((spot ^ r) * height, height)
                yield pltpu.make_async_copy(
                    use[f"message{chunk}_{r}"].at[pl.ds(source, height), :],
                    up_tile.at[n, pl.ds(row, height), pl.ds(h * TILE, TILE)],
                    up_sems.at[n, h, r],
                )
            for g in range(groups):
                yield pltpu.make_async_copy(
                    use[f"message{chunk}_{s}"].at[pl.ds(g * TILE, TILE), :],
                    down_tile.at[n, pl.ds(h * TILE, TILE), pl.ds(g * TILE, TILE)],
                    down_sems.at[n, h, g],
                )

    def beside(kind, names):
        for name in names:
            pair = use[f"{name}_far"], use[name]
            source, target = pair if kind == "in" else pair[::-1]
            yield pltpu.make_async_copy(source, target, use[f"{name}_sem"])

    @pl.when(step == 0)
    def _():
        for n in range(steps):
            for one in copies(n):
                one.start()
        for one in beside("in", late):
            one.start()
        if first:

            def begin(here):
                values = use["tokens"][here, :].astype(F32) + hidden[here, :]
                hidden[here, :] = values
                normed, unused = normalize(values)
                scaled[here, :] = (normed * use["gain"][...]).astype(BF16)

            place_rows(spot, [use[f"mixing{r}"] for r in range(pieces)], use["mixing_all"])
            hidden[...] = dot_nn(use["attended"][...], use["mixing_all"][...])
            over_rows(rows, begin)
            for one in beside("out", ("hidden", "scaled")):
                one.start()

    if first:

        @pl.when(step == pieces // 2)
        def _():
            for one in beside("out", ("keep0", "send0")):
                one.start()

        @pl.when(step == steps - 1)
        def _():
            for one in beside("out", early):
                one.wait()

    for n in range(steps):

        @pl.when(step == n)
        def _():
            for one in copies(n):
                one.wait()

    up = up_tile[step]
    down = down_tile[step]
    upper = dot_nn(scaled[...], up)
    grad_act = dot_nt(cotangent[...], down)
    square = upper * upper
    inner = jnp.tanh(GELU_ROOT * (upper + GELU_CUBE * upper * square))
    half = 0.5 * (1.0 + inner)
    slope = half + 0.5 * upper * (1.0 - inner * inner) * (
        GELU_ROOT * (1.0 + 3.0 * GELU_CUBE * square)
    )
    active = (upper * half).astype(BF16)
    grad_upper = (grad_act * slope).astype(BF16)
    reduced_here = dot_nn(active, down)
    grads_here = dot_nt(grad_upper, up)

    @pl.when(step == 0)
    def _():
        reduced[...] = reduced_here
        grads[...] = grads_here

    @pl.when(step > 0)
    def _():
        reduced[...] += reduced_here
        grads[...] += grads_here

    down_term = dot_tn(active, cotangent[...]).astype(BF16)
    up_term = use["up_term"]
    up_term[...] = dot_tn(scaled[...], grad_upper)
    for n in range(steps):

        @pl.when(step == n)
        def _():
            chunk, pair = owners(n)
            messages = messages_of(chunk)
            for h, s in enumerate(pair):
                out, at = message_of(messages, s)
                for g in range(groups):
                    column = slice(g * TILE, (g + 1) * TILE)
                    part_here = down_term[h * TILE : (h + 1) * TILE, column]
                    if chunk == 1:
                        out[0, at, column, :] = part_here
                    else:
                        out[at, column, :] = part_here
            for s in range(pieces):
                out, at = message_of(messages, s)
                begin = pl.multiple_of((spot ^ s) * height, height)
                for h, t in enumerate(pair):
                    part_here = up_term[
                        pl.ds(begin, height), h * TILE : (h + 1) * TILE
                    ].astype(BF16)
                    row = pl.multiple_of((spot ^ t) * height, height)
                    if chunk == 1:
                        out[1, at, pl.ds(row, height), :] = part_here
                    else:
                        out[at, pl.ds(width + row, height), :] = part_here

    if last:

        @pl.when(step == steps - 1)
        def _():
            sums, grad_mixed, term = use["sums"], use["grad_mixed"], use["term"]
            for one in beside("in", late):
                one.wait()
            sums[...] = jnp.zeros_like(sums)
            place_rows(spot, [use[f"mixing{r}"] for r in range(pieces)], use["mixing_all"])

            def end(here):
                values = hidden[here, :]
                total = use["reduced_in"][here, :] + reduced[here, :]
                use["layer_out"][here, :] = (values + total).astype(BF16)
                normed, inverse = normalize(values)
                grad = use["grads_in"][here, :] + grads[here, :]
                sums[...] += jnp.sum((grad * normed).reshape(STEP // 8, 8, width), axis=0)
                grad_hidden = cotangent[here, :].astype(F32) + norm_back(
                    grad * use["gain"][...], normed, inverse
                )
                use["grad_hidden"][here, :] = grad_hidden
                grad_mixed[here, :] = grad_hidden.astype(BF16)

            over_rows(rows, end)
            use["grad_attended"][...] = dot_nt(grad_mixed[...], use["mixing_all"][...]).astype(BF16)
            term[...] = dot_tn(use["attended"][...], grad_mixed[...])
            tall = 2 * width
            messages = messages_of(part[-1])
            split_out(spot, pieces, term, messages, tall)
            put_vector(
                pieces,
                jnp.sum(sums[...], axis=0, keepdims=True),
                messages,
                tall + height * groups,
                0,
            )


def feed_stage(spot, arrays, gathered, mixing_pieces, part, chunks, ctx_size):
    first, last = part[0] == 0, part[-1] == chunks - 1
    rows, width = arrays["cotangent"].shape
    pieces = len(gathered[part[0]])
    wide = jax.ShapeDtypeStruct((rows, width), F32)
    narrow = jax.ShapeDtypeStruct((rows, width), BF16)
    inputs, outputs, scratch = {}, {}, {}
    for chunk in part:
        more = mixing_rows(width, pieces, ctx_size) if chunk == chunks - 1 else 0
        message = jax.ShapeDtypeStruct((pieces // 2, 2 * width + more, TILE), BF16)
        if chunk == 1:
            message = jax.ShapeDtypeStruct((2, pieces // 2, width, TILE), BF16)
        outputs[f"keep{chunk}"] = outputs[f"send{chunk}"] = message
    inputs["cotangent"] = arrays["cotangent"]
    for chunk in part:
        for r in range(pieces):
            inputs[f"message{chunk}_{r}"] = gathered[chunk][r]
    for r in range(pieces):
        inputs[f"mixing{r}"] = mixing_pieces[r]
    scratch["mixing_all"] = pltpu.VMEM((width, width), BF16)
    early, late = (), ()
    if first:
        for name in ("attended", "tokens", "gain"):
            inputs[name] = arrays[name]
        outputs.update(hidden=wide, scaled=narrow, reduced=wide, grads=wide)
        early = ("hidden", "scaled", "keep0", "send0")
    if last:
        for name in ("gain", "scaled"):
            inputs[name] = arrays[name]
        late = ("attended", "hidden", "reduced_in", "grads_in")
        for name in late:
            inputs[f"{name}_far"] = arrays[name.removesuffix("_in")]
        outputs.update(layer_out=narrow, grad_hidden=wide, grad_attended=narrow)
        scratch.update(
            reduced=pltpu.VMEM((rows, width), F32),
            grads=pltpu.VMEM((rows, width), F32),
            sums=pltpu.VMEM((8, width), F32),
            grad_mixed=pltpu.VMEM((rows, width), BF16),
            term=pltpu.VMEM((width, width), F32),
        )
    for name in early:
        scratch[name] = pltpu.VMEM(outputs[name].shape, outputs[name].dtype)
    for name in late:
        scratch[name] = pltpu.VMEM(inputs[f"{name}_far"].shape, inputs[f"{name}_far"].dtype)
    for name in early + late:
        scratch[f"{name}_sem"] = pltpu.SemaphoreType.DMA
    outputs = {f"{name}_far" if name in early else name: one for name, one in outputs.items()}
    steps = len(part) * (pieces // 2)
    scratch.update(
        up_tile=pltpu.VMEM((steps, width, 2 * TILE), BF16),
        down_tile=pltpu.VMEM((steps, 2 * TILE, width), BF16),
        up_sems=pltpu.SemaphoreType.DMA((steps, 2, pieces)),
        down_sems=pltpu.SemaphoreType.DMA((steps, 2, width // TILE)),
        up_term=pltpu.VMEM((width, 2 * TILE), F32),
    )

    def spec(name, array):
        if name[:7] == "message" or name[-4:] == "_far":
            return pl.BlockSpec(memory_space=pl.ANY)
        once = pl.Buffered(1)
        rank = len(array.shape)
        return pl.BlockSpec(array.shape, lambda i, *_: (0,) * rank, pipeline_mode=once)

    results = pl.pallas_call(
        functools.partial(
            feed_kernel,
            pieces=pieces,
            part=part,
            first=first,
            last=last,
            names=(*inputs, *outputs, *scratch),
            early=early,
            late=late,
        ),
        grid_spec=pltpu.PrefetchScalarGridSpec(
            num_scalar_prefetch=1,
            grid=(steps,),
            in_specs=[spec(*one) for one in inputs.items()],
            out_specs=[spec(*one) for one in outputs.items()],
            scratch_shapes=list(scratch.values()),
        ),
        out_shape=list(outputs.values()),
        compiler_params=params("arbitrary"),
        cost_estimate=weight(),
        name=f"feed{part[0]}",
    )(spot, *inputs.values())
    return {**arrays, **dict(zip((name.removesuffix("_far") for name in outputs), results))}


def query_kernel(spot_ref, scaled, *rest, pieces, seqs):
    grad_queries, weights = rest[:seqs], rest[seqs : seqs + pieces]
    grad_out, keep_out, send_out, weight, term = rest[seqs + pieces :]
    spot = spot_ref[0]
    rows = scaled.shape[0] // seqs
    place_rows(spot, weights, weight)
    for i, one in enumerate(grad_queries):
        here = slice(i * rows, (i + 1) * rows)
        part = dot_tn(scaled[here, :], one[...])
        term[...] = part if i == 0 else term[...] + part
        grad_out[here, :] = dot_nt(one[...], weight[...])
    split_out(spot, pieces, term, (keep_out, send_out))


def query_stage(spot, scaled, grad_queries, weights, ctx_size):
    rows, width = scaled.shape
    pieces = len(weights)
    tall = round_up(width // pieces * (width // TILE), 8 * ctx_size)
    message = jax.ShapeDtypeStruct((pieces // 2, tall, TILE), BF16)
    outs = [jax.ShapeDtypeStruct((rows, width), F32), message, message]
    whole = lambda one: pl.BlockSpec(one.shape, lambda i, *_: (0,) * len(one.shape))
    return pl.pallas_call(
        functools.partial(query_kernel, pieces=pieces, seqs=len(grad_queries)),
        grid_spec=pltpu.PrefetchScalarGridSpec(
            num_scalar_prefetch=1,
            grid=(1,),
            in_specs=[whole(scaled)]
            + [whole(one) for one in grad_queries]
            + [pl.BlockSpec((width // pieces, width), lambda i, *_: (0, 0))] * pieces,
            out_specs=[whole(one) for one in outs],
            scratch_shapes=[
                pltpu.VMEM((width, width), BF16),
                pltpu.VMEM((width, width), F32),
            ],
        ),
        out_shape=outs,
        compiler_params=params(),
        cost_estimate=weight(),
        name="query_grad",
    )(spot, scaled, *grad_queries, *weights)


def last_kernel(spot_ref, tokens, gain, scaled, arrived, grad_scaled, grad_hidden, *rest, pieces):
    weights = rest[:pieces]
    input_grad, keep_out, send_out, weight, sums, term, grad_shared = rest[pieces:]
    spot = spot_ref[0]
    width = tokens.shape[1]
    place_rows(spot, weights, weight)
    sums[...] = jnp.zeros_like(sums)
    places, seqs, here, unused = arrived.shape
    for i in range(seqs):
        total = arrived[0, i].astype(F32)
        for j in range(1, places):
            total = total + arrived[j, i].astype(F32)
        grad_shared[i * here : (i + 1) * here, :] = total.astype(BF16)
    term[...] = dot_tn(scaled[...], grad_shared[...])
    split_out(spot, pieces, term, (keep_out, send_out))

    def run(rows):
        normed, inverse = normalize(tokens[rows, :].astype(F32))
        grad = grad_scaled[rows, :] + dot_nt(grad_shared[rows, :], weight[...])
        sums[...] += jnp.sum((grad * normed).reshape(STEP // 8, 8, width), axis=0)
        input_grad[rows, :] = grad_hidden[rows, :] + norm_back(
            grad * gain[...], normed, inverse
        )

    over_rows(tokens.shape[0], run)
    put_vector(
        pieces, jnp.sum(sums[...], axis=0, keepdims=True), (keep_out, send_out), 0, LANES
    )


def last_stage(spot, tokens, gain, scaled, arrived, grad_scaled, grad_hidden, weights, places):
    rows, width = tokens.shape
    pieces = len(weights)
    message = jax.ShapeDtypeStruct(
        (pieces // 2, round_up(width // pieces, 8 * places), 2 * LANES), BF16
    )
    return pl.pallas_call(
        functools.partial(last_kernel, pieces=pieces),
        grid_spec=pltpu.PrefetchScalarGridSpec(
            num_scalar_prefetch=1,
            grid=(),
            in_specs=[pl.BlockSpec(memory_space=pltpu.VMEM)] * (6 + pieces),
            out_specs=[pl.BlockSpec(memory_space=pltpu.VMEM)] * 3,
            scratch_shapes=[
                pltpu.VMEM((width, LANES), BF16),
                pltpu.VMEM((8, width), F32),
                pltpu.VMEM((width, LANES), F32),
                pltpu.VMEM((rows, LANES), BF16),
            ],
        ),
        out_shape=[jax.ShapeDtypeStruct((rows, width), F32), message, message],
        compiler_params=params(),
        cost_estimate=weight(),
        name="last",
    )(spot, tokens, gain, scaled, arrived, grad_scaled, grad_hidden, *weights)


def put_halves(whole, own, other, at, place, first):
    deep, unused, rows, unused = own.shape
    low = place & 1
    for half, x in ((own, low), (other, 1 - low)):
        for k in range(deep):
            begin = pl.multiple_of((x * deep + (first ^ k)) * rows, 8)
            whole[pl.ds(begin, rows), :] = half[k, at].astype(F32)


def early_kernel(place_ref, own, other, down_out, up_out, whole, *, chunks, pieces):
    width = down_out.shape[1]
    height = width // pieces
    place = place_ref[0]
    for chunk in range(own.shape[1]):
        put_halves(whole, own, other, chunk, place, place >> 1)
        for g in range(width // TILE):
            down_out[chunk * TILE : (chunk + 1) * TILE, g * TILE : (g + 1) * TILE] = whole[
                g * TILE : (g + 1) * TILE, :
            ]
        for j in range(pieces):
            row, column = width + j * height, (j * chunks + chunk) * TILE
            up_out[:, column : column + TILE] = whole[row : row + height, :]


def early_stage(place, own, other, chunks, pieces, width):
    shape = lambda *dims: jax.ShapeDtypeStruct(dims, F32)
    vmem = pl.BlockSpec(memory_space=pltpu.VMEM)
    return pl.pallas_call(
        functools.partial(early_kernel, chunks=chunks, pieces=pieces),
        grid_spec=pltpu.PrefetchScalarGridSpec(
            num_scalar_prefetch=1,
            grid=(),
            in_specs=[vmem] * 2,
            out_specs=[vmem] * 2,
            scratch_shapes=[pltpu.VMEM((2 * width, TILE), F32)],
        ),
        out_shape=[shape(chunks * TILE, width), shape(width // pieces, pieces * chunks * TILE)],
        compiler_params=params(),
        cost_estimate=weight(),
        name="early_sums",
    )(place, own, other)


def final_kernel(
    place_ref, own, other, late, down_in, up_in,
    down_out, up_out, mixing_out, query_out, shared_out, gains_out,
    whole, down_part, up_part, sems,
    *, chunks, pieces, query_rows,
):
    height, width = mixing_out.shape
    groups = width // TILE
    place = place_ref[0]

    def columns(out, first_row, rows):
        for g in range(groups):
            row = first_row + g * rows
            out[:, g * TILE : (g + 1) * TILE] = whole[row : row + rows, :]

    def load(begin, rows):
        for c in range(late.shape[0]):
            whole[c * rows : (c + 1) * rows, :] = late[c, begin : begin + rows, :].astype(F32)

    put_halves(whole, own, other, 0, place, place >> 1)
    columns(down_part, 0, TILE)
    copies = [
        pltpu.make_async_copy(
            down_part, down_out.at[pl.ds((chunks - 1) * TILE, TILE), :], sems.at[pieces]
        )
    ]
    for j in range(pieces):
        up_part[j] = whole[width + j * height : width + (j + 1) * height, :]
        column = (j * chunks + chunks - 1) * TILE
        copies.append(
            pltpu.make_async_copy(up_part.at[j], up_out.at[:, pl.ds(column, TILE)], sems.at[j])
        )
    for one in copies:
        one.start()
    columns(mixing_out, 2 * width, height)
    row = 2 * width + groups * height
    for i in range(width // LANES):
        gains_out[1:2, i * LANES : (i + 1) * LANES] = whole[row + i : row + i + 1, 0:LANES]
    load(0, query_rows)
    columns(query_out, 0, height)
    load(query_rows, late.shape[1] - query_rows)
    shared_out[...] = whole[0:height, 0:LANES]
    for i in range(width // LANES):
        gains_out[0:1, i * LANES : (i + 1) * LANES] = whole[i : i + 1, LANES:]
    for one in copies:
        one.wait()


def final_stage(place, own, other, late, down, up, query_rows, chunks, pieces, width):
    height = width // pieces
    shape = lambda *dims: jax.ShapeDtypeStruct(dims, F32)
    tallest = max(2 * own.shape[0] * own.shape[2], late.shape[0] * late.shape[1])
    vmem, anywhere = pl.BlockSpec(memory_space=pltpu.VMEM), pl.BlockSpec(memory_space=pl.ANY)
    return pl.pallas_call(
        functools.partial(
            final_kernel, chunks=chunks, pieces=pieces, query_rows=query_rows
        ),
        grid_spec=pltpu.PrefetchScalarGridSpec(
            num_scalar_prefetch=1,
            grid=(),
            in_specs=[vmem] * 3 + [anywhere] * 2,
            out_specs=[anywhere] * 2 + [vmem] * 4,
            scratch_shapes=[
                pltpu.VMEM((tallest, TILE), F32),
                pltpu.VMEM((TILE, width), F32),
                pltpu.VMEM((pieces, height, TILE), F32),
                pltpu.SemaphoreType.DMA((pieces + 1,)),
            ],
        ),
        out_shape=[
            shape(*down.shape),
            shape(*up.shape),
            shape(height, width),
            shape(height, width),
            shape(height, LANES),
            shape(2, width),
        ],
        input_output_aliases={4: 0, 5: 1},
        compiler_params=params(),
        cost_estimate=weight(),
        name="final",
    )(place, own, other, late, down, up)


def swap(values, axis, size, mask):
    return lax.ppermute(values, axis, [(i, i ^ mask) for i in range(size)])


class Gather:
    def __init__(self, piece, size):
        self.size, self.own = size, piece
        self.far = swap(piece, "wt", size, 2)
        self.near = swap(piece, "wt", size, 1)

    def finish(self):
        return [self.own, self.near, self.far, swap(self.far, "wt", self.size, 1)]


def own_order(values, spot, size):
    mask = 1
    while mask < size:
        split = values.reshape((size // (2 * mask), 2, mask) + values.shape[1:])
        split = jnp.where((spot & mask) != 0, split[:, ::-1], split)
        values = split.reshape(values.shape)
        mask *= 2
    return values


class Transfer:
    def __init__(self, held, sent, routes):
        self.held, self.sent, self.routes, self.coming = held, sent, routes, []

    def launch(self):
        if self.sent:
            self.coming = [swap(one, *route) for one, route in zip(self.sent, self.routes)]
            self.sent = []

    def add(self, pick):
        return pick(self.held).astype(F32) + pick(self.coming[0]).astype(F32)


class Reduction(Transfer):
    def __init__(self, keep, send, place, sizes):
        self.wt_size, self.ctx_size = sizes
        self.groups = self.ctx_size // 2
        self.low, self.high = place & 1, place >> 1
        *outer, rows, self.lanes = keep.shape
        self.rows = rows if len(outer) == 1 else 2 * rows
        inner = (self.groups, self.rows // self.ctx_size, self.lanes)
        split = (*outer, *inner) if len(outer) == 2 else (*outer, 2, *inner)
        super().__init__(
            keep.reshape(split), [send.reshape(split)], [("wt", self.wt_size, 1)]
        )

    def y(self, cuts=()):
        edges = (0, *cuts, self.rows // self.ctx_size)
        self.later = [
            self.add(lambda v: v[1][..., begin:end, :]).astype(BF16)
            for begin, end in zip(edges, edges[1:])
        ]
        self.held = self.add(lambda v: v[0]).astype(BF16)
        self.sent = [self.later.pop(0)]
        self.routes = [("wt", self.wt_size, 2)]

    def y_more(self):
        self.before, self.sent = self.coming, [self.later.pop(0)]

    def y_joined(self):
        self.coming = [jnp.concatenate(self.before + self.coming, axis=-2)]

    def x(self):
        half = lambda x: self.add(lambda v: lax.dynamic_index_in_dim(v, x, 0, False)).astype(BF16)
        self.held, self.sent = half(self.low), [half(1 - self.low)]
        self.routes = [("ctx", self.ctx_size, 1)]

    def far(self):
        return [("ctx", self.ctx_size, 2 * k) for k in range(1, self.groups)]

    def z(self, *others):
        def part(k):
            pick = lambda v: lax.dynamic_index_in_dim(v, self.high ^ k, 0, False)
            return jnp.stack([one.add(pick) for one in (self, *others)]).astype(BF16)

        self.sent = [part(k) for k in range(1, self.groups)]
        self.held = part(0)
        self.routes = self.far()

    def total(self):
        parts = [self.held.astype(F32)] + [one.astype(F32) for one in self.coming]
        while len(parts) > 1:
            parts = [parts[i] + parts[i + 1] for i in range(0, len(parts), 2)]
        return parts[0].astype(BF16)

    def z_back(self):
        self.held = self.total()
        self.sent = [self.held] * (self.groups - 1)

    def x_back(self):
        self.held = jnp.stack([self.held] + self.coming)
        self.sent = [self.held]
        self.routes = [("ctx", self.ctx_size, 1)]

    def everywhere(self):
        return self.add(lambda v: v).astype(BF16).reshape(
            self.ctx_size, self.rows // self.ctx_size, self.lanes
        )


def tie(main, *reductions, came=()):
    state = [(one.held, one.sent) for one in reductions]
    main, state, coming = lax.optimization_barrier((main, state, [one.coming for one in came]))
    for one, (held, sent) in zip(reductions, state):
        one.held, one.sent = held, sent
    for one, values in zip(came, coming):
        one.coming = values
    for one in reductions:
        one.launch()
    return main


def body(
    tokens,
    documents,
    first_gain,
    query_weight,
    shared_weight,
    mixing_weight,
    second_gain,
    up_weight,
    down_weight,
    cotangent,
    *,
    wt_size,
    ctx_size,
):
    sizes = (wt_size, ctx_size)
    seqs, rows, width = tokens.shape
    count = seqs * rows
    spot_index = lax.axis_index("wt")
    place = lax.axis_index("ctx")
    spot = spot_index.astype(jnp.int32).reshape(1)
    length = ctx_size * rows
    doc_most = length * 5 // 8
    before = min(ctx_size - 1, -(-(doc_most - 1) // rows))
    blocks = before + 1
    height = width // wt_size
    chunks = up_weight.shape[1] // wt_size // TILE

    gain_rows = -(-height // LANES)
    pad = lambda gain: jnp.pad(gain, (0, gain_rows * LANES - height)).reshape(gain_rows, LANES)
    small = jnp.concatenate([shared_weight, pad(first_gain), pad(second_gain)], axis=0)
    small = jnp.pad(small, ((0, -small.shape[0] % 16), (0, 0)))
    small_pieces = Gather(small, wt_size).finish()
    query_gather = Gather(query_weight, wt_size)

    gains = jnp.stack([one[height : height + 2 * gain_rows] for one in small_pieces])
    gains = gains.reshape(wt_size, 2, gain_rows * LANES)[:, :, :height].astype(F32)
    gains = own_order(gains, spot_index, wt_size)
    gain_one = gains[:, 0].reshape(1, width)
    gain_two = gains[:, 1].reshape(1, width)

    inputs = tokens.reshape(count, width)
    doc_lines = documents.astype(BF16).reshape(seqs, rows // LANES, LANES)
    scaled_one, shared = first_stage(spot, inputs, gain_one, doc_lines, small_pieces, ctx_size)
    shared, query_gather.far, mixing_weight, *packed = lax.optimization_barrier(
        (shared, query_gather.far, mixing_weight, up_weight, down_weight)
    )
    keyvals = lax.all_to_all(shared, "ctx", 0, 0).reshape(ctx_size, seqs, rows + DOC_ROWS, LANES)
    packed = list(pack_stage(*packed, chunks, wt_size))
    gathers = [Gather(packed[0], wt_size)]
    mixing_gather = Gather(mixing_weight, wt_size)
    query_pieces = query_gather.finish()
    place_one = place.astype(jnp.int32).reshape(1)

    queries = project(spot, scaled_one, query_pieces).reshape(seqs, rows, width)
    keyvals, gathers[0].far, mixing_gather.far, queries, packed[1:] = lax.optimization_barrier(
        (keyvals, gathers[0].far, mixing_gather.far, queries, packed[1:])
    )
    gathered = [gathers[0].finish()]
    mixing_pieces = mixing_gather.finish()
    gathers.append(Gather(packed[1], wt_size))
    starts, exact, attended, logs = attend(place_one, queries, keyvals, blocks)
    attended, gathers[1].far, packed[2:] = lax.optimization_barrier(
        (attended, gathers[1].far, packed[2:])
    )
    gathered.append(gathers[1].finish())
    gathers += [Gather(one, wt_size) for one in packed[2:]]

    arrays = {
        "attended": attended.reshape(count, width),
        "tokens": inputs,
        "gain": gain_two,
        "cotangent": cotangent.reshape(count, width),
    }
    feed = lambda arrays, part: feed_stage(
        spot, arrays, gathered, mixing_pieces, part, chunks, ctx_size
    )
    arrays = feed(arrays, (0, 1))
    zero, one = (
        Reduction(arrays[f"keep{chunk}"], arrays[f"send{chunk}"], place, sizes) for chunk in (0, 1)
    )
    arrays, gathers[-1].far = tie((arrays, gathers[-1].far), zero, one)
    gathered.append(gathers[-1].finish())
    arrays = tie(arrays, zero, one, came=[zero])
    zero.y()
    arrays = tie(arrays, zero, one, came=[one])
    one.x()
    arrays = tie(arrays, zero, one)
    arrays = feed(arrays, (2,))
    two = Reduction(arrays["keep2"], arrays["send2"], place, sizes)
    grad_attended = tie(arrays["grad_attended"], zero, one, two, came=[zero, one])
    zero.x()
    one.y()
    grad_attended = tie(grad_attended, zero, one, two, came=[two])
    two.y([round_up(two.rows // ctx_size // 3, 8)])
    grad_attended = tie(grad_attended, zero, one, two).reshape(seqs, rows, width)
    grad_queries, terms = [], []
    for seq in range(seqs):
        part, keep, send = attend_back(
            seq, place_one, queries, starts, exact, logs, grad_attended, keyvals, blocks
        )
        came = [zero, one, two] if seq == 0 else [zero, two]
        term = Transfer(keep, [send], [("ctx", ctx_size, 1)])
        part, grad_attended = tie((part, grad_attended), *came, term, *terms, came=came + terms)
        grad_queries.append(part[0])
        terms.append(term)
        if seq == 0:
            zero.z(one)
            two.y_more()
            grad_attended = tie(grad_attended, zero, two)
    two.y_joined()
    two.x()
    zero.z_back()
    grad_queries = tie(grad_queries, zero, two)
    grad_scaled, keep, send = query_stage(spot, scaled_one, grad_queries, query_pieces, ctx_size)
    query = Reduction(keep, send, place, sizes)
    grad_scaled = tie(grad_scaled, zero, query, *terms, came=terms[1:])
    arriving = jnp.stack([one.add(lambda v: v).astype(BF16) for one in terms], axis=1)
    arriving, grad_scaled = tie((arriving, grad_scaled), query)
    arriving = lax.all_to_all(
        arriving,
        "ctx",
        0,
        0,
        axis_index_groups=[list(range(x, ctx_size, 2)) for x in range(2)],
    )
    query.y()
    grad_scaled = tie(grad_scaled, query)
    grad_scaled = tie(grad_scaled, two, came=[two])
    two.z()
    grad_scaled, arriving = tie((grad_scaled, arriving), two)
    input_grad, keep, send = last_stage(
        spot, inputs, gain_one, scaled_one, arriving, grad_scaled, arrays["grad_hidden"], small_pieces, ctx_size
    )
    shared = Reduction(keep, send, place, sizes)
    input_grad = tie(input_grad, zero, two, shared, query, came=[two, query])
    two.z_back()
    input_grad = tie(input_grad, two)
    input_grad = tie(input_grad, shared, query, came=[shared])
    shared.y()
    input_grad = tie(input_grad, shared)
    zero.x_back()
    input_grad = tie(input_grad, zero)
    input_grad = tie(input_grad, shared, query, came=[shared])
    late = jnp.concatenate([query.everywhere(), shared.everywhere()], axis=1)
    late = lax.all_to_all(late, "ctx", 0, 0)
    two.x_back()
    input_grad = tie(input_grad, two)
    late = jnp.sum(late.astype(F32), axis=0).astype(BF16)
    late = lax.all_to_all(jnp.broadcast_to(late, (ctx_size,) + late.shape), "ctx", 0, 0)
    two.launch()
    down_grad, up_grad = early_stage(
        place_one, zero.held, zero.coming[0], chunks, wt_size, width
    )
    down_grad, up_grad, two.coming = lax.optimization_barrier((down_grad, up_grad, two.coming))
    down_grad, up_grad, mixing_grad, query_grad, shared_grad, gain_grads = final_stage(
        place_one,
        two.held,
        two.coming[0],
        late,
        down_grad,
        up_grad,
        query.rows // ctx_size,
        chunks,
        wt_size,
        width,
    )
    gain_grads = lax.dynamic_slice_in_dim(gain_grads, spot_index * height, height, 1)
    return (
        arrays["layer_out"].reshape(seqs, rows, width),
        input_grad.reshape(seqs, rows, width),
        gain_grads[0],
        query_grad,
        shared_grad,
        mixing_grad,
        gain_grads[1],
        up_grad,
        down_grad,
    )


def solution(mesh):
    in_specs = (
        P("wt", "ctx", None),
        P("wt", "ctx"),
        P("wt"),
        P("wt", None),
        P("wt", None),
        P("wt", None),
        P("wt"),
        P("wt", None),
        P("wt", None),
        P("wt", "ctx", None),
    )
    out_specs = (
        P("wt", "ctx", None),
        P("wt", "ctx", None),
        P("wt"),
        P("wt", None),
        P("wt", None),
        P("wt", None),
        P("wt"),
        P("wt", None),
        P("wt", None),
    )
    run = functools.partial(body, wt_size=mesh.shape["wt"], ctx_size=mesh.shape["ctx"])
    return jax.shard_map(run, mesh=mesh, in_specs=in_specs, out_specs=out_specs, check_vma=False)
```

```python
import functools
import math

import jax
import jax.numpy as jnp
from jax import lax
from jax.experimental import pallas as pl
from jax.experimental.pallas import tpu as pltpu
from jax.sharding import PartitionSpec as P

HEADS = 12
HEAD_DIM = 64
PAIRS = HEADS // 2
LANES = 128
EPSILON = 1e-05
BIAS = -1e30
SCALE = math.log2(math.e) / HEAD_DIM**0.5
F32 = jnp.float32
BF16 = jnp.bfloat16
GELU_ROOT = math.sqrt(2.0 / math.pi)
GELU_CUBE = 0.044715


def params(*semantics):
    return pltpu.CompilerParams(
        dimension_semantics=semantics or None, vmem_limit_bytes=56 * 1024 * 1024
    )


def weight():
    return pl.CostEstimate(flops=1, bytes_accessed=1, transcendentals=0)


def dot_nn(a, b):
    return lax.dot_general(a, b, (((1,), (0,)), ((), ())), preferred_element_type=F32)


def dot_nt(a, b):
    return lax.dot_general(a, b, (((1,), (1,)), ((), ())), preferred_element_type=F32)


def dot_tn(a, b):
    return lax.dot_general(a, b, (((0,), (0,)), ((), ())), preferred_element_type=F32)


def normalize(values):
    center = values - jnp.mean(values, axis=-1, keepdims=True)
    spread = jnp.mean(center * center, axis=-1, keepdims=True)
    inverse = lax.rsqrt(spread + EPSILON)
    return center * inverse, inverse


def norm_back(grad, normed, inverse):
    mean_grad = jnp.mean(grad, axis=-1, keepdims=True)
    mean_both = jnp.mean(grad * normed, axis=-1, keepdims=True)
    return (grad - mean_grad - normed * mean_both) * inverse


def place_rows(spot, pieces, scratch):
    height = scratch.shape[0] // len(pieces)
    for r, piece in enumerate(pieces):
        begin = pl.multiple_of((spot ^ r) * height, height)
        scratch[pl.ds(begin, height), :] = piece[0:height, :]


STEP = 256


def over_rows(rows, run):
    def one(index, carried):
        run(pl.ds(pl.multiple_of(index * STEP, STEP), STEP))
        return carried

    lax.fori_loop(0, rows // STEP, one, 0)


TILE = 256


def pack_kernel(up, down, *outs, chunks, pieces):
    width = down.shape[1]
    height = up.shape[0]
    for chunk, out in enumerate(outs):
        for g in range(width // TILE):
            out[g * TILE : (g + 1) * TILE, :] = down[
                chunk * TILE : (chunk + 1) * TILE, g * TILE : (g + 1) * TILE
            ]
        for j in range(pieces):
            row, column = width + j * height, (j * chunks + chunk) * TILE
            out[row : row + height, :] = up[:, column : column + TILE]


def pack_stage(up, down, chunks, pieces):
    width = down.shape[1]
    return pl.pallas_call(
        functools.partial(pack_kernel, chunks=chunks, pieces=pieces),
        in_specs=[pl.BlockSpec(memory_space=pltpu.VMEM)] * 2,
        out_specs=[pl.BlockSpec(memory_space=pltpu.VMEM)] * chunks,
        out_shape=[jax.ShapeDtypeStruct((2 * width, TILE), BF16)] * chunks,
        compiler_params=params(),
        cost_estimate=weight(),
        name="pack",
    )(up, down)


DOC_ROWS = 16


def first_kernel(spot_ref, tokens, gain, documents, *rest, pieces):
    weights = rest[:pieces]
    scaled_out, shared_out, weight = rest[pieces:]
    place_rows(spot_ref[0], weights, weight)
    seqs, doc_lines, unused = documents.shape
    places, tall, unused = shared_out.shape
    tall = tall // seqs
    rows = tall - DOC_ROWS
    per_seq = rows // STEP

    def run(index, carried):
        here = pl.ds(pl.multiple_of(index * STEP, STEP), STEP)
        normed, unused = normalize(tokens[here, :].astype(F32))
        scaled_out[here, :] = (normed * gain[...]).astype(BF16)
        return carried

    lax.fori_loop(0, seqs * per_seq, run, 0)
    shared = dot_nn(scaled_out[...], weight[...]).astype(BF16)

    def put(c, carried):
        for seq in range(seqs):
            begin = seq * tall
            shared_out[c, begin : begin + rows, :] = shared[seq * rows : (seq + 1) * rows, :]
            begin = begin + rows
            shared_out[c, begin : begin + DOC_ROWS, :] = jnp.zeros((DOC_ROWS, LANES), BF16)
            shared_out[c, begin : begin + doc_lines, :] = documents[seq]
        return carried

    lax.fori_loop(0, places, put, 0)


def first_stage(spot, tokens, gain, documents, weights, places):
    count, width = tokens.shape
    columns = weights[0].shape[1]
    seqs, doc_lines, unused = documents.shape
    return pl.pallas_call(
        functools.partial(first_kernel, pieces=len(weights)),
        grid_spec=pltpu.PrefetchScalarGridSpec(
            num_scalar_prefetch=1,
            grid=(),
            in_specs=[pl.BlockSpec(memory_space=pltpu.VMEM)] * (3 + len(weights)),
            out_specs=[pl.BlockSpec(memory_space=pltpu.VMEM)] * 2,
            scratch_shapes=[pltpu.VMEM((width, columns), BF16)],
        ),
        out_shape=[
            jax.ShapeDtypeStruct((count, width), BF16),
            jax.ShapeDtypeStruct((places, count + seqs * DOC_ROWS, columns), BF16),
        ],
        compiler_params=params(),
        cost_estimate=weight(),
        name="first_norm",
    )(spot, tokens, gain, documents, *weights)


def project_kernel(spot_ref, operand, *rest, pieces):
    weights = rest[:pieces]
    out, weight_all = rest[pieces:]
    place_rows(spot_ref[0], weights, weight_all)
    out[...] = dot_nn(operand[...], weight_all[...]).astype(out.dtype)


def project(spot, operand, weights):
    rows, width = operand.shape
    columns = weights[0].shape[1]
    return pl.pallas_call(
        functools.partial(project_kernel, pieces=len(weights)),
        grid_spec=pltpu.PrefetchScalarGridSpec(
            num_scalar_prefetch=1,
            grid=(),
            in_specs=[pl.BlockSpec(memory_space=pltpu.VMEM)] * (1 + len(weights)),
            out_specs=pl.BlockSpec(memory_space=pltpu.VMEM),
            scratch_shapes=[pltpu.VMEM((width, columns), BF16)],
        ),
        out_shape=jax.ShapeDtypeStruct((rows, columns), BF16),
        compiler_params=params(),
        cost_estimate=weight(),
        name="project",
    )(spot, operand, *weights)


def low_lanes(shape):
    return lax.broadcasted_iota(jnp.int32, shape, len(shape) - 1) < HEAD_DIM


def swap_halves(values):
    return pltpu.roll(values, HEAD_DIM, 1)


def stacked_pairs(ref):
    return jnp.concatenate(
        [ref[0, :, p * LANES : (p + 1) * LANES] for p in range(PAIRS)], axis=0
    )


def tile_bias(starts, key_begin, row_begin, tile_rows, tile_keys):
    key_place = key_begin + lax.broadcasted_iota(jnp.int32, (tile_rows, tile_keys), 1)
    row_place = row_begin + lax.broadcasted_iota(jnp.int32, (tile_rows, tile_keys), 0)
    first = jnp.concatenate([starts] * (tile_keys // LANES), axis=1)
    allowed = (key_place >= first) & (key_place <= row_place)
    bias = jnp.where(allowed, 0.0, BIAS)
    bias = jnp.concatenate([bias, bias], axis=1)
    return jnp.concatenate([bias] * PAIRS, axis=0)


def block_at(place_ref, j, blocks):
    return jnp.maximum(place_ref[0] - (blocks - 1) + j, 0)


def attend_kernel(
    place_ref, queries, keyvals, starts_out, exact_out, rounded_out, logs_out, *rest,
    blocks, tile_rows, tile_keys
):
    key_even, key_odd, value_even, value_odd, score_scratch, most, total = rest
    rows = keyvals.shape[2] - DOC_ROWS
    tile = pl.program_id(1)

    @pl.when(tile == 0)
    def _():
        low = low_lanes((rows, LANES))
        for j in range(blocks):
            whole = keyvals[block_at(place_ref, j, blocks), 0, 0:rows, :].astype(F32)
            turned = swap_halves(whole)
            place = pl.ds(j * rows, rows)
            key_even[place, :] = jnp.where(low, whole, 0.0).astype(BF16)
            key_odd[place, :] = jnp.where(low, 0.0, turned).astype(BF16)
            value_even[place, 0:LANES] = jnp.where(low, turned, 0.0).astype(BF16)
            value_even[place, LANES:] = jnp.where(low, 1.0, 0.0).astype(BF16)
            value_odd[place, 0:LANES] = jnp.where(low, 0.0, whole).astype(BF16)
            value_odd[place, LANES:] = jnp.where(low, 0.0, 1.0).astype(BF16)

    own = keyvals[place_ref[0], 0, rows:, :].astype(F32)
    lines = rows // LANES
    marks = [jnp.broadcast_to(own[h : h + 1, :], (LANES, LANES)).T for h in range(lines)]
    marks = jnp.concatenate(marks, axis=0)
    if tile_rows != rows:
        marks = sum(
            jnp.where(tile == t, marks[t * tile_rows : (t + 1) * tile_rows, :], 0.0)
            for t in range(rows // tile_rows)
        )

    def smaller(j, count):
        lines = keyvals[block_at(place_ref, j, blocks), 0, rows:, :].astype(F32)
        missing = place_ref[0] - (blocks - 1) + j < 0
        for h in range(rows // LANES):
            line = jnp.where(missing, -1.0, lines[h : h + 1, :])
            count = count + jnp.where(line < marks, 1.0, 0.0)
        return count

    count = lax.fori_loop(0, blocks, smaller, jnp.zeros((tile_rows, LANES), F32))
    count = jnp.sum(count, axis=1, keepdims=True).astype(jnp.int32)
    starts = starts_out
    starts[0] = jnp.broadcast_to(count, (tile_rows, LANES))
    row_begin = (blocks - 1) * rows + tile * tile_rows
    begin = jnp.min(starts[0]) // tile_keys
    end = (row_begin + tile_rows - 1) // tile_keys + 1
    stacked = stacked_pairs(queries)
    most[...] = jnp.full_like(most, -3e38)
    copies = tile_keys // LANES

    def score(index):
        key_begin = pl.multiple_of(index * tile_keys, tile_keys)
        place = pl.ds(key_begin, tile_keys)
        both = jnp.concatenate([key_even[place, :], key_odd[place, :]], axis=0)
        values = dot_nt(stacked, both) + tile_bias(
            starts[0], key_begin, row_begin, tile_rows, tile_keys
        )
        score_scratch[index - begin] = values
        half = []
        for h in range(2):
            part = values[:, h * tile_keys : h * tile_keys + LANES]
            for q in range(1, copies):
                at = h * tile_keys + q * LANES
                part = jnp.maximum(part, values[:, at : at + LANES])
            half.append(part)
        return jnp.concatenate(half, axis=1)

    def output(index):
        place = pl.ds(pl.multiple_of(index * tile_keys, tile_keys), tile_keys)
        both = jnp.concatenate([value_even[place, :], value_odd[place, :]], axis=0)
        shift = jnp.concatenate([most[:, 0:LANES]] * copies + [most[:, LANES:]] * copies, axis=1)
        powers = jnp.exp2((score_scratch[index - begin] - shift) * SCALE).astype(BF16)
        return dot_nn(powers, both)

    def in_pairs(one, join, total):
        def two(index, carried):
            at = begin + 2 * index
            total[...] = join(total[...], join(one(at), one(at + 1)))
            return carried

        count = end - begin
        lax.fori_loop(0, count // 2, two, 0)

        @pl.when(count % 2 == 1)
        def _():
            total[...] = join(total[...], one(end - 1))

    in_pairs(score, jnp.maximum, most)
    stack = PAIRS * tile_rows
    for h in range(2):
        part = jnp.max(most[:, h * LANES : (h + 1) * LANES], axis=1, keepdims=True)
        most[:, h * LANES : (h + 1) * LANES] = jnp.broadcast_to(part, (stack, LANES))
    total[...] = jnp.zeros_like(total)
    in_pairs(output, jnp.add, total)
    low = low_lanes((tile_rows, LANES))
    for p in range(PAIRS):
        at = pl.ds(p * tile_rows, tile_rows)
        lanes = slice(p * LANES, (p + 1) * LANES)
        sums = total[at, LANES:]
        out = total[at, 0:LANES] / sums
        exact_out[0, :, lanes] = out
        rounded_out[0, :, lanes] = out.astype(BF16)
        shift = jnp.where(low, most[at, 0:LANES], most[at, LANES:])
        logs_out[0, :, lanes] = shift * SCALE + jnp.log2(sums)


def attend_back_kernel(
    place_ref, queries, starts, exact, logs, grads, keyvals, *rest,
    seq, blocks, tile_rows, tile_keys
):
    grad_queries, keep, send, *rest = rest
    (
        key_even, key_odd, value_even, value_odd,
        key_total, value_total, query_total,
        log_even, log_odd, delta_even, delta_odd,
    ) = rest
    rows = keyvals.shape[2] - DOC_ROWS
    tile = pl.program_id(0)

    @pl.when(tile == 0)
    def _():
        low = low_lanes((rows, LANES))
        for j in range(blocks):
            whole = keyvals[block_at(place_ref, j, blocks), 0, 0:rows, :].astype(F32)
            turned = swap_halves(whole)
            place = pl.ds(j * rows, rows)
            key_even[place, :] = jnp.where(low, whole, 0.0).astype(BF16)
            key_odd[place, :] = jnp.where(low, 0.0, turned).astype(BF16)
            value_even[place, :] = jnp.where(low, turned, 0.0).astype(BF16)
            value_odd[place, :] = jnp.where(low, 0.0, whole).astype(BF16)
        key_total[...] = jnp.zeros_like(key_total)
        value_total[...] = jnp.zeros_like(value_total)

    row_begin = (blocks - 1) * rows + tile * tile_rows
    begin = jnp.min(starts[0]) // tile_keys
    end = (row_begin + tile_rows - 1) // tile_keys + 1
    stacked = stacked_pairs(queries)
    grad_stacked = stacked_pairs(grads)
    stacked_turned = stacked.T
    grad_turned = grad_stacked.T
    stack = PAIRS * tile_rows
    low = low_lanes((tile_rows, LANES))
    for p in range(PAIRS):
        at = pl.ds(p * tile_rows, tile_rows)
        lanes = slice(p * LANES, (p + 1) * LANES)
        log = logs[0, :, lanes]
        log_turned = swap_halves(log)
        log_even[at, :] = jnp.where(low, log, log_turned)
        log_odd[at, :] = jnp.where(low, log_turned, log)
        terms_here = exact[0, :, lanes] * grads[0, :, lanes].astype(F32)
        even = jnp.sum(jnp.where(low, terms_here, 0.0), axis=1, keepdims=True)
        odd = jnp.sum(jnp.where(low, 0.0, terms_here), axis=1, keepdims=True)
        delta_even[at, :] = jnp.broadcast_to(even, (tile_rows, LANES))
        delta_odd[at, :] = jnp.broadcast_to(odd, (tile_rows, LANES))
    query_total[...] = jnp.zeros_like(query_total)

    def step(index, carried):
        key_begin = pl.multiple_of(index * tile_keys, tile_keys)
        place = pl.ds(key_begin, tile_keys)
        keys = jnp.concatenate([key_even[place, :], key_odd[place, :]], axis=0)
        values = jnp.concatenate([value_even[place, :], value_odd[place, :]], axis=0)
        copies = tile_keys // LANES
        log = jnp.concatenate([log_even[...]] * copies + [log_odd[...]] * copies, axis=1)
        delta = jnp.concatenate([delta_even[...]] * copies + [delta_odd[...]] * copies, axis=1)
        scores = dot_nt(stacked, keys) + tile_bias(
            starts[0], key_begin, row_begin, tile_rows, tile_keys
        )
        chances = jnp.exp2(scores * SCALE - log)
        grad_probs = dot_nt(grad_stacked, values)
        grad_scores = (chances * (grad_probs - delta)).astype(BF16)
        query_total[...] += dot_nn(grad_scores, keys)
        key_total[index] += dot_nn(stacked_turned, grad_scores)
        value_total[index] += dot_nn(grad_turned, chances.astype(BF16))
        return carried

    lax.fori_loop(begin, end, step, 0)
    root = 1.0 / HEAD_DIM**0.5
    for p in range(PAIRS):
        at = pl.ds(p * tile_rows, tile_rows)
        lanes = slice(p * LANES, (p + 1) * LANES)
        grad_queries[0, :, lanes] = (query_total[at, :] * root).astype(BF16)

    @pl.when(tile == pl.num_programs(0) - 1)
    def _():
        per_block = rows // tile_keys
        keep[...] = jnp.zeros_like(keep)
        send[...] = jnp.zeros_like(send)

        def block_terms(j, carried):
            for i in range(per_block):
                index = j * per_block + i
                key = key_total[index]
                value = value_total[index]
                key = key[0:HEAD_DIM, 0:tile_keys] + key[HEAD_DIM:, tile_keys:]
                value = value[0:HEAD_DIM, 0:tile_keys] + value[HEAD_DIM:, tile_keys:]
                both = jnp.concatenate([key * root, value], axis=0)
                both = both.T.astype(BF16)
                owner = block_at(place_ref, j, blocks)
                here = slice(i * tile_keys, (i + 1) * tile_keys)
                same = (owner & 1) == (place_ref[0] & 1)

                @pl.when(same)
                def _():
                    keep[owner >> 1, here, :] = both

                @pl.when(jnp.logical_not(same))
                def _():
                    send[owner >> 1, here, :] = both

            return carried

        missing = jnp.maximum(blocks - 1 - place_ref[0], 0)
        lax.fori_loop(missing, blocks, block_terms, 0)


def attention_sizes(rows, blocks, kept):
    tile_keys = 256 if rows % 256 == 0 else 128
    tile_rows = 128
    if kept and rows % 256 == 0 and blocks * rows * 256 * HEADS * 4 < 24 * 1024 * 1024:
        tile_rows = 256
    return tile_rows, tile_keys, blocks * rows // tile_keys


def attend(place, queries, keyvals, blocks):
    unused, seqs, tall, unused = keyvals.shape
    rows = tall - DOC_ROWS
    width = queries.shape[2]
    tile_rows, tile_keys, key_tiles = attention_sizes(rows, blocks, True)
    stack = PAIRS * tile_rows
    keys = blocks * rows
    row_spec = lambda lanes: pl.BlockSpec((1, tile_rows, lanes), lambda s, t, *_: (s, t, 0))
    wide = lambda dtype: jax.ShapeDtypeStruct((seqs, rows, width), dtype)
    return pl.pallas_call(
        functools.partial(
            attend_kernel, blocks=blocks, tile_rows=tile_rows, tile_keys=tile_keys
        ),
        grid_spec=pltpu.PrefetchScalarGridSpec(
            num_scalar_prefetch=1,
            grid=(seqs, rows // tile_rows),
            in_specs=[
                row_spec(width),
                pl.BlockSpec((keyvals.shape[0], 1, tall, LANES), lambda s, t, *_: (0, s, 0, 0)),
            ],
            out_specs=[row_spec(LANES)] + [row_spec(width)] * 3,
            scratch_shapes=[
                pltpu.VMEM((keys, LANES), BF16),
                pltpu.VMEM((keys, LANES), BF16),
                pltpu.VMEM((keys, 2 * LANES), BF16),
                pltpu.VMEM((keys, 2 * LANES), BF16),
                pltpu.VMEM((key_tiles, stack, 2 * tile_keys), F32),
                pltpu.VMEM((stack, 2 * LANES), F32),
                pltpu.VMEM((stack, 2 * LANES), F32),
            ],
        ),
        out_shape=[
            jax.ShapeDtypeStruct((seqs, rows, LANES), jnp.int32),
            wide(F32),
            wide(BF16),
            wide(F32),
        ],
        compiler_params=params("arbitrary", "arbitrary"),
        cost_estimate=weight(),
        name="attend",
    )(place, queries, keyvals)


def attend_back(
    seq, place, queries, starts, exact, logs, grads, keyvals, blocks
):
    seqs, rows, width = queries.shape
    ctx_size = keyvals.shape[0]
    tile_rows, tile_keys, key_tiles = attention_sizes(rows, blocks, False)
    stack = PAIRS * tile_rows
    keys = blocks * rows
    row_spec = lambda lanes: pl.BlockSpec((1, tile_rows, lanes), lambda t, *_: (seq, t, 0))
    return pl.pallas_call(
        functools.partial(
            attend_back_kernel, seq=seq, blocks=blocks, tile_rows=tile_rows, tile_keys=tile_keys
        ),
        grid_spec=pltpu.PrefetchScalarGridSpec(
            num_scalar_prefetch=1,
            grid=(rows // tile_rows,),
            in_specs=[row_spec(width), row_spec(LANES)]
            + [row_spec(width)] * 3
            + [pl.BlockSpec((ctx_size, 1, keyvals.shape[2], LANES), lambda t, *_: (0, seq, 0, 0))],
            out_specs=[
                pl.BlockSpec((1, tile_rows, width), lambda t, *_: (0, t, 0)),
            ]
            + [pl.BlockSpec((ctx_size // 2, rows, LANES), lambda t, *_: (0, 0, 0))] * 2,
            scratch_shapes=[pltpu.VMEM((keys, LANES), BF16)] * 4
            + [pltpu.VMEM((key_tiles, LANES, 2 * tile_keys), F32)] * 2
            + [pltpu.VMEM((stack, LANES), F32)] * 5,
        ),
        out_shape=[
            jax.ShapeDtypeStruct((1, rows, width), BF16),
        ]
        + [jax.ShapeDtypeStruct((ctx_size // 2, rows, LANES), BF16)] * 2,
        compiler_params=params("arbitrary"),
        cost_estimate=weight(),
        name="attend_back",
    )(place, queries, starts, exact, logs, grads, keyvals)


def round_up(count, unit):
    return -(-count // unit) * unit


def mixing_rows(width, pieces, ctx_size):
    unit = 8 * ctx_size
    tall = 2 * width + width // pieces * (width // TILE)
    return round_up(tall + width // LANES, unit) - 2 * width


def message_of(messages, s):
    return messages[s & 1], s >> 1


def split_out(spot, pieces, source, messages, first_row=0):
    height, lanes = source.shape[0] // pieces, messages[0].shape[2]
    across = min(lanes, source.shape[1])
    for s in range(pieces):
        out, at = message_of(messages, s)
        begin = pl.multiple_of((spot ^ s) * height, height)
        for g in range(source.shape[1] // across):
            row = first_row + g * height
            out[at, row : row + height, 0:across] = source[
                pl.ds(begin, height), g * lanes : g * lanes + across
            ].astype(BF16)


def put_vector(pieces, vector, messages, first_row, begin):
    height, lanes = messages[0].shape[1] - first_row, messages[0].shape[2]
    count = vector.shape[1] // LANES
    row = lax.broadcasted_iota(jnp.int32, (height, LANES), 0)
    block = jnp.zeros((height, LANES), F32)
    for i in range(count):
        block = jnp.where(row == i, vector[:, i * LANES : (i + 1) * LANES], block)
    for s in range(pieces):
        out, at = message_of(messages, s)
        out[at, first_row:, begin : begin + LANES] = block.astype(BF16)
        if begin == 0:
            out[at, first_row:, LANES:] = jnp.zeros((height, lanes - LANES), BF16)


def feed_kernel(spot_ref, *refs, pieces, part, first, last, names, early, late):
    use = dict(zip(names, refs))
    spot = spot_ref[0]
    step = pl.program_id(0)
    steps = len(part) * (pieces // 2)
    cotangent = use["cotangent"]
    reduced, grads, scaled, hidden = use["reduced"], use["grads"], use["scaled"], use["hidden"]
    up_tile, down_tile, up_sems, down_sems = (
        use["up_tile"], use["down_tile"], use["up_sems"], use["down_sems"]
    )
    rows, width = cotangent.shape
    height = width // pieces
    groups = width // TILE

    def messages_of(chunk):
        return use[f"keep{chunk}"], use[f"send{chunk}"]

    def owners(n):
        chunk, at = divmod(n, pieces // 2)
        return part[chunk], (2 * at, 2 * at + 1)

    def copies(n):
        chunk, pair = owners(n)
        for h, s in enumerate(pair):
            source = pl.multiple_of(width + (spot ^ s) * height, height)
            for r in range(pieces):
                row = pl.multiple_of((spot ^ r) * height, height)
                yield pltpu.make_async_copy(
                    use[f"message{chunk}_{r}"].at[pl.ds(source, height), :],
                    up_tile.at[n, pl.ds(row, height), pl.ds(h * TILE, TILE)],
                    up_sems.at[n, h, r],
                )
            for g in range(groups):
                yield pltpu.make_async_copy(
                    use[f"message{chunk}_{s}"].at[pl.ds(g * TILE, TILE), :],
                    down_tile.at[n, pl.ds(h * TILE, TILE), pl.ds(g * TILE, TILE)],
                    down_sems.at[n, h, g],
                )

    def beside(kind, names):
        for name in names:
            pair = use[f"{name}_far"], use[name]
            source, target = pair if kind == "in" else pair[::-1]
            yield pltpu.make_async_copy(source, target, use[f"{name}_sem"])

    @pl.when(step == 0)
    def _():
        for n in range(steps):
            for one in copies(n):
                one.start()
        for one in beside("in", late):
            one.start()
        if first:

            def begin(here):
                values = use["tokens"][here, :].astype(F32) + hidden[here, :]
                hidden[here, :] = values
                normed, unused = normalize(values)
                scaled[here, :] = (normed * use["gain"][...]).astype(BF16)

            place_rows(spot, [use[f"mixing{r}"] for r in range(pieces)], use["mixing_all"])
            hidden[...] = dot_nn(use["attended"][...], use["mixing_all"][...])
            over_rows(rows, begin)
            for one in beside("out", ("hidden", "scaled")):
                one.start()

    if first:

        @pl.when(step == pieces // 2)
        def _():
            for one in beside("out", ("keep0", "send0")):
                one.start()

        @pl.when(step == steps - 1)
        def _():
            for one in beside("out", early):
                one.wait()

    for n in range(steps):

        @pl.when(step == n)
        def _():
            for one in copies(n):
                one.wait()

    up = up_tile[step]
    down = down_tile[step]
    upper = dot_nn(scaled[...], up)
    grad_act = dot_nt(cotangent[...], down)
    square = upper * upper
    inner = jnp.tanh(GELU_ROOT * (upper + GELU_CUBE * upper * square))
    half = 0.5 * (1.0 + inner)
    slope = half + 0.5 * upper * (1.0 - inner * inner) * (
        GELU_ROOT * (1.0 + 3.0 * GELU_CUBE * square)
    )
    active = (upper * half).astype(BF16)
    grad_upper = (grad_act * slope).astype(BF16)
    reduced_here = dot_nn(active, down)
    grads_here = dot_nt(grad_upper, up)

    @pl.when(step == 0)
    def _():
        reduced[...] = reduced_here
        grads[...] = grads_here

    @pl.when(step > 0)
    def _():
        reduced[...] += reduced_here
        grads[...] += grads_here

    down_term = dot_tn(active, cotangent[...]).astype(BF16)
    up_term = use["up_term"]
    up_term[...] = dot_tn(scaled[...], grad_upper)
    for n in range(steps):

        @pl.when(step == n)
        def _():
            chunk, pair = owners(n)
            messages = messages_of(chunk)
            for h, s in enumerate(pair):
                out, at = message_of(messages, s)
                for g in range(groups):
                    column = slice(g * TILE, (g + 1) * TILE)
                    part_here = down_term[h * TILE : (h + 1) * TILE, column]
                    if chunk == 1:
                        out[0, at, column, :] = part_here
                    else:
                        out[at, column, :] = part_here
            for s in range(pieces):
                out, at = message_of(messages, s)
                begin = pl.multiple_of((spot ^ s) * height, height)
                for h, t in enumerate(pair):
                    part_here = up_term[
                        pl.ds(begin, height), h * TILE : (h + 1) * TILE
                    ].astype(BF16)
                    row = pl.multiple_of((spot ^ t) * height, height)
                    if chunk == 1:
                        out[1, at, pl.ds(row, height), :] = part_here
                    else:
                        out[at, pl.ds(width + row, height), :] = part_here

    if last:

        @pl.when(step == steps - 1)
        def _():
            sums, grad_mixed, term = use["sums"], use["grad_mixed"], use["term"]
            for one in beside("in", late):
                one.wait()
            sums[...] = jnp.zeros_like(sums)
            place_rows(spot, [use[f"mixing{r}"] for r in range(pieces)], use["mixing_all"])

            def end(here):
                values = hidden[here, :]
                total = use["reduced_in"][here, :] + reduced[here, :]
                use["layer_out"][here, :] = (values + total).astype(BF16)
                normed, inverse = normalize(values)
                grad = use["grads_in"][here, :] + grads[here, :]
                sums[...] += jnp.sum((grad * normed).reshape(STEP // 8, 8, width), axis=0)
                grad_hidden = cotangent[here, :].astype(F32) + norm_back(
                    grad * use["gain"][...], normed, inverse
                )
                use["grad_hidden"][here, :] = grad_hidden
                grad_mixed[here, :] = grad_hidden.astype(BF16)

            over_rows(rows, end)
            use["grad_attended"][...] = dot_nt(grad_mixed[...], use["mixing_all"][...]).astype(BF16)
            term[...] = dot_tn(use["attended"][...], grad_mixed[...])
            tall = 2 * width
            messages = messages_of(part[-1])
            split_out(spot, pieces, term, messages, tall)
            put_vector(
                pieces,
                jnp.sum(sums[...], axis=0, keepdims=True),
                messages,
                tall + height * groups,
                0,
            )


def feed_stage(spot, arrays, gathered, mixing_pieces, part, chunks, ctx_size):
    first, last = part[0] == 0, part[-1] == chunks - 1
    rows, width = arrays["cotangent"].shape
    pieces = len(gathered[part[0]])
    wide = jax.ShapeDtypeStruct((rows, width), F32)
    narrow = jax.ShapeDtypeStruct((rows, width), BF16)
    inputs, outputs, scratch = {}, {}, {}
    for chunk in part:
        more = mixing_rows(width, pieces, ctx_size) if chunk == chunks - 1 else 0
        message = jax.ShapeDtypeStruct((pieces // 2, 2 * width + more, TILE), BF16)
        if chunk == 1:
            message = jax.ShapeDtypeStruct((2, pieces // 2, width, TILE), BF16)
        outputs[f"keep{chunk}"] = outputs[f"send{chunk}"] = message
    inputs["cotangent"] = arrays["cotangent"]
    for chunk in part:
        for r in range(pieces):
            inputs[f"message{chunk}_{r}"] = gathered[chunk][r]
    for r in range(pieces):
        inputs[f"mixing{r}"] = mixing_pieces[r]
    scratch["mixing_all"] = pltpu.VMEM((width, width), BF16)
    early, late = (), ()
    if first:
        for name in ("attended", "tokens", "gain"):
            inputs[name] = arrays[name]
        outputs.update(hidden=wide, scaled=narrow, reduced=wide, grads=wide)
        early = ("hidden", "scaled", "keep0", "send0")
    if last:
        for name in ("gain", "scaled"):
            inputs[name] = arrays[name]
        late = ("attended", "hidden", "reduced_in", "grads_in")
        for name in late:
            inputs[f"{name}_far"] = arrays[name.removesuffix("_in")]
        outputs.update(layer_out=narrow, grad_hidden=wide, grad_attended=narrow)
        scratch.update(
            reduced=pltpu.VMEM((rows, width), F32),
            grads=pltpu.VMEM((rows, width), F32),
            sums=pltpu.VMEM((8, width), F32),
            grad_mixed=pltpu.VMEM((rows, width), BF16),
            term=pltpu.VMEM((width, width), F32),
        )
    for name in early:
        scratch[name] = pltpu.VMEM(outputs[name].shape, outputs[name].dtype)
    for name in late:
        scratch[name] = pltpu.VMEM(inputs[f"{name}_far"].shape, inputs[f"{name}_far"].dtype)
    for name in early + late:
        scratch[f"{name}_sem"] = pltpu.SemaphoreType.DMA
    outputs = {f"{name}_far" if name in early else name: one for name, one in outputs.items()}
    steps = len(part) * (pieces // 2)
    scratch.update(
        up_tile=pltpu.VMEM((steps, width, 2 * TILE), BF16),
        down_tile=pltpu.VMEM((steps, 2 * TILE, width), BF16),
        up_sems=pltpu.SemaphoreType.DMA((steps, 2, pieces)),
        down_sems=pltpu.SemaphoreType.DMA((steps, 2, width // TILE)),
        up_term=pltpu.VMEM((width, 2 * TILE), F32),
    )

    def spec(name, array):
        if name[:7] == "message" or name[-4:] == "_far":
            return pl.BlockSpec(memory_space=pl.ANY)
        once = pl.Buffered(1)
        rank = len(array.shape)
        return pl.BlockSpec(array.shape, lambda i, *_: (0,) * rank, pipeline_mode=once)

    results = pl.pallas_call(
        functools.partial(
            feed_kernel,
            pieces=pieces,
            part=part,
            first=first,
            last=last,
            names=(*inputs, *outputs, *scratch),
            early=early,
            late=late,
        ),
        grid_spec=pltpu.PrefetchScalarGridSpec(
            num_scalar_prefetch=1,
            grid=(steps,),
            in_specs=[spec(*one) for one in inputs.items()],
            out_specs=[spec(*one) for one in outputs.items()],
            scratch_shapes=list(scratch.values()),
        ),
        out_shape=list(outputs.values()),
        compiler_params=params("arbitrary"),
        cost_estimate=weight(),
        name=f"feed{part[0]}",
    )(spot, *inputs.values())
    return {**arrays, **dict(zip((name.removesuffix("_far") for name in outputs), results))}


def query_kernel(spot_ref, scaled, *rest, pieces, seqs):
    grad_queries, weights = rest[:seqs], rest[seqs : seqs + pieces]
    grad_out, keep_out, send_out, weight, term = rest[seqs + pieces :]
    spot = spot_ref[0]
    rows = scaled.shape[0] // seqs
    place_rows(spot, weights, weight)
    for i, one in enumerate(grad_queries):
        here = slice(i * rows, (i + 1) * rows)
        part = dot_tn(scaled[here, :], one[...])
        term[...] = part if i == 0 else term[...] + part
        grad_out[here, :] = dot_nt(one[...], weight[...])
    split_out(spot, pieces, term, (keep_out, send_out))


def query_stage(spot, scaled, grad_queries, weights, ctx_size):
    rows, width = scaled.shape
    pieces = len(weights)
    tall = round_up(width // pieces * (width // TILE), 8 * ctx_size)
    message = jax.ShapeDtypeStruct((pieces // 2, tall, TILE), BF16)
    outs = [jax.ShapeDtypeStruct((rows, width), F32), message, message]
    whole = lambda one: pl.BlockSpec(one.shape, lambda i, *_: (0,) * len(one.shape))
    return pl.pallas_call(
        functools.partial(query_kernel, pieces=pieces, seqs=len(grad_queries)),
        grid_spec=pltpu.PrefetchScalarGridSpec(
            num_scalar_prefetch=1,
            grid=(1,),
            in_specs=[whole(scaled)]
            + [whole(one) for one in grad_queries]
            + [pl.BlockSpec((width // pieces, width), lambda i, *_: (0, 0))] * pieces,
            out_specs=[whole(one) for one in outs],
            scratch_shapes=[
                pltpu.VMEM((width, width), BF16),
                pltpu.VMEM((width, width), F32),
            ],
        ),
        out_shape=outs,
        compiler_params=params(),
        cost_estimate=weight(),
        name="query_grad",
    )(spot, scaled, *grad_queries, *weights)


def last_kernel(spot_ref, tokens, gain, scaled, arrived, grad_scaled, grad_hidden, *rest, pieces):
    weights = rest[:pieces]
    input_grad, keep_out, send_out, weight, sums, term, grad_shared = rest[pieces:]
    spot = spot_ref[0]
    width = tokens.shape[1]
    place_rows(spot, weights, weight)
    sums[...] = jnp.zeros_like(sums)
    places, seqs, here, unused = arrived.shape
    for i in range(seqs):
        total = arrived[0, i].astype(F32)
        for j in range(1, places):
            total = total + arrived[j, i].astype(F32)
        grad_shared[i * here : (i + 1) * here, :] = total.astype(BF16)
    term[...] = dot_tn(scaled[...], grad_shared[...])
    split_out(spot, pieces, term, (keep_out, send_out))

    def run(rows):
        normed, inverse = normalize(tokens[rows, :].astype(F32))
        grad = grad_scaled[rows, :] + dot_nt(grad_shared[rows, :], weight[...])
        sums[...] += jnp.sum((grad * normed).reshape(STEP // 8, 8, width), axis=0)
        input_grad[rows, :] = grad_hidden[rows, :] + norm_back(
            grad * gain[...], normed, inverse
        )

    over_rows(tokens.shape[0], run)
    put_vector(
        pieces, jnp.sum(sums[...], axis=0, keepdims=True), (keep_out, send_out), 0, LANES
    )


def last_stage(spot, tokens, gain, scaled, arrived, grad_scaled, grad_hidden, weights, places):
    rows, width = tokens.shape
    pieces = len(weights)
    message = jax.ShapeDtypeStruct(
        (pieces // 2, round_up(width // pieces, 8 * places), 2 * LANES), BF16
    )
    return pl.pallas_call(
        functools.partial(last_kernel, pieces=pieces),
        grid_spec=pltpu.PrefetchScalarGridSpec(
            num_scalar_prefetch=1,
            grid=(),
            in_specs=[pl.BlockSpec(memory_space=pltpu.VMEM)] * (6 + pieces),
            out_specs=[pl.BlockSpec(memory_space=pltpu.VMEM)] * 3,
            scratch_shapes=[
                pltpu.VMEM((width, LANES), BF16),
                pltpu.VMEM((8, width), F32),
                pltpu.VMEM((width, LANES), F32),
                pltpu.VMEM((rows, LANES), BF16),
            ],
        ),
        out_shape=[jax.ShapeDtypeStruct((rows, width), F32), message, message],
        compiler_params=params(),
        cost_estimate=weight(),
        name="last",
    )(spot, tokens, gain, scaled, arrived, grad_scaled, grad_hidden, *weights)


def put_halves(whole, own, other, at, place, first):
    deep, unused, rows, unused = own.shape
    low = place & 1
    for half, x in ((own, low), (other, 1 - low)):
        for k in range(deep):
            begin = pl.multiple_of((x * deep + (first ^ k)) * rows, 8)
            whole[pl.ds(begin, rows), :] = half[k, at].astype(F32)


def early_kernel(place_ref, own, other, down_out, up_out, whole, *, chunks, pieces):
    width = down_out.shape[1]
    height = width // pieces
    place = place_ref[0]
    for chunk in range(own.shape[1]):
        put_halves(whole, own, other, chunk, place, place >> 1)
        for g in range(width // TILE):
            down_out[chunk * TILE : (chunk + 1) * TILE, g * TILE : (g + 1) * TILE] = whole[
                g * TILE : (g + 1) * TILE, :
            ]
        for j in range(pieces):
            row, column = width + j * height, (j * chunks + chunk) * TILE
            up_out[:, column : column + TILE] = whole[row : row + height, :]


def early_stage(place, own, other, chunks, pieces, width):
    shape = lambda *dims: jax.ShapeDtypeStruct(dims, F32)
    vmem = pl.BlockSpec(memory_space=pltpu.VMEM)
    return pl.pallas_call(
        functools.partial(early_kernel, chunks=chunks, pieces=pieces),
        grid_spec=pltpu.PrefetchScalarGridSpec(
            num_scalar_prefetch=1,
            grid=(),
            in_specs=[vmem] * 2,
            out_specs=[vmem] * 2,
            scratch_shapes=[pltpu.VMEM((2 * width, TILE), F32)],
        ),
        out_shape=[shape(chunks * TILE, width), shape(width // pieces, pieces * chunks * TILE)],
        compiler_params=params(),
        cost_estimate=weight(),
        name="early_sums",
    )(place, own, other)


def final_kernel(
    place_ref, spot_ref, own, other, late, down_in, up_in,
    down_out, up_out, mixing_out, query_out, shared_out, first_out, second_out,
    whole, down_part, up_part, sems,
    *, chunks, pieces, query_rows,
):
    height, width = mixing_out.shape
    groups = width // TILE
    place = place_ref[0]

    def columns(out, first_row, rows):
        for g in range(groups):
            row = first_row + g * rows
            out[:, g * TILE : (g + 1) * TILE] = whole[row : row + rows, :]

    def load(begin, rows):
        for c in range(late.shape[0]):
            whole[c * rows : (c + 1) * rows, :] = late[c, begin : begin + rows, :].astype(F32)

    def own_gain(out, row, begin):
        lines = [
            whole[row + i : row + i + 1, begin : begin + LANES] for i in range(width // LANES)
        ]
        vector = jnp.concatenate(lines, axis=1)
        total = jnp.zeros((1, height), F32)
        for o in range(pieces):
            mine = vector[:, o * height : (o + 1) * height]
            total = jnp.where(spot_ref[0] == o, mine, total)
        out[...] = total

    put_halves(whole, own, other, 0, place, place >> 1)
    columns(down_part, 0, TILE)
    copies = [
        pltpu.make_async_copy(
            down_part, down_out.at[pl.ds((chunks - 1) * TILE, TILE), :], sems.at[pieces]
        )
    ]
    for j in range(pieces):
        up_part[j] = whole[width + j * height : width + (j + 1) * height, :]
        column = (j * chunks + chunks - 1) * TILE
        copies.append(
            pltpu.make_async_copy(up_part.at[j], up_out.at[:, pl.ds(column, TILE)], sems.at[j])
        )
    for one in copies:
        one.start()
    columns(mixing_out, 2 * width, height)
    row = 2 * width + groups * height
    own_gain(second_out, row, 0)
    load(0, query_rows)
    columns(query_out, 0, height)
    load(query_rows, late.shape[1] - query_rows)
    shared_out[...] = whole[0:height, 0:LANES]
    own_gain(first_out, 0, LANES)
    for one in copies:
        one.wait()


def final_stage(place, spot, own, other, late, down, up, query_rows, chunks, pieces, width):
    height = width // pieces
    shape = lambda *dims: jax.ShapeDtypeStruct(dims, F32)
    tallest = max(2 * own.shape[0] * own.shape[2], late.shape[0] * late.shape[1])
    vmem, anywhere = pl.BlockSpec(memory_space=pltpu.VMEM), pl.BlockSpec(memory_space=pl.ANY)
    return pl.pallas_call(
        functools.partial(
            final_kernel, chunks=chunks, pieces=pieces, query_rows=query_rows
        ),
        grid_spec=pltpu.PrefetchScalarGridSpec(
            num_scalar_prefetch=2,
            grid=(),
            in_specs=[vmem] * 3 + [anywhere] * 2,
            out_specs=[anywhere] * 2 + [vmem] * 5,
            scratch_shapes=[
                pltpu.VMEM((tallest, TILE), F32),
                pltpu.VMEM((TILE, width), F32),
                pltpu.VMEM((pieces, height, TILE), F32),
                pltpu.SemaphoreType.DMA((pieces + 1,)),
            ],
        ),
        out_shape=[
            shape(*down.shape),
            shape(*up.shape),
            shape(height, width),
            shape(height, width),
            shape(height, LANES),
            shape(1, height),
            shape(1, height),
        ],
        input_output_aliases={5: 0, 6: 1},
        compiler_params=params(),
        cost_estimate=weight(),
        name="final",
    )(place, spot, own, other, late, down, up)


def swap(values, axis, size, mask):
    return lax.ppermute(values, axis, [(i, i ^ mask) for i in range(size)])


class Gather:
    def __init__(self, piece, size):
        self.size, self.own = size, piece
        self.far = swap(piece, "wt", size, 2)
        self.near = swap(piece, "wt", size, 1)

    def finish(self):
        return [self.own, self.near, self.far, swap(self.far, "wt", self.size, 1)]


def own_order(values, spot, size):
    mask = 1
    while mask < size:
        split = values.reshape((size // (2 * mask), 2, mask) + values.shape[1:])
        split = jnp.where((spot & mask) != 0, split[:, ::-1], split)
        values = split.reshape(values.shape)
        mask *= 2
    return values


class Transfer:
    def __init__(self, held, sent, routes):
        self.held, self.sent, self.routes, self.coming = held, sent, routes, []

    def launch(self):
        if self.sent:
            self.coming = [swap(one, *route) for one, route in zip(self.sent, self.routes)]
            self.sent = []

    def add(self, pick):
        return pick(self.held).astype(F32) + pick(self.coming[0]).astype(F32)


class Reduction(Transfer):
    def __init__(self, keep, send, place, sizes):
        self.wt_size, self.ctx_size = sizes
        self.groups = self.ctx_size // 2
        self.low, self.high = place & 1, place >> 1
        *outer, rows, self.lanes = keep.shape
        self.rows = rows if len(outer) == 1 else 2 * rows
        inner = (self.groups, self.rows // self.ctx_size, self.lanes)
        split = (*outer, *inner) if len(outer) == 2 else (*outer, 2, *inner)
        super().__init__(
            keep.reshape(split), [send.reshape(split)], [("wt", self.wt_size, 1)]
        )

    def y(self, cuts=()):
        edges = (0, *cuts, self.rows // self.ctx_size)
        self.later = [
            self.add(lambda v: v[1][..., begin:end, :]).astype(BF16)
            for begin, end in zip(edges, edges[1:])
        ]
        self.held = self.add(lambda v: v[0]).astype(BF16)
        self.sent = [self.later.pop(0)]
        self.routes = [("wt", self.wt_size, 2)]

    def y_more(self):
        self.before, self.sent = self.coming, [self.later.pop(0)]

    def y_joined(self):
        self.coming = [jnp.concatenate(self.before + self.coming, axis=-2)]

    def x(self):
        half = lambda x: self.add(lambda v: lax.dynamic_index_in_dim(v, x, 0, False)).astype(BF16)
        self.held, self.sent = half(self.low), [half(1 - self.low)]
        self.routes = [("ctx", self.ctx_size, 1)]

    def far(self):
        return [("ctx", self.ctx_size, 2 * k) for k in range(1, self.groups)]

    def z(self, *others):
        def part(k):
            pick = lambda v: lax.dynamic_index_in_dim(v, self.high ^ k, 0, False)
            return jnp.stack([one.add(pick) for one in (self, *others)]).astype(BF16)

        self.sent = [part(k) for k in range(1, self.groups)]
        self.held = part(0)
        self.routes = self.far()

    def total(self):
        parts = [self.held.astype(F32)] + [one.astype(F32) for one in self.coming]
        while len(parts) > 1:
            parts = [parts[i] + parts[i + 1] for i in range(0, len(parts), 2)]
        return parts[0].astype(BF16)

    def z_back(self):
        self.held = self.total()
        self.sent = [self.held] * (self.groups - 1)

    def x_back(self):
        self.held = jnp.stack([self.held] + self.coming)
        self.sent = [self.held]
        self.routes = [("ctx", self.ctx_size, 1)]

    def everywhere(self):
        return self.add(lambda v: v).astype(BF16).reshape(
            self.ctx_size, self.rows // self.ctx_size, self.lanes
        )


def tie(main, *reductions, came=()):
    state = [(one.held, one.sent) for one in reductions]
    main, state, coming = lax.optimization_barrier((main, state, [one.coming for one in came]))
    for one, (held, sent) in zip(reductions, state):
        one.held, one.sent = held, sent
    for one, values in zip(came, coming):
        one.coming = values
    for one in reductions:
        one.launch()
    return main


def body(
    tokens,
    documents,
    first_gain,
    query_weight,
    shared_weight,
    mixing_weight,
    second_gain,
    up_weight,
    down_weight,
    cotangent,
    *,
    wt_size,
    ctx_size,
):
    sizes = (wt_size, ctx_size)
    seqs, rows, width = tokens.shape
    count = seqs * rows
    spot_index = lax.axis_index("wt")
    place = lax.axis_index("ctx")
    spot = spot_index.astype(jnp.int32).reshape(1)
    length = ctx_size * rows
    doc_most = length * 5 // 8
    before = min(ctx_size - 1, -(-(doc_most - 1) // rows))
    blocks = before + 1
    height = width // wt_size
    chunks = up_weight.shape[1] // wt_size // TILE

    gain_rows = -(-height // LANES)
    pad = lambda gain: jnp.pad(gain, (0, gain_rows * LANES - height)).reshape(gain_rows, LANES)
    small = jnp.concatenate([shared_weight, pad(first_gain), pad(second_gain)], axis=0)
    small = jnp.pad(small, ((0, -small.shape[0] % 16), (0, 0)))
    small_pieces = Gather(small, wt_size).finish()
    query_gather = Gather(query_weight, wt_size)

    gains = jnp.stack([one[height : height + 2 * gain_rows] for one in small_pieces])
    gains = gains.reshape(wt_size, 2, gain_rows * LANES)[:, :, :height].astype(F32)
    gains = own_order(gains, spot_index, wt_size)
    gain_one = gains[:, 0].reshape(1, width)
    gain_two = gains[:, 1].reshape(1, width)

    inputs = tokens.reshape(count, width)
    doc_lines = documents.astype(BF16).reshape(seqs, rows // LANES, LANES)
    scaled_one, shared = first_stage(spot, inputs, gain_one, doc_lines, small_pieces, ctx_size)
    shared, query_gather.far, mixing_weight, *packed = lax.optimization_barrier(
        (shared, query_gather.far, mixing_weight, up_weight, down_weight)
    )
    keyvals = lax.all_to_all(shared, "ctx", 0, 0).reshape(ctx_size, seqs, rows + DOC_ROWS, LANES)
    packed = list(pack_stage(*packed, chunks, wt_size))
    gathers = [Gather(packed[0], wt_size)]
    mixing_gather = Gather(mixing_weight, wt_size)
    query_pieces = query_gather.finish()
    place_one = place.astype(jnp.int32).reshape(1)

    queries = project(spot, scaled_one, query_pieces).reshape(seqs, rows, width)
    keyvals, gathers[0].far, mixing_gather.far, queries, packed[1:] = lax.optimization_barrier(
        (keyvals, gathers[0].far, mixing_gather.far, queries, packed[1:])
    )
    gathered = [gathers[0].finish()]
    mixing_pieces = mixing_gather.finish()
    gathers.append(Gather(packed[1], wt_size))
    starts, exact, attended, logs = attend(place_one, queries, keyvals, blocks)
    attended, gathers[1].far, packed[2:] = lax.optimization_barrier(
        (attended, gathers[1].far, packed[2:])
    )
    gathered.append(gathers[1].finish())
    gathers += [Gather(one, wt_size) for one in packed[2:]]

    arrays = {
        "attended": attended.reshape(count, width),
        "tokens": inputs,
        "gain": gain_two,
        "cotangent": cotangent.reshape(count, width),
    }
    feed = lambda arrays, part: feed_stage(
        spot, arrays, gathered, mixing_pieces, part, chunks, ctx_size
    )
    arrays = feed(arrays, (0, 1))
    zero, one = (
        Reduction(arrays[f"keep{chunk}"], arrays[f"send{chunk}"], place, sizes) for chunk in (0, 1)
    )
    arrays, gathers[-1].far = tie((arrays, gathers[-1].far), zero, one)
    gathered.append(gathers[-1].finish())
    arrays = tie(arrays, zero, one, came=[zero])
    zero.y()
    arrays = tie(arrays, zero, one, came=[one])
    one.x()
    arrays = tie(arrays, zero, one)
    arrays = feed(arrays, (2,))
    two = Reduction(arrays["keep2"], arrays["send2"], place, sizes)
    grad_attended = tie(arrays["grad_attended"], zero, one, two, came=[zero, one])
    zero.x()
    one.y()
    grad_attended = tie(grad_attended, zero, one, two, came=[two])
    two.y([round_up(two.rows // ctx_size // 3, 8)])
    grad_attended = tie(grad_attended, zero, one, two).reshape(seqs, rows, width)
    grad_queries, terms = [], []
    for seq in range(seqs):
        part, keep, send = attend_back(
            seq, place_one, queries, starts, exact, logs, grad_attended, keyvals, blocks
        )
        came = [zero, one, two] if seq == 0 else [zero, two]
        term = Transfer(keep, [send], [("ctx", ctx_size, 1)])
        part, grad_attended = tie((part, grad_attended), *came, term, *terms, came=came + terms)
        grad_queries.append(part[0])
        terms.append(term)
        if seq == 0:
            zero.z(one)
            two.y_more()
            grad_attended = tie(grad_attended, zero, two)
    two.y_joined()
    two.x()
    zero.z_back()
    grad_queries = tie(grad_queries, zero, two)
    grad_scaled, keep, send = query_stage(spot, scaled_one, grad_queries, query_pieces, ctx_size)
    query = Reduction(keep, send, place, sizes)
    grad_scaled = tie(grad_scaled, zero, query, *terms, came=terms[1:])
    arriving = jnp.stack([one.add(lambda v: v).astype(BF16) for one in terms], axis=1)
    arriving, grad_scaled = tie((arriving, grad_scaled), query)
    arriving = lax.all_to_all(
        arriving,
        "ctx",
        0,
        0,
        axis_index_groups=[list(range(x, ctx_size, 2)) for x in range(2)],
    )
    query.y()
    grad_scaled = tie(grad_scaled, query)
    grad_scaled = tie(grad_scaled, two, came=[two])
    two.z()
    grad_scaled, arriving = tie((grad_scaled, arriving), two)
    input_grad, keep, send = last_stage(
        spot, inputs, gain_one, scaled_one, arriving, grad_scaled, arrays["grad_hidden"], small_pieces, ctx_size
    )
    shared = Reduction(keep, send, place, sizes)
    input_grad = tie(input_grad, zero, two, shared, query, came=[two, query])
    two.z_back()
    input_grad = tie(input_grad, two)
    input_grad = tie(input_grad, shared, query, came=[shared])
    shared.y()
    input_grad = tie(input_grad, shared)
    zero.x_back()
    input_grad = tie(input_grad, zero)
    input_grad = tie(input_grad, shared, query, came=[shared])
    late = jnp.concatenate([query.everywhere(), shared.everywhere()], axis=1)
    late = lax.all_to_all(late, "ctx", 0, 0)
    two.x_back()
    input_grad = tie(input_grad, two)
    late = jnp.sum(late.astype(F32), axis=0).astype(BF16)
    late = lax.all_to_all(jnp.broadcast_to(late, (ctx_size,) + late.shape), "ctx", 0, 0)
    two.launch()
    down_grad, up_grad = early_stage(
        place_one, zero.held, zero.coming[0], chunks, wt_size, width
    )
    down_grad, up_grad, two.coming = lax.optimization_barrier((down_grad, up_grad, two.coming))
    down_grad, up_grad, mixing_grad, query_grad, shared_grad, first_grad, second_grad = final_stage(
        place_one,
        spot,
        two.held,
        two.coming[0],
        late,
        down_grad,
        up_grad,
        query.rows // ctx_size,
        chunks,
        wt_size,
        width,
    )
    return (
        arrays["layer_out"].reshape(seqs, rows, width),
        input_grad.reshape(seqs, rows, width),
        first_grad.reshape(height),
        query_grad,
        shared_grad,
        mixing_grad,
        second_grad.reshape(height),
        up_grad,
        down_grad,
    )


def solution(mesh):
    in_specs = (
        P("wt", "ctx", None),
        P("wt", "ctx"),
        P("wt"),
        P("wt", None),
        P("wt", None),
        P("wt", None),
        P("wt"),
        P("wt", None),
        P("wt", None),
        P("wt", "ctx", None),
    )
    out_specs = (
        P("wt", "ctx", None),
        P("wt", "ctx", None),
        P("wt"),
        P("wt", None),
        P("wt", None),
        P("wt", None),
        P("wt"),
        P("wt", None),
        P("wt", None),
    )
    run = functools.partial(body, wt_size=mesh.shape["wt"], ctx_size=mesh.shape["ctx"])
    return jax.shard_map(run, mesh=mesh, in_specs=in_specs, out_specs=out_specs, check_vma=False)
```
